32 devices in a mesh: dp: 4 (over z), fsdp: 8 (over y, x, core).
Axes of the slice: x: 2, y: 2, z: 4, core: 2. Of those that a mesh axis runs over, the one named last changes fastest.
Arguments:
- tokens: bfloat16 [32, 2, 640, 512], P(('dp', 'fsdp')), may hold values from -6 to 6
- parents: int32 [8, 2, 16], replicated, may hold values from -1 to 4, as said below
- norm1_gain: float32 [512], P('fsdp'), may hold values from 0.25 to 1.75
- norm1_bias: float32 [512], P('fsdp'), may hold values from -1.75 to 1.75
- w_query: float32 [512, 512], P('fsdp'), may hold values from -0.25 to 0.25
- w_key: float32 [512, 512], P('fsdp'), may hold values from -0.25 to 0.25
- w_value: float32 [512, 512], P('fsdp'), may hold values from -0.25 to 0.25
- w_output: float32 [512, 512], P('fsdp'), may hold values from -0.75 to 0.75
- output_bias: float32 [512], P('fsdp'), may hold values from -1.75 to 1.75
- norm2_gain: float32 [512], P('fsdp'), may hold values from 0.25 to 1.75
- norm2_bias: float32 [512], P('fsdp'), may hold values from -1.75 to 1.75
- w_inner: float32 [512, 2048], P('fsdp'), may hold values from -0.25 to 0.25
- inner_bias: float32 [2048], P('fsdp'), may hold values from -1.75 to 1.75
- w_outer: float32 [2048, 512], P('fsdp'), may hold values from -0.1875 to 0.1875
- outer_bias: float32 [512], P('fsdp'), may hold values from -1.75 to 1.75
- cotangent: bfloat16 [32, 2, 640, 512], P(('dp', 'fsdp')), may hold values from -12 to 12
Outputs:
- layer_out: bfloat16 [32, 2, 640, 512], P(('dp', 'fsdp'))
- grad_tokens: bfloat16 [32, 2, 640, 512], P(('dp', 'fsdp'))
- grad_norm1_gain: float32 [512], P('fsdp')
- grad_norm1_bias: float32 [512], P('fsdp')
- grad_w_query: float32 [512, 512], P('fsdp')
- grad_w_key: float32 [512, 512], P('fsdp')
- grad_w_value: float32 [512, 512], P('fsdp')
- grad_w_output: float32 [512, 512], P('fsdp')
- grad_output_bias: float32 [512], P('fsdp')
- grad_norm2_gain: float32 [512], P('fsdp')
- grad_norm2_bias: float32 [512], P('fsdp')
- grad_w_inner: float32 [512, 2048], P('fsdp')
- grad_inner_bias: float32 [2048], P('fsdp')
- grad_w_outer: float32 [2048, 512], P('fsdp')
- grad_outer_bias: float32 [512], P('fsdp')
The draws below stay inside these ranges and needn't reach their ends.
Inputs may be any that keep to these rules, and one draw needn't show every extreme that they name: `parents`: for every tree, column 0 (the trunk) and columns 13 to 15 hold -1, columns 1 to 4 (the branches) hold 0, and columns 5 to 12 (the leaves) name the branches 1 to 4, each exactly twice.
All inputs are finite; a program needn't handle non-finite values.
Results may differ from the reference program's by a relative error of at most 0.019.
Values may be sent and summed in bfloat16 or wider, within the bound.
A program may use at most 320 MiB of HBM per device.

```python
import math
import jax
import jax.numpy as jnp
from jax import lax

D = 512
H = 8
HD = 64
FF = 2048
MICRO = 2
DEV_TOK = 640
SLOTS = 32
QUADS = 8
N_FSDP = 8


def draw_parents(key, part):
    tree_count = QUADS * MICRO
    tree_keys = jax.random.split(key, tree_count)
    leaf_parents = jnp.array([1, 1, 2, 2, 3, 3, 4, 4], dtype=jnp.int32)
    shuffled = jax.vmap(lambda tree_key: jax.random.permutation(tree_key, leaf_parents))(tree_keys)
    trunk_col = jnp.full((tree_count, 1), -1, jnp.int32)
    branch_cols = jnp.zeros((tree_count, 4), jnp.int32)
    padding = jnp.full((tree_count, 3), -1, jnp.int32)
    table = jnp.concatenate([trunk_col, branch_cols, shuffled, padding], axis=1)
    return table.reshape(QUADS, MICRO, 16)


def spiked(drawn, key, source, target, shards_of, factor):
    owner, partner = [(jnp.arange(drawn.shape[axis_at]) // (drawn.shape[axis_at] // shards_of)).reshape([-1 if axis == axis_at else 1 for axis in range(drawn.ndim)]) for axis_at in (source, target)]
    chosen = jax.random.permutation(key, shards_of)[partner]
    strong = (owner == chosen) | (owner == (partner + shards_of // 2) % shards_of)
    return jnp.where(strong, factor * drawn, drawn)


def block_scale(own_key, extent, pieces, low, top_value):
    level, own = 1.0, jax.random.fold_in(own_key, 6)
    for dim, parts in pieces:
        heights = jnp.exp(jax.random.uniform(jax.random.fold_in(own, dim), (parts,), jnp.float32, low / len(pieces), top_value / len(pieces)))
        level = level * jnp.repeat(heights, extent[dim] // parts).reshape([-1 if axis == dim else 1 for axis in range(len(extent))])
    return level


def noise(stream_key, extent, deviation, reach, shards=(), kind=jnp.bfloat16):
    values = deviation * jax.random.normal(stream_key, extent, jnp.float32)
    if shards:
        values = values * block_scale(stream_key, extent, shards, -0.22, 0.18)
    return jnp.clip(values, -reach, reach).astype(kind)


def bell_draw_with(own_key, shape, width, bound, cuts, heavy, kind=jnp.bfloat16):
    result = width * jax.random.normal(own_key, shape, jnp.float32)
    if cuts:
        result = result * block_scale(own_key, shape, cuts, -0.22, 0.18)
    return jnp.clip(spiked(result, jax.random.fold_in(own_key, 3), *heavy), -bound, bound).astype(kind)


def setup_inputs(seed: int = 0) -> dict:
    arg_keys = jax.random.split(jax.random.key(seed), 17)
    return {
        "tokens": noise(arg_keys[0], (SLOTS, MICRO, DEV_TOK, D), 1.0, 6.0, ((0, 32),)),
        "parents": draw_parents(jax.random.fold_in(arg_keys[16], 71), 0),
        "norm1_gain": jnp.clip(1.0 + 0.15 * jax.random.normal(arg_keys[2], (D,), jnp.float32), 0.25, 1.75),
        "norm1_bias": noise(arg_keys[3], (D,), 0.3, 1.75, ((0, 8),), jnp.float32),
        "w_query": noise(arg_keys[4], (D, D), D ** -0.5, 0.25, ((0, 8),), jnp.float32),
        "w_key": noise(arg_keys[5], (D, D), D ** -0.5, 0.25, ((0, 8),), jnp.float32),
        "w_value": noise(arg_keys[6], (D, D), D ** -0.5, 0.25, ((0, 8),), jnp.float32),
        "w_output": noise(arg_keys[7], (D, D), 64 ** -0.5, 0.75, ((0, 8),), jnp.float32),
        "output_bias": noise(arg_keys[8], (D,), 0.3, 1.75, ((0, 8),), jnp.float32),
        "norm2_gain": jnp.clip(1.0 + 0.15 * jax.random.normal(arg_keys[9], (D,), jnp.float32), 0.25, 1.75),
        "norm2_bias": noise(arg_keys[10], (D,), 0.3, 1.75, ((0, 8),), jnp.float32),
        "w_inner": noise(arg_keys[11], (D, FF), D ** -0.5, 0.25, ((0, 8),), jnp.float32),
        "inner_bias": noise(arg_keys[12], (FF,), 0.3, 1.75, ((0, 8),), jnp.float32),
        "w_outer": noise(arg_keys[13], (FF, D), (FF // 2) ** -0.5, 0.1875, ((0, 8),), jnp.float32),
        "outer_bias": noise(arg_keys[14], (D,), 0.3, 1.75, ((0, 8),), jnp.float32),
        "cotangent": bell_draw_with(arg_keys[15], (SLOTS, MICRO, DEV_TOK, D), 1.0, 12.0, ((0, 32),), (0, 3, 32, 2.75)),
    }


@jax.custom_vjp
def low(v):
    return lax.optimization_barrier(v.astype(jnp.bfloat16)).astype(jnp.float32)

@jax.custom_vjp
def low_back(v):
    return v

def low_keep(v):
    return (low(v), None)

def low_pass(kept, grad):
    return (grad,)

def back_keep(v):
    return (v, None)

def back_low(kept, grad):
    return (low(grad),)
low.defvjp(low_keep, low_pass)
low_back.defvjp(back_keep, back_low)

def highest_dot(left_side, right_side):
    return jnp.dot(left_side, right_side, precision=lax.Precision.HIGHEST, preferred_element_type=jnp.float32)

def norm_rows(values, norm_gain, norm_shift):
    row_mean = lax.optimization_barrier(jnp.mean(values, axis=-1, keepdims=True))
    centred = values - row_mean
    spread = lax.optimization_barrier(jnp.mean(centred * centred, axis=-1, keepdims=True))
    return centred * lax.rsqrt(spread + 1e-06) * norm_gain + norm_shift

def tree_layout(length):
    seg_len = length // 20
    positions = jnp.arange(length, dtype=jnp.int32)
    block_index = positions // seg_len
    offset_in = positions % seg_len
    trunk_len = 8 * seg_len
    segment = jnp.where(block_index < 8, 0, block_index - 7).astype(jnp.int32)
    path_place = jnp.where(block_index < 8, positions, jnp.where(block_index < 12, trunk_len + offset_in, trunk_len + seg_len + offset_in)).astype(jnp.int32)
    return (segment, path_place)

def parent_of(parent_row, segment):
    columns = jnp.arange(parent_row.shape[0], dtype=jnp.int32)
    picked = jnp.where(segment[:, None] == columns[None, :], parent_row[None, :], 0)
    return lax.optimization_barrier(jnp.sum(picked, axis=1)).astype(jnp.int32)

def visible_keys(query_segment, query_place, key_segment, key_place, parent_row):
    parent_seg = parent_of(parent_row, query_segment)
    grand_seg = jnp.where(parent_seg < 0, -1, parent_of(parent_row, jnp.maximum(parent_seg, 0)))
    related = (key_segment[None, :] == query_segment[:, None]) | (key_segment[None, :] == parent_seg[:, None]) | (key_segment[None, :] == grand_seg[:, None])
    return related & (key_place[None, :] <= query_place[:, None])

def head_slopes(head_count, tree_length):
    return 2.0 ** (2.0 - 4.0 * jnp.arange(head_count, dtype=jnp.float32) / head_count) / tree_length

def tree_layer(tree_rows, params, parent_row):
    gain_one, shift_one, query_weight, key_weight, value_weight, output_weight, output_shift, gain_two, shift_two, inner_weight, inner_shift, outer_weight, outer_shift = [low(entry_value) for entry_value in params]
    length = tree_rows.shape[0]
    segment, path_place = tree_layout(length)
    related = visible_keys(segment, path_place, segment, path_place, parent_row)
    distances = (path_place[:, None] - path_place[None, :]).astype(jnp.float32)
    position_bias = -head_slopes(H, length)[:, None, None] * distances[None, :, :]
    normed_one = low(norm_rows(tree_rows, gain_one, shift_one))
    query_heads = low(low_back(highest_dot(normed_one, query_weight))).reshape(length, H, HD)
    key_heads = low(low_back(highest_dot(normed_one, key_weight))).reshape(length, H, HD)
    value_heads = low(low_back(highest_dot(normed_one, value_weight))).reshape(length, H, HD)
    scores = jnp.einsum('qhd,khd->hqk', query_heads, key_heads, precision=lax.Precision.HIGHEST) * (1.0 / math.sqrt(HD)) + position_bias
    scores = low_back(scores)
    scores = jnp.where(related[None, :, :], scores, -1e+30)
    attn_probs = low(jax.nn.softmax(scores, axis=-1))
    head_mix = jnp.einsum('hqk,khd->qhd', attn_probs, value_heads, precision=lax.Precision.HIGHEST)
    head_mix = low(low_back(head_mix)).reshape(length, H * HD)
    attn_branch = low_back(highest_dot(head_mix, output_weight) + output_shift)
    resid_mid = tree_rows + attn_branch
    normed_two = low(norm_rows(resid_mid, gain_two, shift_two))
    inner_vals = low_back(highest_dot(normed_two, inner_weight) + inner_shift)
    activated = low(jax.nn.gelu(inner_vals, approximate=True))
    ffn_branch = low_back(highest_dot(activated, outer_weight) + outer_shift)
    return resid_mid + ffn_branch

def arrange(blocks):
    slot_count, micro_count, row_count, model_width = blocks.shape
    rows_split = blocks.reshape(slot_count // N_FSDP, N_FSDP, micro_count, row_count, model_width)
    rows_split = jnp.roll(rows_split, 2, axis=1)
    grouped = rows_split.reshape(slot_count // 4, 4, micro_count, row_count, model_width)
    grouped = jnp.transpose(grouped, (0, 2, 1, 3, 4))
    return grouped.reshape(slot_count // 4 * micro_count, 4 * row_count, model_width)

def unarrange(trees, slot_count, micro_count):
    tree_count, length, model_width = trees.shape
    grouped = trees.reshape(slot_count // 4, micro_count, 4, length // 4, model_width)
    grouped = jnp.transpose(grouped, (0, 2, 1, 3, 4))
    rows_split = grouped.reshape(slot_count // N_FSDP, N_FSDP, micro_count, length // 4, model_width)
    rows_split = jnp.roll(rows_split, -2, axis=1)
    return rows_split.reshape(slot_count, micro_count, length // 4, model_width)

def reference(tokens, parents, norm1_gain, norm1_bias, w_query, w_key, w_value, w_output, output_bias, norm2_gain, norm2_bias, w_inner, inner_bias, w_outer, outer_bias, cotangent):
    params = (norm1_gain, norm1_bias, w_query, w_key, w_value, w_output, output_bias, norm2_gain, norm2_bias, w_inner, inner_bias, w_outer, outer_bias)
    tree_inputs = arrange(tokens.astype(jnp.float32))
    tree_cotangents = arrange(cotangent.astype(jnp.float32))
    parent_rows = parents.reshape(-1, parents.shape[2])
    layer_step = jax.checkpoint(tree_layer)

    def forward(tree_values, weights_all):

        def scan_step(carry_value, item_pair):
            return (carry_value, layer_step(item_pair[0], weights_all, item_pair[1]))
        unused_carry, outputs = lax.scan(scan_step, jnp.zeros((), jnp.float32), (tree_values, parent_rows))
        return outputs
    outputs, pullback = jax.vjp(forward, tree_inputs, params)
    grad_inputs, grad_params = pullback(tree_cotangents)
    slot_count, micro_count = (tokens.shape[0], tokens.shape[1])
    layer_out = unarrange(outputs, slot_count, micro_count).astype(jnp.bfloat16)
    grad_tokens = unarrange(grad_inputs, slot_count, micro_count).astype(jnp.bfloat16)
    return (layer_out, grad_tokens, grad_params[0], grad_params[1], grad_params[2], grad_params[3], grad_params[4], grad_params[5], grad_params[6], grad_params[7], grad_params[8], grad_params[9], grad_params[10], grad_params[11], grad_params[12])
```

```python
import functools
import math

import jax
import jax.numpy as jnp
from jax import lax
from jax.experimental import pallas as pl
from jax.experimental.pallas import tpu as pltpu
from jax.sharding import PartitionSpec as P

H = 8
T = 256
f32, bf16 = jnp.float32, jnp.bfloat16


def mm(a, b):
    return jnp.dot(a, b, preferred_element_type=f32)


def mm_tn(a, b):
    return lax.dot_general(a, b, (((0,), (0,)), ((), ())), preferred_element_type=f32)


def mm_nt(a, b):
    return lax.dot_general(a, b, (((1,), (1,)), ((), ())), preferred_element_type=f32)


def iota(shape, dim):
    return lax.broadcasted_iota(jnp.int32, shape, dim)


def branch_of(par):
    return jnp.where(par <= 1, 1, jnp.where(par == 2, 2, jnp.where(par == 3, 3, 4)))


def attn_fwd_kernel(heads, seg, parents_ref, kaug_ref, qT_ref, vT_ref, oT_ref, lse_ref, s_scr):
    trunk = 8 * seg
    ntr = trunk // T
    vr = vT_ref.shape[0] // heads
    causal_t = iota((T, T), 0) <= iota((T, T), 1)
    causal_b = iota((seg, seg), 0) <= iota((seg, seg), 1)

    def finish(h, cols, m, acc):
        l = acc[64:65, :]
        oT_ref[pl.ds(pl.multiple_of(h * 64, 64), 64), cols] = (acc[:64] / l).astype(bf16)
        lse_ref[pl.ds(pl.multiple_of(h * 8, 8), 8), cols] = jnp.broadcast_to(m + jnp.log(l), (8, T))

    def head(h, _):
        hk = pl.ds(pl.multiple_of(h * 128, 128), 128)
        hv = pl.ds(pl.multiple_of(h * vr, vr), vr)

        def full_scores(q, n):
            m = None
            for c in range(n):
                s = mm(kaug_ref[c * T:(c + 1) * T, hk], q)
                s_scr[c * T:(c + 1) * T, :] = s
                cm = jnp.max(s, axis=0, keepdims=True)
                m = cm if m is None else jnp.maximum(m, cm)
            return m

        def full_mix(m, n, acc):
            for c in range(n):
                p = jnp.exp(s_scr[c * T:(c + 1) * T, :] - m).astype(bf16)
                t = mm(vT_ref[hv, c * T:(c + 1) * T], p)
                acc = t if acc is None else acc + t
            return acc

        for t in range(ntr):
            cols = slice(t * T, (t + 1) * T)
            q = qT_ref[hk, cols]
            sd = jnp.where(causal_t, mm(kaug_ref[cols, hk], q), -1e30)
            m = jnp.max(sd, axis=0, keepdims=True)
            if t:
                m = jnp.maximum(m, full_scores(q, t))
            acc = mm(vT_ref[hv, cols], jnp.exp(sd - m).astype(bf16))
            acc = full_mix(m, t, acc)
            finish(h, cols, m, acc)

        def tail_tile(i, leaf):
            b0 = 8 + 2 * i
            cols = pl.ds(pl.multiple_of(b0 * seg, T), T)
            q = qT_ref[hk, cols]
            rows = []
            for half in range(2):
                own = pl.ds(pl.multiple_of((b0 + half) * seg, seg), seg)
                rows.append([own])
                if leaf:
                    par = branch_of(parents_ref[b0 + half - 7])
                    rows[-1].append(pl.ds(pl.multiple_of((7 + par) * seg, seg), seg))
            m = full_scores(q, ntr)
            ext = []
            for e in range(len(rows[0])):
                pieces = []
                for half in range(2):
                    s = mm(kaug_ref[rows[half][e], hk], q[:, half * seg:(half + 1) * seg])
                    if e == 0:
                        s = jnp.where(causal_b, s, -1e30)
                    pieces.append(s)
                s = jnp.concatenate(pieces, axis=1)
                m = jnp.maximum(m, jnp.max(s, axis=0, keepdims=True))
                ext.append(s)
            acc = None
            for e in range(len(ext)):
                p = jnp.exp(ext[e] - m).astype(bf16)
                t = jnp.concatenate(
                    [mm(vT_ref[hv, rows[half][e]], p[:, half * seg:(half + 1) * seg]) for half in range(2)],
                    axis=1)
                acc = t if acc is None else acc + t
            acc = full_mix(m, ntr, acc)
            finish(h, cols, m, acc)

        lax.fori_loop(0, 2, lambda i, c: (tail_tile(i, False), c)[1], 0)
        lax.fori_loop(2, 6, lambda i, c: (tail_tile(i, True), c)[1], 0)
        return 0

    lax.fori_loop(0, heads, head, 0)


def attn_bwd_kernel(heads, seg, parents_ref, kaug_ref, vaug_ref, qT_ref, doT_ref, kT_ref, dopad_ref, qpad_ref,
                    oT_ref, lse_ref, dqT_ref, dkv_ref, acc_scr):
    trunk = 8 * seg
    ntr = trunk // T
    causal_t = iota((T, T), 0) <= iota((T, T), 1)
    causal_b = iota((seg, seg), 0) <= iota((seg, seg), 1)

    def head(h, _):
        hk = pl.ds(pl.multiple_of(h * 128, 128), 128)
        h64 = pl.ds(pl.multiple_of(h * 64, 64), 64)
        acc_scr[...] = jnp.zeros_like(acc_scr)

        def prep(cols):
            q = qT_ref[hk, cols]
            do = doT_ref[h64, cols]
            lse = jnp.max(lse_ref[pl.ds(pl.multiple_of(h * 8, 8), 8), cols], axis=0, keepdims=True)
            delta = jnp.sum(do.astype(f32) * oT_ref[h64, cols].astype(f32), axis=0, keepdims=True)
            rhs = jnp.concatenate([dopad_ref[cols, hk], qpad_ref[cols, hk]], axis=0)
            return q, do, lse, delta, rhs

        def rows_of(ref, blk, n, lanes):
            return ref[pl.ds(blk, n), :, lanes].reshape(n * seg, lanes.size)

        def piece(blk, n, q, do, lse, delta, rhs, mask):
            s = mm(rows_of(kaug_ref, blk, n, hk), q) - lse
            p = jnp.exp(s)
            if mask is not None:
                p = jnp.where(mask, p, 0.0)
            dp = mm(rows_of(vaug_ref, blk, n, hk), do)
            ds = (p * (dp - delta)).astype(bf16)
            pd = jnp.concatenate([p.astype(bf16), ds], axis=1)
            acc_scr[pl.ds(blk, n)] += mm(pd, rhs).reshape(n, seg, 128)
            return mm(kT_ref[h64, pl.ds(pl.multiple_of(blk * seg, seg), n * seg)], ds)

        def padded(do):
            return jnp.concatenate([do, jnp.zeros_like(do)], axis=0)

        for t in range(ntr):
            cols = slice(t * T, (t + 1) * T)
            q, do, lse, delta, rhs = prep(cols)
            dop = padded(do)
            dq = piece(2 * t, 2, q, dop, lse, delta, rhs, causal_t)
            for c in range(t):
                dq += piece(2 * c, 2, q, dop, lse, delta, rhs, None)
            dqT_ref[h64, cols] = (dq * 0.125).astype(bf16)

        def tail_tile(i, leaf):
            b0 = 8 + 2 * i
            cols = pl.ds(pl.multiple_of(b0 * seg, T), T)
            q, do, lse, delta, rhs = prep(cols)
            dop = padded(do)
            parts = []
            for half in range(2):
                hs = slice(half * seg, (half + 1) * seg)
                rh = jnp.concatenate([rhs[half * seg:(half + 1) * seg], rhs[T + half * seg:T + (half + 1) * seg]], axis=0)
                a = (q[:, hs], dop[:, hs], lse[:, hs], delta[:, hs], rh)
                d = piece(b0 + half, 1, *a, causal_b)
                if leaf:
                    par = branch_of(parents_ref[b0 + half - 7])
                    d += piece(7 + par, 1, *a, None)
                parts.append(d)
            dq = jnp.concatenate(parts, axis=1)
            for c in range(ntr):
                dq += piece(2 * c, 2, q, dop, lse, delta, rhs, None)
            dqT_ref[h64, cols] = (dq * 0.125).astype(bf16)

        lax.fori_loop(0, 2, lambda i, c: (tail_tile(i, False), c)[1], 0)
        lax.fori_loop(2, 6, lambda i, c: (tail_tile(i, True), c)[1], 0)
        dkv_ref[:, hk] = acc_scr[...].reshape(20 * seg, 128).astype(bf16)
        return 0

    lax.fori_loop(0, heads, head, 0)

VM = pl.BlockSpec(memory_space=pltpu.VMEM)
SM = pl.BlockSpec(memory_space=pltpu.SMEM)

def attn_fwd(parents, kaug, qT, vT, heads):
    n = kaug.shape[0]
    return pl.pallas_call(
        functools.partial(attn_fwd_kernel, heads, n // 20),
        out_shape=(jax.ShapeDtypeStruct((heads * 64, n), bf16), jax.ShapeDtypeStruct((heads * 8, n), f32)),
        in_specs=[SM, VM, VM, VM], out_specs=(VM, VM),
        scratch_shapes=[pltpu.VMEM((n // 20 * 8, T), f32)],
        name="attn_fwd",
        compiler_params=pltpu.CompilerParams(vmem_limit_bytes=48 << 20),
    )(parents, kaug, qT, vT)

def attn_bwd(parents, kaug, vaug, qT, doT, kT, dopad, qpad, oT, lse, heads):
    n = kaug.shape[0]
    return pl.pallas_call(
        functools.partial(attn_bwd_kernel, heads, n // 20),
        out_shape=(jax.ShapeDtypeStruct((heads * 64, n), bf16), jax.ShapeDtypeStruct((n, heads * 128), bf16)),
        in_specs=[SM] + [VM] * 9, out_specs=(VM, VM),
        scratch_shapes=[pltpu.VMEM((20, n // 20, 128), f32)],
        name="attn_bwd",
        compiler_params=pltpu.CompilerParams(vmem_limit_bytes=48 << 20),
    )(parents, kaug.reshape(20, n // 20, -1), vaug.reshape(20, n // 20, -1), qT, doT, kT, dopad, qpad, oT, lse)


def normed(values, gain, shift):
    mean = jnp.mean(values, axis=-1, keepdims=True)
    centred = values - mean
    inv = lax.rsqrt(jnp.mean(centred * centred, axis=-1, keepdims=True) + 1e-06)
    unit = centred * inv
    return unit, inv, (unit * gain + shift).astype(bf16)


def norm_back(grad, unit, inv, gain):
    dn = grad * gain
    m1 = jnp.mean(dn, axis=-1, keepdims=True)
    m2 = jnp.mean(dn * unit, axis=-1, keepdims=True)
    return (dn - m1 - unit * m2) * inv


def gelu_and_slope(u):
    c = math.sqrt(2.0 / math.pi)
    t = jnp.tanh(c * (u + 0.044715 * u * u * u))
    g = 0.5 * u * (1.0 + t)
    slope = 0.5 * (1.0 + t) + 0.5 * u * (1.0 - t * t) * c * (1.0 + 3 * 0.044715 * u * u)
    return g, slope


def split3(x):
    out = []
    for _ in range(3):
        low = lax.reduce_precision(x, 8, 7)
        out.append(low)
        x = x - low
    return out


def on_device(tokens, parents, n1g, n1b, wq, wk, wv, wo, ob, n2g, n2b, wi, ib, wu, ub, cotangent):
    F = lax.axis_size("fsdp")
    fi = lax.axis_index("fsdp")
    place = (fi + 2) % F
    half = (place % 4) // 2
    core = fi % 2
    quad = lax.axis_index("dp") * (F // 4) + place // 4
    parent_row = parents[quad, half]
    _, _, rows, width = tokens.shape
    heads = H // 2
    hw = heads * 64
    tree = 4 * rows
    seg = tree // 20
    partner = [(i, ((((i + 2) % F) ^ 2) + F - 2) % F) for i in range(F)]
    sibling = [(i, i ^ 1) for i in range(F)]

    def swap(x, perm):
        return lax.ppermute(x, "fsdp", perm)

    def own(x):
        return lax.dynamic_index_in_dim(x[0], half, 0, keepdims=False)

    def other(x):
        return lax.dynamic_index_in_dim(x[0], 1 - half, 0, keepdims=False)

    def pair(mine, received):
        low = jnp.where(half == 0, mine, received)
        high = jnp.where(half == 0, received, mine)
        return jnp.concatenate([low, high], axis=0)

    def from_pair(x):
        low, high = x[:rows], x[rows:]
        return jnp.where(half == 0, low, high), jnp.where(half == 0, high, low)

    def whole(mine, theirs):
        a = jnp.where(core == 0, mine, theirs)
        b = jnp.where(core == 0, theirs, mine)
        return jnp.concatenate([a[:rows], b[:rows], a[rows:], b[rows:]], axis=0)

    def mine_of(x, c):
        a = jnp.concatenate([x[:rows], x[2 * rows:3 * rows]], axis=0)
        b = jnp.concatenate([x[rows:2 * rows], x[3 * rows:]], axis=0)
        return jnp.where(c == 0, a, b)

    x_my = pair(own(tokens), swap(other(tokens), partner))
    x_tree = whole(x_my, swap(x_my, sibling)).astype(f32)
    dy_my = pair(own(cotangent), swap(other(cotangent), partner))
    x_my = x_my.astype(f32)

    def gather(x):
        return lax.all_gather(x.astype(bf16), "fsdp", axis=0, tiled=True)

    vec = jnp.concatenate([n1g, n1b, ob, n2g, n2b, ub, ib])[None]
    vec = gather(vec).astype(f32)
    n = n1g.shape[0]
    n1g, n1b, ob, n2g, n2b, ub = [vec[:, i * n:(i + 1) * n].reshape(-1) for i in range(6)]
    ib = vec[:, 6 * n:].reshape(-1)
    wqkv = gather(jnp.concatenate([wq, wk, wv], axis=1))
    woi = gather(jnp.concatenate([wo, wi], axis=1))
    wu = gather(wu)
    wo, wi = woi[:, :width], woi[:, width:]
    cols = [lax.dynamic_slice_in_dim(wqkv, i * width + core * hw, hw, 1) for i in range(3)]
    wq, wk, wv = cols

    def padded(w, before):
        w = w.reshape(-1, heads, 64)
        return jnp.pad(w, ((0, 0), (0, 0), (64 * before, 64 - 64 * before))).reshape(-1, heads * 128)

    unit1, inv1, a1_tree = normed(x_tree, n1g, n1b)
    pos = jnp.arange(tree, dtype=jnp.int32)
    blk, off = pos // seg, pos % seg
    spot = jnp.where(blk < 8, pos, jnp.where(blk < 12, 8 * seg + off, 9 * seg + off))
    lane = jnp.arange(heads * 128, dtype=jnp.int32) % 128
    hi = (spot // 8 * 8)[:, None]
    lo = (spot % 8)[:, None]
    aug = jnp.where((lane >= 64) & (lane < 67), hi, jnp.where((lane >= 67) & (lane < 70), lo, 0)).astype(f32)
    kaug = (mm(a1_tree, padded(wk, 0)) + aug).astype(bf16)
    vaug = mm(a1_tree, padded(wv, 0)).astype(bf16)
    q = mm(a1_tree, wq).astype(bf16)
    qs = q * bf16(0.125)
    head_id = (core * heads + jnp.arange(heads)).astype(f32)
    slopes = jnp.exp2(2.0 - 4.0 * head_id / H) / tree
    srow = jnp.stack(split3(slopes) * 2, axis=1)
    srow = jnp.pad(srow, ((0, 0), (0, 58))).astype(bf16)
    qT = jnp.concatenate(
        [qs.T.reshape(heads, 64, tree), jnp.broadcast_to(srow[:, :, None], (heads, 64, tree))], axis=1
    ).reshape(heads * 128, tree)
    v = mm(a1_tree, wv).astype(bf16)
    vT = jnp.concatenate([v.T.reshape(heads, 64, tree), jnp.ones((heads, 16, tree), bf16)], axis=1)
    vT = vT.reshape(heads * 80, tree)
    oT, lse = attn_fwd(parent_row, kaug, qT, vT, heads)
    o = oT.T
    o_mine, o_out = mine_of(o, core), mine_of(o, 1 - core)
    o_in = swap(o_out, sibling)
    o_full = jnp.where(core == 0, jnp.concatenate([o_mine, o_in], axis=1), jnp.concatenate([o_in, o_mine], axis=1))

    x2 = x_my + mm(o_full, wo) + ob
    unit2, inv2, a2 = normed(x2, n2g, n2b)
    u = mm(a2, wi) + ib
    g, slope = gelu_and_slope(u)
    g = g.astype(bf16)
    y = (x2 + mm(g, wu) + ub).astype(bf16)
    y_keep, y_send = from_pair(y)
    y_back = swap(y_send, partner)

    g_wu = mm_tn(g, dy_my)
    dy = dy_my.astype(f32)
    g_ub = jnp.sum(dy, axis=0)
    du = (mm_nt(dy_my, wu) * slope).astype(bf16)
    g_wi = mm_tn(a2, du)
    g_ib = jnp.sum(du.astype(f32), axis=0)
    da2 = mm_nt(du, wi)
    g_n2g = jnp.sum(da2 * unit2, axis=0)
    g_n2b = jnp.sum(da2, axis=0)
    dx2 = dy + norm_back(da2, unit2, inv2, n2g)
    dx2_low = dx2.astype(bf16)
    g_wo = mm_tn(o_full, dx2_low)
    g_ob = jnp.sum(dx2_low.astype(f32), axis=0)
    dx2_tree = whole(dx2_low, swap(dx2_low, sibling))
    wo_rows = lax.dynamic_slice_in_dim(wo, core * hw, hw, 0)
    do = mm_nt(dx2_tree, wo_rows).astype(bf16)

    def pad_heads(x, before):
        x = x.reshape(-1, heads, 64)
        return jnp.pad(x, ((0, 0), (0, 0), (64 * before, 64 - 64 * before))).reshape(-1, heads * 128)

    k = kaug.reshape(tree, heads, 128)[:, :, :64].reshape(tree, hw)
    dqT, dkv = attn_bwd(parent_row, kaug, vaug, qT, do.T, k.T, pad_heads(do, 0), pad_heads(qs, 1), oT, lse, heads)
    dq = dqT.T
    dkv = dkv.reshape(tree, heads, 2, 64)
    dv, dk = dkv[:, :, 0].reshape(tree, hw), dkv[:, :, 1].reshape(tree, hw)
    g_wq, g_wk, g_wv = mm_tn(a1_tree, dq), mm_tn(a1_tree, dk), mm_tn(a1_tree, dv)
    da1 = mm_nt(dq, wq) + mm_nt(dk, wk) + mm_nt(dv, wv)
    da1_mine = mine_of(da1, core) + swap(mine_of(da1, 1 - core).astype(bf16), sibling).astype(f32)
    u1, i1 = mine_of(unit1, core), mine_of(inv1, core)
    g_n1g = jnp.sum(da1_mine * u1, axis=0)
    g_n1b = jnp.sum(da1_mine, axis=0)
    dx = (dx2 + norm_back(da1_mine, u1, i1, n1g)).astype(bf16)
    dx_keep, dx_send = from_pair(dx)
    dx_back = swap(dx_send, partner)

    def scatter(x):
        x = lax.psum_scatter(x.astype(bf16), "fsdp", scatter_dimension=0, tiled=True)
        return lax.psum(x, "dp").astype(f32)

    g_qkv = jnp.stack([g_wq, g_wk, g_wv], axis=1)
    z = jnp.zeros_like(g_qkv)
    g_qkv = jnp.where(core == 0, jnp.concatenate([g_qkv, z], axis=2), jnp.concatenate([z, g_qkv], axis=2))
    big1 = scatter(jnp.concatenate([g_qkv.reshape(width, 3 * width), g_wo, g_wi], axis=1))
    big2 = scatter(g_wu)
    svec = jnp.concatenate(
        [v_.reshape(F, -1) for v_ in (g_n1g, g_n1b, g_ob, g_n2g, g_n2b, g_ub, g_ib)], axis=1)
    svec = scatter(svec)[0]
    sv = [svec[i * n:(i + 1) * n] for i in range(6)] + [svec[6 * n:]]
    o_wq, o_wk, o_wv, o_wo, o_wi = [big1[:, i * width:(i + 1) * width] for i in range(4)] + [big1[:, 4 * width:]]

    def both(keep, back):
        return jnp.where(half == 0, jnp.stack([keep, back]), jnp.stack([back, keep]))[None]

    return (both(y_keep, y_back), both(dx_keep, dx_back), sv[0], sv[1], o_wq, o_wk, o_wv, o_wo, sv[2], sv[3], sv[4],
            o_wi, sv[6], big2, sv[5])


def solution(mesh):
    tok = P(("dp", "fsdp"), None, None, None)
    v, m = P("fsdp"), P("fsdp", None)
    return jax.shard_map(
        on_device,
        mesh=mesh,
        in_specs=(tok, P(), v, v, m, m, m, m, v, v, v, m, v, m, v, tok),
        out_specs=(tok, tok, v, v, m, m, m, m, v, v, v, m, v, m, v),
        check_vma=False,
    )
```

```python
import functools
import math

import jax
import jax.numpy as jnp
import ml_dtypes
import numpy as np
from jax import lax
from jax.experimental import pallas as pl
from jax.experimental.pallas import tpu as pltpu
from jax.sharding import PartitionSpec as P

H = 8
T = 256
f32, bf16 = jnp.float32, jnp.bfloat16
VM = pl.BlockSpec(memory_space=pltpu.VMEM)
SM = pl.BlockSpec(memory_space=pltpu.SMEM)


def mm(a, b):
    return jnp.dot(a, b, preferred_element_type=f32)


def mm_tn(a, b):
    return lax.dot_general(a, b, (((0,), (0,)), ((), ())), preferred_element_type=f32)


def mm_nt(a, b):
    return lax.dot_general(a, b, (((1,), (1,)), ((), ())), preferred_element_type=f32)


def iota(shape, dim):
    return lax.broadcasted_iota(jnp.int32, shape, dim)


def chosen(par, read):
    out = read(0)
    for b in range(1, 4):
        out = jnp.where(par == b + 1, read(b), out)
    return out


def attend(heads, seg, parents_ref, kaug_ref, qT_ref, vT_ref, oT_ref, lse_ref, s_scr, between):
    trunk = 8 * seg
    ntr = trunk // T
    vr = vT_ref.shape[0] // heads
    causal_t = iota((T, T), 0) <= iota((T, T), 1)
    causal_b = iota((seg, seg), 0) <= iota((seg, seg), 1)

    def finish(h, cols, m, acc):
        l = acc[64:65, :]
        oT_ref[pl.ds(pl.multiple_of(h * 64, 64), 64), cols] = (acc[:64] / l).astype(bf16)
        lse_ref[pl.ds(pl.multiple_of(h * 8, 8), 8), cols] = jnp.broadcast_to(m + jnp.log(l), (8, T))

    def head(h, _):
        between(h)
        hk = pl.ds(pl.multiple_of(h * 128, 128), 128)
        hv = pl.ds(pl.multiple_of(h * vr, vr), vr)

        def keys(blk, n):
            return kaug_ref[pl.ds(blk, n), :, hk].reshape(n * seg, 128)

        def full_scores(q, n):
            m = None
            for c in range(n):
                s = mm(keys(2 * c, 2), q)
                s_scr[c * T:(c + 1) * T, :] = s
                cm = jnp.max(s, axis=0, keepdims=True)
                m = cm if m is None else jnp.maximum(m, cm)
            return m

        def full_mix(m, n, acc):
            for c in range(n):
                p = jnp.exp(s_scr[c * T:(c + 1) * T, :] - m).astype(bf16)
                t = mm(vT_ref[hv, c * T:(c + 1) * T], p)
                acc = t if acc is None else acc + t
            return acc

        for t in range(ntr):
            cols = slice(t * T, (t + 1) * T)
            q = qT_ref[hk, cols]
            sd = jnp.where(causal_t, mm(keys(2 * t, 2), q), -1e30)
            m = jnp.max(sd, axis=0, keepdims=True)
            if t:
                m = jnp.maximum(m, full_scores(q, t))
            acc = mm(vT_ref[hv, cols], jnp.exp(sd - m).astype(bf16))
            acc = full_mix(m, t, acc)
            finish(h, cols, m, acc)

        def tail_tile(i, leaf):
            b0 = 8 + 2 * i
            cols = pl.ds(pl.multiple_of(b0 * seg, T), T)
            q = qT_ref[hk, cols]
            rows = []
            for half in range(2):
                rows.append([b0 + half])
                if leaf:
                    rows[-1].append(parents_ref[b0 + half - 7])
            m = full_scores(q, ntr)
            ext = []
            for e in range(len(rows[0])):
                pieces = []
                for half in range(2):
                    kk = keys(rows[half][0], 1) if e == 0 else chosen(rows[half][1], lambda b: keys(8 + b, 1))
                    s = mm(kk, q[:, half * seg:(half + 1) * seg])
                    if e == 0:
                        s = jnp.where(causal_b, s, -1e30)
                    pieces.append(s)
                s = jnp.concatenate(pieces, axis=1)
                m = jnp.maximum(m, jnp.max(s, axis=0, keepdims=True))
                ext.append(s)
            acc = None
            for e in range(len(ext)):
                p = jnp.exp(ext[e] - m).astype(bf16)
                t = []
                for half in range(2):
                    if e == 0:
                        vv = vT_ref[hv, pl.ds(pl.multiple_of(rows[half][0] * seg, seg), seg)]
                    else:
                        vv = chosen(rows[half][1], lambda b: vT_ref[hv, (8 + b) * seg:(9 + b) * seg])
                    t.append(mm(vv, p[:, half * seg:(half + 1) * seg]))
                t = jnp.concatenate(t, axis=1)
                acc = t if acc is None else acc + t
            acc = full_mix(m, ntr, acc)
            finish(h, cols, m, acc)

        lax.fori_loop(0, 2, lambda i, c: (tail_tile(i, False), c)[1], 0)
        lax.fori_loop(2, 6, lambda i, c: (tail_tile(i, True), c)[1], 0)
        return 0

    lax.fori_loop(0, heads, head, 0)


def attend_back(heads, seg, parents_ref, kaug_ref, v_ref, qT_ref, doT_ref, kT_ref, do_ref, qn_ref,
                oT_ref, lse_ref, dqT_ref, dk_ref, dv_ref, accK, accV, between):
    ntr = 8 * seg // T
    causal_t = iota((T, T), 0) <= iota((T, T), 1)
    causal_b = iota((seg, seg), 0) <= iota((seg, seg), 1)
    low_rows = iota((128, T), 0) < 64
    low_lanes = iota((T, 128), 1) < 64

    def pair(pr, _):
        between(pr)
        lanes = pl.ds(pl.multiple_of(pr * 128, 128), 128)
        hk = [pl.ds(pl.multiple_of(pr * 256 + 128 * e, 128), 128) for e in range(2)]
        h64 = [pl.ds(pl.multiple_of(pr * 128 + 64 * e, 64), 64) for e in range(2)]
        accK[...] = jnp.zeros_like(accK)
        accV[...] = jnp.zeros_like(accV)

        def stack(x):
            z = jnp.zeros_like(x)
            return jnp.concatenate([jnp.where(low_lanes, x, z), jnp.where(low_lanes, z, x)], axis=0)

        def prep(cols):
            doT = doT_ref[lanes, cols]
            z = jnp.zeros_like(doT)
            prod = doT.astype(f32) * oT_ref[lanes, cols].astype(f32)
            q, do, lse, delta = [], [], [], []
            for e in range(2):
                q.append(qT_ref[hk[e], cols])
                do.append(jnp.where(low_rows, doT, z) if e == 0 else jnp.where(low_rows, z, doT))
                at = pl.multiple_of((pr * 2 + e) * 8, 8)
                lse.append(jnp.max(lse_ref[pl.ds(at, 8), cols], axis=0, keepdims=True))
                delta.append(jnp.sum(prod[64 * e:64 * e + 64], axis=0, keepdims=True))
            return q, do, lse, delta, stack(do_ref[cols, lanes]), stack(qn_ref[cols, lanes])

        def piece(blk, n, sl, args, mask, par=None):
            q, do, lse, delta, rv, rk = args
            ps, dss, dq = [], [], []

            def rows_of(ref, at):
                if par is None:
                    return ref[pl.ds(blk, n), :, at].reshape(n * seg, 128)
                return chosen(par, lambda b: ref[8 + b, :, at])

            vv = rows_of(v_ref, lanes)
            for e in range(2):
                kk = rows_of(kaug_ref, hk[e])
                p = jnp.exp(mm(kk, q[e][:, sl]) - lse[e][:, sl])
                if mask is not None:
                    p = jnp.where(mask, p, 0.0)
                dp = mm(vv, do[e][:, sl])
                ds = (p * (dp - delta[e][:, sl])).astype(bf16)
                if par is None:
                    kT = kT_ref[h64[e], pl.ds(pl.multiple_of(blk * seg, seg), n * seg)]
                else:
                    kT = chosen(par, lambda b: kT_ref[h64[e], (8 + b) * seg:(9 + b) * seg])
                dq.append(mm(kT, ds))
                ps.append(p.astype(bf16))
                dss.append(ds)
            if sl.stop - sl.start != T:
                rv = jnp.concatenate([rv[sl], rv[T + sl.start:T + sl.stop]], axis=0)
                rk = jnp.concatenate([rk[sl], rk[T + sl.start:T + sl.stop]], axis=0)
            av = mm(jnp.concatenate(ps, axis=1), rv)
            ak = mm(jnp.concatenate(dss, axis=1), rk)
            if par is None:
                accV[pl.ds(blk, n)] += av.reshape(n, seg, 128)
                accK[pl.ds(blk, n)] += ak.reshape(n, seg, 128)
            else:
                for b in range(4):
                    here = jnp.where(par == b + 1, 1.0, 0.0)
                    accK[8 + b] += ak * here
                    accV[8 + b] += av * here
            return dq

        def emit(cols, dq):
            for e in range(2):
                dqT_ref[h64[e], cols] = (dq[e] * 0.125).astype(bf16)

        full = slice(0, T)
        for t in range(ntr):
            cols = slice(t * T, (t + 1) * T)
            args = prep(cols)
            dq = piece(2 * t, 2, full, args, causal_t)
            for c in range(t):
                dq = [a + b for a, b in zip(dq, piece(2 * c, 2, full, args, None))]
            emit(cols, dq)

        def tail_tile(i, leaf):
            b0 = 8 + 2 * i
            cols = pl.ds(pl.multiple_of(b0 * seg, T), T)
            args = prep(cols)
            halves = []
            for half in range(2):
                sl = slice(half * seg, (half + 1) * seg)
                d = piece(b0 + half, 1, sl, args, causal_b)
                if leaf:
                    par = parents_ref[b0 + half - 7]
                    d = [x + y for x, y in zip(d, piece(8, 1, sl, args, None, par))]
                halves.append(d)
            dq = [jnp.concatenate([halves[0][e], halves[1][e]], axis=1) for e in range(2)]
            for c in range(ntr):
                dq = [a + b for a, b in zip(dq, piece(2 * c, 2, full, args, None))]
            emit(cols, dq)

        lax.fori_loop(0, 2, lambda i, c: (tail_tile(i, False), c)[1], 0)
        lax.fori_loop(2, 6, lambda i, c: (tail_tile(i, True), c)[1], 0)
        dk_ref[:, :, lanes] = accK[...].astype(bf16)
        dv_ref[:, :, lanes] = accV[...].astype(bf16)
        return 0

    lax.fori_loop(0, heads // 2, pair, 0)


def slope_parts(head, head_count, length):
    x = np.float32(2.0 ** (2.0 - 4.0 * head / head_count) / length)
    out = []
    for _ in range(3):
        low = np.float32(ml_dtypes.bfloat16(x))
        out.append(float(low))
        x = np.float32(x - low)
    return out


def remote(src, dst, send_sem, recv_sem, target):
    return pltpu.make_async_remote_copy(
        src_ref=src, dst_ref=dst, send_sem=send_sem, recv_sem=recv_sem,
        device_id={"fsdp": target}, device_id_type=pl.DeviceIdType.MESH)


def where_am_i(F):
    f = lax.axis_index("fsdp")
    place = lax.rem(f + 2, F)
    part = lax.rem(place, 4)
    half = part // 2
    core = lax.rem(f, 2)
    base = place - part
    partner = lax.rem(base + lax.rem(part + 2, 4) + F - 2, F)
    sibling = f + 1 - 2 * core
    return f, part, half, core, partner, sibling


def greet(F, f, core, sibling):
    barrier = pltpu.get_barrier_semaphore()
    for d in range(1, F // 2):
        pl.semaphore_signal(barrier, inc=1, device_id={"fsdp": lax.rem(f + 2 * d, F)},
                            device_id_type=pl.DeviceIdType.MESH)
    pl.semaphore_signal(barrier, inc=1, device_id={"fsdp": sibling}, device_id_type=pl.DeviceIdType.MESH)
    pl.semaphore_wait(barrier, F // 2)


def front_kernel(F, n, parents_ref, tok_ref, cot_ref, wq_ref, wk_ref, wv_ref, wo_ref, wi_ref, wu_ref, vec_ref,
                 xt_ref, a1_ref, kaug_ref, v_ref, kT_ref, qn_ref, qT_ref, oT_ref, lse_ref, oF_ref, dy_ref,
                 wqkv_ref, woi_ref, wuf_ref, rows_ref,
                 vecs, vT_scr, s_scr, tsend, trecv, gsend, grecv):
    f, part, half, core, partner, sibling = where_am_i(F)
    rows, width = tok_ref.shape[1:]
    seg = rows // 5
    heads = H // 2
    hw = heads * 64
    tree = 4 * rows
    r = wq_ref.shape[0]
    ru = wu_ref.shape[0]
    part1 = part + 1 - 2 * core
    part2 = lax.rem(part + 2, 4)
    part3 = lax.rem(part1 + 2, 4)

    own = pl.ds(pl.multiple_of(f * r, r), r)
    ownu = pl.ds(pl.multiple_of(f * ru, ru), ru)
    vecs[f] = vec_ref[...]
    wqkv_ref[own, 0:width] = wq_ref[...].astype(bf16)
    wqkv_ref[own, width:2 * width] = wk_ref[...].astype(bf16)
    wqkv_ref[own, 2 * width:3 * width] = wv_ref[...].astype(bf16)

    greet(F, f, core, sibling)

    def slot(g, src):
        if g == 0:
            return vecs.at[src]
        if g == 3:
            return wuf_ref.at[pl.ds(pl.multiple_of(src * ru, ru), ru)]
        ref = wqkv_ref if g == 1 else woi_ref
        return ref.at[pl.ds(pl.multiple_of(src * r, r), r)]

    def direct(g, d):
        return remote(slot(g, f), slot(g, f), gsend.at[g, d], grecv.at[g, d],
                      sibling if d == 0 else lax.rem(f + 2 * d, F))

    def came(g, d):
        src = sibling if d == 0 else lax.rem(f + F - 2 * d, F)
        remote(slot(g, src), slot(g, src), gsend.at[g, d], grecv.at[g, d], sibling).wait_recv()

    def forward(g, d):
        src = lax.rem(f + F - 2 * d, F)
        return remote(slot(g, src), slot(g, src), gsend.at[g, F // 2 + d], grecv.at[g, F // 2 + d], sibling)

    def forwarded(g, d):
        src = lax.rem(sibling + F - 2 * d, F)
        remote(slot(g, src), slot(g, src), gsend.at[g, F // 2 + d], grecv.at[g, F // 2 + d], sibling).wait_recv()

    chips = range(1, F // 2)

    def send_all(g):
        for d in range(F // 2):
            direct(g, d).start()

    def pass_on(g):
        for d in chips:
            came(g, d)
            forward(g, d).start()

    def receive_rest(g):
        came(g, 0)
        for d in chips:
            forwarded(g, d)

    x_out = remote(tok_ref.at[1 - half], xt_ref.at[part], tsend.at[0], trecv.at[0], partner)
    x_sib = remote(tok_ref.at[half], xt_ref.at[part], tsend.at[1], trecv.at[1], sibling)
    x_fwd = remote(xt_ref.at[part2], xt_ref.at[part2], tsend.at[2], trecv.at[2], sibling)
    dy_out = remote(cot_ref.at[1 - half], dy_ref.at[half], tsend.at[3], trecv.at[3], partner)
    dy_own = pltpu.make_async_copy(cot_ref.at[half], dy_ref.at[half], tsend.at[4])

    send_all(0)
    send_all(1)
    x_out.start()
    x_sib.start()
    dy_own.start()
    xt_ref[part] = tok_ref[half]
    woi_ref[own, 0:width] = wo_ref[...].astype(bf16)
    woi_ref[own, width:] = wi_ref[...].astype(bf16)
    wuf_ref[ownu, :] = wu_ref[...].astype(bf16)
    pass_on(0)
    pass_on(1)
    receive_rest(0)

    table = jnp.max(vecs[...], axis=1).astype(bf16)
    words = table.shape[1]

    def vector_row(first, m, length):
        col = iota((words, length), 1)
        pick = iota((words, length), 0) == first + (col & (m - 1))
        spread = mm(table, pick.astype(bf16))
        shift = m.bit_length() - 1
        mine = iota((F, length), 0) == (iota((F, length), 1) >> shift)
        return jnp.sum(jnp.where(mine, spread, 0.0), axis=0, keepdims=True)

    for i in range(6):
        rows_ref[:, i * width:(i + 1) * width] = jnp.broadcast_to(vector_row(i * n, n, width), (8, width))
    hidden = rows_ref.shape[1] - 6 * width
    rows_ref[:, 6 * width:] = jnp.broadcast_to(vector_row(6 * n, hidden // F, hidden), (8, hidden))

    receive_rest(1)

    lane = iota((seg, 128), 1)
    offs = iota((seg, 128), 0)
    arow = iota((64, rows), 0)

    def project(p):
        x = xt_ref[p].astype(f32)
        gain = rows_ref[0:1, 0:width]
        shift = rows_ref[0:1, width:2 * width]
        mean = jnp.mean(x, axis=-1, keepdims=True)
        x = x - mean
        inv = lax.rsqrt(jnp.mean(x * x, axis=-1, keepdims=True) + 1e-06)
        a1 = (x * inv * gain + shift).astype(bf16)
        a1_ref[p] = a1

        def proj(i):
            return mm(a1, wqkv_ref[:, pl.ds(pl.multiple_of(i * width + core * hw, hw), hw)])

        cols = pl.ds(pl.multiple_of(p * rows, rows), rows)
        q = (proj(0) * 0.125).astype(bf16)
        qn_ref[p] = q
        qT = q.T
        k = proj(1).astype(bf16)
        kT_ref[:, cols] = k.T
        v = proj(2).astype(bf16)
        v_ref[pl.ds(p * 5, 5)] = v.reshape(5, seg, hw)
        vT = v.T
        for h in range(heads):
            a, b = slope_parts(h, H, tree), slope_parts(heads + h, H, tree)
            aug = jnp.zeros((64, rows), f32)
            for j in range(3):
                s = jnp.where(core == 0, a[j], b[j])
                aug = jnp.where((arow == j) | (arow == j + 3), s, aug)
            aug = aug.astype(bf16)
            lo, hi = 128 * h + 64 * (h % 2), 128 * h + 64 - 64 * (h % 2)
            qT_ref[lo:lo + 64, cols] = qT[64 * h:64 * h + 64]
            qT_ref[hi:hi + 64, cols] = aug
            vT_scr[80 * h:80 * h + 64, cols] = vT[64 * h:64 * h + 64]
            vT_scr[80 * h + 64:80 * h + 80, cols] = jnp.ones((16, rows), bf16)
        for b in range(5):
            blk = p * 5 + b
            start = jnp.where(blk < 8, blk * seg, jnp.where(blk < 12, 8 * seg, 9 * seg))
            spot = offs + start
            hi = (spot & -8).astype(f32)
            lo = (spot & 7).astype(f32)
            for h in range(heads):
                at = 64 - 64 * (h % 2)
                l = lane - at
                aug = jnp.where((l >= 0) & (l < 3), hi, jnp.where((l >= 3) & (l < 6), lo, 0.0)).astype(bf16)
                keep = (lane < 64) if h % 2 == 0 else (lane >= 64)
                kk = k[b * seg:(b + 1) * seg, 128 * (h // 2):128 * (h // 2) + 128]
                kaug_ref[blk, :, 128 * h:128 * h + 128] = jnp.where(keep, kk, aug)

    x_sib.wait_recv()
    order = [part, part1, part2, part3]
    lax.fori_loop(0, 2, lambda i, c: (project(jnp.where(i == 0, part, part1)), c)[1], 0)
    x_out.wait_recv()
    x_fwd.start()
    send_all(2)
    send_all(3)
    dy_out.start()
    x_fwd.wait_recv()
    lax.fori_loop(0, 2, lambda i, c: (project(jnp.where(i == 0, part2, part3)), c)[1], 0)

    def between(h):
        @pl.when(h == 2)
        def _():
            pass_on(2)

    attend(heads, seg, parents_ref, kaug_ref, qT_ref, vT_scr, oT_ref, lse_ref, s_scr, between)

    pass_on(3)
    other = 1 - core
    sent = []
    for i in range(2):
        cols = pl.ds(pl.multiple_of((other + 2 * i) * rows, rows), rows)
        mine = pl.ds(pl.multiple_of((core + 2 * i) * rows, rows), rows)
        at = (pl.ds(pl.multiple_of(core * hw, hw), hw), slice(i * rows, (i + 1) * rows))
        c = remote(oT_ref.at[:, cols], oF_ref.at[at], tsend.at[5 + i], trecv.at[5 + i], sibling)
        c.start()
        sent.append(c)
        oF_ref[at] = oT_ref[:, mine]
    for c in sent:
        c.wait()
    receive_rest(2)
    receive_rest(3)
    dy_own.wait()
    dy_out.wait()
    x_out.wait_send()
    x_sib.wait_send()
    x_fwd.wait_send()
    for g in range(4):
        for d in range(F // 2):
            direct(g, d).wait_send()
        for d in chips:
            forward(g, d).wait_send()


def front(F, parents, tokens, cotangent, weights, vec, n):
    _, rows, width = tokens.shape
    tree = 4 * rows
    heads = H // 2
    hw = heads * 64
    seg = rows // 5
    hidden = weights[4].shape[1]
    out = [
        ((4, rows, width), bf16), ((4, rows, width), bf16), ((20, seg, heads * 128), bf16), ((20, seg, hw), bf16),
        ((hw, tree), bf16), ((4, rows, hw), bf16), ((heads * 128, tree), bf16), ((hw, tree), bf16),
        ((heads * 8, tree), f32), ((2 * hw, 2 * rows), bf16), ((2, rows, width), bf16),
        ((width, 3 * width), bf16), ((width, width + hidden), bf16), ((hidden, width), bf16),
        ((8, 6 * width + hidden), f32),
    ]
    specs = [VM] * len(out)
    specs[10] = pl.BlockSpec(memory_space=pl.ANY)
    dma = pltpu.SemaphoreType.DMA
    return pl.pallas_call(
        functools.partial(front_kernel, F, n),
        out_shape=[jax.ShapeDtypeStruct(s, d) for s, d in out],
        in_specs=[SM, VM, pl.BlockSpec(memory_space=pl.ANY)] + [VM] * 7,
        out_specs=specs,
        scratch_shapes=[
            pltpu.VMEM((F,) + vec.shape, f32),
            pltpu.VMEM((heads * 80, tree), bf16), pltpu.VMEM((8 * seg, T), f32),
            dma((7,)), dma((7,)), dma((4, F)), dma((4, F)),
        ],
        name="front",
        compiler_params=pltpu.CompilerParams(vmem_limit_bytes=56 << 20, collective_id=0, has_side_effects=True),
    )(parents, tokens, cotangent, *weights, vec)


def attn_bwd(parents, kaug, v, qT, doT, kT, do, qn, oT, lse):
    tree = qT.shape[1]
    heads = H // 2
    hw = heads * 64
    seg = tree // 20

    def kernel(*refs):
        attend_back(heads, seg, *refs, lambda h: None)

    return pl.pallas_call(
        kernel,
        out_shape=(jax.ShapeDtypeStruct((hw, tree), bf16), jax.ShapeDtypeStruct((20, seg, hw), bf16),
                   jax.ShapeDtypeStruct((20, seg, hw), bf16)),
        in_specs=[SM] + [VM] * 9, out_specs=(VM, VM, VM),
        scratch_shapes=[pltpu.VMEM((20, seg, 128), f32)] * 2,
        name="attn_bwd",
        compiler_params=pltpu.CompilerParams(vmem_limit_bytes=40 << 20),
    )(parents, kaug, v, qT, doT, kT, do, qn, oT, lse)


def normed(values, gain, shift):
    mean = jnp.mean(values, axis=-1, keepdims=True)
    centred = values - mean
    inv = lax.rsqrt(jnp.mean(centred * centred, axis=-1, keepdims=True) + 1e-06)
    unit = centred * inv
    return unit, inv, (unit * gain + shift).astype(bf16)


def norm_back(grad, unit, inv, gain):
    dn = grad * gain
    m1 = jnp.mean(dn, axis=-1, keepdims=True)
    m2 = jnp.mean(dn * unit, axis=-1, keepdims=True)
    return (dn - m1 - unit * m2) * inv


def gelu_and_slope(u):
    c = math.sqrt(2.0 / math.pi)
    t = jnp.tanh(c * (u + 0.044715 * u * u * u))
    g = 0.5 * u * (1.0 + t)
    slope = 0.5 * (1.0 + t) + 0.5 * u * (1.0 - t * t) * c * (1.0 + 3 * 0.044715 * u * u)
    return g, slope


def on_device(tokens, parents, n1g, n1b, wq, wk, wv, wo, ob, n2g, n2b, wi, ib, wu, ub, cotangent):
    F = lax.axis_size("fsdp")
    fi = lax.axis_index("fsdp")
    place = (fi + 2) % F
    half = (place % 4) // 2
    core = fi % 2
    quad = lax.axis_index("dp") * (F // 4) + place // 4
    parent_row = parents[quad, half]
    _, _, rows, width = tokens.shape
    heads = H // 2
    hw = heads * 64
    tree = 4 * rows
    partner = [(i, ((((i + 2) % F) ^ 2) + F - 2) % F) for i in range(F)]
    sibling = [(i, i ^ 1) for i in range(F)]

    def swap(x, perm):
        return lax.ppermute(x, "fsdp", perm)

    def from_pair(x):
        low, high = x[:rows], x[rows:]
        return jnp.where(half == 0, low, high), jnp.where(half == 0, high, low)

    def whole(mine, theirs):
        a = jnp.where(core == 0, mine, theirs)
        b = jnp.where(core == 0, theirs, mine)
        return jnp.concatenate([a[:rows], b[:rows], a[rows:], b[rows:]], axis=0)

    def mine_of(x, c):
        a = jnp.concatenate([x[:rows], x[2 * rows:3 * rows]], axis=0)
        b = jnp.concatenate([x[rows:2 * rows], x[3 * rows:]], axis=0)
        return jnp.where(c == 0, a, b)

    n = n1g.shape[0]
    vec = jnp.concatenate([n1g, n1b, ob, n2g, n2b, ub, ib])
    vec = lax.reduce_precision(vec, 8, 7)
    vec = jnp.broadcast_to(jnp.pad(vec, (0, -vec.shape[0] % 128)), (8, vec.shape[0] + -vec.shape[0] % 128))
    (xt, a1, kaug, v, kT, qn, qT, oT, lse, oF, dy_my, wqkv, woi, wu, vrows) = front(
        F, parent_row, tokens[0], cotangent[0], (wq, wk, wv, wo, wi, wu), vec, n)
    n1g, n1b, ob, n2g, n2b, ub = [vrows[0, i * width:(i + 1) * width] for i in range(6)]
    ib = vrows[0, 6 * width:]
    wo, wi = woi[:, :width], woi[:, width:]
    wq, wk, wv = [lax.dynamic_slice_in_dim(wqkv, i * width + core * hw, hw, 1) for i in range(3)]
    x_my = mine_of(xt.reshape(tree, width), core).astype(f32)
    a1_tree = a1.reshape(tree, width)
    dy_my = dy_my.reshape(2 * rows, width)

    x2 = x_my + mm_tn(oF, wo) + ob
    unit2, inv2, a2 = normed(x2, n2g, n2b)
    u = mm(a2, wi) + ib
    g, slope = gelu_and_slope(u)
    g = g.astype(bf16)
    y = (x2 + mm(g, wu) + ub).astype(bf16)
    y_keep, y_send = from_pair(y)
    y_back = swap(y_send, partner)

    g_wu = mm_tn(g, dy_my)
    dy = dy_my.astype(f32)
    g_ub = jnp.sum(dy, axis=0)
    du = (mm_nt(dy_my, wu) * slope).astype(bf16)
    g_wi = mm_tn(a2, du)
    g_ib = jnp.sum(du.astype(f32), axis=0)
    da2 = mm_nt(du, wi)
    g_n2g = jnp.sum(da2 * unit2, axis=0)
    g_n2b = jnp.sum(da2, axis=0)
    dx2 = dy + norm_back(da2, unit2, inv2, n2g)
    dx2_low = dx2.astype(bf16)
    g_wo = mm(oF, dx2_low)
    g_ob = jnp.sum(dx2_low.astype(f32), axis=0)
    dx2_tree = whole(dx2_low, swap(dx2_low, sibling))
    wo_rows = lax.dynamic_slice_in_dim(wo, core * hw, hw, 0)
    do = mm_nt(dx2_tree, wo_rows).astype(bf16)

    dqT, dk, dv = attn_bwd(parent_row, kaug, v, qT, do.T, kT, do, qn.reshape(tree, hw), oT, lse)
    dq, dk, dv = dqT.T, dk.reshape(tree, hw), dv.reshape(tree, hw)
    g_wq, g_wk, g_wv = mm_tn(a1_tree, dq), mm_tn(a1_tree, dk), mm_tn(a1_tree, dv)
    da1 = mm_nt(dq, wq) + mm_nt(dk, wk) + mm_nt(dv, wv)
    da1_mine = mine_of(da1, core) + swap(mine_of(da1, 1 - core).astype(bf16), sibling).astype(f32)
    u1, i1, _ = normed(x_my, n1g, n1b)
    g_n1g = jnp.sum(da1_mine * u1, axis=0)
    g_n1b = jnp.sum(da1_mine, axis=0)
    dx = (dx2 + norm_back(da1_mine, u1, i1, n1g)).astype(bf16)
    dx_keep, dx_send = from_pair(dx)
    dx_back = swap(dx_send, partner)

    def scatter(x):
        x = lax.psum_scatter(x.astype(bf16), "fsdp", scatter_dimension=0, tiled=True)
        return lax.psum(x, "dp").astype(f32)

    g_qkv = jnp.stack([g_wq, g_wk, g_wv], axis=1)
    z = jnp.zeros_like(g_qkv)
    g_qkv = jnp.where(core == 0, jnp.concatenate([g_qkv, z], axis=2), jnp.concatenate([z, g_qkv], axis=2))
    big1 = scatter(jnp.concatenate([g_qkv.reshape(width, 3 * width), g_wo, g_wi], axis=1))
    big2 = scatter(g_wu)
    svec = jnp.concatenate(
        [v_.reshape(F, -1) for v_ in (g_n1g, g_n1b, g_ob, g_n2g, g_n2b, g_ub, g_ib)], axis=1)
    svec = scatter(svec)[0]
    sv = [svec[i * n:(i + 1) * n] for i in range(6)] + [svec[6 * n:]]
    o_wq, o_wk, o_wv, o_wo, o_wi = [big1[:, i * width:(i + 1) * width] for i in range(4)] + [big1[:, 4 * width:]]

    def both(keep, back):
        return jnp.where(half == 0, jnp.stack([keep, back]), jnp.stack([back, keep]))[None]

    return (both(y_keep, y_back), both(dx_keep, dx_back), sv[0], sv[1], o_wq, o_wk, o_wv, o_wo, sv[2], sv[3], sv[4],
            o_wi, sv[6], big2, sv[5])


def solution(mesh):
    tok = P(("dp", "fsdp"), None, None, None)
    v, m = P("fsdp"), P("fsdp", None)
    return jax.shard_map(
        on_device,
        mesh=mesh,
        in_specs=(tok, P(), v, v, m, m, m, m, v, v, v, m, v, m, v, tok),
        out_specs=(tok, tok, v, v, m, m, m, m, v, v, v, m, v, m, v),
        check_vma=False,
    )
```

```python
import functools
import math

import jax
import jax.numpy as jnp
import ml_dtypes
import numpy as np
from jax import lax
from jax.experimental import pallas as pl
from jax.experimental.pallas import tpu as pltpu
from jax.sharding import PartitionSpec as P

H = 8
T = 256
f32, bf16 = jnp.float32, jnp.bfloat16
VM = pl.BlockSpec(memory_space=pltpu.VMEM)
SM = pl.BlockSpec(memory_space=pltpu.SMEM)


def mm(a, b):
    return jnp.dot(a, b, preferred_element_type=f32)


def mm_tn(a, b):
    return lax.dot_general(a, b, (((0,), (0,)), ((), ())), preferred_element_type=f32)


def mm_nt(a, b):
    return lax.dot_general(a, b, (((1,), (1,)), ((), ())), preferred_element_type=f32)


def iota(shape, dim):
    return lax.broadcasted_iota(jnp.int32, shape, dim)


def chosen(par, read):
    out = read(0)
    for b in range(1, 4):
        out = jnp.where(par == b + 1, read(b), out)
    return out


def attend(heads, seg, parents_ref, kaug_ref, qT_ref, vT_ref, oT_ref, lse_ref, s_scr, between):
    trunk = 8 * seg
    ntr = trunk // T
    vr = vT_ref.shape[0] // heads
    causal_t = iota((T, T), 0) <= iota((T, T), 1)
    causal_b = iota((seg, seg), 0) <= iota((seg, seg), 1)

    def finish(h, cols, m, acc):
        l = acc[64:65, :]
        oT_ref[pl.ds(pl.multiple_of(h * 64, 64), 64), cols] = (acc[:64] / l).astype(bf16)
        lse_ref[pl.ds(pl.multiple_of(h * 8, 8), 8), cols] = jnp.broadcast_to(m + jnp.log(l), (8, T))

    def head(h, _):
        between(h)
        hk = pl.ds(pl.multiple_of(h * 128, 128), 128)
        hv = pl.ds(pl.multiple_of(h * vr, vr), vr)

        def keys(blk, n):
            return kaug_ref[pl.ds(blk, n), :, hk].reshape(n * seg, 128)

        def full_scores(q, n):
            m = None
            for c in range(n):
                s = mm(keys(2 * c, 2), q)
                s_scr[c * T:(c + 1) * T, :] = s
                cm = jnp.max(s, axis=0, keepdims=True)
                m = cm if m is None else jnp.maximum(m, cm)
            return m

        def full_mix(m, n, acc):
            for c in range(n):
                p = jnp.exp(s_scr[c * T:(c + 1) * T, :] - m).astype(bf16)
                t = mm(vT_ref[hv, c * T:(c + 1) * T], p)
                acc = t if acc is None else acc + t
            return acc

        for t in range(ntr):
            cols = slice(t * T, (t + 1) * T)
            q = qT_ref[hk, cols]
            sd = jnp.where(causal_t, mm(keys(2 * t, 2), q), -1e30)
            m = jnp.max(sd, axis=0, keepdims=True)
            if t:
                m = jnp.maximum(m, full_scores(q, t))
            acc = mm(vT_ref[hv, cols], jnp.exp(sd - m).astype(bf16))
            acc = full_mix(m, t, acc)
            finish(h, cols, m, acc)

        def tail_tile(i, leaf):
            b0 = 8 + 2 * i
            cols = pl.ds(pl.multiple_of(b0 * seg, T), T)
            q = qT_ref[hk, cols]
            rows = []
            for half in range(2):
                rows.append([b0 + half])
                if leaf:
                    rows[-1].append(parents_ref[b0 + half - 7])
            m = full_scores(q, ntr)
            ext = []
            for e in range(len(rows[0])):
                pieces = []
                for half in range(2):
                    kk = keys(rows[half][0], 1) if e == 0 else chosen(rows[half][1], lambda b: keys(8 + b, 1))
                    s = mm(kk, q[:, half * seg:(half + 1) * seg])
                    if e == 0:
                        s = jnp.where(causal_b, s, -1e30)
                    pieces.append(s)
                s = jnp.concatenate(pieces, axis=1)
                m = jnp.maximum(m, jnp.max(s, axis=0, keepdims=True))
                ext.append(s)
            acc = None
            for e in range(len(ext)):
                p = jnp.exp(ext[e] - m).astype(bf16)
                t = []
                for half in range(2):
                    if e == 0:
                        vv = vT_ref[hv, pl.ds(pl.multiple_of(rows[half][0] * seg, seg), seg)]
                    else:
                        vv = chosen(rows[half][1], lambda b: vT_ref[hv, (8 + b) * seg:(9 + b) * seg])
                    t.append(mm(vv, p[:, half * seg:(half + 1) * seg]))
                t = jnp.concatenate(t, axis=1)
                acc = t if acc is None else acc + t
            acc = full_mix(m, ntr, acc)
            finish(h, cols, m, acc)

        lax.fori_loop(0, 2, lambda i, c: (tail_tile(i, False), c)[1], 0)
        lax.fori_loop(2, 6, lambda i, c: (tail_tile(i, True), c)[1], 0)
        return 0

    lax.fori_loop(0, heads, head, 0)


def attend_back(heads, seg, parents_ref, kaug_ref, v_ref, qT_ref, doT_ref, kT_ref, do_ref, qn_ref,
                oT_ref, lse_ref, dqT_ref, dk_ref, dv_ref, accK, accV, between):
    ntr = 8 * seg // T
    causal_t = iota((T, T), 0) <= iota((T, T), 1)
    causal_b = iota((seg, seg), 0) <= iota((seg, seg), 1)
    low_rows = iota((128, T), 0) < 64
    low_lanes = iota((T, 128), 1) < 64

    def pair(pr, _):
        between(pr)
        lanes = pl.ds(pl.multiple_of(pr * 128, 128), 128)
        hk = [pl.ds(pl.multiple_of(pr * 256 + 128 * e, 128), 128) for e in range(2)]
        h64 = [pl.ds(pl.multiple_of(pr * 128 + 64 * e, 64), 64) for e in range(2)]
        accK[...] = jnp.zeros_like(accK)
        accV[...] = jnp.zeros_like(accV)

        def stack(x):
            z = jnp.zeros_like(x)
            return jnp.concatenate([jnp.where(low_lanes, x, z), jnp.where(low_lanes, z, x)], axis=0)

        def prep(cols):
            doT = doT_ref[lanes, cols]
            z = jnp.zeros_like(doT)
            prod = doT.astype(f32) * oT_ref[lanes, cols].astype(f32)
            q, do, lse, delta = [], [], [], []
            for e in range(2):
                q.append(qT_ref[hk[e], cols])
                do.append(jnp.where(low_rows, doT, z) if e == 0 else jnp.where(low_rows, z, doT))
                at = pl.multiple_of((pr * 2 + e) * 8, 8)
                lse.append(jnp.max(lse_ref[pl.ds(at, 8), cols], axis=0, keepdims=True))
                delta.append(jnp.sum(prod[64 * e:64 * e + 64], axis=0, keepdims=True))
            return q, do, lse, delta, stack(do_ref[cols, lanes]), stack(qn_ref[cols, lanes])

        def piece(blk, n, sl, args, mask, par=None):
            q, do, lse, delta, rv, rk = args
            ps, dss, dq = [], [], []

            def rows_of(ref, at):
                if par is None:
                    return ref[pl.ds(blk, n), :, at].reshape(n * seg, 128)
                return chosen(par, lambda b: ref[8 + b, :, at])

            vv = rows_of(v_ref, lanes)
            for e in range(2):
                kk = rows_of(kaug_ref, hk[e])
                p = jnp.exp(mm(kk, q[e][:, sl]) - lse[e][:, sl])
                if mask is not None:
                    p = jnp.where(mask, p, 0.0)
                dp = mm(vv, do[e][:, sl])
                ds = (p * (dp - delta[e][:, sl])).astype(bf16)
                if par is None:
                    kT = kT_ref[h64[e], pl.ds(pl.multiple_of(blk * seg, seg), n * seg)]
                else:
                    kT = chosen(par, lambda b: kT_ref[h64[e], (8 + b) * seg:(9 + b) * seg])
                dq.append(mm(kT, ds))
                ps.append(p.astype(bf16))
                dss.append(ds)
            if sl.stop - sl.start != T:
                rv = jnp.concatenate([rv[sl], rv[T + sl.start:T + sl.stop]], axis=0)
                rk = jnp.concatenate([rk[sl], rk[T + sl.start:T + sl.stop]], axis=0)
            av = mm(jnp.concatenate(ps, axis=1), rv)
            ak = mm(jnp.concatenate(dss, axis=1), rk)
            if par is None:
                accV[pl.ds(blk, n)] += av.reshape(n, seg, 128)
                accK[pl.ds(blk, n)] += ak.reshape(n, seg, 128)
            else:
                for b in range(4):
                    here = jnp.where(par == b + 1, 1.0, 0.0)
                    accK[8 + b] += ak * here
                    accV[8 + b] += av * here
            return dq

        def emit(cols, dq):
            for e in range(2):
                dqT_ref[h64[e], cols] = (dq[e] * 0.125).astype(bf16)

        full = slice(0, T)
        for t in range(ntr):
            cols = slice(t * T, (t + 1) * T)
            args = prep(cols)
            dq = piece(2 * t, 2, full, args, causal_t)
            for c in range(t):
                dq = [a + b for a, b in zip(dq, piece(2 * c, 2, full, args, None))]
            emit(cols, dq)

        def tail_tile(i, leaf):
            b0 = 8 + 2 * i
            cols = pl.ds(pl.multiple_of(b0 * seg, T), T)
            args = prep(cols)
            halves = []
            for half in range(2):
                sl = slice(half * seg, (half + 1) * seg)
                d = piece(b0 + half, 1, sl, args, causal_b)
                if leaf:
                    par = parents_ref[b0 + half - 7]
                    d = [x + y for x, y in zip(d, piece(8, 1, sl, args, None, par))]
                halves.append(d)
            dq = [jnp.concatenate([halves[0][e], halves[1][e]], axis=1) for e in range(2)]
            for c in range(ntr):
                dq = [a + b for a, b in zip(dq, piece(2 * c, 2, full, args, None))]
            emit(cols, dq)

        lax.fori_loop(0, 2, lambda i, c: (tail_tile(i, False), c)[1], 0)
        lax.fori_loop(2, 6, lambda i, c: (tail_tile(i, True), c)[1], 0)
        dk_ref[:, :, lanes] = accK[...].astype(bf16)
        dv_ref[:, :, lanes] = accV[...].astype(bf16)
        return 0

    lax.fori_loop(0, heads // 2, pair, 0)


def slope_parts(head, head_count, length):
    x = np.float32(2.0 ** (2.0 - 4.0 * head / head_count) / length)
    out = []
    for _ in range(3):
        low = np.float32(ml_dtypes.bfloat16(x))
        out.append(float(low))
        x = np.float32(x - low)
    return out


def remote(src, dst, send_sem, recv_sem, target):
    return pltpu.make_async_remote_copy(
        src_ref=src, dst_ref=dst, send_sem=send_sem, recv_sem=recv_sem,
        device_id={"fsdp": target}, device_id_type=pl.DeviceIdType.MESH)


def where_am_i(F):
    f = lax.axis_index("fsdp")
    place = lax.rem(f + 2, F)
    part = lax.rem(place, 4)
    half = part // 2
    core = lax.rem(f, 2)
    base = place - part
    partner = lax.rem(base + lax.rem(part + 2, 4) + F - 2, F)
    sibling = f + 1 - 2 * core
    return f, part, half, core, partner, sibling


def greet(F, f, core, sibling):
    barrier = pltpu.get_barrier_semaphore()
    for d in range(1, F // 2):
        pl.semaphore_signal(barrier, inc=1, device_id={"fsdp": lax.rem(f + 2 * d, F)},
                            device_id_type=pl.DeviceIdType.MESH)
    pl.semaphore_signal(barrier, inc=1, device_id={"fsdp": sibling}, device_id_type=pl.DeviceIdType.MESH)
    pl.semaphore_wait(barrier, F // 2)


def front_kernel(F, n, parents_ref, tok_ref, cot_ref, wq_ref, wk_ref, wv_ref, wo_ref, wi_ref, wu_ref, vec_ref,
                 xt_ref, a1T_ref, kaug_ref, v_ref, kT_ref, qn_ref, qT_ref, oT_ref, lse_ref, oF_ref, dy_ref,
                 wqkv_ref, woi_ref, wuf_ref, rows_ref,
                 vecs, vT_scr, s_scr, tsend, trecv, gsend, grecv):
    f, part, half, core, partner, sibling = where_am_i(F)
    rows, width = tok_ref.shape[1:]
    seg = rows // 5
    heads = H // 2
    hw = heads * 64
    tree = 4 * rows
    r = wq_ref.shape[0]
    ru = wu_ref.shape[0]
    part1 = part + 1 - 2 * core
    part2 = lax.rem(part + 2, 4)
    part3 = lax.rem(part1 + 2, 4)

    own = pl.ds(pl.multiple_of(f * r, r), r)
    ownu = pl.ds(pl.multiple_of(f * ru, ru), ru)
    vecs[f] = vec_ref[...]
    wqkv_ref[own, 0:width] = wq_ref[...].astype(bf16)
    wqkv_ref[own, width:2 * width] = wk_ref[...].astype(bf16)
    wqkv_ref[own, 2 * width:3 * width] = wv_ref[...].astype(bf16)

    greet(F, f, core, sibling)

    def slot(g, src):
        if g == 0:
            return vecs.at[src]
        if g == 3:
            return wuf_ref.at[pl.ds(pl.multiple_of(src * ru, ru), ru)]
        ref = wqkv_ref if g == 1 else woi_ref
        return ref.at[pl.ds(pl.multiple_of(src * r, r), r)]

    def direct(g, d):
        return remote(slot(g, f), slot(g, f), gsend.at[g, d], grecv.at[g, d],
                      sibling if d == 0 else lax.rem(f + 2 * d, F))

    def came(g, d):
        src = sibling if d == 0 else lax.rem(f + F - 2 * d, F)
        remote(slot(g, src), slot(g, src), gsend.at[g, d], grecv.at[g, d], sibling).wait_recv()

    def forward(g, d):
        src = lax.rem(f + F - 2 * d, F)
        return remote(slot(g, src), slot(g, src), gsend.at[g, F // 2 + d], grecv.at[g, F // 2 + d], sibling)

    def forwarded(g, d):
        src = lax.rem(sibling + F - 2 * d, F)
        remote(slot(g, src), slot(g, src), gsend.at[g, F // 2 + d], grecv.at[g, F // 2 + d], sibling).wait_recv()

    chips = range(1, F // 2)

    def send_all(g):
        for d in range(F // 2):
            direct(g, d).start()

    def pass_on(g):
        for d in chips:
            came(g, d)
            forward(g, d).start()

    def receive_rest(g):
        came(g, 0)
        for d in chips:
            forwarded(g, d)

    x_out = remote(tok_ref.at[1 - half], xt_ref.at[part], tsend.at[0], trecv.at[0], partner)
    x_sib = remote(tok_ref.at[half], xt_ref.at[part], tsend.at[1], trecv.at[1], sibling)
    x_fwd = remote(xt_ref.at[part2], xt_ref.at[part2], tsend.at[2], trecv.at[2], sibling)
    dy_out = remote(cot_ref.at[1 - half], dy_ref.at[half], tsend.at[3], trecv.at[3], partner)
    dy_own = pltpu.make_async_copy(cot_ref.at[half], dy_ref.at[half], tsend.at[4])

    send_all(0)
    send_all(1)
    x_out.start()
    x_sib.start()
    dy_own.start()
    xt_ref[part] = tok_ref[half]
    woi_ref[own, 0:width] = wo_ref[...].astype(bf16)
    woi_ref[own, width:] = wi_ref[...].astype(bf16)
    wuf_ref[ownu, :] = wu_ref[...].astype(bf16)
    pass_on(0)
    pass_on(1)
    receive_rest(0)

    table = jnp.max(vecs[...], axis=1).astype(bf16)
    words = table.shape[1]

    def vector_row(first, m, length):
        col = iota((words, length), 1)
        pick = iota((words, length), 0) == first + (col & (m - 1))
        spread = mm(table, pick.astype(bf16))
        shift = m.bit_length() - 1
        mine = iota((F, length), 0) == (iota((F, length), 1) >> shift)
        return jnp.sum(jnp.where(mine, spread, 0.0), axis=0, keepdims=True)

    for i in range(6):
        rows_ref[:, i * width:(i + 1) * width] = jnp.broadcast_to(vector_row(i * n, n, width), (8, width))
    hidden = rows_ref.shape[1] - 6 * width
    rows_ref[:, 6 * width:] = jnp.broadcast_to(vector_row(6 * n, hidden // F, hidden), (8, hidden))

    receive_rest(1)

    lane = iota((seg, 128), 1)
    offs = iota((seg, 128), 0)
    arow = iota((64, rows), 0)

    def project(p):
        x = xt_ref[p].astype(f32)
        gain = rows_ref[0:1, 0:width]
        shift = rows_ref[0:1, width:2 * width]
        mean = jnp.mean(x, axis=-1, keepdims=True)
        x = x - mean
        inv = lax.rsqrt(jnp.mean(x * x, axis=-1, keepdims=True) + 1e-06)
        a1 = (x * inv * gain + shift).astype(bf16)

        def proj(i):
            return mm(a1, wqkv_ref[:, pl.ds(pl.multiple_of(i * width + core * hw, hw), hw)])

        cols = pl.ds(pl.multiple_of(p * rows, rows), rows)
        a1T_ref[:, cols] = a1.T
        q = (proj(0) * 0.125).astype(bf16)
        qn_ref[cols, :] = q
        qT = q.T
        k = proj(1).astype(bf16)
        kT_ref[:, cols] = k.T
        v = proj(2).astype(bf16)
        v_ref[pl.ds(p * 5, 5)] = v.reshape(5, seg, hw)
        vT = v.T
        for h in range(heads):
            a, b = slope_parts(h, H, tree), slope_parts(heads + h, H, tree)
            aug = jnp.zeros((64, rows), f32)
            for j in range(3):
                s = jnp.where(core == 0, a[j], b[j])
                aug = jnp.where((arow == j) | (arow == j + 3), s, aug)
            aug = aug.astype(bf16)
            lo, hi = 128 * h + 64 * (h % 2), 128 * h + 64 - 64 * (h % 2)
            qT_ref[lo:lo + 64, cols] = qT[64 * h:64 * h + 64]
            qT_ref[hi:hi + 64, cols] = aug
            vT_scr[80 * h:80 * h + 64, cols] = vT[64 * h:64 * h + 64]
            vT_scr[80 * h + 64:80 * h + 80, cols] = jnp.ones((16, rows), bf16)
        for b in range(5):
            blk = p * 5 + b
            start = jnp.where(blk < 8, blk * seg, jnp.where(blk < 12, 8 * seg, 9 * seg))
            spot = offs + start
            hi = (spot & -8).astype(f32)
            lo = (spot & 7).astype(f32)
            for h in range(heads):
                at = 64 - 64 * (h % 2)
                l = lane - at
                aug = jnp.where((l >= 0) & (l < 3), hi, jnp.where((l >= 3) & (l < 6), lo, 0.0)).astype(bf16)
                keep = (lane < 64) if h % 2 == 0 else (lane >= 64)
                kk = k[b * seg:(b + 1) * seg, 128 * (h // 2):128 * (h // 2) + 128]
                kaug_ref[blk, :, 128 * h:128 * h + 128] = jnp.where(keep, kk, aug)

    x_sib.wait_recv()
    order = [part, part1, part2, part3]
    lax.fori_loop(0, 2, lambda i, c: (project(jnp.where(i == 0, part, part1)), c)[1], 0)
    x_out.wait_recv()
    x_fwd.start()
    send_all(2)
    send_all(3)
    dy_out.start()
    x_fwd.wait_recv()
    lax.fori_loop(0, 2, lambda i, c: (project(jnp.where(i == 0, part2, part3)), c)[1], 0)

    def between(h):
        @pl.when(h == 2)
        def _():
            pass_on(2)

    attend(heads, seg, parents_ref, kaug_ref, qT_ref, vT_scr, oT_ref, lse_ref, s_scr, between)

    pass_on(3)
    other = 1 - core
    sent = []
    for i in range(2):
        cols = pl.ds(pl.multiple_of((other + 2 * i) * rows, rows), rows)
        mine = pl.ds(pl.multiple_of((core + 2 * i) * rows, rows), rows)
        at = (pl.ds(pl.multiple_of(core * hw, hw), hw), slice(i * rows, (i + 1) * rows))
        c = remote(oT_ref.at[:, cols], oF_ref.at[at], tsend.at[5 + i], trecv.at[5 + i], sibling)
        c.start()
        sent.append(c)
        oF_ref[at] = oT_ref[:, mine]
    for c in sent:
        c.wait()
    receive_rest(2)
    receive_rest(3)
    dy_own.wait()
    dy_out.wait()
    x_out.wait_send()
    x_sib.wait_send()
    x_fwd.wait_send()
    for g in range(4):
        for d in range(F // 2):
            direct(g, d).wait_send()
        for d in chips:
            forward(g, d).wait_send()


def front(F, parents, tokens, cotangent, weights, vec, n):
    _, rows, width = tokens.shape
    tree = 4 * rows
    heads = H // 2
    hw = heads * 64
    seg = rows // 5
    hidden = weights[4].shape[1]
    out = [
        ((4, rows, width), bf16), ((width, tree), bf16), ((20, seg, heads * 128), bf16), ((20, seg, hw), bf16),
        ((hw, tree), bf16), ((tree, hw), bf16), ((heads * 128, tree), bf16), ((hw, tree), bf16),
        ((heads * 8, tree), f32), ((2 * hw, 2 * rows), bf16), ((2, rows, width), bf16),
        ((width, 3 * width), bf16), ((width, width + hidden), bf16), ((hidden, width), bf16),
        ((8, 6 * width + hidden), f32),
    ]
    specs = [VM] * len(out)
    specs[10] = pl.BlockSpec(memory_space=pl.ANY)
    dma = pltpu.SemaphoreType.DMA
    return pl.pallas_call(
        functools.partial(front_kernel, F, n),
        out_shape=[jax.ShapeDtypeStruct(s, d) for s, d in out],
        in_specs=[SM, VM, pl.BlockSpec(memory_space=pl.ANY)] + [VM] * 7,
        out_specs=specs,
        scratch_shapes=[
            pltpu.VMEM((F,) + vec.shape, f32),
            pltpu.VMEM((heads * 80, tree), bf16), pltpu.VMEM((8 * seg, T), f32),
            dma((7,)), dma((7,)), dma((4, F)), dma((4, F)),
        ],
        name="front",
        compiler_params=pltpu.CompilerParams(vmem_limit_bytes=56 << 20, collective_id=0, has_side_effects=True),
    )(parents, tokens, cotangent, *weights, vec)


def fold(x):
    return x.astype(f32)


class Chain:
    def __init__(self, F, f, sums, got, block, zgot, final, send, recv):
        self.F, self.f, self.sums, self.got, self.block = F, f, sums, got, block
        self.zgot, self.final, self.send, self.recv = zgot, final, send, recv
        self.chip = f // 2
        self.chips = F // 2
        self.planes = lax.axis_size("dp")
        self.plane = lax.axis_index("dp")
        self.rows = sums.shape[1]
        self.zrows = block.shape[0] // self.planes

    def _b(self, d):
        return remote(self.sums.at[lax.rem(self.chip + d, self.chips)], self.got.at[d - 1],
                      self.send.at[d], self.recv.at[d], lax.rem(self.f + 2 * d, self.F))

    def _chunk(self, z):
        return pl.ds(pl.multiple_of(z * self.zrows, 16), self.zrows)

    def _c(self, e):
        z = lax.rem(self.plane + e, self.planes)
        i = self.chips + e
        return pltpu.make_async_remote_copy(
            src_ref=self.block.at[self._chunk(z)], dst_ref=self.zgot.at[e - 1],
            send_sem=self.send.at[i], recv_sem=self.recv.at[i],
            device_id={"dp": z}, device_id_type=pl.DeviceIdType.MESH)

    def _d(self, e, src=None):
        z = lax.rem(self.plane + e, self.planes)
        i = self.chips + self.planes + e
        here = self._chunk(self.plane if src is None else src)
        return pltpu.make_async_remote_copy(
            src_ref=self.final.at[here], dst_ref=self.final.at[here],
            send_sem=self.send.at[i], recv_sem=self.recv.at[i],
            device_id={"dp": z}, device_id_type=pl.DeviceIdType.MESH)

    def start_plane(self):
        for d in range(1, self.chips):
            self._b(d).start()

    def start_z(self):
        for d in range(1, self.chips):
            self._b(d).wait_recv()
        total = fold(self.sums[self.chip])
        for d in range(1, self.chips):
            total = total + fold(self.got[d - 1])
        self.block[0:self.rows] = total.astype(bf16)
        for e in range(1, self.planes):
            self._c(e).start()

    def start_back(self):
        for e in range(1, self.planes):
            self._c(e).wait_recv()
        here = self._chunk(self.plane)
        total = fold(self.block[here])
        for e in range(1, self.planes):
            total = total + fold(self.zgot[e - 1])
        self.final[here] = total.astype(bf16)
        for e in range(1, self.planes):
            self._d(e).start()

    def receive(self):
        for e in range(1, self.planes):
            self._d(e, lax.rem(self.plane + self.planes - e, self.planes)).wait_recv()

    def close(self):
        for d in range(1, self.chips):
            self._b(d).wait_send()
        for e in range(1, self.planes):
            self._c(e).wait_send()
            self._d(e).wait_send()


def back_kernel(F, parents_ref, kaug_ref, v_ref, qT_ref, kT_ref, qn_ref, oT_ref, lse_ref, a1T_ref, wqkv_ref, wo_ref,
                xt_ref, dxl_ref, dx2_ref, y_ref, g1_ref, vin_ref, n1_ref,
                lo_ref, gt_ref, gwq_ref, gwk_ref, gwv_ref, gwo_ref, gwi_ref, gwu_ref, vout_ref,
                dxs, wo_scr, doT, do, dqT, dk, dv, accK, accV, dx2s, das, dar, xs,
                a_sum, a_got, b_got, blk1, z1, fin1, sum2, got2, blk2, z2, fin2, rs2,
                vs, vgot, dxo, tsend, trecv, send1, recv1, send2, recv2, vsend, vrecv, lsem):
    f, part, half, core, partner, sibling = where_am_i(F)
    planes = lax.axis_size("dp")
    plane = lax.axis_index("dp")
    heads = H // 2
    hw = heads * 64
    _, rows, width = dxl_ref.shape
    seg = rows // 5
    chips = F // 2
    other = 1 - core

    load_g = pltpu.make_async_copy(g1_ref.at[:, core], a_sum, lsem.at[0])
    load_w = pltpu.make_async_copy(wo_ref.at[pl.ds(pl.multiple_of(core * hw, hw), hw), 0:width], wo_scr, lsem.at[1])
    load_d = pltpu.make_async_copy(dx2_ref, dx2s, lsem.at[2])
    keep_y = pltpu.make_async_copy(y_ref.at[half], lo_ref.at[half], lsem.at[3])
    load_x = [pltpu.make_async_copy(xt_ref.at[core + 2 * i], xs.at[i], lsem.at[4 + i]) for i in range(2)]
    for c in [load_w, load_g, load_d, keep_y] + load_x:
        c.start()

    barrier = pltpu.get_barrier_semaphore()
    for d in range(1, chips):
        pl.semaphore_signal(barrier, inc=1, device_id={"fsdp": lax.rem(f + 2 * d, F)},
                            device_id_type=pl.DeviceIdType.MESH)
    for e in range(1, planes):
        pl.semaphore_signal(barrier, inc=1, device_id={"dp": lax.rem(plane + e, planes)},
                            device_id_type=pl.DeviceIdType.MESH)
    pl.semaphore_signal(barrier, inc=1, device_id={"fsdp": sibling}, device_id_type=pl.DeviceIdType.MESH)
    pl.semaphore_wait(barrier, chips + planes - 1)

    dx_sw = remote(dxl_ref, dxs, tsend.at[0], trecv.at[0], sibling)
    a_out = remote(g1_ref.at[:, other], a_got, tsend.at[1], trecv.at[1], sibling)
    y_out = remote(y_ref.at[1 - half], lo_ref.at[half], tsend.at[2], trecv.at[2], partner)
    dx_sw.start()
    a_out.start()

    def make_do(p, x):
        cols = pl.ds(pl.multiple_of(p * rows, rows), rows)
        d = mm_nt(x, wo_scr[...]).astype(bf16)
        do[cols, :] = d
        doT[:, cols] = d.T

    load_w.wait()
    lax.fori_loop(0, 2, lambda i, c: (make_do(core + 2 * i, dxl_ref[i]), c)[1], 0)
    dx_sw.wait_recv()
    lax.fori_loop(0, 2, lambda i, c: (make_do(other + 2 * i, dxs[i]), c)[1], 0)

    one = Chain(F, f, a_sum, b_got, blk1, z1, fin1, send1, recv1)
    two = Chain(F, f, sum2, got2, blk2, z2, fin2, send2, recv2)
    load_g.wait()
    a_out.wait_recv()

    def add_block(j, c):
        a_sum[j] = (fold(a_sum[j]) + fold(a_got[j])).astype(bf16)
        return c

    lax.fori_loop(0, chips, add_block, 0)
    one.start_plane()
    y_out.start()

    def between(pr):
        @pl.when(pr == 1)
        def _():
            one.start_z()

    attend_back(heads, seg, parents_ref, kaug_ref, v_ref, qT_ref, doT, kT_ref, do, qn_ref, oT_ref, lse_ref,
                dqT, dk, dv, accK, accV, between)
    one.start_back()

    cq = [pl.ds(pl.multiple_of(i * width + core * hw, hw), hw) for i in range(3)]

    def natural(p):
        cols = pl.ds(pl.multiple_of(p * rows, rows), rows)
        dq = dqT[:, cols].T
        do[cols, :] = dq
        return (dq, dk[pl.ds(p * 5, 5)].reshape(rows, hw), dv[pl.ds(p * 5, 5)].reshape(rows, hw))

    def da1_of(p):
        parts = natural(p)
        return sum(mm_nt(parts[i], wqkv_ref[:, cq[i]]) for i in range(3))

    da_out = [remote(das.at[i], dar.at[i], tsend.at[3 + i], trecv.at[3 + i], sibling) for i in range(2)]
    for i in range(2):
        das[i] = da1_of(other + 2 * i).astype(bf16)
        da_out[i].start()

    for i in range(2):
        do[pl.ds(pl.multiple_of((core + 2 * i) * rows, rows), rows), :] = (
            dqT[:, pl.ds(pl.multiple_of((core + 2 * i) * rows, rows), rows)].T)
    r2 = 2 * gwq_ref.shape[0]
    tree = 4 * rows
    sources = [do[...], dk[...].reshape(tree, hw), dv[...].reshape(tree, hw)]
    for i in range(3):
        g = mm(a1T_ref[...], sources[i]).astype(bf16)
        for j in range(chips):
            sum2[j, :, i * hw:(i + 1) * hw] = g[j * r2:(j + 1) * r2]
    two.start_plane()

    load_d.wait()
    dx_out = remote(dxo.at[1 - half], gt_ref.at[half], tsend.at[5], trecv.at[5], partner)
    keep_dx = pltpu.make_async_copy(dxo.at[half], gt_ref.at[half], lsem.at[6])
    gsum, bsum = None, None
    for c in load_x:
        c.wait()
    for step in range(2):
        i = (1 - half) if step == 0 else half
        da = da1_of(core + 2 * i)
        if step == 0:
            da_out[0].wait_recv()
            da_out[1].wait_recv()
        da = da + fold(dar[i])
        x = fold(xs[i])
        x = x - jnp.mean(x, axis=-1, keepdims=True)
        inv = lax.rsqrt(jnp.mean(x * x, axis=-1, keepdims=True) + 1e-06)
        unit = x * inv
        dn = da * n1_ref[0:1, 0:width]
        m1 = jnp.mean(dn, axis=-1, keepdims=True)
        m2 = jnp.mean(dn * unit, axis=-1, keepdims=True)
        dxo[i] = (dx2s[i] + (dn - m1 - unit * m2) * inv).astype(bf16)
        if step == 0:
            dx_out.start()
        else:
            keep_dx.start()
        gs = jnp.sum(da * unit, axis=0, keepdims=True)
        bs = jnp.sum(da, axis=0, keepdims=True)
        gsum = gs if gsum is None else gsum + gs
        bsum = bs if bsum is None else bsum + bs

    row = iota((16, width), 0)
    vs[0] = vin_ref[...] + jnp.where(row == 0, gsum, 0.0) + jnp.where(row == 1, bsum, 0.0)
    v_sib = remote(vs.at[0], vgot.at[0], vsend.at[0], vrecv.at[0], sibling)
    v_sib.start()

    two.start_z()
    v_sib.wait_recv()
    vs[1] = vs[0] + vgot[0]
    v_chip = [remote(vs.at[1], vgot.at[d], vsend.at[d], vrecv.at[d], lax.rem(f + 2 * d, F)) for d in range(1, chips)]
    for c in v_chip:
        c.start()
    for c in v_chip:
        c.wait_recv()
    total = vs[1]
    for d in range(1, chips):
        total = total + vgot[d]
    vgot[chips + plane] = total

    def v_z(e, sender):
        return pltpu.make_async_remote_copy(
            src_ref=vgot.at[chips + sender], dst_ref=vgot.at[chips + sender],
            send_sem=vsend.at[chips + e], recv_sem=vrecv.at[chips + e],
            device_id={"dp": lax.rem(plane + e, planes)}, device_id_type=pl.DeviceIdType.MESH)

    for e in range(1, planes):
        v_z(e, plane).start()

    two.start_back()
    one.receive()
    r = gwo_ref.shape[0]
    ru = gwu_ref.shape[0]
    gwu_ref[...] = fold(fin1[0:ru])
    pieces = gwi_ref.shape[1] // width
    for c in range(pieces):
        gwi_ref[:, c * width:(c + 1) * width] = fold(fin1[ru + c * r:ru + (c + 1) * r])
    gwo_ref[...] = fold(fin1[ru + pieces * r:ru + (pieces + 1) * r])

    two.receive()
    s_out = remote(fin2.at[pl.ds(pl.multiple_of(other * r, r), r)], rs2, tsend.at[6], trecv.at[6], sibling)
    s_out.start()
    mine = fin2[pl.ds(pl.multiple_of(core * r, r), r), :]
    here = pl.ds(pl.multiple_of(core * hw, hw), hw)
    there = pl.ds(pl.multiple_of(other * hw, hw), hw)
    outs = (gwq_ref, gwk_ref, gwv_ref)
    for i in range(3):
        outs[i][:, here] = fold(mine[:, i * hw:(i + 1) * hw])
    for e in range(1, planes):
        v_z(e, lax.rem(plane + planes - e, planes)).wait_recv()
    total = vgot[chips]
    for z in range(1, planes):
        total = total + vgot[chips + z]
    vout_ref[...] = total
    s_out.wait_recv()
    for i in range(3):
        outs[i][:, there] = fold(rs2[:, i * hw:(i + 1) * hw])

    dx_out.wait_recv()
    y_out.wait_recv()
    keep_y.wait()
    keep_dx.wait()
    one.close()
    two.close()
    for c in [dx_sw, a_out, y_out, dx_out, s_out, v_sib] + da_out + v_chip:
        c.wait_send()
    for e in range(1, planes):
        v_z(e, plane).wait_send()


def back(F, DP, parents, kaug, v, qT, kT, qn, oT, lse, a1T, wqkv, woi, xt, dxl, dx2, y, g1, vin, n1):
    _, rows, width = dxl.shape
    heads = H // 2
    hw = heads * 64
    tree = 4 * rows
    seg = rows // 5
    chips = F // 2
    hidden = woi.shape[1] - width
    r, ru = width // F, hidden // F
    R1 = g1.shape[2]
    r2 = 2 * r

    def zrows(n):
        return -(-n // (16 * DP)) * 16

    Z1, Z2 = zrows(R1), zrows(r2)
    ANY = pl.BlockSpec(memory_space=pl.ANY)
    dma = pltpu.SemaphoreType.DMA
    out = [((2, rows, width), bf16), ((2, rows, width), bf16), ((r, width), f32), ((r, width), f32), ((r, width), f32),
           ((r, width), f32), ((r, hidden), f32), ((ru, width), f32), ((16, width), f32)]
    scratch = [
        ((2, rows, width), bf16), ((hw, width), bf16), ((hw, tree), bf16), ((tree, hw), bf16), ((hw, tree), bf16),
        ((20, seg, hw), bf16), ((20, seg, hw), bf16), ((20, seg, 128), f32), ((20, seg, 128), f32),
        ((2, rows, width), f32), ((2, rows, width), bf16), ((2, rows, width), bf16), ((2, rows, width), bf16),
        ((chips, R1, width), bf16), ((chips, R1, width), bf16), ((chips - 1, R1, width), bf16),
        ((Z1 * DP, width), bf16), ((DP - 1, Z1, width), bf16), ((Z1 * DP, width), bf16),
        ((chips, r2, 3 * hw), bf16), ((chips - 1, r2, 3 * hw), bf16), ((Z2 * DP, 3 * hw), bf16),
        ((DP - 1, Z2, 3 * hw), bf16), ((Z2 * DP, 3 * hw), bf16), ((r, 3 * hw), bf16),
        ((2, 16, width), f32), ((chips + DP, 16, width), f32), ((2, rows, width), bf16),
    ]
    nsem = chips + 2 * DP
    return pl.pallas_call(
        functools.partial(back_kernel, F),
        out_shape=[jax.ShapeDtypeStruct(s, d) for s, d in out],
        in_specs=[SM] + [VM] * 9 + [ANY, ANY, VM, ANY, ANY, ANY, VM, VM],
        out_specs=[ANY, ANY] + [VM] * 7,
        scratch_shapes=[pltpu.VMEM(s, d) for s, d in scratch] + [
            dma((7,)), dma((7,)), dma((nsem,)), dma((nsem,)), dma((nsem,)), dma((nsem,)),
            dma((chips + DP,)), dma((chips + DP,)), dma((7,))],
        name="back",
        compiler_params=pltpu.CompilerParams(vmem_limit_bytes=62 << 20, collective_id=1, has_side_effects=True),
    )(parents, kaug, v, qT, kT, qn, oT, lse, a1T, wqkv, woi, xt, dxl, dx2, y, g1, vin, n1)


def normed(values, gain, shift):
    mean = jnp.mean(values, axis=-1, keepdims=True)
    centred = values - mean
    inv = lax.rsqrt(jnp.mean(centred * centred, axis=-1, keepdims=True) + 1e-06)
    unit = centred * inv
    return unit, inv, (unit * gain + shift).astype(bf16)


def norm_back(grad, unit, inv, gain):
    dn = grad * gain
    m1 = jnp.mean(dn, axis=-1, keepdims=True)
    m2 = jnp.mean(dn * unit, axis=-1, keepdims=True)
    return (dn - m1 - unit * m2) * inv


def gelu_and_slope(u):
    c = math.sqrt(2.0 / math.pi)
    t = jnp.tanh(c * (u + 0.044715 * u * u * u))
    g = 0.5 * u * (1.0 + t)
    slope = 0.5 * (1.0 + t) + 0.5 * u * (1.0 - t * t) * c * (1.0 + 3 * 0.044715 * u * u)
    return g, slope


def on_device(tokens, parents, n1g, n1b, wq, wk, wv, wo, ob, n2g, n2b, wi, ib, wu, ub, cotangent):
    F = lax.axis_size("fsdp")
    fi = lax.axis_index("fsdp")
    place = (fi + 2) % F
    half = (place % 4) // 2
    core = fi % 2
    quad = lax.axis_index("dp") * (F // 4) + place // 4
    parent_row = parents[quad, half]
    _, _, rows, width = tokens.shape
    heads = H // 2
    hw = heads * 64
    tree = 4 * rows

    def mine_of(x, c):
        a = jnp.concatenate([x[:rows], x[2 * rows:3 * rows]], axis=0)
        b = jnp.concatenate([x[rows:2 * rows], x[3 * rows:]], axis=0)
        return jnp.where(c == 0, a, b)

    n = n1g.shape[0]
    vec = jnp.concatenate([n1g, n1b, ob, n2g, n2b, ub, ib])
    vec = lax.reduce_precision(vec, 8, 7)
    vec = jnp.broadcast_to(jnp.pad(vec, (0, -vec.shape[0] % 128)), (8, vec.shape[0] + -vec.shape[0] % 128))
    (xt, a1T, kaug, v, kT, qn, qT, oT, lse, oF, dy_my, wqkv, woi, wu, vrows) = front(
        F, parent_row, tokens[0], cotangent[0], (wq, wk, wv, wo, wi, wu), vec, n)
    n1g, n1b, ob, n2g, n2b, ub = [vrows[0, i * width:(i + 1) * width] for i in range(6)]
    ib = vrows[0, 6 * width:]
    wo, wi = woi[:, :width], woi[:, width:]
    x_my = mine_of(xt.reshape(tree, width), core).astype(f32)
    dy_my = dy_my.reshape(2 * rows, width)

    x2 = x_my + mm_tn(oF, wo) + ob
    unit2, inv2, a2 = normed(x2, n2g, n2b)
    u = mm(a2, wi) + ib
    g, slope = gelu_and_slope(u)
    g = g.astype(bf16)
    y = (x2 + mm(g, wu) + ub).astype(bf16)
    g_wu = mm_tn(g, dy_my)
    dy = dy_my.astype(f32)
    g_ub = jnp.sum(dy, axis=0)
    du = (mm_nt(dy_my, wu) * slope).astype(bf16)
    g_wi = mm_tn(a2, du)
    g_ib = jnp.sum(du.astype(f32), axis=0)
    da2 = mm_nt(du, wi)
    g_n2g = jnp.sum(da2 * unit2, axis=0)
    g_n2b = jnp.sum(da2, axis=0)
    dx2 = dy + norm_back(da2, unit2, inv2, n2g)
    dx2_low = dx2.astype(bf16)
    g_wo = mm(oF, dx2_low)
    g_ob = jnp.sum(dx2_low.astype(f32), axis=0)
    hidden = wi.shape[1]
    r, ru = width // F, hidden // F
    g1 = jnp.concatenate([
        g_wu.reshape(F, ru, width),
        g_wi.reshape(F, r, hidden // width, width).transpose(0, 2, 1, 3).reshape(F, hidden // F, width),
        g_wo.reshape(F, r, width)], axis=1).astype(bf16)
    g1 = g1.reshape(F // 2, 2, -1, width)
    zero = jnp.zeros((2, width), f32)
    vin = jnp.concatenate([zero, g_ob[None], g_n2g[None], g_n2b[None], g_ub[None], g_ib.reshape(-1, width)], axis=0)
    vin = jnp.pad(vin, ((0, 16 - vin.shape[0]), (0, 0)))
    lo, gt, gwq, gwk, gwv, gwo, gwi, gwu, vout = back(
        F, lax.axis_size("dp"), parent_row, kaug, v, qT, kT, qn, oT, lse, a1T, wqkv, woi, xt,
        dx2_low.reshape(2, rows, width), dx2.reshape(2, rows, width), y.reshape(2, rows, width), g1, vin,
        vrows)
    sv = lax.dynamic_slice_in_dim(vout[:6], fi * n, n, 1)
    sib = lax.dynamic_slice_in_dim(vout[6:6 + hidden // width].reshape(-1), fi * ru, ru, 0)
    return (lo[None], gt[None], sv[0], sv[1], gwq, gwk, gwv, gwo, sv[2], sv[3], sv[4], gwi, sib, gwu, sv[5])


def solution(mesh):
    tok = P(("dp", "fsdp"), None, None, None)
    v, m = P("fsdp"), P("fsdp", None)
    return jax.shard_map(
        on_device,
        mesh=mesh,
        in_specs=(tok, P(), v, v, m, m, m, m, v, v, v, m, v, m, v, tok),
        out_specs=(tok, tok, v, v, m, m, m, m, v, v, v, m, v, m, v),
        check_vma=False,
    )
```

```python
import functools
import math

import jax
import jax.numpy as jnp
import ml_dtypes
import numpy as np
from jax import lax
from jax.experimental import pallas as pl
from jax.experimental.pallas import tpu as pltpu
from jax.sharding import PartitionSpec as P

H = 8
T = 256
f32, bf16 = jnp.float32, jnp.bfloat16
VM = pl.BlockSpec(memory_space=pltpu.VMEM)
SM = pl.BlockSpec(memory_space=pltpu.SMEM)


def mm(a, b):
    return jnp.dot(a, b, preferred_element_type=f32)


def mm_tn(a, b):
    return lax.dot_general(a, b, (((0,), (0,)), ((), ())), preferred_element_type=f32)


def mm_nt(a, b):
    return lax.dot_general(a, b, (((1,), (1,)), ((), ())), preferred_element_type=f32)


def iota(shape, dim):
    return lax.broadcasted_iota(jnp.int32, shape, dim)


def chosen(par, read):
    out = read(0)
    for b in range(1, 4):
        out = jnp.where(par == b + 1, read(b), out)
    return out


def attend(heads, seg, parents_ref, kaug_ref, qT_ref, vT_ref, oT_ref, lse_ref, s_scr, between):
    trunk = 8 * seg
    ntr = trunk // T
    vr = vT_ref.shape[0] // heads
    causal_t = iota((T, T), 0) <= iota((T, T), 1)
    causal_b = iota((seg, seg), 0) <= iota((seg, seg), 1)

    def finish(h, cols, m, acc):
        l = acc[64:65, :]
        oT_ref[pl.ds(pl.multiple_of(h * 64, 64), 64), cols] = (acc[:64] / l).astype(bf16)
        lse_ref[pl.ds(pl.multiple_of(h * 8, 8), 8), cols] = jnp.broadcast_to(m + jnp.log(l), (8, T))

    def head(h, _):
        between(h)
        hk = pl.ds(pl.multiple_of(h * 128, 128), 128)
        hv = pl.ds(pl.multiple_of(h * vr, vr), vr)

        def keys(blk, n):
            return kaug_ref[pl.ds(blk, n), :, hk].reshape(n * seg, 128)

        def full_scores(q, n):
            m = None
            for c in range(n):
                s = mm(keys(2 * c, 2), q)
                s_scr[c * T:(c + 1) * T, :] = s
                cm = jnp.max(s, axis=0, keepdims=True)
                m = cm if m is None else jnp.maximum(m, cm)
            return m

        def full_mix(m, n, acc):
            for c in range(n):
                p = jnp.exp(s_scr[c * T:(c + 1) * T, :] - m).astype(bf16)
                t = mm(vT_ref[hv, c * T:(c + 1) * T], p)
                acc = t if acc is None else acc + t
            return acc

        for t in range(ntr):
            cols = slice(t * T, (t + 1) * T)
            q = qT_ref[hk, cols]
            sd = jnp.where(causal_t, mm(keys(2 * t, 2), q), -1e30)
            m = jnp.max(sd, axis=0, keepdims=True)
            if t:
                m = jnp.maximum(m, full_scores(q, t))
            acc = mm(vT_ref[hv, cols], jnp.exp(sd - m).astype(bf16))
            acc = full_mix(m, t, acc)
            finish(h, cols, m, acc)

        def tail_tile(i, leaf):
            b0 = 8 + 2 * i
            cols = pl.ds(pl.multiple_of(b0 * seg, T), T)
            q = qT_ref[hk, cols]
            rows = []
            for half in range(2):
                rows.append([b0 + half])
                if leaf:
                    rows[-1].append(parents_ref[b0 + half - 7])
            m = full_scores(q, ntr)
            ext = []
            for e in range(len(rows[0])):
                pieces = []
                for half in range(2):
                    kk = keys(rows[half][0], 1) if e == 0 else chosen(rows[half][1], lambda b: keys(8 + b, 1))
                    s = mm(kk, q[:, half * seg:(half + 1) * seg])
                    if e == 0:
                        s = jnp.where(causal_b, s, -1e30)
                    pieces.append(s)
                s = jnp.concatenate(pieces, axis=1)
                m = jnp.maximum(m, jnp.max(s, axis=0, keepdims=True))
                ext.append(s)
            acc = None
            for e in range(len(ext)):
                p = jnp.exp(ext[e] - m).astype(bf16)
                t = []
                for half in range(2):
                    if e == 0:
                        vv = vT_ref[hv, pl.ds(pl.multiple_of(rows[half][0] * seg, seg), seg)]
                    else:
                        vv = chosen(rows[half][1], lambda b: vT_ref[hv, (8 + b) * seg:(9 + b) * seg])
                    t.append(mm(vv, p[:, half * seg:(half + 1) * seg]))
                t = jnp.concatenate(t, axis=1)
                acc = t if acc is None else acc + t
            acc = full_mix(m, ntr, acc)
            finish(h, cols, m, acc)

        lax.fori_loop(0, 2, lambda i, c: (tail_tile(i, False), c)[1], 0)
        lax.fori_loop(2, 6, lambda i, c: (tail_tile(i, True), c)[1], 0)
        return 0

    lax.fori_loop(0, heads, head, 0)


def attend_back(heads, seg, parents_ref, kaug_ref, v_ref, qT_ref, doT_ref, kT_ref, do_ref, qn_ref,
                oT_ref, lse_ref, dqT_ref, dk_ref, dv_ref, accK, accV, between):
    ntr = 8 * seg // T
    causal_t = iota((T, T), 0) <= iota((T, T), 1)
    causal_b = iota((seg, seg), 0) <= iota((seg, seg), 1)
    low_rows = iota((128, T), 0) < 64
    low_lanes = iota((T, 128), 1) < 64

    def pair(pr, _):
        between(pr)
        lanes = pl.ds(pl.multiple_of(pr * 128, 128), 128)
        hk = [pl.ds(pl.multiple_of(pr * 256 + 128 * e, 128), 128) for e in range(2)]
        h64 = [pl.ds(pl.multiple_of(pr * 128 + 64 * e, 64), 64) for e in range(2)]
        accK[...] = jnp.zeros_like(accK)
        accV[...] = jnp.zeros_like(accV)

        def stack(x):
            z = jnp.zeros_like(x)
            return jnp.concatenate([jnp.where(low_lanes, x, z), jnp.where(low_lanes, z, x)], axis=0)

        def prep(cols):
            doT = doT_ref[lanes, cols]
            z = jnp.zeros_like(doT)
            prod = doT.astype(f32) * oT_ref[lanes, cols].astype(f32)
            q, do, lse, delta = [], [], [], []
            for e in range(2):
                q.append(qT_ref[hk[e], cols])
                do.append(jnp.where(low_rows, doT, z) if e == 0 else jnp.where(low_rows, z, doT))
                at = pl.multiple_of((pr * 2 + e) * 8, 8)
                lse.append(jnp.max(lse_ref[pl.ds(at, 8), cols], axis=0, keepdims=True))
                delta.append(jnp.sum(prod[64 * e:64 * e + 64], axis=0, keepdims=True))
            return q, do, lse, delta, stack(do_ref[cols, lanes]), stack(qn_ref[cols, lanes])

        def piece(blk, n, sl, args, mask, par=None):
            q, do, lse, delta, rv, rk = args
            ps, dss, dq = [], [], []

            def rows_of(ref, at):
                if par is None:
                    return ref[pl.ds(blk, n), :, at].reshape(n * seg, 128)
                return chosen(par, lambda b: ref[8 + b, :, at])

            vv = rows_of(v_ref, lanes)
            for e in range(2):
                kk = rows_of(kaug_ref, hk[e])
                p = jnp.exp(mm(kk, q[e][:, sl]) - lse[e][:, sl])
                if mask is not None:
                    p = jnp.where(mask, p, 0.0)
                dp = mm(vv, do[e][:, sl])
                ds = (p * (dp - delta[e][:, sl])).astype(bf16)
                if par is None:
                    kT = kT_ref[h64[e], pl.ds(pl.multiple_of(blk * seg, seg), n * seg)]
                else:
                    kT = chosen(par, lambda b: kT_ref[h64[e], (8 + b) * seg:(9 + b) * seg])
                dq.append(mm(kT, ds))
                ps.append(p.astype(bf16))
                dss.append(ds)
            if sl.stop - sl.start != T:
                rv = jnp.concatenate([rv[sl], rv[T + sl.start:T + sl.stop]], axis=0)
                rk = jnp.concatenate([rk[sl], rk[T + sl.start:T + sl.stop]], axis=0)
            av = mm(jnp.concatenate(ps, axis=1), rv)
            ak = mm(jnp.concatenate(dss, axis=1), rk)
            if par is None:
                accV[pl.ds(blk, n)] += av.reshape(n, seg, 128)
                accK[pl.ds(blk, n)] += ak.reshape(n, seg, 128)
            else:
                for b in range(4):
                    here = jnp.where(par == b + 1, 1.0, 0.0)
                    accK[8 + b] += ak * here
                    accV[8 + b] += av * here
            return dq

        def emit(cols, dq):
            for e in range(2):
                dqT_ref[h64[e], cols] = (dq[e] * 0.125).astype(bf16)

        full = slice(0, T)
        for t in range(ntr):
            cols = slice(t * T, (t + 1) * T)
            args = prep(cols)
            dq = piece(2 * t, 2, full, args, causal_t)
            for c in range(t):
                dq = [a + b for a, b in zip(dq, piece(2 * c, 2, full, args, None))]
            emit(cols, dq)

        def tail_tile(i, leaf):
            b0 = 8 + 2 * i
            cols = pl.ds(pl.multiple_of(b0 * seg, T), T)
            args = prep(cols)
            halves = []
            for half in range(2):
                sl = slice(half * seg, (half + 1) * seg)
                d = piece(b0 + half, 1, sl, args, causal_b)
                if leaf:
                    par = parents_ref[b0 + half - 7]
                    d = [x + y for x, y in zip(d, piece(8, 1, sl, args, None, par))]
                halves.append(d)
            dq = [jnp.concatenate([halves[0][e], halves[1][e]], axis=1) for e in range(2)]
            for c in range(ntr):
                dq = [a + b for a, b in zip(dq, piece(2 * c, 2, full, args, None))]
            emit(cols, dq)

        lax.fori_loop(0, 2, lambda i, c: (tail_tile(i, False), c)[1], 0)
        lax.fori_loop(2, 6, lambda i, c: (tail_tile(i, True), c)[1], 0)
        dk_ref[:, :, lanes] = accK[...].astype(bf16)
        dv_ref[:, :, lanes] = accV[...].astype(bf16)
        return 0

    lax.fori_loop(0, heads // 2, pair, 0)


def slope_parts(head, head_count, length):
    x = np.float32(2.0 ** (2.0 - 4.0 * head / head_count) / length)
    out = []
    for _ in range(3):
        low = np.float32(ml_dtypes.bfloat16(x))
        out.append(float(low))
        x = np.float32(x - low)
    return out


def remote(src, dst, send_sem, recv_sem, target):
    return pltpu.make_async_remote_copy(
        src_ref=src, dst_ref=dst, send_sem=send_sem, recv_sem=recv_sem,
        device_id={"fsdp": target}, device_id_type=pl.DeviceIdType.MESH)


def where_am_i(F):
    f = lax.axis_index("fsdp")
    place = lax.rem(f + 2, F)
    part = lax.rem(place, 4)
    half = part // 2
    core = lax.rem(f, 2)
    base = place - part
    partner = lax.rem(base + lax.rem(part + 2, 4) + F - 2, F)
    sibling = f + 1 - 2 * core
    return f, part, half, core, partner, sibling


def greet(F, f, core, sibling):
    barrier = pltpu.get_barrier_semaphore()
    for d in range(1, F // 2):
        pl.semaphore_signal(barrier, inc=1, device_id={"fsdp": lax.rem(f + 2 * d, F)},
                            device_id_type=pl.DeviceIdType.MESH)
    pl.semaphore_signal(barrier, inc=1, device_id={"fsdp": sibling}, device_id_type=pl.DeviceIdType.MESH)
    pl.semaphore_wait(barrier, F // 2)


def front_kernel(F, n, parents_ref, tok_ref, cot_ref, wq_ref, wk_ref, wv_ref, wo_ref, wi_ref, wu_ref, vec_ref,
                 xt_ref, a1T_ref, kaug_ref, v_ref, kT_ref, qn_ref, qT_ref, oT_ref, lse_ref, oF_ref, dy_ref,
                 wqkv_ref, woi_ref, wuf_ref, rows_ref,
                 vecs, vT_scr, s_scr, tsend, trecv, gsend, grecv):
    f, part, half, core, partner, sibling = where_am_i(F)
    rows, width = tok_ref.shape[1:]
    seg = rows // 5
    heads = H // 2
    hw = heads * 64
    tree = 4 * rows
    r = wq_ref.shape[0]
    ru = wu_ref.shape[0]
    part1 = part + 1 - 2 * core
    part2 = lax.rem(part + 2, 4)
    part3 = lax.rem(part1 + 2, 4)

    own = pl.ds(pl.multiple_of(f * r, r), r)
    ownu = pl.ds(pl.multiple_of(f * ru, ru), ru)
    vecs[f] = vec_ref[...]
    wqkv_ref[own, 0:width] = wq_ref[...].astype(bf16)
    wqkv_ref[own, width:2 * width] = wk_ref[...].astype(bf16)
    wqkv_ref[own, 2 * width:3 * width] = wv_ref[...].astype(bf16)

    greet(F, f, core, sibling)

    def slot(g, src):
        if g == 0:
            return vecs.at[src]
        if g == 3:
            return wuf_ref.at[pl.ds(pl.multiple_of(src * ru, ru), ru)]
        ref = wqkv_ref if g == 1 else woi_ref
        return ref.at[pl.ds(pl.multiple_of(src * r, r), r)]

    def direct(g, d):
        return remote(slot(g, f), slot(g, f), gsend.at[g, d], grecv.at[g, d],
                      sibling if d == 0 else lax.rem(f + 2 * d, F))

    def came(g, d):
        src = sibling if d == 0 else lax.rem(f + F - 2 * d, F)
        remote(slot(g, src), slot(g, src), gsend.at[g, d], grecv.at[g, d], sibling).wait_recv()

    def forward(g, d):
        src = lax.rem(f + F - 2 * d, F)
        return remote(slot(g, src), slot(g, src), gsend.at[g, F // 2 + d], grecv.at[g, F // 2 + d], sibling)

    def forwarded(g, d):
        src = lax.rem(sibling + F - 2 * d, F)
        remote(slot(g, src), slot(g, src), gsend.at[g, F // 2 + d], grecv.at[g, F // 2 + d], sibling).wait_recv()

    chips = range(1, F // 2)

    def send_all(g):
        for d in range(F // 2):
            direct(g, d).start()

    def pass_on(g):
        for d in chips:
            came(g, d)
            forward(g, d).start()

    def receive_rest(g):
        came(g, 0)
        for d in chips:
            forwarded(g, d)

    x_out = remote(tok_ref.at[1 - half], xt_ref.at[part], tsend.at[0], trecv.at[0], partner)
    x_sib = remote(tok_ref.at[half], xt_ref.at[part], tsend.at[1], trecv.at[1], sibling)
    x_fwd = remote(xt_ref.at[part2], xt_ref.at[part2], tsend.at[2], trecv.at[2], sibling)
    dy_out = remote(cot_ref.at[1 - half], dy_ref.at[half], tsend.at[3], trecv.at[3], partner)
    dy_own = pltpu.make_async_copy(cot_ref.at[half], dy_ref.at[half], tsend.at[4])

    send_all(0)
    send_all(1)
    x_out.start()
    x_sib.start()
    dy_own.start()
    xt_ref[part] = tok_ref[half]
    woi_ref[own, 0:width] = wo_ref[...].astype(bf16)
    woi_ref[own, width:] = wi_ref[...].astype(bf16)
    wuf_ref[ownu, :] = wu_ref[...].astype(bf16)
    pass_on(0)
    pass_on(1)
    receive_rest(0)

    table = jnp.max(vecs[...], axis=1).astype(bf16)
    words = table.shape[1]

    def vector_row(first, m, length):
        col = iota((words, length), 1)
        pick = iota((words, length), 0) == first + (col & (m - 1))
        spread = mm(table, pick.astype(bf16))
        shift = m.bit_length() - 1
        mine = iota((F, length), 0) == (iota((F, length), 1) >> shift)
        return jnp.sum(jnp.where(mine, spread, 0.0), axis=0, keepdims=True)

    for i in range(6):
        rows_ref[:, i * width:(i + 1) * width] = jnp.broadcast_to(vector_row(i * n, n, width), (8, width))
    hidden = rows_ref.shape[1] - 6 * width
    rows_ref[:, 6 * width:] = jnp.broadcast_to(vector_row(6 * n, hidden // F, hidden), (8, hidden))

    receive_rest(1)

    lane = iota((seg, 128), 1)
    offs = iota((seg, 128), 0)
    arow = iota((64, rows), 0)

    def project(p):
        x = xt_ref[p].astype(f32)
        gain = rows_ref[0:1, 0:width]
        shift = rows_ref[0:1, width:2 * width]
        mean = jnp.mean(x, axis=-1, keepdims=True)
        x = x - mean
        inv = lax.rsqrt(jnp.mean(x * x, axis=-1, keepdims=True) + 1e-06)
        a1 = (x * inv * gain + shift).astype(bf16)

        def proj(i):
            return mm(a1, wqkv_ref[:, pl.ds(pl.multiple_of(i * width + core * hw, hw), hw)])

        cols = pl.ds(pl.multiple_of(p * rows, rows), rows)
        a1T_ref[:, cols] = a1.T
        q = (proj(0) * 0.125).astype(bf16)
        qn_ref[cols, :] = q
        qT = q.T
        k = proj(1).astype(bf16)
        kT_ref[:, cols] = k.T
        v = proj(2).astype(bf16)
        v_ref[pl.ds(p * 5, 5)] = v.reshape(5, seg, hw)
        vT = v.T
        for h in range(heads):
            a, b = slope_parts(h, H, tree), slope_parts(heads + h, H, tree)
            aug = jnp.zeros((64, rows), f32)
            for j in range(3):
                s = jnp.where(core == 0, a[j], b[j])
                aug = jnp.where((arow == j) | (arow == j + 3), s, aug)
            aug = aug.astype(bf16)
            lo, hi = 128 * h + 64 * (h % 2), 128 * h + 64 - 64 * (h % 2)
            qT_ref[lo:lo + 64, cols] = qT[64 * h:64 * h + 64]
            qT_ref[hi:hi + 64, cols] = aug
            vT_scr[80 * h:80 * h + 64, cols] = vT[64 * h:64 * h + 64]
            vT_scr[80 * h + 64:80 * h + 80, cols] = jnp.ones((16, rows), bf16)
        for b in range(5):
            blk = p * 5 + b
            start = jnp.where(blk < 8, blk * seg, jnp.where(blk < 12, 8 * seg, 9 * seg))
            spot = offs + start
            hi = (spot & -8).astype(f32)
            lo = (spot & 7).astype(f32)
            for h in range(heads):
                at = 64 - 64 * (h % 2)
                l = lane - at
                aug = jnp.where((l >= 0) & (l < 3), hi, jnp.where((l >= 3) & (l < 6), lo, 0.0)).astype(bf16)
                keep = (lane < 64) if h % 2 == 0 else (lane >= 64)
                kk = k[b * seg:(b + 1) * seg, 128 * (h // 2):128 * (h // 2) + 128]
                kaug_ref[blk, :, 128 * h:128 * h + 128] = jnp.where(keep, kk, aug)

    x_sib.wait_recv()
    order = [part, part1, part2, part3]
    lax.fori_loop(0, 2, lambda i, c: (project(jnp.where(i == 0, part, part1)), c)[1], 0)
    x_out.wait_recv()
    x_fwd.start()
    send_all(2)
    send_all(3)
    dy_out.start()
    x_fwd.wait_recv()
    lax.fori_loop(0, 2, lambda i, c: (project(jnp.where(i == 0, part2, part3)), c)[1], 0)

    def between(h):
        @pl.when(h == 2)
        def _():
            pass_on(2)

    attend(heads, seg, parents_ref, kaug_ref, qT_ref, vT_scr, oT_ref, lse_ref, s_scr, between)

    pass_on(3)
    other = 1 - core
    sent = []
    for i in range(2):
        cols = pl.ds(pl.multiple_of((other + 2 * i) * rows, rows), rows)
        mine = pl.ds(pl.multiple_of((core + 2 * i) * rows, rows), rows)
        at = (pl.ds(pl.multiple_of(core * hw, hw), hw), slice(i * rows, (i + 1) * rows))
        c = remote(oT_ref.at[:, cols], oF_ref.at[at], tsend.at[5 + i], trecv.at[5 + i], sibling)
        c.start()
        sent.append(c)
        oF_ref[at] = oT_ref[:, mine]
    for c in sent:
        c.wait()
    receive_rest(2)
    receive_rest(3)
    dy_own.wait()
    dy_out.wait()
    x_out.wait_send()
    x_sib.wait_send()
    x_fwd.wait_send()
    for g in range(4):
        for d in range(F // 2):
            direct(g, d).wait_send()
        for d in chips:
            forward(g, d).wait_send()


def front(F, parents, tokens, cotangent, weights, vec, n):
    _, rows, width = tokens.shape
    tree = 4 * rows
    heads = H // 2
    hw = heads * 64
    seg = rows // 5
    hidden = weights[4].shape[1]
    out = [
        ((4, rows, width), bf16), ((width, tree), bf16), ((20, seg, heads * 128), bf16), ((20, seg, hw), bf16),
        ((hw, tree), bf16), ((tree, hw), bf16), ((heads * 128, tree), bf16), ((hw, tree), bf16),
        ((heads * 8, tree), f32), ((2 * hw, 2 * rows), bf16), ((2, rows, width), bf16),
        ((width, 3 * width), bf16), ((width, width + hidden), bf16), ((hidden, width), bf16),
        ((8, 6 * width + hidden), f32),
    ]
    specs = [VM] * len(out)
    specs[10] = pl.BlockSpec(memory_space=pl.ANY)
    dma = pltpu.SemaphoreType.DMA
    return pl.pallas_call(
        functools.partial(front_kernel, F, n),
        out_shape=[jax.ShapeDtypeStruct(s, d) for s, d in out],
        in_specs=[SM, VM, pl.BlockSpec(memory_space=pl.ANY)] + [VM] * 7,
        out_specs=specs,
        scratch_shapes=[
            pltpu.VMEM((F,) + vec.shape, f32),
            pltpu.VMEM((heads * 80, tree), bf16), pltpu.VMEM((8 * seg, T), f32),
            dma((7,)), dma((7,)), dma((4, F)), dma((4, F)),
        ],
        name="front",
        compiler_params=pltpu.CompilerParams(vmem_limit_bytes=56 << 20, collective_id=0, has_side_effects=True),
    )(parents, tokens, cotangent, *weights, vec)


def fold(x):
    return x.astype(f32)


class Chain:
    def __init__(self, F, f, sums, got, block, zgot, final, send, recv):
        self.F, self.f, self.sums, self.got, self.block = F, f, sums, got, block
        self.zgot, self.final, self.send, self.recv = zgot, final, send, recv
        self.chip = f // 2
        self.chips = F // 2
        self.planes = lax.axis_size("dp")
        self.plane = lax.axis_index("dp")
        self.rows = sums.shape[1]
        self.zrows = block.shape[0] // self.planes

    def _b(self, d):
        return remote(self.sums.at[lax.rem(self.chip + d, self.chips)], self.got.at[d - 1],
                      self.send.at[d], self.recv.at[d], lax.rem(self.f + 2 * d, self.F))

    def _chunk(self, z):
        return pl.ds(pl.multiple_of(z * self.zrows, 16), self.zrows)

    def _c(self, e):
        z = lax.rem(self.plane + e, self.planes)
        i = self.chips + e
        return pltpu.make_async_remote_copy(
            src_ref=self.block.at[self._chunk(z)], dst_ref=self.zgot.at[e - 1],
            send_sem=self.send.at[i], recv_sem=self.recv.at[i],
            device_id={"dp": z}, device_id_type=pl.DeviceIdType.MESH)

    def _d(self, e, src=None):
        z = lax.rem(self.plane + e, self.planes)
        i = self.chips + self.planes + e
        here = self._chunk(self.plane if src is None else src)
        return pltpu.make_async_remote_copy(
            src_ref=self.final.at[here], dst_ref=self.final.at[here],
            send_sem=self.send.at[i], recv_sem=self.recv.at[i],
            device_id={"dp": z}, device_id_type=pl.DeviceIdType.MESH)

    def start_plane(self):
        for d in range(1, self.chips):
            self._b(d).start()

    def start_z(self):
        for d in range(1, self.chips):
            self._b(d).wait_recv()
        total = fold(self.sums[self.chip])
        for d in range(1, self.chips):
            total = total + fold(self.got[d - 1])
        self.block[0:self.rows] = total.astype(bf16)
        for e in range(1, self.planes):
            self._c(e).start()

    def start_back(self):
        for e in range(1, self.planes):
            self._c(e).wait_recv()
        here = self._chunk(self.plane)
        total = fold(self.block[here])
        for e in range(1, self.planes):
            total = total + fold(self.zgot[e - 1])
        self.final[here] = total.astype(bf16)
        for e in range(1, self.planes):
            self._d(e).start()

    def receive(self):
        for e in range(1, self.planes):
            self._d(e, lax.rem(self.plane + self.planes - e, self.planes)).wait_recv()

    def close(self):
        for d in range(1, self.chips):
            self._b(d).wait_send()
        for e in range(1, self.planes):
            self._c(e).wait_send()
            self._d(e).wait_send()


def back_kernel(F, parents_ref, kaug_ref, v_ref, qT_ref, kT_ref, qn_ref, oT_ref, lse_ref, a1T_ref, wqkv_ref, wo_ref,
                xt_ref, dxl_ref, dx2_ref, y_ref, g1_ref, vin_ref, n1_ref,
                lo_ref, gt_ref, gwq_ref, gwk_ref, gwv_ref, gwo_ref, gwi_ref, gwu_ref, vout_ref,
                dxs, wo_scr, doT, do, dqT, dk, dv, accK, accV, dx2s, das, dar, xs,
                a_sum, a_got, b_got, blk1, z1, fin1, sum2, got2, blk2, z2, fin2, rs2,
                vs, vgot, dxo, tsend, trecv, send1, recv1, send2, recv2, vsend, vrecv, lsem):
    f, part, half, core, partner, sibling = where_am_i(F)
    planes = lax.axis_size("dp")
    plane = lax.axis_index("dp")
    heads = H // 2
    hw = heads * 64
    _, rows, width = dxl_ref.shape
    seg = rows // 5
    chips = F // 2
    other = 1 - core

    load_g = pltpu.make_async_copy(g1_ref.at[:, core], a_sum, lsem.at[0])
    load_w = pltpu.make_async_copy(wo_ref.at[pl.ds(pl.multiple_of(core * hw, hw), hw), 0:width], wo_scr, lsem.at[1])
    load_d = pltpu.make_async_copy(dx2_ref, dx2s, lsem.at[2])
    keep_y = pltpu.make_async_copy(y_ref.at[half], lo_ref.at[half], lsem.at[3])
    load_x = [pltpu.make_async_copy(xt_ref.at[core + 2 * i], xs.at[i], lsem.at[4 + i]) for i in range(2)]
    for c in [load_w, load_g, load_d, keep_y] + load_x:
        c.start()

    barrier = pltpu.get_barrier_semaphore()
    for d in range(1, chips):
        pl.semaphore_signal(barrier, inc=1, device_id={"fsdp": lax.rem(f + 2 * d, F)},
                            device_id_type=pl.DeviceIdType.MESH)
    for e in range(1, planes):
        pl.semaphore_signal(barrier, inc=1, device_id={"dp": lax.rem(plane + e, planes)},
                            device_id_type=pl.DeviceIdType.MESH)
    pl.semaphore_signal(barrier, inc=1, device_id={"fsdp": sibling}, device_id_type=pl.DeviceIdType.MESH)
    pl.semaphore_wait(barrier, chips + planes - 1)

    dx_sw = remote(dxl_ref, dxs, tsend.at[0], trecv.at[0], sibling)
    a_out = remote(g1_ref.at[:, other], a_got, tsend.at[1], trecv.at[1], sibling)
    y_out = remote(y_ref.at[1 - half], lo_ref.at[half], tsend.at[2], trecv.at[2], partner)
    dx_sw.start()
    a_out.start()

    def make_do(p, x):
        cols = pl.ds(pl.multiple_of(p * rows, rows), rows)
        d = mm_nt(x, wo_scr[...]).astype(bf16)
        do[cols, :] = d
        doT[:, cols] = d.T

    load_w.wait()
    lax.fori_loop(0, 2, lambda i, c: (make_do(core + 2 * i, dxl_ref[i]), c)[1], 0)
    dx_sw.wait_recv()
    lax.fori_loop(0, 2, lambda i, c: (make_do(other + 2 * i, dxs[i]), c)[1], 0)

    one = Chain(F, f, a_sum, b_got, blk1, z1, fin1, send1, recv1)
    two = Chain(F, f, sum2, got2, blk2, z2, fin2, send2, recv2)
    load_g.wait()
    a_out.wait_recv()

    def add_block(j, c):
        a_sum[j] = (fold(a_sum[j]) + fold(a_got[j])).astype(bf16)
        return c

    lax.fori_loop(0, chips, add_block, 0)
    one.start_plane()
    y_out.start()

    def between(pr):
        @pl.when(pr == 1)
        def _():
            one.start_z()

    attend_back(heads, seg, parents_ref, kaug_ref, v_ref, qT_ref, doT, kT_ref, do, qn_ref, oT_ref, lse_ref,
                dqT, dk, dv, accK, accV, between)
    one.start_back()

    cq = [pl.ds(pl.multiple_of(i * width + core * hw, hw), hw) for i in range(3)]

    def natural(p):
        cols = pl.ds(pl.multiple_of(p * rows, rows), rows)
        dq = dqT[:, cols].T
        do[cols, :] = dq
        return (dq, dk[pl.ds(p * 5, 5)].reshape(rows, hw), dv[pl.ds(p * 5, 5)].reshape(rows, hw))

    def da1_of(p):
        parts = natural(p)
        return sum(mm_nt(parts[i], wqkv_ref[:, cq[i]]) for i in range(3))

    da_out = [remote(das.at[i], dar.at[i], tsend.at[3 + i], trecv.at[3 + i], sibling) for i in range(2)]
    for i in range(2):
        das[i] = da1_of(other + 2 * i).astype(bf16)
        da_out[i].start()

    for i in range(2):
        do[pl.ds(pl.multiple_of((core + 2 * i) * rows, rows), rows), :] = (
            dqT[:, pl.ds(pl.multiple_of((core + 2 * i) * rows, rows), rows)].T)
    r2 = 2 * gwq_ref.shape[0]
    tree = 4 * rows
    sources = [do[...], dk[...].reshape(tree, hw), dv[...].reshape(tree, hw)]
    for i in range(3):
        g = mm(a1T_ref[...], sources[i]).astype(bf16)
        for j in range(chips):
            sum2[j, :, i * hw:(i + 1) * hw] = g[j * r2:(j + 1) * r2]
    two.start_plane()

    load_d.wait()
    dx_out = remote(dxo.at[1 - half], gt_ref.at[half], tsend.at[5], trecv.at[5], partner)
    keep_dx = pltpu.make_async_copy(dxo.at[half], gt_ref.at[half], lsem.at[6])
    gsum, bsum = None, None
    for c in load_x:
        c.wait()
    for step in range(2):
        i = (1 - half) if step == 0 else half
        da = da1_of(core + 2 * i)
        if step == 0:
            da_out[0].wait_recv()
            da_out[1].wait_recv()
        da = da + fold(dar[i])
        x = fold(xs[i])
        x = x - jnp.mean(x, axis=-1, keepdims=True)
        inv = lax.rsqrt(jnp.mean(x * x, axis=-1, keepdims=True) + 1e-06)
        unit = x * inv
        dn = da * n1_ref[0:1, 0:width]
        m1 = jnp.mean(dn, axis=-1, keepdims=True)
        m2 = jnp.mean(dn * unit, axis=-1, keepdims=True)
        dxo[i] = (dx2s[i] + (dn - m1 - unit * m2) * inv).astype(bf16)
        if step == 0:
            dx_out.start()
        else:
            keep_dx.start()
        gs = jnp.sum(da * unit, axis=0, keepdims=True)
        bs = jnp.sum(da, axis=0, keepdims=True)
        gsum = gs if gsum is None else gsum + gs
        bsum = bs if bsum is None else bsum + bs

    row = iota((16, width), 0)
    vs[0] = vin_ref[...] + jnp.where(row == 0, gsum, 0.0) + jnp.where(row == 1, bsum, 0.0)
    v_sib = remote(vs.at[0], vgot.at[0], vsend.at[0], vrecv.at[0], sibling)
    v_sib.start()

    two.start_z()
    v_sib.wait_recv()
    vs[1] = vs[0] + vgot[0]
    v_chip = [remote(vs.at[1], vgot.at[d], vsend.at[d], vrecv.at[d], lax.rem(f + 2 * d, F)) for d in range(1, chips)]
    for c in v_chip:
        c.start()
    for c in v_chip:
        c.wait_recv()
    total = vs[1]
    for d in range(1, chips):
        total = total + vgot[d]
    vgot[chips + plane] = total

    def v_z(e, sender):
        return pltpu.make_async_remote_copy(
            src_ref=vgot.at[chips + sender], dst_ref=vgot.at[chips + sender],
            send_sem=vsend.at[chips + e], recv_sem=vrecv.at[chips + e],
            device_id={"dp": lax.rem(plane + e, planes)}, device_id_type=pl.DeviceIdType.MESH)

    for e in range(1, planes):
        v_z(e, plane).start()

    two.start_back()
    one.receive()
    r = gwo_ref.shape[0]
    ru = gwu_ref.shape[0]
    gwu_ref[...] = fold(fin1[0:ru])
    pieces = gwi_ref.shape[1] // width
    for c in range(pieces):
        gwi_ref[:, c * width:(c + 1) * width] = fold(fin1[ru + c * r:ru + (c + 1) * r])
    gwo_ref[...] = fold(fin1[ru + pieces * r:ru + (pieces + 1) * r])

    two.receive()
    s_out = remote(fin2.at[pl.ds(pl.multiple_of(other * r, r), r)], rs2, tsend.at[6], trecv.at[6], sibling)
    s_out.start()
    mine = fin2[pl.ds(pl.multiple_of(core * r, r), r), :]
    here = pl.ds(pl.multiple_of(core * hw, hw), hw)
    there = pl.ds(pl.multiple_of(other * hw, hw), hw)
    outs = (gwq_ref, gwk_ref, gwv_ref)
    for i in range(3):
        outs[i][:, here] = fold(mine[:, i * hw:(i + 1) * hw])
    for e in range(1, planes):
        v_z(e, lax.rem(plane + planes - e, planes)).wait_recv()
    total = vgot[chips]
    for z in range(1, planes):
        total = total + vgot[chips + z]
    vout_ref[...] = total
    s_out.wait_recv()
    for i in range(3):
        outs[i][:, there] = fold(rs2[:, i * hw:(i + 1) * hw])

    dx_out.wait_recv()
    y_out.wait_recv()
    keep_y.wait()
    keep_dx.wait()
    one.close()
    two.close()
    for c in [dx_sw, a_out, y_out, dx_out, s_out, v_sib] + da_out + v_chip:
        c.wait_send()
    for e in range(1, planes):
        v_z(e, plane).wait_send()


def back(F, DP, parents, kaug, v, qT, kT, qn, oT, lse, a1T, wqkv, woi, xt, dxl, dx2, y, g1, vin, n1):
    _, rows, width = dxl.shape
    heads = H // 2
    hw = heads * 64
    tree = 4 * rows
    seg = rows // 5
    chips = F // 2
    hidden = woi.shape[1] - width
    r, ru = width // F, hidden // F
    R1 = g1.shape[2]
    r2 = 2 * r

    def zrows(n):
        return -(-n // (16 * DP)) * 16

    Z1, Z2 = zrows(R1), zrows(r2)
    ANY = pl.BlockSpec(memory_space=pl.ANY)
    dma = pltpu.SemaphoreType.DMA
    out = [((2, rows, width), bf16), ((2, rows, width), bf16), ((r, width), f32), ((r, width), f32), ((r, width), f32),
           ((r, width), f32), ((r, hidden), f32), ((ru, width), f32), ((16, width), f32)]
    scratch = [
        ((2, rows, width), bf16), ((hw, width), bf16), ((hw, tree), bf16), ((tree, hw), bf16), ((hw, tree), bf16),
        ((20, seg, hw), bf16), ((20, seg, hw), bf16), ((20, seg, 128), f32), ((20, seg, 128), f32),
        ((2, rows, width), f32), ((2, rows, width), bf16), ((2, rows, width), bf16), ((2, rows, width), bf16),
        ((chips, R1, width), bf16), ((chips, R1, width), bf16), ((chips - 1, R1, width), bf16),
        ((Z1 * DP, width), bf16), ((DP - 1, Z1, width), bf16), ((Z1 * DP, width), bf16),
        ((chips, r2, 3 * hw), bf16), ((chips - 1, r2, 3 * hw), bf16), ((Z2 * DP, 3 * hw), bf16),
        ((DP - 1, Z2, 3 * hw), bf16), ((Z2 * DP, 3 * hw), bf16), ((r, 3 * hw), bf16),
        ((2, 16, width), f32), ((chips + DP, 16, width), f32), ((2, rows, width), bf16),
    ]
    nsem = chips + 2 * DP
    return pl.pallas_call(
        functools.partial(back_kernel, F),
        out_shape=[jax.ShapeDtypeStruct(s, d) for s, d in out],
        in_specs=[SM] + [VM] * 9 + [ANY, ANY, VM, ANY, ANY, ANY, VM, VM],
        out_specs=[ANY, ANY] + [VM] * 7,
        scratch_shapes=[pltpu.VMEM(s, d) for s, d in scratch] + [
            dma((7,)), dma((7,)), dma((nsem,)), dma((nsem,)), dma((nsem,)), dma((nsem,)),
            dma((chips + DP,)), dma((chips + DP,)), dma((7,))],
        name="back",
        compiler_params=pltpu.CompilerParams(vmem_limit_bytes=62 << 20, collective_id=1, has_side_effects=True),
    )(parents, kaug, v, qT, kT, qn, oT, lse, a1T, wqkv, woi, xt, dxl, dx2, y, g1, vin, n1)


def ffn_kernel(F, xt_ref, oF_ref, dy_ref, woi_ref, wu_ref, rows_ref,
               y_ref, dxl_ref, dx2_ref, g1_ref, vin_ref, xs, a2s, gs, dus, lsem):
    core = lax.rem(lax.axis_index("fsdp"), 2)
    half_rows, width = xs.shape[1:]
    hidden = wu_ref.shape[0]
    tiles = hidden // width
    r, ru = width // F, hidden // F
    C = 256
    loads = [pltpu.make_async_copy(xt_ref.at[core + 2 * i], xs.at[i], lsem.at[i]) for i in range(2)]
    for c in loads:
        c.start()
    vin_ref[...] = jnp.zeros_like(vin_ref)
    for c in loads:
        c.wait()
    c1 = math.sqrt(2.0 / math.pi)
    c2 = c1 * 0.044715

    def vector(i):
        return rows_ref[0:1, i * width:(i + 1) * width]

    def add_sum(i, x):
        vin_ref[i:i + 1, :] += jnp.sum(x, axis=0, keepdims=True)

    def chunk(c, start, x):
        at = pl.ds(pl.multiple_of(start, 128), x.shape[0])
        x2 = fold(x) + mm_tn(oF_ref[:, at], woi_ref[:, 0:width]) + vector(2)
        centred = x2 - jnp.mean(x2, axis=-1, keepdims=True)
        inv = lax.rsqrt(jnp.mean(centred * centred, axis=-1, keepdims=True) + 1e-06)
        unit = centred * inv
        a2 = (unit * vector(3) + vector(4)).astype(bf16)
        a2s[at, :] = a2
        dy = dy_ref[at, :]
        y = x2 + vector(5)
        da2 = None
        for t in range(tiles):
            ft = slice(t * width, (t + 1) * width)
            wt = slice(width + t * width, width + (t + 1) * width)
            u = mm(a2, woi_ref[:, wt]) + rows_ref[0:1, 6 * width + t * width:6 * width + (t + 1) * width]
            uu = u * u
            th = jnp.tanh(u * (c1 + c2 * uu))
            p = 0.5 + 0.5 * th
            g = (u * p).astype(bf16)
            slope = p + u * (0.5 - 0.5 * th * th) * (c1 + 3.0 * c2 * uu)
            gs[at, ft] = g
            y = y + mm(g, wu_ref[ft, :])
            du = (mm_nt(dy, wu_ref[ft, :]) * slope).astype(bf16)
            dus[at, ft] = du
            add_sum(6 + t, fold(du))
            d = mm_nt(du, woi_ref[:, wt])
            da2 = d if da2 is None else da2 + d
        y_ref[at, :] = y.astype(bf16)
        dyf = fold(dy)
        dn = da2 * vector(3)
        m1 = jnp.mean(dn, axis=-1, keepdims=True)
        m2 = jnp.mean(dn * unit, axis=-1, keepdims=True)
        dx2 = dyf + (dn - m1 - unit * m2) * inv
        dxl = dx2.astype(bf16)
        dx2_ref[at, :] = dx2
        dxl_ref[at, :] = dxl
        add_sum(2, fold(dxl))
        add_sum(3, da2 * unit)
        add_sum(4, da2)
        add_sum(5, dyf)

    lax.fori_loop(0, 2, lambda c, k: (chunk(c, c * half_rows, xs[c]), k)[1], 0)

    nb = C // ru

    def outer(t, _):
        val = mm_tn(gs[:, pl.ds(pl.multiple_of(t * C, C), C)], dy_ref[...]).astype(bf16)
        g1_ref[pl.ds(t * nb, nb), 0:ru, :] = val.reshape(nb, ru, width)
        return 0

    lax.fori_loop(0, hidden // C, outer, 0)
    a2T = a2s[...].T
    for t in range(tiles):
        val = mm(a2T, dus[:, t * width:(t + 1) * width]).astype(bf16)
        g1_ref[:, ru + t * r:ru + (t + 1) * r, :] = val.reshape(F, r, width)
    val = mm(oF_ref[...], dxl_ref[...]).astype(bf16)
    g1_ref[:, ru + tiles * r:ru + (tiles + 1) * r, :] = val.reshape(F, r, width)


def ffn(F, xt, oF, dy, woi, wu, vrows):
    _, rows, width = xt.shape
    hidden = wu.shape[0]
    n = 2 * rows
    R1 = hidden // F + (hidden // width + 1) * (width // F)
    out = [((n, width), bf16), ((n, width), bf16), ((n, width), f32), ((F, R1, width), bf16), ((16, width), f32)]
    scratch = [((2, rows, width), bf16), ((n, width), bf16), ((n, hidden), bf16), ((n, hidden), bf16)]
    return pl.pallas_call(
        functools.partial(ffn_kernel, F),
        out_shape=[jax.ShapeDtypeStruct(s, d) for s, d in out],
        in_specs=[pl.BlockSpec(memory_space=pl.ANY)] + [VM] * 5,
        out_specs=[VM] * 5,
        scratch_shapes=[pltpu.VMEM(s, d) for s, d in scratch] + [pltpu.SemaphoreType.DMA((2,))],
        name="ffn",
        compiler_params=pltpu.CompilerParams(vmem_limit_bytes=48 << 20),
    )(xt, oF, dy, woi, wu, vrows)


def on_device(tokens, parents, n1g, n1b, wq, wk, wv, wo, ob, n2g, n2b, wi, ib, wu, ub, cotangent):
    F = lax.axis_size("fsdp")
    fi = lax.axis_index("fsdp")
    place = (fi + 2) % F
    half = (place % 4) // 2
    quad = lax.axis_index("dp") * (F // 4) + place // 4
    parent_row = parents[quad, half]
    _, _, rows, width = tokens.shape

    n = n1g.shape[0]
    vec = jnp.concatenate([n1g, n1b, ob, n2g, n2b, ub, ib])
    vec = lax.reduce_precision(vec, 8, 7)
    vec = jnp.broadcast_to(jnp.pad(vec, (0, -vec.shape[0] % 128)), (8, vec.shape[0] + -vec.shape[0] % 128))
    (xt, a1T, kaug, v, kT, qn, qT, oT, lse, oF, dy_my, wqkv, woi, wu, vrows) = front(
        F, parent_row, tokens[0], cotangent[0], (wq, wk, wv, wo, wi, wu), vec, n)
    n_rows = (2, rows, width)
    y, dxl, dx2, g1, vin = ffn(F, xt, oF, dy_my.reshape(2 * rows, width), woi, wu, vrows)
    lo, gt, gwq, gwk, gwv, gwo, gwi, gwu, vout = back(
        F, lax.axis_size("dp"), parent_row, kaug, v, qT, kT, qn, oT, lse, a1T, wqkv, woi, xt,
        dxl.reshape(n_rows), dx2.reshape(n_rows), y.reshape(n_rows), g1.reshape(F // 2, 2, -1, width), vin, vrows)
    hidden = wu.shape[0]
    ru = hidden // F
    sv = lax.dynamic_slice_in_dim(vout[:6], fi * n, n, 1)
    sib = lax.dynamic_slice_in_dim(vout[6:6 + hidden // width].reshape(-1), fi * ru, ru, 0)
    return (lo[None], gt[None], sv[0], sv[1], gwq, gwk, gwv, gwo, sv[2], sv[3], sv[4], gwi, sib, gwu, sv[5])


def solution(mesh):
    tok = P(("dp", "fsdp"), None, None, None)
    v, m = P("fsdp"), P("fsdp", None)
    return jax.shard_map(
        on_device,
        mesh=mesh,
        in_specs=(tok, P(), v, v, m, m, m, m, v, v, v, m, v, m, v, tok),
        out_specs=(tok, tok, v, v, m, m, m, m, v, v, v, m, v, m, v),
        check_vma=False,
    )
```

```python
import functools
import math

import jax
import jax.numpy as jnp
import ml_dtypes
import numpy as np
from jax import lax
from jax.experimental import pallas as pl
from jax.experimental.pallas import tpu as pltpu
from jax.sharding import PartitionSpec as P

H = 8
T = 256
f32, bf16 = jnp.float32, jnp.bfloat16
VM = pl.BlockSpec(memory_space=pltpu.VMEM)
SM = pl.BlockSpec(memory_space=pltpu.SMEM)


def mm(a, b):
    return jnp.dot(a, b, preferred_element_type=f32)


def mm_tn(a, b):
    return lax.dot_general(a, b, (((0,), (0,)), ((), ())), preferred_element_type=f32)


def mm_nt(a, b):
    return lax.dot_general(a, b, (((1,), (1,)), ((), ())), preferred_element_type=f32)


def iota(shape, dim):
    return lax.broadcasted_iota(jnp.int32, shape, dim)


def chosen(par, read):
    out = read(0)
    for b in range(1, 4):
        out = jnp.where(par == b + 1, read(b), out)
    return out


def attend(heads, seg, parents_ref, kaug_ref, qT_ref, vT_ref, oT_ref, lse_ref, s_scr, between):
    trunk = 8 * seg
    ntr = trunk // T
    vr = vT_ref.shape[0] // heads
    causal_t = iota((T, T), 0) <= iota((T, T), 1)
    causal_b = iota((seg, seg), 0) <= iota((seg, seg), 1)

    def finish(h, cols, m, acc):
        l = acc[64:65, :]
        oT_ref[pl.ds(pl.multiple_of(h * 64, 64), 64), cols] = (acc[:64] / l).astype(bf16)
        lse_ref[pl.ds(pl.multiple_of(h * 8, 8), 8), cols] = jnp.broadcast_to(m + jnp.log(l), (8, T))

    def head(h, _):
        between(h)
        hk = pl.ds(pl.multiple_of(h * 128, 128), 128)
        hv = pl.ds(pl.multiple_of(h * vr, vr), vr)

        def keys(blk, n):
            return kaug_ref[pl.ds(blk, n), :, hk].reshape(n * seg, 128)

        def full_scores(q, n):
            m = None
            for c in range(n):
                s = mm(keys(2 * c, 2), q)
                s_scr[c * T:(c + 1) * T, :] = s
                cm = jnp.max(s, axis=0, keepdims=True)
                m = cm if m is None else jnp.maximum(m, cm)
            return m

        def full_mix(m, n, acc):
            for c in range(n):
                p = jnp.exp(s_scr[c * T:(c + 1) * T, :] - m).astype(bf16)
                t = mm(vT_ref[hv, c * T:(c + 1) * T], p)
                acc = t if acc is None else acc + t
            return acc

        for t in range(ntr):
            cols = slice(t * T, (t + 1) * T)
            q = qT_ref[hk, cols]
            sd = jnp.where(causal_t, mm(keys(2 * t, 2), q), -1e30)
            m = jnp.max(sd, axis=0, keepdims=True)
            if t:
                m = jnp.maximum(m, full_scores(q, t))
            acc = mm(vT_ref[hv, cols], jnp.exp(sd - m).astype(bf16))
            acc = full_mix(m, t, acc)
            finish(h, cols, m, acc)

        def tail_tile(i, leaf):
            b0 = 8 + 2 * i
            cols = pl.ds(pl.multiple_of(b0 * seg, T), T)
            q = qT_ref[hk, cols]
            rows = []
            for half in range(2):
                rows.append([b0 + half])
                if leaf:
                    rows[-1].append(parents_ref[b0 + half - 7])
            m = full_scores(q, ntr)
            ext = []
            for e in range(len(rows[0])):
                pieces = []
                for half in range(2):
                    kk = keys(rows[half][0], 1) if e == 0 else chosen(rows[half][1], lambda b: keys(8 + b, 1))
                    s = mm(kk, q[:, half * seg:(half + 1) * seg])
                    if e == 0:
                        s = jnp.where(causal_b, s, -1e30)
                    pieces.append(s)
                s = jnp.concatenate(pieces, axis=1)
                m = jnp.maximum(m, jnp.max(s, axis=0, keepdims=True))
                ext.append(s)
            acc = None
            for e in range(len(ext)):
                p = jnp.exp(ext[e] - m).astype(bf16)
                t = []
                for half in range(2):
                    if e == 0:
                        vv = vT_ref[hv, pl.ds(pl.multiple_of(rows[half][0] * seg, seg), seg)]
                    else:
                        vv = chosen(rows[half][1], lambda b: vT_ref[hv, (8 + b) * seg:(9 + b) * seg])
                    t.append(mm(vv, p[:, half * seg:(half + 1) * seg]))
                t = jnp.concatenate(t, axis=1)
                acc = t if acc is None else acc + t
            acc = full_mix(m, ntr, acc)
            finish(h, cols, m, acc)

        lax.fori_loop(0, 2, lambda i, c: (tail_tile(i, False), c)[1], 0)
        lax.fori_loop(2, 6, lambda i, c: (tail_tile(i, True), c)[1], 0)
        return 0

    lax.fori_loop(0, heads, head, 0)


def attend_back(heads, seg, parents_ref, kaug_ref, v_ref, qT_ref, doT_ref, kT_ref, do_ref, qn_ref,
                oT_ref, lse_ref, dqT_ref, dqkv_ref, accK, accV, hook):
    ntr = 8 * seg // T
    causal_t = iota((T, T), 0) <= iota((T, T), 1)
    causal_b = iota((seg, seg), 0) <= iota((seg, seg), 1)
    low_rows = iota((128, T), 0) < 64
    low_lanes = iota((T, 128), 1) < 64

    def pair(pr, _):
        hook("start", pr)
        lanes = pl.ds(pl.multiple_of(pr * 128, 128), 128)
        hk = [pl.ds(pl.multiple_of(pr * 256 + 128 * e, 128), 128) for e in range(2)]
        h64 = [pl.ds(pl.multiple_of(pr * 128 + 64 * e, 64), 64) for e in range(2)]
        accK[...] = jnp.zeros_like(accK)
        accV[...] = jnp.zeros_like(accV)

        def stack(x):
            z = jnp.zeros_like(x)
            return jnp.concatenate([jnp.where(low_lanes, x, z), jnp.where(low_lanes, z, x)], axis=0)

        def prep(cols):
            doT = doT_ref[lanes, cols]
            z = jnp.zeros_like(doT)
            prod = doT.astype(f32) * oT_ref[lanes, cols].astype(f32)
            q, do, lse, delta = [], [], [], []
            for e in range(2):
                q.append(qT_ref[hk[e], cols])
                do.append(jnp.where(low_rows, doT, z) if e == 0 else jnp.where(low_rows, z, doT))
                at = pl.multiple_of((pr * 2 + e) * 8, 8)
                lse.append(jnp.max(lse_ref[pl.ds(at, 8), cols], axis=0, keepdims=True))
                delta.append(jnp.sum(prod[64 * e:64 * e + 64], axis=0, keepdims=True))
            return q, do, lse, delta, stack(do_ref[cols, lanes]), stack(qn_ref[cols, lanes])

        def piece(blk, n, sl, args, mask, par=None):
            q, do, lse, delta, rv, rk = args
            ps, dss, dq = [], [], []

            def rows_of(ref, at):
                if par is None:
                    return ref[pl.ds(blk, n), :, at].reshape(n * seg, 128)
                return chosen(par, lambda b: ref[8 + b, :, at])

            vv = rows_of(v_ref, lanes)
            for e in range(2):
                kk = rows_of(kaug_ref, hk[e])
                p = jnp.exp(mm(kk, q[e][:, sl]) - lse[e][:, sl])
                if mask is not None:
                    p = jnp.where(mask, p, 0.0)
                dp = mm(vv, do[e][:, sl])
                ds = (p * (dp - delta[e][:, sl])).astype(bf16)
                if par is None:
                    kT = kT_ref[h64[e], pl.ds(pl.multiple_of(blk * seg, seg), n * seg)]
                else:
                    kT = chosen(par, lambda b: kT_ref[h64[e], (8 + b) * seg:(9 + b) * seg])
                dq.append(mm(kT, ds))
                ps.append(p.astype(bf16))
                dss.append(ds)
            if sl.stop - sl.start != T:
                rv = jnp.concatenate([rv[sl], rv[T + sl.start:T + sl.stop]], axis=0)
                rk = jnp.concatenate([rk[sl], rk[T + sl.start:T + sl.stop]], axis=0)
            av = mm(jnp.concatenate(ps, axis=1), rv)
            ak = mm(jnp.concatenate(dss, axis=1), rk)
            if par is None:
                accV[pl.ds(blk, n)] += av.reshape(n, seg, 128)
                accK[pl.ds(blk, n)] += ak.reshape(n, seg, 128)
            else:
                for b in range(4):
                    here = jnp.where(par == b + 1, 1.0, 0.0)
                    accK[8 + b] += ak * here
                    accV[8 + b] += av * here
            return dq

        def emit(cols, dq):
            for e in range(2):
                dqT_ref[64 * e:64 * e + 64, cols] = (dq[e] * 0.125).astype(bf16)

        full = slice(0, T)
        for t in range(ntr):
            cols = slice(t * T, (t + 1) * T)
            args = prep(cols)
            dq = piece(2 * t, 2, full, args, causal_t)
            for c in range(t):
                dq = [a + b for a, b in zip(dq, piece(2 * c, 2, full, args, None))]
            emit(cols, dq)

        def tail_tile(i, leaf):
            b0 = 8 + 2 * i
            cols = pl.ds(pl.multiple_of(b0 * seg, T), T)
            args = prep(cols)
            halves = []
            for half in range(2):
                sl = slice(half * seg, (half + 1) * seg)
                d = piece(b0 + half, 1, sl, args, causal_b)
                if leaf:
                    par = parents_ref[b0 + half - 7]
                    d = [x + y for x, y in zip(d, piece(8, 1, sl, args, None, par))]
                halves.append(d)
            dq = [jnp.concatenate([halves[0][e], halves[1][e]], axis=1) for e in range(2)]
            for c in range(ntr):
                dq = [a + b for a, b in zip(dq, piece(2 * c, 2, full, args, None))]
            emit(cols, dq)

        hook("mid", pr)
        lax.fori_loop(0, 2, lambda i, c: (tail_tile(i, False), c)[1], 0)
        hook("late", pr)
        lax.fori_loop(2, 6, lambda i, c: (tail_tile(i, True), c)[1], 0)
        first = pr * 384

        def put(i, x):
            dqkv_ref[:, :, pl.ds(pl.multiple_of(first + 128 * i, 128), 128)] = x

        put(0, dqT_ref[...].T.reshape(20, seg, 128))
        put(1, accK[...].astype(bf16))
        put(2, accV[...].astype(bf16))
        hook("end", pr)
        return 0

    lax.fori_loop(0, heads // 2, pair, 0)


class Dense:
    def __init__(self, rows, width, oF_ref, dy_ref, woi_ref, wu_ref, rows_ref, dxl_ref, dx2_ref, g1_ref, vin_ref,
                 a2s, gs, dus):
        self.__dict__.update({k: v for k, v in locals().items() if k != "self"})
        self.hidden = wu_ref.shape[0]
        self.tiles = self.hidden // width

    def chunk(self, start, x, y_ref):
        width, rows_ref, vin_ref = self.width, self.rows_ref, self.vin_ref
        woi_ref, wu_ref = self.woi_ref, self.wu_ref
        c1 = math.sqrt(2.0 / math.pi)
        c2 = c1 * 0.044715

        def vector(i):
            return rows_ref[0:1, i * width:(i + 1) * width]

        def add_sum(i, x):
            vin_ref[i:i + 1, :] += jnp.sum(x, axis=0, keepdims=True)

        at = pl.ds(pl.multiple_of(start, 128), x.shape[0])
        x2 = fold(x) + mm_tn(self.oF_ref[:, at], woi_ref[:, 0:width]) + vector(2)
        centred = x2 - jnp.mean(x2, axis=-1, keepdims=True)
        inv = lax.rsqrt(jnp.mean(centred * centred, axis=-1, keepdims=True) + 1e-06)
        unit = centred * inv
        a2 = (unit * vector(3) + vector(4)).astype(bf16)
        self.a2s[at, :] = a2
        dy = self.dy_ref[start // x.shape[0]]
        y = x2 + vector(5)
        da2 = None
        for t in range(self.tiles):
            ft = slice(t * width, (t + 1) * width)
            wt = slice(width + t * width, width + (t + 1) * width)
            u = mm(a2, woi_ref[:, wt]) + rows_ref[0:1, 6 * width + t * width:6 * width + (t + 1) * width]
            uu = u * u
            th = jnp.tanh(u * (c1 + c2 * uu))
            p = 0.5 + 0.5 * th
            g = (u * p).astype(bf16)
            slope = p + u * (0.5 - 0.5 * th * th) * (c1 + 3.0 * c2 * uu)
            self.gs[at, ft] = g
            y = y + mm(g, wu_ref[ft, :])
            du = (mm_nt(dy, wu_ref[ft, :]) * slope).astype(bf16)
            self.dus[at, ft] = du
            add_sum(6 + t, fold(du))
            d = mm_nt(du, woi_ref[:, wt])
            da2 = d if da2 is None else da2 + d
        y_ref[...] = y.astype(bf16)
        dyf = fold(dy)
        dn = da2 * vector(3)
        m1 = jnp.mean(dn, axis=-1, keepdims=True)
        m2 = jnp.mean(dn * unit, axis=-1, keepdims=True)
        dx2 = dyf + (dn - m1 - unit * m2) * inv
        dxl = dx2.astype(bf16)
        self.dx2_ref[at, :] = dx2
        self.dxl_ref[at, :] = dxl
        add_sum(2, fold(dxl))
        add_sum(3, da2 * unit)
        add_sum(4, da2)
        add_sum(5, dyf)

    def gradients(self, F):
        width, hidden, tiles, g1_ref = self.width, self.hidden, self.tiles, self.g1_ref
        r, ru = width // F, hidden // F
        nb = T // ru
        dy = self.dy_ref[...].reshape(2 * self.rows, width)

        def outer(t, c):
            val = mm_tn(self.gs[:, pl.ds(pl.multiple_of(t * T, T), T)], dy).astype(bf16)
            g1_ref[pl.ds(t * nb, nb), 0:ru, :] = val.reshape(nb, ru, width)
            return c

        lax.fori_loop(0, hidden // T, outer, 0)
        a2T = self.a2s[...].T
        for t in range(tiles):
            val = mm(a2T, self.dus[:, t * width:(t + 1) * width]).astype(bf16)
            g1_ref[:, ru + t * r:ru + (t + 1) * r, :] = val.reshape(F, r, width)
        val = mm(self.oF_ref[...], self.dxl_ref[...]).astype(bf16)
        g1_ref[:, ru + tiles * r:ru + (tiles + 1) * r, :] = val.reshape(F, r, width)


def slope_parts(head, head_count, length):
    x = np.float32(2.0 ** (2.0 - 4.0 * head / head_count) / length)
    out = []
    for _ in range(3):
        low = np.float32(ml_dtypes.bfloat16(x))
        out.append(float(low))
        x = np.float32(x - low)
    return out


def remote(src, dst, send_sem, recv_sem, target):
    return pltpu.make_async_remote_copy(
        src_ref=src, dst_ref=dst, send_sem=send_sem, recv_sem=recv_sem,
        device_id={"fsdp": target}, device_id_type=pl.DeviceIdType.MESH)


def where_am_i(F):
    f = lax.axis_index("fsdp")
    place = lax.rem(f + 2, F)
    part = lax.rem(place, 4)
    half = part // 2
    core = lax.rem(f, 2)
    base = place - part
    partner = lax.rem(base + lax.rem(part + 2, 4) + F - 2, F)
    sibling = f + 1 - 2 * core
    return f, part, half, core, partner, sibling


def greet(F, f, core, sibling):
    barrier = pltpu.get_barrier_semaphore()
    for d in range(1, F // 2):
        pl.semaphore_signal(barrier, inc=1, device_id={"fsdp": lax.rem(f + 2 * d, F)},
                            device_id_type=pl.DeviceIdType.MESH)
    pl.semaphore_signal(barrier, inc=1, device_id={"fsdp": sibling}, device_id_type=pl.DeviceIdType.MESH)
    pl.semaphore_wait(barrier, F // 2)


def first_kernel(F, n, parents_ref, tok_ref, cot_ref, wq_ref, wk_ref, wv_ref, wo_ref, wi_ref, wu_ref, vec_ref,
                 a1T_out, kaug_out, v_out, kT_out, qn_out, qT_out, oT_out, lse_out, wc_out, wo_out, xs_out, dxl_out,
                 dx2_out, g1_out, lo_ref, vin_ref, rows_ref,
                 xt_ref, a1T_ref, kaug_ref, v_ref, kT_ref, qn_ref, qT_ref, oT_ref, lse_ref, oF_ref, dy_ref,
                 wqkv_ref, woi_ref, wuf_ref, wc, dxl_ref, dx2_ref, g1_ref, a2s, gs, dus,
                 vecs, vT_scr, s_scr, tsend, trecv, gsend, grecv, osem):
    f, part, half, core, partner, sibling = where_am_i(F)
    rows, width = tok_ref.shape[1:]
    seg = rows // 5
    heads = H // 2
    hw = heads * 64
    tree = 4 * rows
    r = wq_ref.shape[0]
    ru = wu_ref.shape[0]
    part1 = part + 1 - 2 * core
    part2 = lax.rem(part + 2, 4)
    part3 = lax.rem(part1 + 2, 4)

    own = pl.ds(pl.multiple_of(f * r, r), r)
    ownu = pl.ds(pl.multiple_of(f * ru, ru), ru)
    vecs[f] = vec_ref[...]
    wqkv_ref[own, 0:width] = wq_ref[...].astype(bf16)
    wqkv_ref[own, width:2 * width] = wk_ref[...].astype(bf16)
    wqkv_ref[own, 2 * width:3 * width] = wv_ref[...].astype(bf16)

    greet(F, f, core, sibling)

    def slot(g, src):
        if g == 0:
            return vecs.at[src]
        if g == 3:
            return wuf_ref.at[pl.ds(pl.multiple_of(src * ru, ru), ru)]
        ref = wqkv_ref if g == 1 else woi_ref
        return ref.at[pl.ds(pl.multiple_of(src * r, r), r)]

    def direct(g, d):
        return remote(slot(g, f), slot(g, f), gsend.at[g, d], grecv.at[g, d],
                      sibling if d == 0 else lax.rem(f + 2 * d, F))

    def came(g, d):
        src = sibling if d == 0 else lax.rem(f + F - 2 * d, F)
        remote(slot(g, src), slot(g, src), gsend.at[g, d], grecv.at[g, d], sibling).wait_recv()

    def forward(g, d):
        src = lax.rem(f + F - 2 * d, F)
        return remote(slot(g, src), slot(g, src), gsend.at[g, F // 2 + d], grecv.at[g, F // 2 + d], sibling)

    def forwarded(g, d):
        src = lax.rem(sibling + F - 2 * d, F)
        remote(slot(g, src), slot(g, src), gsend.at[g, F // 2 + d], grecv.at[g, F // 2 + d], sibling).wait_recv()

    chips = range(1, F // 2)

    def send_all(g):
        for d in range(F // 2):
            direct(g, d).start()

    def pass_on(g):
        for d in chips:
            came(g, d)
            forward(g, d).start()

    def receive_rest(g):
        came(g, 0)
        for d in chips:
            forwarded(g, d)

    x_out = remote(tok_ref.at[1 - half], xt_ref.at[part], tsend.at[0], trecv.at[0], partner)
    x_sib = remote(tok_ref.at[half], xt_ref.at[part], tsend.at[1], trecv.at[1], sibling)
    x_fwd = remote(xt_ref.at[part2], xt_ref.at[part2], tsend.at[2], trecv.at[2], sibling)
    dy_out = remote(cot_ref.at[1 - half], dy_ref.at[half], tsend.at[3], trecv.at[3], partner)
    dy_own = pltpu.make_async_copy(cot_ref.at[half], dy_ref.at[half], tsend.at[4])

    send_all(0)
    send_all(1)
    x_out.start()
    x_sib.start()
    dy_own.start()
    xt_ref[part] = tok_ref[half]
    woi_ref[own, 0:width] = wo_ref[...].astype(bf16)
    woi_ref[own, width:] = wi_ref[...].astype(bf16)
    wuf_ref[ownu, :] = wu_ref[...].astype(bf16)
    pass_on(0)
    pass_on(1)
    receive_rest(0)

    table = jnp.max(vecs[...], axis=1).astype(bf16)
    words = table.shape[1]

    def vector_row(first, m, length):
        col = iota((words, length), 1)
        pick = iota((words, length), 0) == first + (col & (m - 1))
        spread = mm(table, pick.astype(bf16))
        shift = m.bit_length() - 1
        mine = iota((F, length), 0) == (iota((F, length), 1) >> shift)
        return jnp.sum(jnp.where(mine, spread, 0.0), axis=0, keepdims=True)

    def all_rows(first, last):
        for i in range(first, last):
            rows_ref[:, i * width:(i + 1) * width] = jnp.broadcast_to(vector_row(i * n, n, width), (8, width))

    all_rows(0, 2)
    hidden = rows_ref.shape[1] - 6 * width
    receive_rest(1)

    lane = iota((seg, 128), 1)
    offs = iota((seg, 128), 0)
    arow = iota((64, rows), 0)

    def project(p):
        x = xt_ref[p].astype(f32)
        gain = rows_ref[0:1, 0:width]
        shift = rows_ref[0:1, width:2 * width]
        mean = jnp.mean(x, axis=-1, keepdims=True)
        x = x - mean
        inv = lax.rsqrt(jnp.mean(x * x, axis=-1, keepdims=True) + 1e-06)
        a1 = (x * inv * gain + shift).astype(bf16)

        def proj(i):
            return mm(a1, wqkv_ref[:, pl.ds(pl.multiple_of(i * width + core * hw, hw), hw)])

        cols = pl.ds(pl.multiple_of(p * rows, rows), rows)
        a1T_ref[:, cols] = a1.T
        q = (proj(0) * 0.125).astype(bf16)
        qn_ref[cols, :] = q
        qT = q.T
        k = proj(1).astype(bf16)
        kT_ref[:, cols] = k.T
        v = proj(2).astype(bf16)
        v_ref[pl.ds(p * 5, 5)] = v.reshape(5, seg, hw)
        vT = v.T
        for h in range(heads):
            a, b = slope_parts(h, H, tree), slope_parts(heads + h, H, tree)
            aug = jnp.zeros((64, rows), f32)
            for j in range(3):
                s = jnp.where(core == 0, a[j], b[j])
                aug = jnp.where((arow == j) | (arow == j + 3), s, aug)
            aug = aug.astype(bf16)
            lo, hi = 128 * h + 64 * (h % 2), 128 * h + 64 - 64 * (h % 2)
            qT_ref[lo:lo + 64, cols] = qT[64 * h:64 * h + 64]
            qT_ref[hi:hi + 64, cols] = aug
            vT_scr[80 * h:80 * h + 64, cols] = vT[64 * h:64 * h + 64]
            vT_scr[80 * h + 64:80 * h + 80, cols] = jnp.ones((16, rows), bf16)
        for b in range(5):
            blk = p * 5 + b
            start = jnp.where(blk < 8, blk * seg, jnp.where(blk < 12, 8 * seg, 9 * seg))
            spot = offs + start
            hi = (spot & -8).astype(f32)
            lo = (spot & 7).astype(f32)
            for h in range(heads):
                at = 64 - 64 * (h % 2)
                l = lane - at
                aug = jnp.where((l >= 0) & (l < 3), hi, jnp.where((l >= 3) & (l < 6), lo, 0.0)).astype(bf16)
                keep = (lane < 64) if h % 2 == 0 else (lane >= 64)
                kk = k[b * seg:(b + 1) * seg, 128 * (h // 2):128 * (h // 2) + 128]
                kaug_ref[blk, :, 128 * h:128 * h + 128] = jnp.where(keep, kk, aug)

    x_sib.wait_recv()

    def visit(i, c):
        @pl.when(i == 1)
        def _():
            all_rows(2, 6)
            rows_ref[:, 6 * width:] = jnp.broadcast_to(vector_row(6 * n, hidden // F, hidden), (8, hidden))
            x_out.wait_recv()
            x_fwd.start()
            send_all(2)
            send_all(3)
            dy_out.start()

        @pl.when(i == 3)
        def _():
            x_fwd.wait_recv()

        project(jnp.where(i == 0, part, jnp.where(i == 1, part1, jnp.where(i == 2, part2, part3))))
        return c

    lax.fori_loop(0, 4, visit, 0)
    for i in range(heads // 2):
        for k in range(3):
            src = pl.ds(pl.multiple_of(k * width + core * hw + 128 * i, 128), 128)
            wc[:, 384 * i + 128 * k:384 * i + 128 * k + 128] = wqkv_ref[:, src]

    outs = [(a1T_ref, a1T_out), (kaug_ref, kaug_out), (v_ref, v_out), (kT_ref, kT_out), (qn_ref, qn_out),
            (qT_ref, qT_out), (wc, wc_out), (xt_ref.at[core], xs_out.at[0]), (xt_ref.at[core + 2], xs_out.at[1]),
            (oT_ref, oT_out), (lse_ref, lse_out),
            (woi_ref.at[pl.ds(pl.multiple_of(core * hw, hw), hw), 0:width], wo_out),
            (dxl_ref.at[0:rows], dxl_out.at[0]), (dxl_ref.at[rows:2 * rows], dxl_out.at[1]),
            (dx2_ref.at[0:rows], dx2_out.at[0]), (dx2_ref.at[rows:2 * rows], dx2_out.at[1]), (g1_ref, g1_out)]
    copies = [pltpu.make_async_copy(a, b, osem.at[i]) for i, (a, b) in enumerate(outs)]
    for c in copies[:9]:
        c.start()

    def between(h):
        @pl.when(h == 2)
        def _():
            pass_on(2)

    attend(heads, seg, parents_ref, kaug_ref, qT_ref, vT_scr, oT_ref, lse_ref, s_scr, between)

    other = 1 - core
    sent = []
    for i in range(2):
        cols = pl.ds(pl.multiple_of((other + 2 * i) * rows, rows), rows)
        at = (pl.ds(pl.multiple_of(core * hw, hw), hw), slice(i * rows, (i + 1) * rows))
        c = remote(oT_ref.at[:, cols], oF_ref.at[at], tsend.at[5 + i], trecv.at[5 + i], sibling)
        c.start()
        sent.append(c)
    for i in range(2):
        mine = pl.ds(pl.multiple_of((core + 2 * i) * rows, rows), rows)
        at = (pl.ds(pl.multiple_of(core * hw, hw), hw), slice(i * rows, (i + 1) * rows))
        oF_ref[at] = oT_ref[:, mine]
    copies[9].start()
    copies[10].start()
    receive_rest(2)
    copies[11].start()
    pass_on(3)
    for c in sent:
        c.wait_recv()
    receive_rest(3)
    dy_own.wait()

    vin_ref[...] = jnp.zeros_like(vin_ref)
    dense = Dense(rows, width, oF_ref, dy_ref, woi_ref, wuf_ref, rows_ref, dxl_ref, dx2_ref, g1_ref, vin_ref,
                  a2s, gs, dus)
    y_out = remote(xt_ref.at[other + 2 * (1 - half)], lo_ref.at[half],
                   tsend.at[7], trecv.at[7], partner)
    keep_y = pltpu.make_async_copy(xt_ref.at[other + 2 * half], lo_ref.at[half], osem.at[17])

    def dense_step(s, c):
        i = jnp.where(s == 0, half, 1 - half)

        @pl.when(s == 1)
        def _():
            keep_y.start()
            dy_out.wait_recv()

        dense.chunk(i * rows, xt_ref[core + 2 * i], xt_ref.at[other + 2 * i])
        return c

    lax.fori_loop(0, 2, dense_step, 0)
    y_out.start()
    for c in copies[12:16]:
        c.start()
    dense.gradients(F)
    copies[16].start()
    for c in copies:
        c.wait()
    keep_y.wait()
    y_out.wait()
    dy_out.wait_send()
    x_out.wait_send()
    x_sib.wait_send()
    x_fwd.wait_send()
    for c in sent:
        c.wait_send()
    for g in range(4):
        for d in range(F // 2):
            direct(g, d).wait_send()
        for d in chips:
            forward(g, d).wait_send()


def first(F, parents, tokens, cotangent, weights, vec, n):
    _, rows, width = tokens.shape
    tree = 4 * rows
    heads = H // 2
    hw = heads * 64
    seg = rows // 5
    hidden = weights[4].shape[1]
    r, ru = width // F, hidden // F
    R1 = ru + (hidden // width + 1) * r
    two = 2 * rows
    keep = [((width, tree), bf16), ((20, seg, heads * 128), bf16), ((20, seg, hw), bf16), ((hw, tree), bf16),
            ((tree, hw), bf16), ((heads * 128, tree), bf16), ((hw, tree), bf16), ((heads * 8, tree), f32)]
    out = keep + [((width, 3 * hw), bf16), ((hw, width), bf16), ((2, rows, width), bf16), ((2, rows, width), bf16),
                  ((2, rows, width), f32), ((F, R1, width), bf16), ((2, rows, width), bf16),
                  ((16, width), f32), ((8, 6 * width + hidden), f32)]
    scratch = [((4, rows, width), bf16)] + keep + [
        ((2 * hw, two), bf16), ((2, rows, width), bf16), ((width, 3 * width), bf16), ((width, width + hidden), bf16),
        ((hidden, width), bf16), ((width, 3 * hw), bf16), ((two, width), bf16),
        ((two, width), f32), ((F, R1, width), bf16), ((two, width), bf16), ((two, hidden), bf16),
        ((two, hidden), bf16), ((F,) + vec.shape, f32), ((heads * 80, tree), bf16), ((8 * seg, T), f32)]
    ANY = pl.BlockSpec(memory_space=pl.ANY)
    dma = pltpu.SemaphoreType.DMA
    return pl.pallas_call(
        functools.partial(first_kernel, F, n),
        out_shape=[jax.ShapeDtypeStruct(s, d) for s, d in out],
        in_specs=[SM, VM, ANY] + [VM] * 7,
        out_specs=[ANY] * 15 + [VM] * 2,
        scratch_shapes=[pltpu.VMEM(s, d) for s, d in scratch] + [
            dma((8,)), dma((8,)), dma((4, F)), dma((4, F)), dma((18,))],
        name="front",
        compiler_params=pltpu.CompilerParams(vmem_limit_bytes=64 << 20, collective_id=0, has_side_effects=True),
    )(parents, tokens, cotangent, *weights, vec)


def fold(x):
    return x.astype(f32)


class Chain:
    def __init__(self, F, f, sums, got, block, zgot, final, send, recv):
        self.F, self.f, self.sums, self.got, self.block = F, f, sums, got, block
        self.zgot, self.final, self.send, self.recv = zgot, final, send, recv
        self.chip = f // 2
        self.chips = F // 2
        self.planes = lax.axis_size("dp")
        self.plane = lax.axis_index("dp")
        self.rows = sums.shape[1]
        self.zrows = block.shape[0] // self.planes

    def _b(self, d):
        return remote(self.sums.at[lax.rem(self.chip + d, self.chips)], self.got.at[d - 1],
                      self.send.at[d], self.recv.at[d], lax.rem(self.f + 2 * d, self.F))

    def _chunk(self, z):
        return pl.ds(pl.multiple_of(z * self.zrows, 16), self.zrows)

    def _c(self, e):
        z = lax.rem(self.plane + e, self.planes)
        i = self.chips + e
        return pltpu.make_async_remote_copy(
            src_ref=self.block.at[self._chunk(z)], dst_ref=self.zgot.at[e - 1],
            send_sem=self.send.at[i], recv_sem=self.recv.at[i],
            device_id={"dp": z}, device_id_type=pl.DeviceIdType.MESH)

    def _d(self, e, src=None):
        z = lax.rem(self.plane + e, self.planes)
        i = self.chips + self.planes + e
        here = self._chunk(self.plane if src is None else src)
        return pltpu.make_async_remote_copy(
            src_ref=self.final.at[here], dst_ref=self.final.at[here],
            send_sem=self.send.at[i], recv_sem=self.recv.at[i],
            device_id={"dp": z}, device_id_type=pl.DeviceIdType.MESH)

    def start_plane(self):
        for d in range(1, self.chips):
            self._b(d).start()

    def start_z(self):
        for d in range(1, self.chips):
            self._b(d).wait_recv()
        total = fold(self.sums[self.chip])
        for d in range(1, self.chips):
            total = total + fold(self.got[d - 1])
        self.block[0:self.rows] = total.astype(bf16)
        for e in range(1, self.planes):
            self._c(e).start()

    def start_back(self):
        for e in range(1, self.planes):
            self._c(e).wait_recv()
        here = self._chunk(self.plane)
        total = fold(self.block[here])
        for e in range(1, self.planes):
            total = total + fold(self.zgot[e - 1])
        self.final[here] = total.astype(bf16)
        for e in range(1, self.planes):
            self._d(e).start()

    def receive(self):
        for e in range(1, self.planes):
            self._d(e, lax.rem(self.plane + self.planes - e, self.planes)).wait_recv()

    def close(self):
        for d in range(1, self.chips):
            self._b(d).wait_send()
        for e in range(1, self.planes):
            self._c(e).wait_send()
            self._d(e).wait_send()


def last_kernel(F, parents_ref, kaug_h, v_h, qT_h, kT_h, qn_h, oT_h, lse_h, a1T_h, wc_h, wo_h, xs_h, dxl_ref, dx2_h,
                g1_ref, vin_ref, n1_ref,
                gt_ref, gq_ref, fin1, vout_ref,
                kaug_ref, v_ref, qT_ref, kT_ref, qn_ref, oT_ref, lse_ref, a1T_ref, wc, wo_scr, xs, dx2s,
                dxs, doT, do, dqT, dqkv, accK, accV, das, dar,
                a_sum, a_got, b_got, blk1, z1, sum2, got2, blk2, z2, fin2,
                vs, vgot, dxo, tsend, trecv, send1, recv1, send2, recv2, vsend, vrecv, lsem):
    f, part, half, core, partner, sibling = where_am_i(F)
    planes = lax.axis_size("dp")
    plane = lax.axis_index("dp")
    heads = H // 2
    hw = heads * 64
    _, rows, width = dxl_ref.shape
    chips = F // 2
    other = 1 - core
    tree = 4 * rows
    seg = rows // 5

    pairs = [(wo_h, wo_scr), (qT_h, qT_ref), (kaug_h, kaug_ref), (v_h, v_ref), (kT_h, kT_ref), (qn_h, qn_ref),
             (oT_h, oT_ref), (lse_h, lse_ref), (g1_ref.at[:, core], a_sum), (a1T_h, a1T_ref), (wc_h, wc), (xs_h, xs),
             (dx2_h, dx2s)]
    loads = [pltpu.make_async_copy(a, b, lsem.at[i]) for i, (a, b) in enumerate(pairs)]
    for c in loads:
        c.start()

    barrier = pltpu.get_barrier_semaphore()
    for d in range(1, chips):
        pl.semaphore_signal(barrier, inc=1, device_id={"fsdp": lax.rem(f + 2 * d, F)},
                            device_id_type=pl.DeviceIdType.MESH)
    for e in range(1, planes):
        pl.semaphore_signal(barrier, inc=1, device_id={"dp": lax.rem(plane + e, planes)},
                            device_id_type=pl.DeviceIdType.MESH)
    pl.semaphore_signal(barrier, inc=1, device_id={"fsdp": sibling}, device_id_type=pl.DeviceIdType.MESH)
    pl.semaphore_wait(barrier, chips + planes - 1)

    dx_sw = remote(dxl_ref, dxs, tsend.at[0], trecv.at[0], sibling)
    a_out = remote(g1_ref.at[:, other], a_got, tsend.at[1], trecv.at[1], sibling)
    dx_sw.start()
    a_out.start()

    def make_do(p, x):
        cols = pl.ds(pl.multiple_of(p * rows, rows), rows)
        d = mm_nt(x, wo_scr[...]).astype(bf16)
        do[cols, :] = d
        doT[:, cols] = d.T

    loads[0].wait()
    lax.fori_loop(0, 2, lambda i, c: (make_do(core + 2 * i, dxl_ref[i]), c)[1], 0)

    one = Chain(F, f, a_sum, b_got, blk1, z1, fin1, send1, recv1)
    loads[8].wait()
    a_out.wait_recv()

    def add_block(j, c):
        a_sum[j] = (fold(a_sum[j]) + fold(a_got[j])).astype(bf16)
        return c

    lax.fori_loop(0, chips, add_block, 0)
    one.start_plane()
    dx_sw.wait_recv()
    lax.fori_loop(0, 2, lambda i, c: (make_do(other + 2 * i, dxs[i]), c)[1], 0)
    for c in loads[1:8] + loads[9:]:
        c.wait()

    def chain(pr):
        return Chain(F, f, sum2.at[pr], got2.at[pr], blk2.at[pr], z2.at[pr], fin2.at[pr], send2.at[pr], recv2.at[pr])

    two = [chain(0), chain(1)]
    r = width // F
    r2 = 2 * r

    def hook(name, pr):
        if name == "mid":
            @pl.when(pr == 1)
            def _():
                one.start_z()
                two[0].start_z()
        if name == "late":
            @pl.when(pr == 1)
            def _():
                one.start_back()
                two[0].start_back()
        if name == "end":
            g = mm(a1T_ref[...], dqkv[:, :, pl.ds(pl.multiple_of(pr * 384, 384), 384)].reshape(tree, 384)).astype(bf16)
            for j in range(chips):
                sum2[pr, j] = g[j * r2:(j + 1) * r2]
            chain(pr).start_plane()

    attend_back(heads, seg, parents_ref, kaug_ref, v_ref, qT_ref, doT, kT_ref, do, qn_ref, oT_ref, lse_ref,
                dqT, dqkv, accK, accV, hook)

    def da1_of(p):
        return mm_nt(dqkv[pl.ds(p * 5, 5)].reshape(rows, 3 * hw), wc[...])

    def da_out(s):
        i = (1 - half) if s == 0 else half
        return remote(das.at[i], dar.at[i], tsend.at[2 + s], trecv.at[2 + s], sibling)

    dx_out = remote(dxo.at[1 - half], gt_ref.at[half], tsend.at[4], trecv.at[4], partner)
    keep_dx = pltpu.make_async_copy(dxo.at[half], gt_ref.at[half], lsem.at[13])
    vs[0] = vin_ref[...]
    row = iota((16, width), 0)

    def finish_rows(s, c):
        i = jnp.where(s == 0, 1 - half, half)
        das[i] = da1_of(other + 2 * i).astype(bf16)
        for k in range(2):
            @pl.when(s == k)
            def _():
                da_out(k).start()
        x = fold(xs[i])
        x = x - jnp.mean(x, axis=-1, keepdims=True)
        inv = lax.rsqrt(jnp.mean(x * x, axis=-1, keepdims=True) + 1e-06)
        unit = x * inv
        da = da1_of(core + 2 * i)
        for k in range(2):
            @pl.when(s == k)
            def _():
                da_out(k).wait_recv()
        da = da + fold(dar[i])
        dn = da * n1_ref[0:1, 0:width]
        m1 = jnp.mean(dn, axis=-1, keepdims=True)
        m2 = jnp.mean(dn * unit, axis=-1, keepdims=True)
        dxo[i] = (dx2s[i] + (dn - m1 - unit * m2) * inv).astype(bf16)
        gs = jnp.sum(da * unit, axis=0, keepdims=True)
        bs = jnp.sum(da, axis=0, keepdims=True)
        vs[0] += jnp.where(row == 0, gs, 0.0) + jnp.where(row == 1, bs, 0.0)

        @pl.when(s == 0)
        def _():
            dx_out.start()

        @pl.when(s == 1)
        def _():
            keep_dx.start()

        return c

    lax.fori_loop(0, 2, finish_rows, 0)
    v_sib = remote(vs.at[0], vgot.at[0], vsend.at[0], vrecv.at[0], sibling)
    v_sib.start()
    two[1].start_z()
    v_sib.wait_recv()
    vs[1] = vs[0] + vgot[0]
    v_chip = [remote(vs.at[1], vgot.at[d], vsend.at[d], vrecv.at[d], lax.rem(f + 2 * d, F)) for d in range(1, chips)]
    for c in v_chip:
        c.start()
    two[1].start_back()
    for c in v_chip:
        c.wait_recv()
    total = vs[1]
    for d in range(1, chips):
        total = total + vgot[d]
    vgot[chips + plane] = total

    def v_z(e, sender):
        return pltpu.make_async_remote_copy(
            src_ref=vgot.at[chips + sender], dst_ref=vgot.at[chips + sender],
            send_sem=vsend.at[chips + e], recv_sem=vrecv.at[chips + e],
            device_id={"dp": lax.rem(plane + e, planes)}, device_id_type=pl.DeviceIdType.MESH)

    for e in range(1, planes):
        v_z(e, plane).start()

    one.receive()
    s_out = []
    for pr in range(2):
        two[pr].receive()
        c = remote(fin2.at[pr, pl.ds(pl.multiple_of(other * r, r), r)], gq_ref.at[core, pr],
                   tsend.at[5 + pr], trecv.at[5 + pr], sibling)
        c.start()
        gq_ref[core, pr] = fin2[pr, pl.ds(pl.multiple_of(core * r, r), r), :]
        s_out.append(c)
    for e in range(1, planes):
        v_z(e, lax.rem(plane + planes - e, planes)).wait_recv()
    total = vgot[chips]
    for z in range(1, planes):
        total = total + vgot[chips + z]
    vout_ref[...] = total
    for c in s_out:
        c.wait()
    dx_out.wait()
    keep_dx.wait()
    one.close()
    for c in two:
        c.close()
    for c in [dx_sw, a_out, v_sib, da_out(0), da_out(1)] + v_chip:
        c.wait_send()
    for e in range(1, planes):
        v_z(e, plane).wait_send()


def last(F, DP, parents, kept, wc, wo, xs, dxl, dx2, g1, vin, rows_vec):
    a1T, kaug, v, kT, qn, qT, oT, lse = kept
    _, rows, width = dxl.shape
    heads = H // 2
    hw = heads * 64
    tree = 4 * rows
    seg = rows // 5
    chips = F // 2
    r = width // F
    R1 = g1.shape[2]
    r2 = 2 * r

    def zrows(n):
        return -(-n // (16 * DP)) * 16

    Z1, Z2 = zrows(R1), zrows(r2)
    ANY = pl.BlockSpec(memory_space=pl.ANY)
    dma = pltpu.SemaphoreType.DMA
    out = [((2, rows, width), bf16), ((2, 2, r, 384), bf16), ((Z1 * DP, width), bf16), ((16, width), f32)]
    big = [kaug, v, qT, kT, qn, oT, lse, a1T, wc, wo, xs]
    scratch = [(a.shape, a.dtype) for a in big] + [
        ((2, rows, width), f32),
        ((2, rows, width), bf16), ((hw, tree), bf16), ((tree, hw), bf16), ((128, tree), bf16),
        ((20, seg, 3 * hw), bf16), ((20, seg, 128), f32), ((20, seg, 128), f32),
        ((2, rows, width), bf16), ((2, rows, width), bf16),
        ((chips, R1, width), bf16), ((chips, R1, width), bf16), ((chips - 1, R1, width), bf16),
        ((Z1 * DP, width), bf16), ((DP - 1, Z1, width), bf16),
        ((2, chips, r2, 384), bf16), ((2, chips - 1, r2, 384), bf16), ((2, Z2 * DP, 384), bf16),
        ((2, DP - 1, Z2, 384), bf16), ((2, Z2 * DP, 384), bf16),
        ((2, 16, width), f32), ((chips + DP, 16, width), f32), ((2, rows, width), bf16),
    ]
    nsem = chips + 2 * DP
    return pl.pallas_call(
        functools.partial(last_kernel, F),
        out_shape=[jax.ShapeDtypeStruct(s, d) for s, d in out],
        in_specs=[SM] + [ANY] * 11 + [VM, ANY, ANY, VM, VM],
        out_specs=[ANY] + [VM] * 3,
        scratch_shapes=[pltpu.VMEM(s, d) for s, d in scratch] + [
            dma((7,)), dma((7,)), dma((nsem,)), dma((nsem,)), dma((2, nsem)), dma((2, nsem)),
            dma((chips + DP,)), dma((chips + DP,)), dma((14,))],
        name="back",
        compiler_params=pltpu.CompilerParams(vmem_limit_bytes=64 << 20, collective_id=1, has_side_effects=True),
    )(parents, *big, dxl, dx2, g1, vin, rows_vec)


def finish_kernel(lo_in, gt_in, fin1, gq, lo_ref, gt_ref, gwq_ref, gwk_ref, gwv_ref, gwo_ref, gwi_ref, gwu_ref):
    lo_ref[...] = lo_in[...]
    gt_ref[...] = gt_in[...]
    r, width = gwo_ref.shape
    ru = gwu_ref.shape[0]
    gwu_ref[...] = fold(fin1[0:ru])
    pieces = gwi_ref.shape[1] // width
    for c in range(pieces):
        gwi_ref[:, c * width:(c + 1) * width] = fold(fin1[ru + c * r:ru + (c + 1) * r])
    gwo_ref[...] = fold(fin1[ru + pieces * r:ru + (pieces + 1) * r])
    for k, ref in enumerate((gwq_ref, gwk_ref, gwv_ref)):
        for c in range(2):
            for pr in range(2):
                at = (2 * c + pr) * 128
                ref[:, at:at + 128] = fold(gq[c, pr, :, 128 * k:128 * k + 128])


def finish(F, lo, gt, fin1, gq, hidden):
    width = lo.shape[2]
    r, ru = width // F, hidden // F
    shapes = [(r, width)] * 4 + [(r, hidden), (ru, width)]
    return pl.pallas_call(
        finish_kernel,
        out_shape=[jax.ShapeDtypeStruct(lo.shape, bf16), jax.ShapeDtypeStruct(gt.shape, bf16)]
        + [jax.ShapeDtypeStruct(s, f32) for s in shapes],
        in_specs=[VM] * 4,
        out_specs=[VM] * 8,
        name="finish",
    )(lo, gt, fin1, gq)


def on_device(tokens, parents, n1g, n1b, wq, wk, wv, wo, ob, n2g, n2b, wi, ib, wu, ub, cotangent):
    F = lax.axis_size("fsdp")
    fi = lax.axis_index("fsdp")
    place = (fi + 2) % F
    half = (place % 4) // 2
    quad = lax.axis_index("dp") * (F // 4) + place // 4
    parent_row = parents[quad, half]
    _, _, rows, width = tokens.shape

    n = n1g.shape[0]
    vec = jnp.concatenate([n1g, n1b, ob, n2g, n2b, ub, ib])
    vec = lax.reduce_precision(vec, 8, 7)
    vec = jnp.broadcast_to(jnp.pad(vec, (0, -vec.shape[0] % 128)), (8, vec.shape[0] + -vec.shape[0] % 128))
    hidden = wi.shape[1]
    ru = hidden // F
    (a1T, kaug, v, kT, qn, qT, oT, lse, wc, wo_own, xs, dxl, dx2, g1, lo, vin, vrows) = first(
        F, parent_row, tokens[0], cotangent[0], (wq, wk, wv, wo, wi, wu), vec, n)
    gt, gq, fin1, vout = last(
        F, lax.axis_size("dp"), parent_row, (a1T, kaug, v, kT, qn, qT, oT, lse), wc, wo_own, xs, dxl, dx2,
        g1.reshape(F // 2, 2, -1, width), vin, vrows)
    lo, gt, gwq, gwk, gwv, gwo, gwi, gwu = finish(F, lo, gt, fin1, gq, hidden)
    sv = lax.dynamic_slice_in_dim(vout[:6], fi * n, n, 1)
    sib = lax.dynamic_slice_in_dim(vout[6:6 + hidden // width].reshape(-1), fi * ru, ru, 0)
    return (lo[None], gt[None], sv[0], sv[1], gwq, gwk, gwv, gwo, sv[2], sv[3], sv[4], gwi, sib, gwu, sv[5])


def solution(mesh):
    tok = P(("dp", "fsdp"), None, None, None)
    v, m = P("fsdp"), P("fsdp", None)
    return jax.shard_map(
        on_device,
        mesh=mesh,
        in_specs=(tok, P(), v, v, m, m, m, m, v, v, v, m, v, m, v, tok),
        out_specs=(tok, tok, v, v, m, m, m, m, v, v, v, m, v, m, v),
        check_vma=False,
    )
```

```python
import functools
import math

import jax
import jax.numpy as jnp
import ml_dtypes
import numpy as np
from jax import lax
from jax.experimental import pallas as pl
from jax.experimental.pallas import tpu as pltpu
from jax.sharding import PartitionSpec as P

H = 8
T = 256
f32, bf16 = jnp.float32, jnp.bfloat16
VM = pl.BlockSpec(memory_space=pltpu.VMEM)
SM = pl.BlockSpec(memory_space=pltpu.SMEM)


def mm(a, b):
    return jnp.dot(a, b, preferred_element_type=f32)


def mm_tn(a, b):
    return lax.dot_general(a, b, (((0,), (0,)), ((), ())), preferred_element_type=f32)


def mm_nt(a, b):
    return lax.dot_general(a, b, (((1,), (1,)), ((), ())), preferred_element_type=f32)


def iota(shape, dim):
    return lax.broadcasted_iota(jnp.int32, shape, dim)


def chosen(par, read):
    out = read(0)
    for b in range(1, 4):
        out = jnp.where(par == b + 1, read(b), out)
    return out


def attend(heads, seg, parents_ref, kaug_ref, qT_ref, vT_ref, oT_ref, lse_ref, s_scr, between):
    trunk = 8 * seg
    ntr = trunk // T
    vr = vT_ref.shape[0] // heads
    causal_t = iota((T, T), 0) <= iota((T, T), 1)
    causal_b = iota((seg, seg), 0) <= iota((seg, seg), 1)

    def finish(h, cols, m, acc):
        l = acc[64:65, :]
        oT_ref[pl.ds(pl.multiple_of(h * 64, 64), 64), cols] = (acc[:64] / l).astype(bf16)
        lse_ref[pl.ds(pl.multiple_of(h * 8, 8), 8), cols] = jnp.broadcast_to(m + jnp.log(l), (8, T))

    def head(h, _):
        between(h)
        hk = pl.ds(pl.multiple_of(h * 128, 128), 128)
        hv = pl.ds(pl.multiple_of(h * vr, vr), vr)

        def keys(blk, n):
            return kaug_ref[pl.ds(blk, n), :, hk].reshape(n * seg, 128)

        def full_scores(q, n):
            m = None
            for c in range(n):
                s = mm(keys(2 * c, 2), q)
                s_scr[c * T:(c + 1) * T, :] = s
                cm = jnp.max(s, axis=0, keepdims=True)
                m = cm if m is None else jnp.maximum(m, cm)
            return m

        def full_mix(m, n, acc):
            for c in range(n):
                p = jnp.exp(s_scr[c * T:(c + 1) * T, :] - m).astype(bf16)
                t = mm(vT_ref[hv, c * T:(c + 1) * T], p)
                acc = t if acc is None else acc + t
            return acc

        for t in range(ntr):
            cols = slice(t * T, (t + 1) * T)
            q = qT_ref[hk, cols]
            sd = jnp.where(causal_t, mm(keys(2 * t, 2), q), -1e30)
            m = jnp.max(sd, axis=0, keepdims=True)
            if t:
                m = jnp.maximum(m, full_scores(q, t))
            acc = mm(vT_ref[hv, cols], jnp.exp(sd - m).astype(bf16))
            acc = full_mix(m, t, acc)
            finish(h, cols, m, acc)

        def tail_tile(i, leaf):
            b0 = 8 + 2 * i
            cols = pl.ds(pl.multiple_of(b0 * seg, T), T)
            q = qT_ref[hk, cols]
            rows = []
            for half in range(2):
                rows.append([b0 + half])
                if leaf:
                    rows[-1].append(parents_ref[b0 + half - 7])
            m = full_scores(q, ntr)
            ext = []
            for e in range(len(rows[0])):
                pieces = []
                for half in range(2):
                    kk = keys(rows[half][0], 1) if e == 0 else chosen(rows[half][1], lambda b: keys(8 + b, 1))
                    s = mm(kk, q[:, half * seg:(half + 1) * seg])
                    if e == 0:
                        s = jnp.where(causal_b, s, -1e30)
                    pieces.append(s)
                s = jnp.concatenate(pieces, axis=1)
                m = jnp.maximum(m, jnp.max(s, axis=0, keepdims=True))
                ext.append(s)
            acc = None
            for e in range(len(ext)):
                p = jnp.exp(ext[e] - m).astype(bf16)
                t = []
                for half in range(2):
                    if e == 0:
                        vv = vT_ref[hv, pl.ds(pl.multiple_of(rows[half][0] * seg, seg), seg)]
                    else:
                        vv = chosen(rows[half][1], lambda b: vT_ref[hv, (8 + b) * seg:(9 + b) * seg])
                    t.append(mm(vv, p[:, half * seg:(half + 1) * seg]))
                t = jnp.concatenate(t, axis=1)
                acc = t if acc is None else acc + t
            acc = full_mix(m, ntr, acc)
            finish(h, cols, m, acc)

        lax.fori_loop(0, 2, lambda i, c: (tail_tile(i, False), c)[1], 0)
        lax.fori_loop(2, 6, lambda i, c: (tail_tile(i, True), c)[1], 0)
        return 0

    lax.fori_loop(0, heads, head, 0)


def attend_back(heads, seg, parents_ref, kaug_ref, v_ref, qT_ref, doT_ref, kT_ref, do_ref, qn_ref,
                oT_ref, lse_ref, dqT_ref, dqkv_ref, accK, accV, hook):
    ntr = 8 * seg // T
    causal_t = iota((T, T), 0) <= iota((T, T), 1)
    causal_b = iota((seg, seg), 0) <= iota((seg, seg), 1)
    low_rows = iota((128, T), 0) < 64
    low_lanes = iota((T, 128), 1) < 64

    def pair(pr, _):
        hook("start", pr)
        lanes = pl.ds(pl.multiple_of(pr * 128, 128), 128)
        hk = [pl.ds(pl.multiple_of(pr * 256 + 128 * e, 128), 128) for e in range(2)]
        h64 = [pl.ds(pl.multiple_of(pr * 128 + 64 * e, 64), 64) for e in range(2)]
        accK[...] = jnp.zeros_like(accK)
        accV[...] = jnp.zeros_like(accV)

        def stack(x):
            z = jnp.zeros_like(x)
            return jnp.concatenate([jnp.where(low_lanes, x, z), jnp.where(low_lanes, z, x)], axis=0)

        def prep(cols):
            doT = doT_ref[lanes, cols]
            z = jnp.zeros_like(doT)
            prod = doT.astype(f32) * oT_ref[lanes, cols].astype(f32)
            q, do, lse, delta = [], [], [], []
            for e in range(2):
                q.append(qT_ref[hk[e], cols])
                do.append(jnp.where(low_rows, doT, z) if e == 0 else jnp.where(low_rows, z, doT))
                at = pl.multiple_of((pr * 2 + e) * 8, 8)
                lse.append(jnp.max(lse_ref[pl.ds(at, 8), cols], axis=0, keepdims=True))
                delta.append(jnp.sum(prod[64 * e:64 * e + 64], axis=0, keepdims=True))
            return q, do, lse, delta, stack(do_ref[cols, lanes]), stack(qn_ref[cols, lanes])

        def piece(blk, n, sl, args, mask, par=None):
            q, do, lse, delta, rv, rk = args
            ps, dss, dq = [], [], []

            def rows_of(ref, at):
                if par is None:
                    return ref[pl.ds(blk, n), :, at].reshape(n * seg, 128)
                return chosen(par, lambda b: ref[8 + b, :, at])

            vv = rows_of(v_ref, lanes)
            for e in range(2):
                kk = rows_of(kaug_ref, hk[e])
                p = jnp.exp(mm(kk, q[e][:, sl]) - lse[e][:, sl])
                if mask is not None:
                    p = jnp.where(mask, p, 0.0)
                dp = mm(vv, do[e][:, sl])
                ds = (p * (dp - delta[e][:, sl])).astype(bf16)
                if par is None:
                    kT = kT_ref[h64[e], pl.ds(pl.multiple_of(blk * seg, seg), n * seg)]
                else:
                    kT = chosen(par, lambda b: kT_ref[h64[e], (8 + b) * seg:(9 + b) * seg])
                dq.append(mm(kT, ds))
                ps.append(p.astype(bf16))
                dss.append(ds)
            if sl.stop - sl.start != T:
                rv = jnp.concatenate([rv[sl], rv[T + sl.start:T + sl.stop]], axis=0)
                rk = jnp.concatenate([rk[sl], rk[T + sl.start:T + sl.stop]], axis=0)
            av = mm(jnp.concatenate(ps, axis=1), rv)
            ak = mm(jnp.concatenate(dss, axis=1), rk)
            if par is None:
                accV[pl.ds(blk, n)] += av.reshape(n, seg, 128)
                accK[pl.ds(blk, n)] += ak.reshape(n, seg, 128)
            else:
                for b in range(4):
                    here = jnp.where(par == b + 1, 1.0, 0.0)
                    accK[8 + b] += ak * here
                    accV[8 + b] += av * here
            return dq

        def emit(cols, dq):
            for e in range(2):
                dqT_ref[64 * e:64 * e + 64, cols] = (dq[e] * 0.125).astype(bf16)

        full = slice(0, T)
        for t in range(ntr):
            cols = slice(t * T, (t + 1) * T)
            args = prep(cols)
            dq = piece(2 * t, 2, full, args, causal_t)
            for c in range(t):
                dq = [a + b for a, b in zip(dq, piece(2 * c, 2, full, args, None))]
            emit(cols, dq)

        def tail_tile(i, leaf):
            b0 = 8 + 2 * i
            cols = pl.ds(pl.multiple_of(b0 * seg, T), T)
            args = prep(cols)
            halves = []
            for half in range(2):
                sl = slice(half * seg, (half + 1) * seg)
                d = piece(b0 + half, 1, sl, args, causal_b)
                if leaf:
                    par = parents_ref[b0 + half - 7]
                    d = [x + y for x, y in zip(d, piece(8, 1, sl, args, None, par))]
                halves.append(d)
            dq = [jnp.concatenate([halves[0][e], halves[1][e]], axis=1) for e in range(2)]
            for c in range(ntr):
                dq = [a + b for a, b in zip(dq, piece(2 * c, 2, full, args, None))]
            emit(cols, dq)

        hook("mid", pr)
        lax.fori_loop(0, 2, lambda i, c: (tail_tile(i, False), c)[1], 0)
        hook("late", pr)
        lax.fori_loop(2, 6, lambda i, c: (hook("leaf", pr, i), tail_tile(i, True), c)[2], 0)
        first = pr * 384

        def put(i, x):
            dqkv_ref[:, :, pl.ds(pl.multiple_of(first + 128 * i, 128), 128)] = x

        put(0, dqT_ref[...].T.reshape(20, seg, 128))
        put(1, accK[...].astype(bf16))
        put(2, accV[...].astype(bf16))
        hook("end", pr)
        return 0

    lax.fori_loop(0, heads // 2, pair, 0)


class Dense:
    def __init__(self, rows, width, oF_ref, dy_ref, woi_ref, wu_ref, rows_ref, dxl_ref, dx2_ref, ga_ref, gb_ref, vin_ref,
                 a2s, gs, dus):
        self.__dict__.update({k: v for k, v in locals().items() if k != "self"})
        self.hidden = wu_ref.shape[0]
        self.tiles = self.hidden // width

    def chunk(self, start, x, y_ref):
        width, rows_ref, vin_ref = self.width, self.rows_ref, self.vin_ref
        woi_ref, wu_ref = self.woi_ref, self.wu_ref
        c1 = math.sqrt(2.0 / math.pi)
        c2 = c1 * 0.044715

        def vector(i):
            return rows_ref[0:1, i * width:(i + 1) * width]

        def add_sum(i, x):
            vin_ref[i:i + 1, :] += jnp.sum(x, axis=0, keepdims=True)

        at = pl.ds(pl.multiple_of(start, 128), x.shape[0])
        x2 = fold(x) + mm_tn(self.oF_ref[:, at], woi_ref[:, 0:width]) + vector(2)
        centred = x2 - jnp.mean(x2, axis=-1, keepdims=True)
        inv = lax.rsqrt(jnp.mean(centred * centred, axis=-1, keepdims=True) + 1e-06)
        unit = centred * inv
        a2 = (unit * vector(3) + vector(4)).astype(bf16)
        self.a2s[at, :] = a2
        dy = self.dy_ref[start // x.shape[0]]
        y = x2 + vector(5)
        da2 = None
        for t in range(self.tiles):
            ft = slice(t * width, (t + 1) * width)
            wt = slice(width + t * width, width + (t + 1) * width)
            u = mm(a2, woi_ref[:, wt]) + rows_ref[0:1, 6 * width + t * width:6 * width + (t + 1) * width]
            uu = u * u
            th = jnp.tanh(u * (c1 + c2 * uu))
            p = 0.5 + 0.5 * th
            g = (u * p).astype(bf16)
            slope = p + u * (0.5 - 0.5 * th * th) * (c1 + 3.0 * c2 * uu)
            self.gs[at, ft] = g
            y = y + mm(g, wu_ref[ft, :])
            du = (mm_nt(dy, wu_ref[ft, :]) * slope).astype(bf16)
            self.dus[at, ft] = du
            add_sum(6 + t, fold(du))
            d = mm_nt(du, woi_ref[:, wt])
            da2 = d if da2 is None else da2 + d
        y_ref[...] = y.astype(bf16)
        dyf = fold(dy)
        dn = da2 * vector(3)
        m1 = jnp.mean(dn, axis=-1, keepdims=True)
        m2 = jnp.mean(dn * unit, axis=-1, keepdims=True)
        dx2 = dyf + (dn - m1 - unit * m2) * inv
        dxl = dx2.astype(bf16)
        self.dx2_ref[at, :] = dx2
        self.dxl_ref[at, :] = dxl
        add_sum(2, fold(dxl))
        add_sum(3, da2 * unit)
        add_sum(4, da2)
        add_sum(5, dyf)

    def gradients(self, F):
        width, hidden, tiles, gb_ref = self.width, self.hidden, self.tiles, self.gb_ref
        r, ru = width // F, hidden // F
        nb = T // ru
        dy = self.dy_ref[...].reshape(2 * self.rows, width)

        def outer(t, c):
            val = mm_tn(self.gs[:, pl.ds(pl.multiple_of(t * T, T), T)], dy).astype(bf16)
            self.ga_ref[pl.ds(t * nb, nb)] = val.reshape(nb, ru, width)
            return c

        lax.fori_loop(0, hidden // T, outer, 0)
        a2T = self.a2s[...].T
        for t in range(tiles):
            val = mm(a2T, self.dus[:, t * width:(t + 1) * width]).astype(bf16)
            gb_ref[:, t * r:(t + 1) * r, :] = val.reshape(F, r, width)
        val = mm(self.oF_ref[...], self.dxl_ref[...]).astype(bf16)
        gb_ref[:, tiles * r:(tiles + 1) * r, :] = val.reshape(F, r, width)


def slope_parts(head, head_count, length):
    x = np.float32(2.0 ** (2.0 - 4.0 * head / head_count) / length)
    out = []
    for _ in range(3):
        low = np.float32(ml_dtypes.bfloat16(x))
        out.append(float(low))
        x = np.float32(x - low)
    return out


def remote(src, dst, send_sem, recv_sem, target):
    return pltpu.make_async_remote_copy(
        src_ref=src, dst_ref=dst, send_sem=send_sem, recv_sem=recv_sem,
        device_id={"fsdp": target}, device_id_type=pl.DeviceIdType.MESH)


def where_am_i(F):
    f = lax.axis_index("fsdp")
    place = lax.rem(f + 2, F)
    part = lax.rem(place, 4)
    half = part // 2
    core = lax.rem(f, 2)
    base = place - part
    partner = lax.rem(base + lax.rem(part + 2, 4) + F - 2, F)
    sibling = f + 1 - 2 * core
    return f, part, half, core, partner, sibling


def greet(F, f, core, sibling):
    barrier = pltpu.get_barrier_semaphore()
    for d in range(1, F // 2):
        pl.semaphore_signal(barrier, inc=1, device_id={"fsdp": lax.rem(f + 2 * d, F)},
                            device_id_type=pl.DeviceIdType.MESH)
    pl.semaphore_signal(barrier, inc=1, device_id={"fsdp": sibling}, device_id_type=pl.DeviceIdType.MESH)
    pl.semaphore_wait(barrier, F // 2)


def first_kernel(F, n, parents_ref, tok_ref, cot_ref, wq_ref, wk_ref, wv_ref, wo_ref, wi_ref, wu_ref, vec_ref,
                 a1T_out, kaug_out, v_out, kT_out, qn_out, qT_out, oT_out, lse_out, wc_out, wo_out, xs_out, dxl_out,
                 dx2_out, ga_out, gb_out, y_out, vin_ref, rows_ref,
                 xt_ref, a1T_ref, kaug_ref, v_ref, kT_ref, qn_ref, qT_ref, oT_ref, lse_ref, oF_ref, dy_ref,
                 wqkv_ref, woi_ref, wuf_ref, wc, dxl_ref, dx2_ref, ga_ref, gb_ref, a2s, gs, dus,
                 vecs, vT_scr, s_scr, tsend, trecv, gsend, grecv, osem):
    f, part, half, core, partner, sibling = where_am_i(F)
    rows, width = tok_ref.shape[1:]
    seg = rows // 5
    heads = H // 2
    hw = heads * 64
    tree = 4 * rows
    r = wq_ref.shape[0]
    ru = wu_ref.shape[0]
    part1 = part + 1 - 2 * core
    part2 = lax.rem(part + 2, 4)
    part3 = lax.rem(part1 + 2, 4)

    own = pl.ds(pl.multiple_of(f * r, r), r)
    ownu = pl.ds(pl.multiple_of(f * ru, ru), ru)
    vecs[f] = vec_ref[...]
    wqkv_ref[own, 0:width] = wq_ref[...].astype(bf16)
    wqkv_ref[own, width:2 * width] = wk_ref[...].astype(bf16)
    wqkv_ref[own, 2 * width:3 * width] = wv_ref[...].astype(bf16)

    greet(F, f, core, sibling)

    def slot(g, src):
        if g == 0:
            return vecs.at[src]
        if g == 3:
            return wuf_ref.at[pl.ds(pl.multiple_of(src * ru, ru), ru)]
        ref = wqkv_ref if g == 1 else woi_ref
        return ref.at[pl.ds(pl.multiple_of(src * r, r), r)]

    def direct(g, d):
        return remote(slot(g, f), slot(g, f), gsend.at[g, d], grecv.at[g, d],
                      sibling if d == 0 else lax.rem(f + 2 * d, F))

    def came(g, d):
        src = sibling if d == 0 else lax.rem(f + F - 2 * d, F)
        remote(slot(g, src), slot(g, src), gsend.at[g, d], grecv.at[g, d], sibling).wait_recv()

    def forward(g, d):
        src = lax.rem(f + F - 2 * d, F)
        return remote(slot(g, src), slot(g, src), gsend.at[g, F // 2 + d], grecv.at[g, F // 2 + d], sibling)

    def forwarded(g, d):
        src = lax.rem(sibling + F - 2 * d, F)
        remote(slot(g, src), slot(g, src), gsend.at[g, F // 2 + d], grecv.at[g, F // 2 + d], sibling).wait_recv()

    chips = range(1, F // 2)

    def send_all(g):
        for d in range(F // 2):
            direct(g, d).start()

    def pass_on(g):
        for d in chips:
            came(g, d)
            forward(g, d).start()

    def receive_rest(g):
        came(g, 0)
        for d in chips:
            forwarded(g, d)

    x_out = remote(tok_ref.at[1 - half], xt_ref.at[part], tsend.at[0], trecv.at[0], partner)
    x_sib = remote(tok_ref.at[half], xt_ref.at[part], tsend.at[1], trecv.at[1], sibling)
    x_fwd = remote(xt_ref.at[part2], xt_ref.at[part2], tsend.at[2], trecv.at[2], sibling)
    dy_out = remote(cot_ref.at[1 - half], dy_ref.at[half], tsend.at[3], trecv.at[3], partner)
    dy_own = pltpu.make_async_copy(cot_ref.at[half], dy_ref.at[half], tsend.at[4])

    send_all(0)
    send_all(1)
    x_out.start()
    x_sib.start()
    dy_own.start()
    xt_ref[part] = tok_ref[half]
    woi_ref[own, 0:width] = wo_ref[...].astype(bf16)
    woi_ref[own, width:] = wi_ref[...].astype(bf16)
    wuf_ref[ownu, :] = wu_ref[...].astype(bf16)
    pass_on(0)
    pass_on(1)
    receive_rest(0)

    table = jnp.max(vecs[...], axis=1).astype(bf16)
    words = table.shape[1]

    def vector_row(first, m, length):
        col = iota((words, length), 1)
        pick = iota((words, length), 0) == first + (col & (m - 1))
        spread = mm(table, pick.astype(bf16))
        shift = m.bit_length() - 1
        mine = iota((F, length), 0) == (iota((F, length), 1) >> shift)
        return jnp.sum(jnp.where(mine, spread, 0.0), axis=0, keepdims=True)

    def all_rows(first, last):
        for i in range(first, last):
            rows_ref[:, i * width:(i + 1) * width] = jnp.broadcast_to(vector_row(i * n, n, width), (8, width))

    all_rows(0, 2)
    hidden = rows_ref.shape[1] - 6 * width
    receive_rest(1)

    lane = iota((seg, 128), 1)
    offs = iota((seg, 128), 0)
    arow = iota((64, rows), 0)

    def project(p):
        x = xt_ref[p].astype(f32)
        gain = rows_ref[0:1, 0:width]
        shift = rows_ref[0:1, width:2 * width]
        mean = jnp.mean(x, axis=-1, keepdims=True)
        x = x - mean
        inv = lax.rsqrt(jnp.mean(x * x, axis=-1, keepdims=True) + 1e-06)
        a1 = (x * inv * gain + shift).astype(bf16)

        def proj(i):
            return mm(a1, wqkv_ref[:, pl.ds(pl.multiple_of(i * width + core * hw, hw), hw)])

        cols = pl.ds(pl.multiple_of(p * rows, rows), rows)
        a1T_ref[:, cols] = a1.T
        q = (proj(0) * 0.125).astype(bf16)
        qn_ref[cols, :] = q
        qT = q.T
        k = proj(1).astype(bf16)
        kT_ref[:, cols] = k.T
        v = proj(2).astype(bf16)
        v_ref[pl.ds(p * 5, 5)] = v.reshape(5, seg, hw)
        vT = v.T
        for h in range(heads):
            a, b = slope_parts(h, H, tree), slope_parts(heads + h, H, tree)
            aug = jnp.zeros((64, rows), f32)
            for j in range(3):
                s = jnp.where(core == 0, a[j], b[j])
                aug = jnp.where((arow == j) | (arow == j + 3), s, aug)
            aug = aug.astype(bf16)
            lo, hi = 128 * h + 64 * (h % 2), 128 * h + 64 - 64 * (h % 2)
            qT_ref[lo:lo + 64, cols] = qT[64 * h:64 * h + 64]
            qT_ref[hi:hi + 64, cols] = aug
            vT_scr[80 * h:80 * h + 64, cols] = vT[64 * h:64 * h + 64]
            vT_scr[80 * h + 64:80 * h + 80, cols] = jnp.ones((16, rows), bf16)
        for b in range(5):
            blk = p * 5 + b
            start = jnp.where(blk < 8, blk * seg, jnp.where(blk < 12, 8 * seg, 9 * seg))
            spot = offs + start
            hi = (spot & -8).astype(f32)
            lo = (spot & 7).astype(f32)
            for h in range(heads):
                at = 64 - 64 * (h % 2)
                l = lane - at
                aug = jnp.where((l >= 0) & (l < 3), hi, jnp.where((l >= 3) & (l < 6), lo, 0.0)).astype(bf16)
                keep = (lane < 64) if h % 2 == 0 else (lane >= 64)
                kk = k[b * seg:(b + 1) * seg, 128 * (h // 2):128 * (h // 2) + 128]
                kaug_ref[blk, :, 128 * h:128 * h + 128] = jnp.where(keep, kk, aug)

    x_sib.wait_recv()

    def visit(i, c):
        @pl.when(i == 1)
        def _():
            all_rows(2, 6)
            rows_ref[:, 6 * width:] = jnp.broadcast_to(vector_row(6 * n, hidden // F, hidden), (8, hidden))
            x_out.wait_recv()
            x_fwd.start()
            send_all(2)
            send_all(3)

        @pl.when(i == 3)
        def _():
            x_fwd.wait_recv()

        project(jnp.where(i == 0, part, jnp.where(i == 1, part1, jnp.where(i == 2, part2, part3))))
        return c

    lax.fori_loop(0, 4, visit, 0)
    for i in range(heads // 2):
        for k in range(3):
            src = pl.ds(pl.multiple_of(k * width + core * hw + 128 * i, 128), 128)
            wc[:, 384 * i + 128 * k:384 * i + 128 * k + 128] = wqkv_ref[:, src]

    outs = [(a1T_ref, a1T_out), (kaug_ref, kaug_out), (v_ref, v_out), (kT_ref, kT_out), (qn_ref, qn_out),
            (qT_ref, qT_out), (wc, wc_out), (xt_ref.at[core], xs_out.at[0]), (xt_ref.at[core + 2], xs_out.at[1]),
            (oT_ref, oT_out), (lse_ref, lse_out),
            (woi_ref.at[pl.ds(pl.multiple_of(core * hw, hw), hw), 0:width], wo_out),
            (dxl_ref.at[0:rows], dxl_out.at[0]), (dxl_ref.at[rows:2 * rows], dxl_out.at[1]),
            (dx2_ref.at[0:rows], dx2_out.at[0]), (dx2_ref.at[rows:2 * rows], dx2_out.at[1]), (ga_ref, ga_out), (gb_ref, gb_out)]
    copies = [pltpu.make_async_copy(a, b, osem.at[i]) for i, (a, b) in enumerate(outs)]
    for c in copies[:9]:
        c.start()

    def between(h):
        @pl.when(h == 1)
        def _():
            dy_out.start()

        @pl.when(h == 2)
        def _():
            pass_on(2)

    attend(heads, seg, parents_ref, kaug_ref, qT_ref, vT_scr, oT_ref, lse_ref, s_scr, between)

    other = 1 - core
    sent = []
    for i in range(2):
        cols = pl.ds(pl.multiple_of((other + 2 * i) * rows, rows), rows)
        at = (pl.ds(pl.multiple_of(core * hw, hw), hw), slice(i * rows, (i + 1) * rows))
        c = remote(oT_ref.at[:, cols], oF_ref.at[at], tsend.at[5 + i], trecv.at[5 + i], sibling)
        c.start()
        sent.append(c)
    for i in range(2):
        mine = pl.ds(pl.multiple_of((core + 2 * i) * rows, rows), rows)
        at = (pl.ds(pl.multiple_of(core * hw, hw), hw), slice(i * rows, (i + 1) * rows))
        oF_ref[at] = oT_ref[:, mine]
    copies[9].start()
    copies[10].start()
    receive_rest(2)
    copies[11].start()
    pass_on(3)
    for c in sent:
        c.wait_recv()
    receive_rest(3)
    dy_own.wait()

    vin_ref[...] = jnp.zeros_like(vin_ref)
    dense = Dense(rows, width, oF_ref, dy_ref, woi_ref, wuf_ref, rows_ref, dxl_ref, dx2_ref, ga_ref, gb_ref, vin_ref,
                  a2s, gs, dus)
    keep_y = [pltpu.make_async_copy(xt_ref.at[other + 2 * i], y_out.at[i], osem.at[18 + i]) for i in range(2)]

    def dense_step(s, c):
        i = jnp.where(s == 0, half, 1 - half)

        @pl.when(s == 1)
        def _():
            dy_out.wait_recv()

        dense.chunk(i * rows, xt_ref[core + 2 * i], xt_ref.at[other + 2 * i])
        return c

    lax.fori_loop(0, 2, dense_step, 0)
    for c in keep_y + copies[12:16]:
        c.start()
    dense.gradients(F)
    copies[16].start()
    copies[17].start()
    for c in copies + keep_y:
        c.wait()
    dy_out.wait_send()
    x_out.wait_send()
    x_sib.wait_send()
    x_fwd.wait_send()
    for c in sent:
        c.wait_send()
    for g in range(4):
        for d in range(F // 2):
            direct(g, d).wait_send()
        for d in chips:
            forward(g, d).wait_send()


def first(F, parents, tokens, cotangent, weights, vec, n):
    _, rows, width = tokens.shape
    tree = 4 * rows
    heads = H // 2
    hw = heads * 64
    seg = rows // 5
    hidden = weights[4].shape[1]
    r, ru = width // F, hidden // F
    R1 = (hidden // width + 1) * r
    two = 2 * rows
    keep = [((width, tree), bf16), ((20, seg, heads * 128), bf16), ((20, seg, hw), bf16), ((hw, tree), bf16),
            ((tree, hw), bf16), ((heads * 128, tree), bf16), ((hw, tree), bf16), ((heads * 8, tree), f32)]
    out = keep + [((width, 3 * hw), bf16), ((hw, width), bf16), ((2, rows, width), bf16), ((2, rows, width), bf16),
                  ((2, rows, width), f32), ((F, ru, width), bf16), ((F, R1, width), bf16), ((2, rows, width), bf16),
                  ((16, width), f32), ((8, 6 * width + hidden), f32)]
    scratch = [((4, rows, width), bf16)] + keep + [
        ((2 * hw, two), bf16), ((2, rows, width), bf16), ((width, 3 * width), bf16), ((width, width + hidden), bf16),
        ((hidden, width), bf16), ((width, 3 * hw), bf16), ((two, width), bf16),
        ((two, width), f32), ((F, ru, width), bf16), ((F, R1, width), bf16), ((two, width), bf16), ((two, hidden), bf16),
        ((two, hidden), bf16), ((F,) + vec.shape, f32), ((heads * 80, tree), bf16), ((8 * seg, T), f32)]
    ANY = pl.BlockSpec(memory_space=pl.ANY)
    dma = pltpu.SemaphoreType.DMA
    return pl.pallas_call(
        functools.partial(first_kernel, F, n),
        out_shape=[jax.ShapeDtypeStruct(s, d) for s, d in out],
        in_specs=[SM, VM, ANY] + [VM] * 7,
        out_specs=[ANY] * 16 + [VM] * 2,
        scratch_shapes=[pltpu.VMEM(s, d) for s, d in scratch] + [
            dma((7,)), dma((7,)), dma((4, F)), dma((4, F)), dma((20,))],
        name="front",
        compiler_params=pltpu.CompilerParams(vmem_limit_bytes=64 << 20, collective_id=0, has_side_effects=True),
    )(parents, tokens, cotangent, *weights, vec)


def fold(x):
    return x.astype(f32)


class Chain:
    def __init__(self, F, f, sums, got, block, zgot, final, send, recv):
        self.F, self.f, self.sums, self.got, self.block = F, f, sums, got, block
        self.zgot, self.final, self.send, self.recv = zgot, final, send, recv
        self.chip = f // 2
        self.chips = F // 2
        self.planes = lax.axis_size("dp")
        self.plane = lax.axis_index("dp")
        self.rows = sums.shape[1]
        self.zrows = block.shape[0] // self.planes

    def _b(self, d):
        return remote(self.sums.at[lax.rem(self.chip + d, self.chips)], self.got.at[d - 1],
                      self.send.at[d], self.recv.at[d], lax.rem(self.f + 2 * d, self.F))

    def _chunk(self, z):
        return pl.ds(pl.multiple_of(z * self.zrows, 16), self.zrows)

    def _c(self, e):
        z = lax.rem(self.plane + e, self.planes)
        i = self.chips + e
        return pltpu.make_async_remote_copy(
            src_ref=self.block.at[self._chunk(z)], dst_ref=self.zgot.at[e - 1],
            send_sem=self.send.at[i], recv_sem=self.recv.at[i],
            device_id={"dp": z}, device_id_type=pl.DeviceIdType.MESH)

    def _d(self, e, src=None):
        z = lax.rem(self.plane + e, self.planes)
        i = self.chips + self.planes + e
        here = self._chunk(self.plane if src is None else src)
        return pltpu.make_async_remote_copy(
            src_ref=self.final.at[here], dst_ref=self.final.at[here],
            send_sem=self.send.at[i], recv_sem=self.recv.at[i],
            device_id={"dp": z}, device_id_type=pl.DeviceIdType.MESH)

    def start_plane(self):
        for d in range(1, self.chips):
            self._b(d).start()

    def start_z(self):
        for d in range(1, self.chips):
            self._b(d).wait_recv()
        total = fold(self.sums[self.chip])
        for d in range(1, self.chips):
            total = total + fold(self.got[d - 1])
        self.block[0:self.rows] = total.astype(bf16)
        for e in range(1, self.planes):
            self._c(e).start()

    def start_back(self):
        for e in range(1, self.planes):
            self._c(e).wait_recv()
        here = self._chunk(self.plane)
        total = fold(self.block[here])
        for e in range(1, self.planes):
            total = total + fold(self.zgot[e - 1])
        self.final[here] = total.astype(bf16)
        for e in range(1, self.planes):
            self._d(e).start()

    def receive(self):
        for e in range(1, self.planes):
            self._d(e, lax.rem(self.plane + self.planes - e, self.planes)).wait_recv()

    def close(self):
        for d in range(1, self.chips):
            self._b(d).wait_send()
        for e in range(1, self.planes):
            self._c(e).wait_send()
            self._d(e).wait_send()


def last_kernel(F, parents_ref, kaug_h, v_h, qT_h, kT_h, qn_h, oT_h, lse_h, a1T_h, wc_h, wo_h, xs_h, dxl_ref, dx2_h, y_h,
                ga_ref, gb_ref, vin_ref, n1_ref,
                gt_ref, lo_ref, gq_ref, fina, finb, vout_ref,
                kaug_ref, v_ref, qT_ref, kT_ref, qn_ref, oT_ref, lse_ref, a1T_ref, wc, wo_scr, xs, dx2s, ys,
                dxs, doT, do, dqT, dqkv, accK, accV, das, dar,
                suma, sumb, gota, gotb, planea, planeb, blka, blkb, za, zb, sum2, got2, blk2, z2, fin2,
                vs, vgot, dxo, tsend, trecv, senda, recva, sendb, recvb, send2, recv2, vsend, vrecv, lsem):
    f, part, half, core, partner, sibling = where_am_i(F)
    planes = lax.axis_size("dp")
    plane = lax.axis_index("dp")
    heads = H // 2
    hw = heads * 64
    _, rows, width = dxl_ref.shape
    chips = F // 2
    other = 1 - core
    tree = 4 * rows
    seg = rows // 5

    pairs = [(wo_h, wo_scr), (qT_h, qT_ref), (kaug_h, kaug_ref), (v_h, v_ref), (kT_h, kT_ref), (qn_h, qn_ref),
             (oT_h, oT_ref), (lse_h, lse_ref), (ga_ref.at[:, core], suma), (gb_ref.at[:, core], sumb), (a1T_h, a1T_ref), (wc_h, wc), (xs_h, xs),
             (dx2_h, dx2s), (y_h, ys)]
    loads = [pltpu.make_async_copy(a, b, lsem.at[i]) for i, (a, b) in enumerate(pairs)]
    for c in loads:
        c.start()

    barrier = pltpu.get_barrier_semaphore()
    for d in range(1, chips):
        pl.semaphore_signal(barrier, inc=1, device_id={"fsdp": lax.rem(f + 2 * d, F)},
                            device_id_type=pl.DeviceIdType.MESH)
    for e in range(1, planes):
        pl.semaphore_signal(barrier, inc=1, device_id={"dp": lax.rem(plane + e, planes)},
                            device_id_type=pl.DeviceIdType.MESH)
    pl.semaphore_signal(barrier, inc=1, device_id={"fsdp": sibling}, device_id_type=pl.DeviceIdType.MESH)
    pl.semaphore_wait(barrier, chips + planes - 1)

    dx_sw = remote(dxl_ref, dxs, tsend.at[0], trecv.at[0], sibling)
    out_a = remote(ga_ref.at[:, other], gota, tsend.at[1], trecv.at[1], sibling)
    out_b = remote(gb_ref.at[:, other], gotb, tsend.at[7], trecv.at[7], sibling)
    y_out = remote(ys.at[1 - half], lo_ref.at[half], tsend.at[8], trecv.at[8], partner)
    keep_y = pltpu.make_async_copy(ys.at[half], lo_ref.at[half], lsem.at[16])
    dx_sw.start()
    out_a.start()
    out_b.start()

    def make_do(p, x):
        cols = pl.ds(pl.multiple_of(p * rows, rows), rows)
        d = mm_nt(x, wo_scr[...]).astype(bf16)
        do[cols, :] = d
        doT[:, cols] = d.T

    loads[0].wait()
    lax.fori_loop(0, 2, lambda i, c: (make_do(core + 2 * i, dxl_ref[i]), c)[1], 0)

    one_a = Chain(F, f, suma, planea, blka, za, fina, senda, recva)
    one_b = Chain(F, f, sumb, planeb, blkb, zb, finb, sendb, recvb)

    def add_sibling(load, arrived, mine, got):
        load.wait()
        arrived.wait_recv()

        def add_block(j, c):
            mine[j] = (fold(mine[j]) + fold(got[j])).astype(bf16)
            return c

        lax.fori_loop(0, chips, add_block, 0)

    dx_sw.wait_recv()
    lax.fori_loop(0, 2, lambda i, c: (make_do(other + 2 * i, dxs[i]), c)[1], 0)
    add_sibling(loads[8], out_a, suma, gota)
    one_a.start_plane()
    for c in loads[1:8]:
        c.wait()

    def chain(pr):
        return Chain(F, f, sum2.at[pr], got2.at[pr], blk2.at[pr], z2.at[pr], fin2.at[pr], send2.at[pr], recv2.at[pr])

    two = [chain(0), chain(1)]
    r = width // F
    r2 = 2 * r

    def hook(name, pr, i=None):
        if name == "mid":
            @pl.when(pr == 0)
            def _():
                add_sibling(loads[9], out_b, sumb, gotb)
                one_b.start_plane()

            @pl.when(pr == 1)
            def _():
                one_b.start_z()
                loads[14].wait()
                y_out.start()
                keep_y.start()
        if name == "late":
            @pl.when(pr == 1)
            def _():
                one_a.start_back()
        if name == "leaf":
            @pl.when((pr == 0) & (i == 5))
            def _():
                one_a.start_z()

            @pl.when((pr == 1) & (i == 4))
            def _():
                one_b.start_back()
                two[0].start_z()
        if name == "end":
            @pl.when(pr == 0)
            def _():
                for c in loads[10:14]:
                    c.wait()

            @pl.when(pr == 1)
            def _():
                two[0].start_back()

            g = mm(a1T_ref[...], dqkv[:, :, pl.ds(pl.multiple_of(pr * 384, 384), 384)].reshape(tree, 384)).astype(bf16)
            for j in range(chips):
                sum2[pr, j] = g[j * r2:(j + 1) * r2]
            chain(pr).start_plane()

    attend_back(heads, seg, parents_ref, kaug_ref, v_ref, qT_ref, doT, kT_ref, do, qn_ref, oT_ref, lse_ref,
                dqT, dqkv, accK, accV, hook)

    def da1_of(p):
        return mm_nt(dqkv[pl.ds(p * 5, 5)].reshape(rows, 3 * hw), wc[...])

    def da_out(s):
        i = (1 - half) if s == 0 else half
        return remote(das.at[i], dar.at[i], tsend.at[2 + s], trecv.at[2 + s], sibling)

    dx_out = remote(dxo.at[1 - half], gt_ref.at[half], tsend.at[4], trecv.at[4], partner)
    keep_dx = pltpu.make_async_copy(dxo.at[half], gt_ref.at[half], lsem.at[15])
    vs[0] = vin_ref[...]
    row = iota((16, width), 0)

    def finish_rows(s, c):
        i = jnp.where(s == 0, 1 - half, half)
        das[i] = da1_of(other + 2 * i).astype(bf16)
        for k in range(2):
            @pl.when(s == k)
            def _():
                da_out(k).start()
        x = fold(xs[i])
        x = x - jnp.mean(x, axis=-1, keepdims=True)
        inv = lax.rsqrt(jnp.mean(x * x, axis=-1, keepdims=True) + 1e-06)
        unit = x * inv
        da = da1_of(core + 2 * i)
        for k in range(2):
            @pl.when(s == k)
            def _():
                da_out(k).wait_recv()
        da = da + fold(dar[i])
        dn = da * n1_ref[0:1, 0:width]
        m1 = jnp.mean(dn, axis=-1, keepdims=True)
        m2 = jnp.mean(dn * unit, axis=-1, keepdims=True)
        dxo[i] = (dx2s[i] + (dn - m1 - unit * m2) * inv).astype(bf16)
        gs = jnp.sum(da * unit, axis=0, keepdims=True)
        bs = jnp.sum(da, axis=0, keepdims=True)
        vs[0] += jnp.where(row == 0, gs, 0.0) + jnp.where(row == 1, bs, 0.0)

        @pl.when(s == 0)
        def _():
            dx_out.start()

        @pl.when(s == 1)
        def _():
            keep_dx.start()

        return c

    lax.fori_loop(0, 2, finish_rows, 0)
    v_sib = remote(vs.at[0], vgot.at[0], vsend.at[0], vrecv.at[0], sibling)
    v_sib.start()
    two[1].start_z()
    v_sib.wait_recv()
    vs[1] = vs[0] + vgot[0]
    v_chip = [remote(vs.at[1], vgot.at[d], vsend.at[d], vrecv.at[d], lax.rem(f + 2 * d, F)) for d in range(1, chips)]
    for c in v_chip:
        c.start()
    two[1].start_back()
    for c in v_chip:
        c.wait_recv()
    total = vs[1]
    for d in range(1, chips):
        total = total + vgot[d]
    vgot[chips + plane] = total

    def v_z(e, sender):
        return pltpu.make_async_remote_copy(
            src_ref=vgot.at[chips + sender], dst_ref=vgot.at[chips + sender],
            send_sem=vsend.at[chips + e], recv_sem=vrecv.at[chips + e],
            device_id={"dp": lax.rem(plane + e, planes)}, device_id_type=pl.DeviceIdType.MESH)

    for e in range(1, planes):
        v_z(e, plane).start()

    one_a.receive()
    one_b.receive()
    s_out = []
    for pr in range(2):
        two[pr].receive()
        c = remote(fin2.at[pr, pl.ds(pl.multiple_of(other * r, r), r)], gq_ref.at[core, pr],
                   tsend.at[5 + pr], trecv.at[5 + pr], sibling)
        c.start()
        gq_ref[core, pr] = fin2[pr, pl.ds(pl.multiple_of(core * r, r), r), :]
        s_out.append(c)
    for e in range(1, planes):
        v_z(e, lax.rem(plane + planes - e, planes)).wait_recv()
    total = vgot[chips]
    for z in range(1, planes):
        total = total + vgot[chips + z]
    vout_ref[...] = total
    for c in s_out:
        c.wait()
    dx_out.wait()
    keep_dx.wait()
    keep_y.wait()
    y_out.wait()
    one_a.close()
    one_b.close()
    for c in two:
        c.close()
    for c in [dx_sw, out_a, out_b, v_sib, da_out(0), da_out(1)] + v_chip:
        c.wait_send()
    for e in range(1, planes):
        v_z(e, plane).wait_send()


def last(F, DP, parents, kept, wc, wo, xs, dxl, dx2, y, ga, gb, vin, rows_vec):
    a1T, kaug, v, kT, qn, qT, oT, lse = kept
    _, rows, width = dxl.shape
    heads = H // 2
    hw = heads * 64
    tree = 4 * rows
    seg = rows // 5
    chips = F // 2
    r = width // F
    RA, RB = ga.shape[2], gb.shape[2]
    r2 = 2 * r

    def zrows(n):
        return -(-n // (16 * DP)) * 16

    ZA, ZB, Z2 = zrows(RA), zrows(RB), zrows(r2)
    ANY = pl.BlockSpec(memory_space=pl.ANY)
    dma = pltpu.SemaphoreType.DMA
    out = [((2, rows, width), bf16), ((2, rows, width), bf16), ((2, 2, r, 384), bf16), ((ZA * DP, width), bf16),
           ((ZB * DP, width), bf16), ((16, width), f32)]
    big = [kaug, v, qT, kT, qn, oT, lse, a1T, wc, wo, xs]
    scratch = [(a.shape, a.dtype) for a in big] + [
        ((2, rows, width), f32), ((2, rows, width), bf16),
        ((2, rows, width), bf16), ((hw, tree), bf16), ((tree, hw), bf16), ((128, tree), bf16),
        ((20, seg, 3 * hw), bf16), ((20, seg, 128), f32), ((20, seg, 128), f32),
        ((2, rows, width), bf16), ((2, rows, width), bf16),
        ((chips, RA, width), bf16), ((chips, RB, width), bf16), ((chips, RA, width), bf16), ((chips, RB, width), bf16),
        ((chips - 1, RA, width), bf16), ((chips - 1, RB, width), bf16), ((ZA * DP, width), bf16),
        ((ZB * DP, width), bf16), ((DP - 1, ZA, width), bf16), ((DP - 1, ZB, width), bf16),
        ((2, chips, r2, 384), bf16), ((2, chips - 1, r2, 384), bf16), ((2, Z2 * DP, 384), bf16),
        ((2, DP - 1, Z2, 384), bf16), ((2, Z2 * DP, 384), bf16),
        ((2, 16, width), f32), ((chips + DP, 16, width), f32), ((2, rows, width), bf16),
    ]
    nsem = chips + 2 * DP
    return pl.pallas_call(
        functools.partial(last_kernel, F),
        out_shape=[jax.ShapeDtypeStruct(s, d) for s, d in out],
        in_specs=[SM] + [ANY] * 11 + [VM, ANY, ANY, ANY, ANY, VM, VM],
        out_specs=[ANY, ANY] + [VM] * 4,
        scratch_shapes=[pltpu.VMEM(s, d) for s, d in scratch] + [
            dma((9,)), dma((9,)), dma((nsem,)), dma((nsem,)), dma((nsem,)), dma((nsem,)), dma((2, nsem)), dma((2, nsem)),
            dma((chips + DP,)), dma((chips + DP,)), dma((17,))],
        name="back",
        compiler_params=pltpu.CompilerParams(vmem_limit_bytes=64 << 20, collective_id=1, has_side_effects=True),
    )(parents, *big, dxl, dx2, y, ga, gb, vin, rows_vec)


def finish_kernel(lo_in, gt_in, fina, finb, gq, lo_ref, gt_ref, gwq_ref, gwk_ref, gwv_ref, gwo_ref, gwi_ref, gwu_ref):
    lo_ref[...] = lo_in[...]
    gt_ref[...] = gt_in[...]
    r, width = gwo_ref.shape
    ru = gwu_ref.shape[0]
    gwu_ref[...] = fold(fina[0:ru])
    pieces = gwi_ref.shape[1] // width
    for c in range(pieces):
        gwi_ref[:, c * width:(c + 1) * width] = fold(finb[c * r:(c + 1) * r])
    gwo_ref[...] = fold(finb[pieces * r:(pieces + 1) * r])
    for k, ref in enumerate((gwq_ref, gwk_ref, gwv_ref)):
        for c in range(2):
            for pr in range(2):
                at = (2 * c + pr) * 128
                ref[:, at:at + 128] = fold(gq[c, pr, :, 128 * k:128 * k + 128])


def finish(F, lo, gt, fina, finb, gq, hidden):
    width = lo.shape[2]
    r, ru = width // F, hidden // F
    shapes = [(r, width)] * 4 + [(r, hidden), (ru, width)]
    return pl.pallas_call(
        finish_kernel,
        out_shape=[jax.ShapeDtypeStruct(lo.shape, bf16), jax.ShapeDtypeStruct(gt.shape, bf16)]
        + [jax.ShapeDtypeStruct(s, f32) for s in shapes],
        in_specs=[VM] * 5,
        out_specs=[VM] * 8,
        name="finish",
    )(lo, gt, fina, finb, gq)


def on_device(tokens, parents, n1g, n1b, wq, wk, wv, wo, ob, n2g, n2b, wi, ib, wu, ub, cotangent):
    F = lax.axis_size("fsdp")
    fi = lax.axis_index("fsdp")
    place = (fi + 2) % F
    half = (place % 4) // 2
    quad = lax.axis_index("dp") * (F // 4) + place // 4
    parent_row = parents[quad, half]
    _, _, rows, width = tokens.shape

    n = n1g.shape[0]
    vec = jnp.concatenate([n1g, n1b, ob, n2g, n2b, ub, ib])
    vec = lax.reduce_precision(vec, 8, 7)
    vec = jnp.broadcast_to(jnp.pad(vec, (0, -vec.shape[0] % 128)), (8, vec.shape[0] + -vec.shape[0] % 128))
    hidden = wi.shape[1]
    ru = hidden // F
    (a1T, kaug, v, kT, qn, qT, oT, lse, wc, wo_own, xs, dxl, dx2, ga, gb, y, vin, vrows) = first(
        F, parent_row, tokens[0], cotangent[0], (wq, wk, wv, wo, wi, wu), vec, n)
    gt, lo, gq, fina, finb, vout = last(
        F, lax.axis_size("dp"), parent_row, (a1T, kaug, v, kT, qn, qT, oT, lse), wc, wo_own, xs, dxl, dx2, y,
        ga.reshape(F // 2, 2, -1, width), gb.reshape(F // 2, 2, -1, width), vin, vrows)
    lo, gt, gwq, gwk, gwv, gwo, gwi, gwu = finish(F, lo, gt, fina, finb, gq, hidden)
    sv = lax.dynamic_slice_in_dim(vout[:6], fi * n, n, 1)
    sib = lax.dynamic_slice_in_dim(vout[6:6 + hidden // width].reshape(-1), fi * ru, ru, 0)
    return (lo[None], gt[None], sv[0], sv[1], gwq, gwk, gwv, gwo, sv[2], sv[3], sv[4], gwi, sib, gwu, sv[5])


def solution(mesh):
    tok = P(("dp", "fsdp"), None, None, None)
    v, m = P("fsdp"), P("fsdp", None)
    return jax.shard_map(
        on_device,
        mesh=mesh,
        in_specs=(tok, P(), v, v, m, m, m, m, v, v, v, m, v, m, v, tok),
        out_specs=(tok, tok, v, v, m, m, m, m, v, v, v, m, v, m, v),
        check_vma=False,
    )
```

```python
import functools
import math

import jax
import jax.numpy as jnp
import ml_dtypes
import numpy as np
from jax import lax
from jax.experimental import pallas as pl
from jax.experimental.pallas import tpu as pltpu
from jax.sharding import PartitionSpec as P

H = 8
T = 256
f32, bf16 = jnp.float32, jnp.bfloat16
VM = pl.BlockSpec(memory_space=pltpu.VMEM)
SM = pl.BlockSpec(memory_space=pltpu.SMEM)


def mm(a, b):
    return jnp.dot(a, b, preferred_element_type=f32)


def mm_tn(a, b):
    return lax.dot_general(a, b, (((0,), (0,)), ((), ())), preferred_element_type=f32)


def mm_nt(a, b):
    return lax.dot_general(a, b, (((1,), (1,)), ((), ())), preferred_element_type=f32)


def iota(shape, dim):
    return lax.broadcasted_iota(jnp.int32, shape, dim)


def chosen(par, read):
    out = read(0)
    for b in range(1, 4):
        out = jnp.where(par == b + 1, read(b), out)
    return out


def attend(heads, seg, parents_ref, kaug_ref, qT_ref, vT_ref, oT_ref, lse_ref, s_refs, hook):
    ntr = 8 * seg // T
    vr = vT_ref.shape[0] // heads
    causal_t = iota((T, T), 0) <= iota((T, T), 1)
    causal_b = iota((seg, seg), 0) <= iota((seg, seg), 1)
    G = heads

    def group(g, _):
        hook(0)
        hs = [g * G + e for e in range(G)]
        hk = [pl.ds(pl.multiple_of(h * 128, 128), 128) for h in hs]
        hv = [pl.ds(pl.multiple_of(h * vr, vr), vr) for h in hs]

        def keys(e, blk, n):
            return kaug_ref[pl.ds(blk, n), :, hk[e]].reshape(n * seg, 128)

        def finish(e, cols, m, acc):
            h = hs[e]
            l = acc[64:65, :]
            oT_ref[pl.ds(pl.multiple_of(h * 64, 64), 64), cols] = (acc[:64] / l).astype(bf16)
            lse_ref[pl.ds(pl.multiple_of(h * 8, 8), 8), cols] = jnp.broadcast_to(m + jnp.log(l), (8, T))

        def full_scores(e, q, n):
            m = None
            for c in range(n):
                s = mm(keys(e, 2 * c, 2), q)
                s_refs[e][c * T:(c + 1) * T, :] = s
                cm = jnp.max(s, axis=0, keepdims=True)
                m = cm if m is None else jnp.maximum(m, cm)
            return m

        def full_mix(e, m, n, acc):
            for c in range(n):
                p = jnp.exp(s_refs[e][c * T:(c + 1) * T, :] - m).astype(bf16)
                t = mm(vT_ref[hv[e], c * T:(c + 1) * T], p)
                acc = t if acc is None else acc + t
            return acc

        for t in range(ntr):
            cols = slice(t * T, (t + 1) * T)
            sds, ms = [], []
            for e in range(G):
                q = qT_ref[hk[e], cols]
                sd = jnp.where(causal_t, mm(keys(e, 2 * t, 2), q), -1e30)
                m = jnp.max(sd, axis=0, keepdims=True)
                if t:
                    m = jnp.maximum(m, full_scores(e, q, t))
                sds.append(sd)
                ms.append(m)
            for e in range(G):
                acc = mm(vT_ref[hv[e], cols], jnp.exp(sds[e] - ms[e]).astype(bf16))
                acc = full_mix(e, ms[e], t, acc)
                finish(e, cols, ms[e], acc)

        def tail_tile(i, leaf):
            b0 = 8 + 2 * i
            cols = pl.ds(pl.multiple_of(b0 * seg, T), T)
            pars = [parents_ref[b0 + half - 7] for half in range(2)] if leaf else None
            exts, ms = [], []
            for e in range(G):
                q = qT_ref[hk[e], cols]
                m = full_scores(e, q, ntr)
                ext = []
                for x in range(2 if leaf else 1):
                    pieces = []
                    for half in range(2):
                        kk = keys(e, b0 + half, 1) if x == 0 else chosen(pars[half], lambda b: keys(e, 8 + b, 1))
                        s = mm(kk, q[:, half * seg:(half + 1) * seg])
                        if x == 0:
                            s = jnp.where(causal_b, s, -1e30)
                        pieces.append(s)
                    s = jnp.concatenate(pieces, axis=1)
                    m = jnp.maximum(m, jnp.max(s, axis=0, keepdims=True))
                    ext.append(s)
                exts.append(ext)
                ms.append(m)
            for e in range(G):
                acc = None
                for x, s in enumerate(exts[e]):
                    p = jnp.exp(s - ms[e]).astype(bf16)
                    t = []
                    for half in range(2):
                        if x == 0:
                            vv = vT_ref[hv[e], pl.ds(pl.multiple_of((b0 + half) * seg, seg), seg)]
                        else:
                            vv = chosen(pars[half], lambda b: vT_ref[hv[e], (8 + b) * seg:(9 + b) * seg])
                        t.append(mm(vv, p[:, half * seg:(half + 1) * seg]))
                    t = jnp.concatenate(t, axis=1)
                    acc = t if acc is None else acc + t
                acc = full_mix(e, ms[e], ntr, acc)
                finish(e, cols, ms[e], acc)

        hook(1)
        lax.fori_loop(0, 2, lambda i, c: (tail_tile(i, False), c)[1], 0)
        hook(2)
        lax.fori_loop(2, 6, lambda i, c: (hook(3, i), tail_tile(i, True), c)[2], 0)
        return 0

    lax.fori_loop(0, heads // G, group, 0)


def attend_back(heads, seg, parents_ref, kaug_ref, v_ref, qT_ref, doT_ref, kT_ref, do_ref, qn_ref,
                oT_ref, lse_ref, dqT_ref, dqkv_ref, accK, accV, hook):
    ntr = 8 * seg // T
    causal_t = iota((T, T), 0) <= iota((T, T), 1)
    causal_b = iota((seg, seg), 0) <= iota((seg, seg), 1)
    low_rows = iota((128, T), 0) < 64
    low_lanes = iota((T, 128), 1) < 64

    def pair(pr, _):
        hook("start", pr)
        lanes = pl.ds(pl.multiple_of(pr * 128, 128), 128)
        hk = [pl.ds(pl.multiple_of(pr * 256 + 128 * e, 128), 128) for e in range(2)]
        h64 = [pl.ds(pl.multiple_of(pr * 128 + 64 * e, 64), 64) for e in range(2)]
        accK[...] = jnp.zeros_like(accK)
        accV[...] = jnp.zeros_like(accV)

        def stack(x):
            z = jnp.zeros_like(x)
            return jnp.concatenate([jnp.where(low_lanes, x, z), jnp.where(low_lanes, z, x)], axis=0)

        def prep(cols):
            doT = doT_ref[lanes, cols]
            z = jnp.zeros_like(doT)
            prod = doT.astype(f32) * oT_ref[lanes, cols].astype(f32)
            q, do, lse, delta = [], [], [], []
            for e in range(2):
                q.append(qT_ref[hk[e], cols])
                do.append(jnp.where(low_rows, doT, z) if e == 0 else jnp.where(low_rows, z, doT))
                at = pl.multiple_of((pr * 2 + e) * 8, 8)
                lse.append(jnp.max(lse_ref[pl.ds(at, 8), cols], axis=0, keepdims=True))
                delta.append(jnp.sum(prod[64 * e:64 * e + 64], axis=0, keepdims=True))
            return q, do, lse, delta, stack(do_ref[cols, lanes]), stack(qn_ref[cols, lanes])

        def front(blk, n, sl, args, mask, par=None):
            q, do, lse, delta, rv, rk = args

            def rows_of(ref, at):
                if par is None:
                    return ref[pl.ds(blk, n), :, at].reshape(n * seg, 128)
                return chosen(par, lambda b: ref[8 + b, :, at])

            vv = rows_of(v_ref, lanes)
            s = [mm(rows_of(kaug_ref, hk[e]), q[e][:, sl]) for e in range(2)]
            dp = [mm(vv, do[e][:, sl]) for e in range(2)]
            return s, dp

        def rear(blk, n, sl, args, mask, par, s, dp):
            q, do, lse, delta, rv, rk = args
            ps, dss, dq = [], [], []
            for e in range(2):
                p = jnp.exp(s[e] - lse[e][:, sl])
                if mask is not None:
                    p = jnp.where(mask, p, 0.0)
                dss.append((p * (dp[e] - delta[e][:, sl])).astype(bf16))
                ps.append(p.astype(bf16))
            for e in range(2):
                if par is None:
                    kT = kT_ref[h64[e], pl.ds(pl.multiple_of(blk * seg, seg), n * seg)]
                else:
                    kT = chosen(par, lambda b: kT_ref[h64[e], (8 + b) * seg:(9 + b) * seg])
                dq.append(mm(kT, dss[e]))
            if sl.stop - sl.start != T:
                rv = jnp.concatenate([rv[sl], rv[T + sl.start:T + sl.stop]], axis=0)
                rk = jnp.concatenate([rk[sl], rk[T + sl.start:T + sl.stop]], axis=0)
            av = mm(jnp.concatenate(ps, axis=1), rv)
            ak = mm(jnp.concatenate(dss, axis=1), rk)
            if par is None:
                accV[pl.ds(blk, n)] += av.reshape(n, seg, 128)
                accK[pl.ds(blk, n)] += ak.reshape(n, seg, 128)
            else:
                for b in range(4):
                    here = jnp.where(par == b + 1, 1.0, 0.0)
                    accK[8 + b] += ak * here
                    accV[8 + b] += av * here
            return dq

        def run(items):
            out = []
            ready = []
            for item in items:
                ready.append((item, front(*item)))
                if len(ready) > 2:
                    it, (s, dp) = ready.pop(0)
                    out.append(rear(*it, s, dp))
            for it, (s, dp) in ready:
                out.append(rear(*it, s, dp))
            return out

        def emit(cols, dq):
            for e in range(2):
                dqT_ref[64 * e:64 * e + 64, cols] = (dq[e] * 0.125).astype(bf16)

        full = slice(0, T)
        for t in range(ntr):
            cols = slice(t * T, (t + 1) * T)
            args = prep(cols)
            items = [(2 * t, 2, full, args, causal_t, None)] + [(2 * c, 2, full, args, None, None) for c in range(t)]
            res = run(items)
            emit(cols, [sum(x[e] for x in res) for e in range(2)])

        def tail_tile(i, leaf):
            b0 = 8 + 2 * i
            cols = pl.ds(pl.multiple_of(b0 * seg, T), T)
            args = prep(cols)
            items = []
            for half in range(2):
                sl = slice(half * seg, (half + 1) * seg)
                items.append((b0 + half, 1, sl, args, causal_b, None))
                if leaf:
                    items.append((8, 1, sl, args, None, parents_ref[b0 + half - 7]))
            k = len(items) // 2
            items += [(2 * c, 2, full, args, None, None) for c in range(ntr)]
            res = run(items)
            dq = []
            for e in range(2):
                halves = [sum(x[e] for x in res[h * k:(h + 1) * k]) for h in range(2)]
                dq.append(jnp.concatenate(halves, axis=1) + sum(x[e] for x in res[2 * k:]))
            emit(cols, dq)

        hook("mid", pr)
        lax.fori_loop(0, 2, lambda i, c: (tail_tile(i, False), c)[1], 0)
        hook("late", pr)
        lax.fori_loop(2, 6, lambda i, c: (hook("leaf", pr, i), tail_tile(i, True), c)[2], 0)
        first = pr * 384

        def put(i, x):
            dqkv_ref[:, :, pl.ds(pl.multiple_of(first + 128 * i, 128), 128)] = x

        put(0, dqT_ref[...].T.reshape(20, seg, 128))
        put(1, accK[...].astype(bf16))
        put(2, accV[...].astype(bf16))
        hook("end", pr)
        return 0

    lax.fori_loop(0, heads // 2, pair, 0)


class Dense:
    def __init__(self, rows, width, oF_ref, dy_ref, woi_ref, wu_ref, rows_ref, dxl_ref, dx2_ref, ga_ref, gb_ref, vin_ref,
                 a2s, gs, dus):
        self.__dict__.update({k: v for k, v in locals().items() if k != "self"})
        self.hidden = wu_ref.shape[0]
        self.tiles = self.hidden // width

    def chunk(self, start, x, y_ref):
        width, rows_ref, vin_ref = self.width, self.rows_ref, self.vin_ref
        woi_ref, wu_ref = self.woi_ref, self.wu_ref
        c1 = math.sqrt(2.0 / math.pi)
        c2 = c1 * 0.044715

        def vector(i):
            return rows_ref[0:1, i * width:(i + 1) * width]

        def add_sum(i, x):
            vin_ref[i:i + 1, :] += jnp.sum(x, axis=0, keepdims=True)

        at = pl.ds(pl.multiple_of(start, 128), x.shape[0])
        x2 = fold(x) + mm_tn(self.oF_ref[:, at], woi_ref[:, 0:width]) + vector(2)
        centred = x2 - jnp.mean(x2, axis=-1, keepdims=True)
        inv = lax.rsqrt(jnp.mean(centred * centred, axis=-1, keepdims=True) + 1e-06)
        unit = centred * inv
        a2 = (unit * vector(3) + vector(4)).astype(bf16)
        self.a2s[at, :] = a2
        dy = self.dy_ref[start // x.shape[0]]
        y = x2 + vector(5)
        da2 = None
        for t in range(self.tiles):
            ft = slice(t * width, (t + 1) * width)
            wt = slice(width + t * width, width + (t + 1) * width)
            u = mm(a2, woi_ref[:, wt]) + rows_ref[0:1, 6 * width + t * width:6 * width + (t + 1) * width]
            uu = u * u
            th = jnp.tanh(u * (c1 + c2 * uu))
            p = 0.5 + 0.5 * th
            g = (u * p).astype(bf16)
            slope = p + u * (0.5 - 0.5 * th * th) * (c1 + 3.0 * c2 * uu)
            self.gs[at, ft] = g
            y = y + mm(g, wu_ref[ft, :])
            du = (mm_nt(dy, wu_ref[ft, :]) * slope).astype(bf16)
            self.dus[at, ft] = du
            add_sum(6 + t, fold(du))
            d = mm_nt(du, woi_ref[:, wt])
            da2 = d if da2 is None else da2 + d
        y_ref[...] = y.astype(bf16)
        dyf = fold(dy)
        dn = da2 * vector(3)
        m1 = jnp.mean(dn, axis=-1, keepdims=True)
        m2 = jnp.mean(dn * unit, axis=-1, keepdims=True)
        dx2 = dyf + (dn - m1 - unit * m2) * inv
        dxl = dx2.astype(bf16)
        self.dx2_ref[at, :] = dx2
        self.dxl_ref[at, :] = dxl
        add_sum(2, fold(dxl))
        add_sum(3, da2 * unit)
        add_sum(4, da2)
        add_sum(5, dyf)

    def gradients(self, F):
        width, hidden, tiles, gb_ref = self.width, self.hidden, self.tiles, self.gb_ref
        r, ru = width // F, hidden // F
        nb = T // ru
        dy = self.dy_ref[...].reshape(2 * self.rows, width)

        def outer(t, c):
            val = mm_tn(self.gs[:, pl.ds(pl.multiple_of(t * T, T), T)], dy).astype(bf16)
            self.ga_ref[pl.ds(t * nb, nb)] = val.reshape(nb, ru, width)
            return c

        lax.fori_loop(0, hidden // T, outer, 0)
        a2T = self.a2s[...].T
        for t in range(tiles):
            val = mm(a2T, self.dus[:, t * width:(t + 1) * width]).astype(bf16)
            gb_ref[:, t * r:(t + 1) * r, :] = val.reshape(F, r, width)
        val = mm(self.oF_ref[...], self.dxl_ref[...]).astype(bf16)
        gb_ref[:, tiles * r:(tiles + 1) * r, :] = val.reshape(F, r, width)


def slope_parts(head, head_count, length):
    x = np.float32(2.0 ** (2.0 - 4.0 * head / head_count) / length)
    out = []
    for _ in range(3):
        low = np.float32(ml_dtypes.bfloat16(x))
        out.append(float(low))
        x = np.float32(x - low)
    return out


def remote(src, dst, send_sem, recv_sem, target):
    return pltpu.make_async_remote_copy(
        src_ref=src, dst_ref=dst, send_sem=send_sem, recv_sem=recv_sem,
        device_id={"fsdp": target}, device_id_type=pl.DeviceIdType.MESH)


def where_am_i(F):
    f = lax.axis_index("fsdp")
    place = lax.rem(f + 2, F)
    part = lax.rem(place, 4)
    half = part // 2
    core = lax.rem(f, 2)
    base = place - part
    partner = lax.rem(base + lax.rem(part + 2, 4) + F - 2, F)
    sibling = f + 1 - 2 * core
    return f, part, half, core, partner, sibling


def greet(F, f, core, sibling):
    barrier = pltpu.get_barrier_semaphore()
    for d in range(1, F // 2):
        pl.semaphore_signal(barrier, inc=1, device_id={"fsdp": lax.rem(f + 2 * d, F)},
                            device_id_type=pl.DeviceIdType.MESH)
    pl.semaphore_signal(barrier, inc=1, device_id={"fsdp": sibling}, device_id_type=pl.DeviceIdType.MESH)
    pl.semaphore_wait(barrier, F // 2)


def first_kernel(F, n, parents_ref, tok_ref, cot_ref, wq_ref, wk_ref, wv_ref, wo_ref, wi_ref, wu_ref, vec_ref,
                 a1T_out, kaug_out, v_out, kT_out, qn_out, qT_out, oT_out, lse_out, wc_out, wo_out, xs_out, dxl_out,
                 dx2_out, ga_out, gb_out, y_out, vin_ref, rows_ref,
                 xt_ref, a1T_ref, kaug_ref, v_ref, kT_ref, qn_ref, qT_ref, oT_ref, lse_ref, oF_ref, dy_ref,
                 wqkv_ref, woi_ref, wuf_ref, wc, dxl_ref, dx2_ref, ga_ref, gb_ref, a2s, gs, dus,
                 vecs, vT_scr, s_scr, tsend, trecv, gsend, grecv, osem):
    f, part, half, core, partner, sibling = where_am_i(F)
    rows, width = tok_ref.shape[1:]
    seg = rows // 5
    heads = H // 2
    hw = heads * 64
    tree = 4 * rows
    r = wq_ref.shape[0]
    ru = wu_ref.shape[0]
    part1 = part + 1 - 2 * core
    part2 = lax.rem(part + 2, 4)
    part3 = lax.rem(part1 + 2, 4)

    own = pl.ds(pl.multiple_of(f * r, r), r)
    ownu = pl.ds(pl.multiple_of(f * ru, ru), ru)
    vecs[f] = vec_ref[...]
    wqkv_ref[own, 0:width] = wq_ref[...].astype(bf16)
    wqkv_ref[own, width:2 * width] = wk_ref[...].astype(bf16)
    wqkv_ref[own, 2 * width:3 * width] = wv_ref[...].astype(bf16)

    greet(F, f, core, sibling)

    def slot(g, src):
        if g == 0:
            return vecs.at[src]
        if g == 3:
            return wuf_ref.at[pl.ds(pl.multiple_of(src * ru, ru), ru)]
        ref = wqkv_ref if g == 1 else woi_ref
        return ref.at[pl.ds(pl.multiple_of(src * r, r), r)]

    def direct(g, d):
        return remote(slot(g, f), slot(g, f), gsend.at[g, d], grecv.at[g, d],
                      sibling if d == 0 else lax.rem(f + 2 * d, F))

    def came(g, d):
        src = sibling if d == 0 else lax.rem(f + F - 2 * d, F)
        remote(slot(g, src), slot(g, src), gsend.at[g, d], grecv.at[g, d], sibling).wait_recv()

    def forward(g, d):
        src = lax.rem(f + F - 2 * d, F)
        return remote(slot(g, src), slot(g, src), gsend.at[g, F // 2 + d], grecv.at[g, F // 2 + d], sibling)

    def forwarded(g, d):
        src = lax.rem(sibling + F - 2 * d, F)
        remote(slot(g, src), slot(g, src), gsend.at[g, F // 2 + d], grecv.at[g, F // 2 + d], sibling).wait_recv()

    chips = range(1, F // 2)

    def send_all(g):
        for d in range(F // 2):
            direct(g, d).start()

    def pass_on(g):
        for d in chips:
            came(g, d)
            forward(g, d).start()

    def receive_rest(g):
        came(g, 0)
        for d in chips:
            forwarded(g, d)

    x_out = remote(tok_ref.at[1 - half], xt_ref.at[part], tsend.at[0], trecv.at[0], partner)
    x_sib = remote(tok_ref.at[half], xt_ref.at[part], tsend.at[1], trecv.at[1], sibling)
    x_fwd = remote(xt_ref.at[part2], xt_ref.at[part2], tsend.at[2], trecv.at[2], sibling)
    dy_out = remote(cot_ref.at[1 - half], dy_ref.at[half], tsend.at[3], trecv.at[3], partner)
    x_own = pltpu.make_async_copy(tok_ref.at[half], xt_ref.at[part], osem.at[20])
    dy_own = pltpu.make_async_copy(cot_ref.at[half], dy_ref.at[half], tsend.at[4])

    send_all(0)
    send_all(1)
    x_out.start()
    x_sib.start()
    x_own.start()
    dy_own.start()
    woi_ref[own, 0:width] = wo_ref[...].astype(bf16)
    woi_ref[own, width:] = wi_ref[...].astype(bf16)
    wuf_ref[ownu, :] = wu_ref[...].astype(bf16)
    pass_on(0)
    pass_on(1)
    receive_rest(0)

    table = jnp.max(vecs[...], axis=1).astype(bf16)
    words = table.shape[1]

    def vector_row(first, m, length):
        col = iota((words, length), 1)
        pick = iota((words, length), 0) == first + (col & (m - 1))
        spread = mm(table, pick.astype(bf16))
        shift = m.bit_length() - 1
        mine = iota((F, length), 0) == (iota((F, length), 1) >> shift)
        return jnp.sum(jnp.where(mine, spread, 0.0), axis=0, keepdims=True)

    def all_rows(first, last):
        for i in range(first, last):
            rows_ref[:, i * width:(i + 1) * width] = jnp.broadcast_to(vector_row(i * n, n, width), (8, width))

    all_rows(0, 2)
    hidden = rows_ref.shape[1] - 6 * width
    receive_rest(1)

    lane = iota((seg, 128), 1)
    offs = iota((seg, 128), 0)
    arow = iota((64, rows), 0)

    def project(p):
        x = xt_ref[p].astype(f32)
        gain = rows_ref[0:1, 0:width]
        shift = rows_ref[0:1, width:2 * width]
        mean = jnp.mean(x, axis=-1, keepdims=True)
        x = x - mean
        inv = lax.rsqrt(jnp.mean(x * x, axis=-1, keepdims=True) + 1e-06)
        a1 = (x * inv * gain + shift).astype(bf16)

        def proj(i):
            return mm(a1, wqkv_ref[:, pl.ds(pl.multiple_of(i * width + core * hw, hw), hw)])

        cols = pl.ds(pl.multiple_of(p * rows, rows), rows)
        a1T_ref[:, cols] = a1.T
        q = (proj(0) * 0.125).astype(bf16)
        qn_ref[cols, :] = q
        qT = q.T
        k = proj(1).astype(bf16)
        kT_ref[:, cols] = k.T
        v = proj(2).astype(bf16)
        v_ref[pl.ds(p * 5, 5)] = v.reshape(5, seg, hw)
        vT = v.T
        for h in range(heads):
            a, b = slope_parts(h, H, tree), slope_parts(heads + h, H, tree)
            aug = jnp.zeros((64, rows), f32)
            for j in range(3):
                s = jnp.where(core == 0, a[j], b[j])
                aug = jnp.where((arow == j) | (arow == j + 3), s, aug)
            aug = aug.astype(bf16)
            lo, hi = 128 * h + 64 * (h % 2), 128 * h + 64 - 64 * (h % 2)
            qT_ref[lo:lo + 64, cols] = qT[64 * h:64 * h + 64]
            qT_ref[hi:hi + 64, cols] = aug
            vT_scr[80 * h:80 * h + 64, cols] = vT[64 * h:64 * h + 64]
            vT_scr[80 * h + 64:80 * h + 80, cols] = jnp.ones((16, rows), bf16)
        for b in range(5):
            blk = p * 5 + b
            start = jnp.where(blk < 8, blk * seg, jnp.where(blk < 12, 8 * seg, 9 * seg))
            spot = offs + start
            hi = (spot & -8).astype(f32)
            lo = (spot & 7).astype(f32)
            for h in range(heads):
                at = 64 - 64 * (h % 2)
                l = lane - at
                aug = jnp.where((l >= 0) & (l < 3), hi, jnp.where((l >= 3) & (l < 6), lo, 0.0)).astype(bf16)
                keep = (lane < 64) if h % 2 == 0 else (lane >= 64)
                kk = k[b * seg:(b + 1) * seg, 128 * (h // 2):128 * (h // 2) + 128]
                kaug_ref[blk, :, 128 * h:128 * h + 128] = jnp.where(keep, kk, aug)

    x_own.wait()
    x_sib.wait_recv()

    def visit(i, c):
        @pl.when(i == 1)
        def _():
            all_rows(2, 6)
            rows_ref[:, 6 * width:] = jnp.broadcast_to(vector_row(6 * n, hidden // F, hidden), (8, hidden))
            x_out.wait_recv()
            x_fwd.start()
            send_all(2)
            send_all(3)

        @pl.when(i == 3)
        def _():
            x_fwd.wait_recv()

        project(jnp.where(i == 0, part, jnp.where(i == 1, part1, jnp.where(i == 2, part2, part3))))
        return c

    lax.fori_loop(0, 4, visit, 0)
    for i in range(heads // 2):
        for k in range(3):
            src = pl.ds(pl.multiple_of(k * width + core * hw + 128 * i, 128), 128)
            wc[:, 384 * i + 128 * k:384 * i + 128 * k + 128] = wqkv_ref[:, src]

    outs = [(a1T_ref, a1T_out), (kaug_ref, kaug_out), (v_ref, v_out), (kT_ref, kT_out), (qn_ref, qn_out),
            (qT_ref, qT_out), (wc, wc_out), (xt_ref.at[core], xs_out.at[0]), (xt_ref.at[core + 2], xs_out.at[1]),
            (oT_ref, oT_out), (lse_ref, lse_out),
            (woi_ref.at[pl.ds(pl.multiple_of(core * hw, hw), hw), 0:width], wo_out),
            (dxl_ref.at[0:rows], dxl_out.at[0]), (dxl_ref.at[rows:2 * rows], dxl_out.at[1]),
            (dx2_ref.at[0:rows], dx2_out.at[0]), (dx2_ref.at[rows:2 * rows], dx2_out.at[1]), (ga_ref, ga_out), (gb_ref, gb_out)]
    copies = [pltpu.make_async_copy(a, b, osem.at[i]) for i, (a, b) in enumerate(outs)]
    for c in copies[:9]:
        c.start()

    s_refs = [dx2_ref.at[0:8 * seg, 0:T], dx2_ref.at[0:8 * seg, T:2 * T], s_scr.at[0], s_scr.at[1]]

    def hook(stage, i=None):
        if stage == 1:
            dy_out.start()
        if stage == 3:
            @pl.when(i == 4)
            def _():
                pass_on(2)

    attend(heads, seg, parents_ref, kaug_ref, qT_ref, vT_scr, oT_ref, lse_ref, s_refs, hook)

    other = 1 - core
    sent = []
    for i in range(2):
        cols = pl.ds(pl.multiple_of((other + 2 * i) * rows, rows), rows)
        at = (pl.ds(pl.multiple_of(core * hw, hw), hw), slice(i * rows, (i + 1) * rows))
        c = remote(oT_ref.at[:, cols], oF_ref.at[at], tsend.at[5 + i], trecv.at[5 + i], sibling)
        c.start()
        sent.append(c)
    for i in range(2):
        mine = pl.ds(pl.multiple_of((core + 2 * i) * rows, rows), rows)
        at = (pl.ds(pl.multiple_of(core * hw, hw), hw), slice(i * rows, (i + 1) * rows))
        oF_ref[at] = oT_ref[:, mine]
    copies[9].start()
    copies[10].start()
    receive_rest(2)
    copies[11].start()
    pass_on(3)
    for c in sent:
        c.wait_recv()
    receive_rest(3)
    dy_own.wait()

    vin_ref[...] = jnp.zeros_like(vin_ref)
    dense = Dense(rows, width, oF_ref, dy_ref, woi_ref, wuf_ref, rows_ref, dxl_ref, dx2_ref, ga_ref, gb_ref, vin_ref,
                  a2s, gs, dus)
    keep_y = [pltpu.make_async_copy(xt_ref.at[other + 2 * i], y_out.at[i], osem.at[18 + i]) for i in range(2)]

    def dense_step(s, c):
        i = jnp.where(s == 0, half, 1 - half)

        @pl.when(s == 1)
        def _():
            dy_out.wait_recv()

        dense.chunk(i * rows, xt_ref[core + 2 * i], xt_ref.at[other + 2 * i])
        return c

    lax.fori_loop(0, 2, dense_step, 0)
    for c in keep_y + copies[12:16]:
        c.start()
    dense.gradients(F)
    copies[16].start()
    copies[17].start()
    for c in copies + keep_y:
        c.wait()
    dy_out.wait_send()
    x_out.wait_send()
    x_sib.wait_send()
    x_fwd.wait_send()
    for c in sent:
        c.wait_send()
    for g in range(4):
        for d in range(F // 2):
            direct(g, d).wait_send()
        for d in chips:
            forward(g, d).wait_send()


def first(F, parents, tokens, cotangent, weights, vec, n):
    _, rows, width = tokens.shape
    tree = 4 * rows
    heads = H // 2
    hw = heads * 64
    seg = rows // 5
    hidden = weights[4].shape[1]
    r, ru = width // F, hidden // F
    R1 = (hidden // width + 1) * r
    two = 2 * rows
    keep = [((width, tree), bf16), ((20, seg, heads * 128), bf16), ((20, seg, hw), bf16), ((hw, tree), bf16),
            ((tree, hw), bf16), ((heads * 128, tree), bf16), ((hw, tree), bf16), ((heads * 8, tree), f32)]
    out = keep + [((width, 3 * hw), bf16), ((hw, width), bf16), ((2, rows, width), bf16), ((2, rows, width), bf16),
                  ((2, rows, width), f32), ((F, ru, width), bf16), ((F, R1, width), bf16), ((2, rows, width), bf16),
                  ((16, width), f32), ((8, 6 * width + hidden), f32)]
    scratch = [((4, rows, width), bf16)] + keep + [
        ((2 * hw, two), bf16), ((2, rows, width), bf16), ((width, 3 * width), bf16), ((width, width + hidden), bf16),
        ((hidden, width), bf16), ((width, 3 * hw), bf16), ((two, width), bf16),
        ((two, width), f32), ((F, ru, width), bf16), ((F, R1, width), bf16), ((two, width), bf16), ((two, hidden), bf16),
        ((two, hidden), bf16), ((F,) + vec.shape, f32), ((heads * 80, tree), bf16), ((2, 8 * seg, T), f32)]
    ANY = pl.BlockSpec(memory_space=pl.ANY)
    dma = pltpu.SemaphoreType.DMA
    return pl.pallas_call(
        functools.partial(first_kernel, F, n),
        out_shape=[jax.ShapeDtypeStruct(s, d) for s, d in out],
        in_specs=[SM, ANY, ANY] + [VM] * 7,
        out_specs=[ANY] * 16 + [VM] * 2,
        scratch_shapes=[pltpu.VMEM(s, d) for s, d in scratch] + [
            dma((7,)), dma((7,)), dma((4, F)), dma((4, F)), dma((21,))],
        name="front",
        compiler_params=pltpu.CompilerParams(vmem_limit_bytes=64 << 20, collective_id=0, has_side_effects=True),
    )(parents, tokens, cotangent, *weights, vec)


def fold(x):
    return x.astype(f32)


class Chain:
    def __init__(self, F, f, sums, got, block, zgot, final, send, recv, stages=2):
        self.square = F == 8 and stages == 2
        self.F, self.f, self.sums, self.got, self.block = F, f, sums, got, block
        self.zgot, self.final, self.send, self.recv = zgot, final, send, recv
        self.chip = f // 2
        self.chips = F // 2
        self.planes = lax.axis_size("dp")
        self.plane = lax.axis_index("dp")
        self.rows = sums.shape[1]
        self.zrows = block.shape[0] // self.planes

    def _b(self, d):
        return remote(self.sums.at[lax.rem(self.chip + d, self.chips)], self.got.at[d - 1],
                      self.send.at[d], self.recv.at[d], lax.rem(self.f + 2 * d, self.F))

    def _square(self):
        core = lax.rem(self.f, 2)
        x, y = lax.rem(self.chip, 2), self.chip // 2
        along_x, along_y = 2 * y + 1 - x, 2 * (1 - y) + x
        first = jnp.where(core == 0, along_x, along_y)
        second = jnp.where(core == 0, along_y, along_x)
        last = 2 * (1 - y) + 1 - x
        one = [remote(self.sums.at[first], self.got.at[0], self.send.at[1], self.recv.at[1], 2 * first + core),
               remote(self.sums.at[last], self.got.at[1], self.send.at[2], self.recv.at[2], 2 * first + core)]
        two = remote(self.sums.at[second], self.got.at[2], self.send.at[3], self.recv.at[3], 2 * second + core)
        return one, two, second

    def _chunk(self, z):
        return pl.ds(pl.multiple_of(z * self.zrows, 16), self.zrows)

    def _c(self, e):
        z = lax.rem(self.plane + e, self.planes)
        i = self.chips + e
        return pltpu.make_async_remote_copy(
            src_ref=self.block.at[self._chunk(z)], dst_ref=self.zgot.at[e - 1],
            send_sem=self.send.at[i], recv_sem=self.recv.at[i],
            device_id={"dp": z}, device_id_type=pl.DeviceIdType.MESH)

    def _d(self, e, src=None):
        z = lax.rem(self.plane + e, self.planes)
        i = self.chips + self.planes + e
        here = self._chunk(self.plane if src is None else src)
        return pltpu.make_async_remote_copy(
            src_ref=self.final.at[here], dst_ref=self.final.at[here],
            send_sem=self.send.at[i], recv_sem=self.recv.at[i],
            device_id={"dp": z}, device_id_type=pl.DeviceIdType.MESH)

    def start_plane(self):
        if self.square:
            for c in self._square()[0]:
                c.start()
            return
        for d in range(1, self.chips):
            self._b(d).start()

    def mid_plane(self):
        if self.square:
            one, two, second = self._square()
            for c in one:
                c.wait_recv()
            self.sums[second] = (fold(self.sums[second]) + fold(self.got[1])).astype(bf16)
            two.start()

    def start_z(self):
        if self.square:
            self._square()[1].wait_recv()
            total = fold(self.sums[self.chip]) + fold(self.got[0]) + fold(self.got[2])
        else:
            for d in range(1, self.chips):
                self._b(d).wait_recv()
            total = fold(self.sums[self.chip])
            for d in range(1, self.chips):
                total = total + fold(self.got[d - 1])
        self.block[0:self.rows] = total.astype(bf16)
        for e in range(1, self.planes):
            self._c(e).start()

    def start_back(self):
        for e in range(1, self.planes):
            self._c(e).wait_recv()
        here = self._chunk(self.plane)
        total = fold(self.block[here])
        for e in range(1, self.planes):
            total = total + fold(self.zgot[e - 1])
        self.final[here] = total.astype(bf16)
        for e in range(1, self.planes):
            self._d(e).start()

    def receive(self):
        for e in range(1, self.planes):
            self._d(e, lax.rem(self.plane + self.planes - e, self.planes)).wait_recv()

    def close(self):
        if self.square:
            one, two, _ = self._square()
            for c in one + [two]:
                c.wait_send()
        else:
            for d in range(1, self.chips):
                self._b(d).wait_send()
        for e in range(1, self.planes):
            self._c(e).wait_send()
            self._d(e).wait_send()


def last_kernel(F, parents_ref, kaug_h, v_h, qT_h, kT_h, qn_h, oT_h, lse_h, a1T_h, wc_h, wo_h, xs_h, dxl_ref, dx2_h, y_h,
                ga_ref, gb_ref, vin_ref, n1_ref,
                gt_ref, lo_ref, gq_ref, fina, finb, vout_ref,
                kaug_ref, v_ref, qT_ref, kT_ref, qn_ref, oT_ref, lse_ref, a1T_ref, wc, wo_scr, xs, dx2s, ys,
                dxs, doT, do, dqT, dqkv, accK, accV, das, dar,
                suma, sumb, gota, gotb, planea, planeb, blka, blkb, za, zb, sum2, got2, blk2, z2, fin2,
                vs, vgot, dxo, tsend, trecv, senda, recva, sendb, recvb, send2, recv2, vsend, vrecv, lsem):
    f, part, half, core, partner, sibling = where_am_i(F)
    planes = lax.axis_size("dp")
    plane = lax.axis_index("dp")
    heads = H // 2
    hw = heads * 64
    _, rows, width = dxl_ref.shape
    chips = F // 2
    other = 1 - core
    tree = 4 * rows
    seg = rows // 5

    pairs = [(wo_h, wo_scr), (qT_h, qT_ref), (kaug_h, kaug_ref), (v_h, v_ref), (kT_h, kT_ref), (qn_h, qn_ref),
             (oT_h, oT_ref), (lse_h, lse_ref), (ga_ref.at[:, core], suma), (gb_ref.at[:, core], sumb), (a1T_h, a1T_ref), (wc_h, wc), (xs_h, xs),
             (dx2_h, dx2s), (y_h, ys)]
    loads = [pltpu.make_async_copy(a, b, lsem.at[i]) for i, (a, b) in enumerate(pairs)]
    for c in loads:
        c.start()

    barrier = pltpu.get_barrier_semaphore()
    for d in range(1, chips):
        pl.semaphore_signal(barrier, inc=1, device_id={"fsdp": lax.rem(f + 2 * d, F)},
                            device_id_type=pl.DeviceIdType.MESH)
    for e in range(1, planes):
        pl.semaphore_signal(barrier, inc=1, device_id={"dp": lax.rem(plane + e, planes)},
                            device_id_type=pl.DeviceIdType.MESH)
    pl.semaphore_signal(barrier, inc=1, device_id={"fsdp": sibling}, device_id_type=pl.DeviceIdType.MESH)
    pl.semaphore_wait(barrier, chips + planes - 1)

    dx_sw = remote(dxl_ref, dxs, tsend.at[0], trecv.at[0], sibling)
    out_a = remote(ga_ref.at[:, other], gota, tsend.at[1], trecv.at[1], sibling)
    out_b = remote(gb_ref.at[:, other], gotb, tsend.at[7], trecv.at[7], sibling)
    y_out = remote(ys.at[1 - half], lo_ref.at[half], tsend.at[8], trecv.at[8], partner)
    keep_y = pltpu.make_async_copy(ys.at[half], lo_ref.at[half], lsem.at[16])
    dx_sw.start()
    out_a.start()
    out_b.start()

    def make_do(p, x):
        cols = pl.ds(pl.multiple_of(p * rows, rows), rows)
        d = mm_nt(x, wo_scr[...]).astype(bf16)
        do[cols, :] = d
        doT[:, cols] = d.T

    loads[0].wait()
    lax.fori_loop(0, 2, lambda i, c: (make_do(core + 2 * i, dxl_ref[i]), c)[1], 0)

    one_a = Chain(F, f, suma, planea, blka, za, fina, senda, recva)
    one_b = Chain(F, f, sumb, planeb, blkb, zb, finb, sendb, recvb)

    def add_sibling(load, arrived, mine, got):
        load.wait()
        arrived.wait_recv()

        def add_block(j, c):
            mine[j] = (fold(mine[j]) + fold(got[j])).astype(bf16)
            return c

        lax.fori_loop(0, chips, add_block, 0)

    dx_sw.wait_recv()
    lax.fori_loop(0, 2, lambda i, c: (make_do(other + 2 * i, dxs[i]), c)[1], 0)
    add_sibling(loads[8], out_a, suma, gota)
    one_a.start_plane()
    for c in loads[1:8]:
        c.wait()

    def chain(pr):
        return Chain(F, f, sum2.at[pr], got2.at[pr], blk2.at[pr], z2.at[pr], fin2.at[pr], send2.at[pr], recv2.at[pr], 1)

    two = [chain(0), chain(1)]
    r = width // F
    r2 = 2 * r

    def hook(name, pr, i=None):
        if name == "mid":
            @pl.when(pr == 0)
            def _():
                add_sibling(loads[9], out_b, sumb, gotb)
                one_b.start_plane()

            @pl.when(pr == 1)
            def _():
                one_b.start_z()
                loads[14].wait()
                y_out.start()
                keep_y.start()
        if name == "late":
            @pl.when(pr == 0)
            def _():
                one_a.mid_plane()

            @pl.when(pr == 1)
            def _():
                one_a.start_back()
        if name == "leaf":
            @pl.when((pr == 0) & (i == 5))
            def _():
                one_a.start_z()
                one_b.mid_plane()

            @pl.when((pr == 1) & (i == 4))
            def _():
                one_b.start_back()
                two[0].start_z()
        if name == "end":
            @pl.when(pr == 0)
            def _():
                for c in loads[10:14]:
                    c.wait()

            @pl.when(pr == 1)
            def _():
                two[0].start_back()

            g = mm(a1T_ref[...], dqkv[:, :, pl.ds(pl.multiple_of(pr * 384, 384), 384)].reshape(tree, 384)).astype(bf16)
            for j in range(chips):
                sum2[pr, j] = g[j * r2:(j + 1) * r2]
            chain(pr).start_plane()

    attend_back(heads, seg, parents_ref, kaug_ref, v_ref, qT_ref, doT, kT_ref, do, qn_ref, oT_ref, lse_ref,
                dqT, dqkv, accK, accV, hook)

    def da1_of(p):
        return mm_nt(dqkv[pl.ds(p * 5, 5)].reshape(rows, 3 * hw), wc[...])

    def da_out(s):
        i = (1 - half) if s == 0 else half
        return remote(das.at[i], dar.at[i], tsend.at[2 + s], trecv.at[2 + s], sibling)

    dx_out = remote(dxo.at[1 - half], gt_ref.at[half], tsend.at[4], trecv.at[4], partner)
    keep_dx = pltpu.make_async_copy(dxo.at[half], gt_ref.at[half], lsem.at[15])
    vs[0] = vin_ref[...]
    row = iota((16, width), 0)

    def finish_rows(s, c):
        i = jnp.where(s == 0, 1 - half, half)
        das[i] = da1_of(other + 2 * i).astype(bf16)
        for k in range(2):
            @pl.when(s == k)
            def _():
                da_out(k).start()
        x = fold(xs[i])
        x = x - jnp.mean(x, axis=-1, keepdims=True)
        inv = lax.rsqrt(jnp.mean(x * x, axis=-1, keepdims=True) + 1e-06)
        unit = x * inv
        da = da1_of(core + 2 * i)
        for k in range(2):
            @pl.when(s == k)
            def _():
                da_out(k).wait_recv()
        da = da + fold(dar[i])
        dn = da * n1_ref[0:1, 0:width]
        m1 = jnp.mean(dn, axis=-1, keepdims=True)
        m2 = jnp.mean(dn * unit, axis=-1, keepdims=True)
        dxo[i] = (dx2s[i] + (dn - m1 - unit * m2) * inv).astype(bf16)
        gs = jnp.sum(da * unit, axis=0, keepdims=True)
        bs = jnp.sum(da, axis=0, keepdims=True)
        vs[0] += jnp.where(row == 0, gs, 0.0) + jnp.where(row == 1, bs, 0.0)

        @pl.when(s == 0)
        def _():
            dx_out.start()

        @pl.when(s == 1)
        def _():
            keep_dx.start()

        return c

    lax.fori_loop(0, 2, finish_rows, 0)
    v_sib = remote(vs.at[0], vgot.at[0], vsend.at[0], vrecv.at[0], sibling)
    v_sib.start()
    two[1].start_z()
    v_sib.wait_recv()
    vgot[chips + plane] = vs[0] + vgot[0]

    def v_z(e, sender):
        return pltpu.make_async_remote_copy(
            src_ref=vgot.at[chips + sender], dst_ref=vgot.at[chips + sender],
            send_sem=vsend.at[chips + e], recv_sem=vrecv.at[chips + e],
            device_id={"dp": lax.rem(plane + e, planes)}, device_id_type=pl.DeviceIdType.MESH)

    for e in range(1, planes):
        v_z(e, plane).start()
    for e in range(1, planes):
        v_z(e, lax.rem(plane + planes - e, planes)).wait_recv()
    total = vgot[chips]
    for z in range(1, planes):
        total = total + vgot[chips + z]
    vs[1] = total
    v_chip = [remote(vs.at[1], vgot.at[d], vsend.at[d], vrecv.at[d], lax.rem(f + 2 * d, F)) for d in range(1, chips)]
    for c in v_chip:
        c.start()
    two[1].start_back()
    one_a.receive()
    one_b.receive()
    s_out = []
    for pr in range(2):
        two[pr].receive()
        c = remote(fin2.at[pr, pl.ds(pl.multiple_of(other * r, r), r)], gq_ref.at[core, pr],
                   tsend.at[5 + pr], trecv.at[5 + pr], sibling)
        c.start()
        gq_ref[core, pr] = fin2[pr, pl.ds(pl.multiple_of(core * r, r), r), :]
        s_out.append(c)
    for c in v_chip:
        c.wait_recv()
    total = vs[1]
    for d in range(1, chips):
        total = total + vgot[d]
    vout_ref[...] = total
    for c in s_out:
        c.wait()
    dx_out.wait()
    keep_dx.wait()
    keep_y.wait()
    y_out.wait()
    one_a.close()
    one_b.close()
    for c in two:
        c.close()
    for c in [dx_sw, out_a, out_b, v_sib, da_out(0), da_out(1)] + v_chip:
        c.wait_send()
    for e in range(1, planes):
        v_z(e, plane).wait_send()


def last(F, DP, parents, kept, wc, wo, xs, dxl, dx2, y, ga, gb, vin, rows_vec):
    a1T, kaug, v, kT, qn, qT, oT, lse = kept
    _, rows, width = dxl.shape
    heads = H // 2
    hw = heads * 64
    tree = 4 * rows
    seg = rows // 5
    chips = F // 2
    r = width // F
    RA, RB = ga.shape[2], gb.shape[2]
    r2 = 2 * r

    def zrows(n):
        return -(-n // (16 * DP)) * 16

    ZA, ZB, Z2 = zrows(RA), zrows(RB), zrows(r2)
    ANY = pl.BlockSpec(memory_space=pl.ANY)
    dma = pltpu.SemaphoreType.DMA
    out = [((2, rows, width), bf16), ((2, rows, width), bf16), ((2, 2, r, 384), bf16), ((ZA * DP, width), bf16),
           ((ZB * DP, width), bf16), ((16, width), f32)]
    big = [kaug, v, qT, kT, qn, oT, lse, a1T, wc, wo, xs]
    scratch = [(a.shape, a.dtype) for a in big] + [
        ((2, rows, width), f32), ((2, rows, width), bf16),
        ((2, rows, width), bf16), ((hw, tree), bf16), ((tree, hw), bf16), ((128, tree), bf16),
        ((20, seg, 3 * hw), bf16), ((20, seg, 128), f32), ((20, seg, 128), f32),
        ((2, rows, width), bf16), ((2, rows, width), bf16),
        ((chips, RA, width), bf16), ((chips, RB, width), bf16), ((chips, RA, width), bf16), ((chips, RB, width), bf16),
        ((chips - 1, RA, width), bf16), ((chips - 1, RB, width), bf16), ((ZA * DP, width), bf16),
        ((ZB * DP, width), bf16), ((DP - 1, ZA, width), bf16), ((DP - 1, ZB, width), bf16),
        ((2, chips, r2, 384), bf16), ((2, chips - 1, r2, 384), bf16), ((2, Z2 * DP, 384), bf16),
        ((2, DP - 1, Z2, 384), bf16), ((2, Z2 * DP, 384), bf16),
        ((2, 16, width), f32), ((chips + DP, 16, width), f32), ((2, rows, width), bf16),
    ]
    nsem = chips + 2 * DP
    return pl.pallas_call(
        functools.partial(last_kernel, F),
        out_shape=[jax.ShapeDtypeStruct(s, d) for s, d in out],
        in_specs=[SM] + [ANY] * 11 + [VM, ANY, ANY, ANY, ANY, VM, VM],
        out_specs=[ANY, ANY] + [VM] * 4,
        scratch_shapes=[pltpu.VMEM(s, d) for s, d in scratch] + [
            dma((9,)), dma((9,)), dma((nsem,)), dma((nsem,)), dma((nsem,)), dma((nsem,)), dma((2, nsem)), dma((2, nsem)),
            dma((chips + DP,)), dma((chips + DP,)), dma((17,))],
        name="back",
        compiler_params=pltpu.CompilerParams(vmem_limit_bytes=64 << 20, collective_id=1, has_side_effects=True),
    )(parents, *big, dxl, dx2, y, ga, gb, vin, rows_vec)


def finish_kernel(lo_in, gt_in, fina, finb, gq, lo_ref, gt_ref, gwq_ref, gwk_ref, gwv_ref, gwo_ref, gwi_ref, gwu_ref):
    lo_ref[...] = lo_in[...]
    gt_ref[...] = gt_in[...]
    r, width = gwo_ref.shape
    ru = gwu_ref.shape[0]
    gwu_ref[...] = fold(fina[0:ru])
    pieces = gwi_ref.shape[1] // width
    for c in range(pieces):
        gwi_ref[:, c * width:(c + 1) * width] = fold(finb[c * r:(c + 1) * r])
    gwo_ref[...] = fold(finb[pieces * r:(pieces + 1) * r])
    for k, ref in enumerate((gwq_ref, gwk_ref, gwv_ref)):
        for c in range(2):
            for pr in range(2):
                at = (2 * c + pr) * 128
                ref[:, at:at + 128] = fold(gq[c, pr, :, 128 * k:128 * k + 128])


def finish(F, lo, gt, fina, finb, gq, hidden):
    width = lo.shape[2]
    r, ru = width // F, hidden // F
    shapes = [(r, width)] * 4 + [(r, hidden), (ru, width)]
    return pl.pallas_call(
        finish_kernel,
        out_shape=[jax.ShapeDtypeStruct(lo.shape, bf16), jax.ShapeDtypeStruct(gt.shape, bf16)]
        + [jax.ShapeDtypeStruct(s, f32) for s in shapes],
        in_specs=[VM] * 5,
        out_specs=[VM] * 8,
        name="finish",
    )(lo, gt, fina, finb, gq)


def on_device(tokens, parents, n1g, n1b, wq, wk, wv, wo, ob, n2g, n2b, wi, ib, wu, ub, cotangent):
    F = lax.axis_size("fsdp")
    fi = lax.axis_index("fsdp")
    place = (fi + 2) % F
    half = (place % 4) // 2
    quad = lax.axis_index("dp") * (F // 4) + place // 4
    parent_row = parents[quad, half]
    _, _, rows, width = tokens.shape

    n = n1g.shape[0]
    vec = jnp.concatenate([n1g, n1b, ob, n2g, n2b, ub, ib])
    vec = lax.reduce_precision(vec, 8, 7)
    vec = jnp.broadcast_to(jnp.pad(vec, (0, -vec.shape[0] % 128)), (8, vec.shape[0] + -vec.shape[0] % 128))
    hidden = wi.shape[1]
    ru = hidden // F
    (a1T, kaug, v, kT, qn, qT, oT, lse, wc, wo_own, xs, dxl, dx2, ga, gb, y, vin, vrows) = first(
        F, parent_row, tokens[0], cotangent[0], (wq, wk, wv, wo, wi, wu), vec, n)
    gt, lo, gq, fina, finb, vout = last(
        F, lax.axis_size("dp"), parent_row, (a1T, kaug, v, kT, qn, qT, oT, lse), wc, wo_own, xs, dxl, dx2, y,
        ga.reshape(F // 2, 2, -1, width), gb.reshape(F // 2, 2, -1, width), vin, vrows)
    lo, gt, gwq, gwk, gwv, gwo, gwi, gwu = finish(F, lo, gt, fina, finb, gq, hidden)
    sv = lax.dynamic_slice_in_dim(vout[:6], fi * n, n, 1)
    sib = lax.dynamic_slice_in_dim(vout[6:6 + hidden // width].reshape(-1), fi * ru, ru, 0)
    return (lo[None], gt[None], sv[0], sv[1], gwq, gwk, gwv, gwo, sv[2], sv[3], sv[4], gwi, sib, gwu, sv[5])


def solution(mesh):
    tok = P(("dp", "fsdp"), None, None, None)
    v, m = P("fsdp"), P("fsdp", None)
    return jax.shard_map(
        on_device,
        mesh=mesh,
        in_specs=(tok, P(), v, v, m, m, m, m, v, v, v, m, v, m, v, tok),
        out_specs=(tok, tok, v, v, m, m, m, m, v, v, v, m, v, m, v),
        check_vma=False,
    )
```

```python
import functools
import math

import jax
import jax.numpy as jnp
import ml_dtypes
import numpy as np
from jax import lax
from jax.experimental import pallas as pl
from jax.experimental.pallas import tpu as pltpu
from jax.sharding import PartitionSpec as P

H = 8
T = 256
f32, bf16 = jnp.float32, jnp.bfloat16
VM = pl.BlockSpec(memory_space=pltpu.VMEM)
SM = pl.BlockSpec(memory_space=pltpu.SMEM)


def mm(a, b):
    return jnp.dot(a, b, preferred_element_type=f32)


def mm_tn(a, b):
    return lax.dot_general(a, b, (((0,), (0,)), ((), ())), preferred_element_type=f32)


def mm_nt(a, b):
    return lax.dot_general(a, b, (((1,), (1,)), ((), ())), preferred_element_type=f32)


def iota(shape, dim):
    return lax.broadcasted_iota(jnp.int32, shape, dim)


def chosen(par, read):
    out = read(0)
    for b in range(1, 4):
        out = jnp.where(par == b + 1, read(b), out)
    return out


def attend(heads, seg, parents_ref, kaug_ref, qT_ref, vT_ref, oT_ref, lse_ref, s_refs, hook):
    ntr = 8 * seg // T
    vr = vT_ref.shape[0] // heads
    causal_t = iota((T, T), 0) <= iota((T, T), 1)
    causal_b = iota((seg, seg), 0) <= iota((seg, seg), 1)
    G = heads

    def group(g, _):
        hook(0)
        hs = [g * G + e for e in range(G)]
        hk = [pl.ds(pl.multiple_of(h * 128, 128), 128) for h in hs]
        hv = [pl.ds(pl.multiple_of(h * vr, vr), vr) for h in hs]

        def keys(e, blk, n):
            return kaug_ref[pl.ds(blk, n), :, hk[e]].reshape(n * seg, 128)

        def finish(e, cols, m, acc):
            h = hs[e]
            l = acc[64:65, :]
            oT_ref[pl.ds(pl.multiple_of(h * 64, 64), 64), cols] = (acc[:64] / l).astype(bf16)
            lse_ref[pl.ds(pl.multiple_of(h * 8, 8), 8), cols] = jnp.broadcast_to(m + jnp.log(l), (8, T))

        def full_scores(e, q, n):
            m = None
            for c in range(n):
                s = mm(keys(e, 2 * c, 2), q)
                s_refs[e][c * T:(c + 1) * T, :] = s
                cm = jnp.max(s, axis=0, keepdims=True)
                m = cm if m is None else jnp.maximum(m, cm)
            return m

        def full_mix(e, m, n, acc):
            for c in range(n):
                p = jnp.exp(s_refs[e][c * T:(c + 1) * T, :] - m).astype(bf16)
                t = mm(vT_ref[hv[e], c * T:(c + 1) * T], p)
                acc = t if acc is None else acc + t
            return acc

        for t in range(ntr):
            cols = slice(t * T, (t + 1) * T)
            sds, ms = [], []
            for e in range(G):
                q = qT_ref[hk[e], cols]
                sd = jnp.where(causal_t, mm(keys(e, 2 * t, 2), q), -1e30)
                m = jnp.max(sd, axis=0, keepdims=True)
                if t:
                    m = jnp.maximum(m, full_scores(e, q, t))
                sds.append(sd)
                ms.append(m)
            for e in range(G):
                acc = mm(vT_ref[hv[e], cols], jnp.exp(sds[e] - ms[e]).astype(bf16))
                acc = full_mix(e, ms[e], t, acc)
                finish(e, cols, ms[e], acc)

        def tail_tile(i, leaf):
            b0 = 8 + 2 * i
            cols = pl.ds(pl.multiple_of(b0 * seg, T), T)
            pars = [parents_ref[b0 + half - 7] for half in range(2)] if leaf else None
            exts, ms = [], []
            for e in range(G):
                q = qT_ref[hk[e], cols]
                m = full_scores(e, q, ntr)
                ext = []
                for x in range(2 if leaf else 1):
                    pieces = []
                    for half in range(2):
                        kk = keys(e, b0 + half, 1) if x == 0 else chosen(pars[half], lambda b: keys(e, 8 + b, 1))
                        s = mm(kk, q[:, half * seg:(half + 1) * seg])
                        if x == 0:
                            s = jnp.where(causal_b, s, -1e30)
                        pieces.append(s)
                    s = jnp.concatenate(pieces, axis=1)
                    m = jnp.maximum(m, jnp.max(s, axis=0, keepdims=True))
                    ext.append(s)
                exts.append(ext)
                ms.append(m)
            for e in range(G):
                acc = None
                for x, s in enumerate(exts[e]):
                    p = jnp.exp(s - ms[e]).astype(bf16)
                    t = []
                    for half in range(2):
                        if x == 0:
                            vv = vT_ref[hv[e], pl.ds(pl.multiple_of((b0 + half) * seg, seg), seg)]
                        else:
                            vv = chosen(pars[half], lambda b: vT_ref[hv[e], (8 + b) * seg:(9 + b) * seg])
                        t.append(mm(vv, p[:, half * seg:(half + 1) * seg]))
                    t = jnp.concatenate(t, axis=1)
                    acc = t if acc is None else acc + t
                acc = full_mix(e, ms[e], ntr, acc)
                finish(e, cols, ms[e], acc)

        hook(1)
        lax.fori_loop(0, 2, lambda i, c: (tail_tile(i, False), c)[1], 0)
        hook(2)
        lax.fori_loop(2, 6, lambda i, c: (hook(3, i), tail_tile(i, True), c)[2], 0)
        return 0

    lax.fori_loop(0, heads // G, group, 0)


def attend_back(heads, seg, parents_ref, kaug_ref, v_ref, qT_ref, doT_ref, kT_ref, do_ref, qn_ref,
                oT_ref, lse_ref, dqT_ref, dqkv_ref, accK, accV, hook):
    ntr = 8 * seg // T
    causal_t = iota((T, T), 0) <= iota((T, T), 1)
    causal_b = iota((seg, seg), 0) <= iota((seg, seg), 1)
    low_rows = iota((128, T), 0) < 64
    low_lanes = iota((T, 128), 1) < 64

    def pair(pr, _):
        hook("start", pr)
        lanes = pl.ds(pl.multiple_of(pr * 128, 128), 128)
        hk = [pl.ds(pl.multiple_of(pr * 256 + 128 * e, 128), 128) for e in range(2)]
        h64 = [pl.ds(pl.multiple_of(pr * 128 + 64 * e, 64), 64) for e in range(2)]
        accK[...] = jnp.zeros_like(accK)
        accV[...] = jnp.zeros_like(accV)

        def stack(x):
            z = jnp.zeros_like(x)
            return jnp.concatenate([jnp.where(low_lanes, x, z), jnp.where(low_lanes, z, x)], axis=0)

        def prep(cols):
            doT = doT_ref[lanes, cols]
            z = jnp.zeros_like(doT)
            prod = doT.astype(f32) * oT_ref[lanes, cols].astype(f32)
            q, do, lse, delta = [], [], [], []
            for e in range(2):
                q.append(qT_ref[hk[e], cols])
                do.append(jnp.where(low_rows, doT, z) if e == 0 else jnp.where(low_rows, z, doT))
                at = pl.multiple_of((pr * 2 + e) * 8, 8)
                lse.append(jnp.max(lse_ref[pl.ds(at, 8), cols], axis=0, keepdims=True))
                delta.append(jnp.sum(prod[64 * e:64 * e + 64], axis=0, keepdims=True))
            return q, do, lse, delta, stack(do_ref[cols, lanes]), stack(qn_ref[cols, lanes])

        def front(blk, n, sl, args, mask, par=None):
            q, do, lse, delta, rv, rk = args

            def rows_of(ref, at):
                if par is None:
                    return ref[pl.ds(blk, n), :, at].reshape(n * seg, 128)
                return chosen(par, lambda b: ref[8 + b, :, at])

            vv = rows_of(v_ref, lanes)
            s = [mm(rows_of(kaug_ref, hk[e]), q[e][:, sl]) for e in range(2)]
            dp = [mm(vv, do[e][:, sl]) for e in range(2)]
            return s, dp

        def rear(blk, n, sl, args, mask, par, s, dp):
            q, do, lse, delta, rv, rk = args
            ps, dss, dq = [], [], []
            for e in range(2):
                p = jnp.exp(s[e] - lse[e][:, sl])
                if mask is not None:
                    p = jnp.where(mask, p, 0.0)
                dss.append((p * (dp[e] - delta[e][:, sl])).astype(bf16))
                ps.append(p.astype(bf16))
            for e in range(2):
                if par is None:
                    kT = kT_ref[h64[e], pl.ds(pl.multiple_of(blk * seg, seg), n * seg)]
                else:
                    kT = chosen(par, lambda b: kT_ref[h64[e], (8 + b) * seg:(9 + b) * seg])
                dq.append(mm(kT, dss[e]))
            if sl.stop - sl.start != T:
                rv = jnp.concatenate([rv[sl], rv[T + sl.start:T + sl.stop]], axis=0)
                rk = jnp.concatenate([rk[sl], rk[T + sl.start:T + sl.stop]], axis=0)
            av = mm(jnp.concatenate(ps, axis=1), rv)
            ak = mm(jnp.concatenate(dss, axis=1), rk)
            if par is None:
                accV[pl.ds(blk, n)] += av.reshape(n, seg, 128)
                accK[pl.ds(blk, n)] += ak.reshape(n, seg, 128)
            else:
                for b in range(4):
                    here = jnp.where(par == b + 1, 1.0, 0.0)
                    accK[8 + b] += ak * here
                    accV[8 + b] += av * here
            return dq

        def run(items):
            out = []
            ready = []
            for item in items:
                ready.append((item, front(*item)))
                if len(ready) > 2:
                    it, (s, dp) = ready.pop(0)
                    out.append(rear(*it, s, dp))
            for it, (s, dp) in ready:
                out.append(rear(*it, s, dp))
            return out

        def emit(cols, dq):
            for e in range(2):
                dqT_ref[64 * e:64 * e + 64, cols] = (dq[e] * 0.125).astype(bf16)

        full = slice(0, T)
        for t in range(ntr):
            cols = slice(t * T, (t + 1) * T)
            args = prep(cols)
            items = [(2 * t, 2, full, args, causal_t, None)] + [(2 * c, 2, full, args, None, None) for c in range(t)]
            res = run(items)
            emit(cols, [sum(x[e] for x in res) for e in range(2)])

        def tail_tile(i, leaf):
            b0 = 8 + 2 * i
            cols = pl.ds(pl.multiple_of(b0 * seg, T), T)
            args = prep(cols)
            items = []
            for half in range(2):
                sl = slice(half * seg, (half + 1) * seg)
                items.append((b0 + half, 1, sl, args, causal_b, None))
                if leaf:
                    items.append((8, 1, sl, args, None, parents_ref[b0 + half - 7]))
            k = len(items) // 2
            items += [(2 * c, 2, full, args, None, None) for c in range(ntr)]
            res = run(items)
            dq = []
            for e in range(2):
                halves = [sum(x[e] for x in res[h * k:(h + 1) * k]) for h in range(2)]
                dq.append(jnp.concatenate(halves, axis=1) + sum(x[e] for x in res[2 * k:]))
            emit(cols, dq)

        hook("mid", pr)
        lax.fori_loop(0, 2, lambda i, c: (tail_tile(i, False), c)[1], 0)
        hook("late", pr)
        lax.fori_loop(2, 6, lambda i, c: (hook("leaf", pr, i), tail_tile(i, True), c)[2], 0)
        first = pr * 384

        def put(i, x):
            dqkv_ref[:, :, pl.ds(pl.multiple_of(first + 128 * i, 128), 128)] = x

        put(0, dqT_ref[...].T.reshape(20, seg, 128))
        put(1, accK[...].astype(bf16))
        put(2, accV[...].astype(bf16))
        hook("end", pr)
        return 0

    lax.fori_loop(0, heads // 2, pair, 0)


class Dense:
    def __init__(self, rows, width, oF_ref, dy_ref, woi_ref, wu_ref, rows_ref, dxl_ref, dx2_ref, ga_ref, gb_ref, vin_ref,
                 a2s, gs, dus):
        self.__dict__.update({k: v for k, v in locals().items() if k != "self"})
        self.hidden = wu_ref.shape[0]
        self.tiles = self.hidden // width

    def chunk(self, start, x, y_ref=None, back=True):
        width, rows_ref, vin_ref = self.width, self.rows_ref, self.vin_ref
        woi_ref, wu_ref = self.woi_ref, self.wu_ref
        c1 = math.sqrt(2.0 / math.pi)
        c2 = c1 * 0.044715

        def vector(i):
            return rows_ref[0:1, i * width:(i + 1) * width]

        def add_sum(i, x):
            vin_ref[i:i + 1, :] += jnp.sum(x, axis=0, keepdims=True)

        at = pl.ds(pl.multiple_of(start, 128), x.shape[0])
        x2 = fold(x) + mm_tn(self.oF_ref[:, at], woi_ref[:, 0:width]) + vector(2)
        centred = x2 - jnp.mean(x2, axis=-1, keepdims=True)
        inv = lax.rsqrt(jnp.mean(centred * centred, axis=-1, keepdims=True) + 1e-06)
        unit = centred * inv
        a2 = (unit * vector(3) + vector(4)).astype(bf16)
        if back:
            self.a2s[at, :] = a2
            dy = self.dy_ref[start // x.shape[0]]
        y = x2 + vector(5)
        da2 = None
        for t in range(self.tiles):
            ft = slice(t * width, (t + 1) * width)
            wt = slice(width + t * width, width + (t + 1) * width)
            u = mm(a2, woi_ref[:, wt]) + rows_ref[0:1, 6 * width + t * width:6 * width + (t + 1) * width]
            uu = u * u
            th = jnp.tanh(u * (c1 + c2 * uu))
            p = 0.5 + 0.5 * th
            g = (u * p).astype(bf16)
            if y_ref is not None:
                y = y + mm(g, wu_ref[ft, :])
            if not back:
                continue
            slope = p + u * (0.5 - 0.5 * th * th) * (c1 + 3.0 * c2 * uu)
            self.gs[at, ft] = g
            du = (mm_nt(dy, wu_ref[ft, :]) * slope).astype(bf16)
            self.dus[at, ft] = du
            add_sum(6 + t, fold(du))
            d = mm_nt(du, woi_ref[:, wt])
            da2 = d if da2 is None else da2 + d
        if y_ref is not None:
            y_ref[...] = y.astype(bf16)
        if not back:
            return
        dyf = fold(dy)
        dn = da2 * vector(3)
        m1 = jnp.mean(dn, axis=-1, keepdims=True)
        m2 = jnp.mean(dn * unit, axis=-1, keepdims=True)
        dx2 = dyf + (dn - m1 - unit * m2) * inv
        dxl = dx2.astype(bf16)
        self.dx2_ref[at, :] = dx2
        self.dxl_ref[at, :] = dxl
        add_sum(2, fold(dxl))
        add_sum(3, da2 * unit)
        add_sum(4, da2)
        add_sum(5, dyf)

    def gradients(self, F):
        width, hidden, tiles, gb_ref = self.width, self.hidden, self.tiles, self.gb_ref
        r, ru = width // F, hidden // F
        nb = T // ru
        dy = self.dy_ref[...].reshape(2 * self.rows, width)

        def outer(t, c):
            val = mm_tn(self.gs[:, pl.ds(pl.multiple_of(t * T, T), T)], dy).astype(bf16)
            self.ga_ref[pl.ds(t * nb, nb)] = val.reshape(nb, ru, width)
            return c

        lax.fori_loop(0, hidden // T, outer, 0)
        a2T = self.a2s[...].T
        for t in range(tiles):
            val = mm(a2T, self.dus[:, t * width:(t + 1) * width]).astype(bf16)
            gb_ref[:, t * r:(t + 1) * r, :] = val.reshape(F, r, width)
        val = mm(self.oF_ref[...], self.dxl_ref[...]).astype(bf16)
        gb_ref[:, tiles * r:(tiles + 1) * r, :] = val.reshape(F, r, width)


def slope_parts(head, head_count, length):
    x = np.float32(2.0 ** (2.0 - 4.0 * head / head_count) / length)
    out = []
    for _ in range(3):
        low = np.float32(ml_dtypes.bfloat16(x))
        out.append(float(low))
        x = np.float32(x - low)
    return out


def remote(src, dst, send_sem, recv_sem, target):
    return pltpu.make_async_remote_copy(
        src_ref=src, dst_ref=dst, send_sem=send_sem, recv_sem=recv_sem,
        device_id={"fsdp": target}, device_id_type=pl.DeviceIdType.MESH)


def where_am_i(F):
    f = lax.axis_index("fsdp")
    place = lax.rem(f + 2, F)
    part = lax.rem(place, 4)
    half = part // 2
    core = lax.rem(f, 2)
    base = place - part
    partner = lax.rem(base + lax.rem(part + 2, 4) + F - 2, F)
    sibling = f + 1 - 2 * core
    return f, part, half, core, partner, sibling


def greet(F, f, core, sibling, across):
    barrier = pltpu.get_barrier_semaphore()
    peers = [{"fsdp": lax.rem(f + 2 * d, F)} for d in range(1, F // 2)] + [{"fsdp": sibling}]
    if across:
        plane = lax.axis_index("dp")
        peers.append({"dp": plane + 1 - 2 * lax.rem(plane, 2)})
    for peer in peers:
        pl.semaphore_signal(barrier, inc=1, device_id=peer, device_id_type=pl.DeviceIdType.MESH)
    pl.semaphore_wait(barrier, len(peers))


def first_kernel(F, n, parents_ref, tok_ref, cot_ref, wq_ref, wk_ref, wv_ref, wo_ref, wi_ref, wu_ref, vec_ref,
                 a1T_out, kaug_out, v_out, kT_out, qn_out, qT_out, oT_out, lse_out, wc_out, wo_out, xs_out, dxl_out,
                 dx2_out, ga_out, gb_out, lo_ref, vin_ref, rows_ref,
                 xt_ref, a1T_ref, kaug_ref, v_ref, kT_ref, qn_ref, qT_ref, oT_ref, lse_ref, oF_ref, dy_ref,
                 wqkv_ref, woi_ref, wuf_ref, wc, dxl_ref, dx2_ref, ga_ref, gb_ref, a2s, gs, dus,
                 vecs, vT_scr, s_scr, tsend, trecv, gsend, grecv, zsend, zrecv, osem):
    f, part, half, core, partner, sibling = where_am_i(F)
    rows, width = tok_ref.shape[1:]
    seg = rows // 5
    heads = H // 2
    hw = heads * 64
    tree = 4 * rows
    r = wq_ref.shape[0]
    ru = wu_ref.shape[0]
    part1 = part + 1 - 2 * core
    part2 = lax.rem(part + 2, 4)
    part3 = lax.rem(part1 + 2, 4)

    own = pl.ds(pl.multiple_of(f * r, r), r)
    ownu = pl.ds(pl.multiple_of(f * ru, ru), ru)
    vecs[f] = vec_ref[...]
    wqkv_ref[own, 0:width] = wq_ref[...].astype(bf16)
    wqkv_ref[own, width:2 * width] = wk_ref[...].astype(bf16)
    wqkv_ref[own, 2 * width:3 * width] = wv_ref[...].astype(bf16)

    greet(F, f, core, sibling, lax.axis_size("dp") % 2 == 0)

    def slot(g, src):
        if g == 0:
            return vecs.at[src]
        if g == 3:
            return wuf_ref.at[pl.ds(pl.multiple_of(src * ru, ru), ru)]
        ref = wqkv_ref if g == 1 else woi_ref
        return ref.at[pl.ds(pl.multiple_of(src * r, r), r)]

    planes = lax.axis_size("dp")
    plane = lax.axis_index("dp")
    shared = r % 32 == 0 and planes % 2 == 0
    parity = lax.rem(plane, 2)
    opposite = plane + 1 - 2 * parity
    chips = range(1, F // 2)

    def part_of(g, src, which=None):
        if g != 2 or not shared or which is None:
            return slot(g, src)
        return woi_ref.at[pl.ds(pl.multiple_of(src * r + which * (r // 2), 16), r // 2)]

    def source(d, of=None):
        return lax.rem((f if of is None else of) + F - 2 * d, F)

    def direct(g, d):
        if d == 0:
            return remote(slot(g, f), slot(g, f), gsend.at[g, 0], grecv.at[g, 0], sibling)
        return remote(part_of(g, f, parity), part_of(g, f, parity), gsend.at[g, d], grecv.at[g, d], lax.rem(f + 2 * d, F))

    def came(g, d):
        ref = slot(g, sibling) if d == 0 else part_of(g, source(d), parity)
        remote(ref, ref, gsend.at[g, d], grecv.at[g, d], sibling).wait_recv()

    def forward(g, d, of=None):
        ref = part_of(g, source(d, of), parity)
        return remote(ref, ref, gsend.at[g, F // 2 + d], grecv.at[g, F // 2 + d], sibling)

    def across(d, which):
        ref = part_of(2, source(d), which)
        return pltpu.make_async_remote_copy(
            src_ref=ref, dst_ref=ref, send_sem=zsend.at[d], recv_sem=zrecv.at[d],
            device_id={"dp": opposite}, device_id_type=pl.DeviceIdType.MESH)

    def forward_across(d, of=None):
        ref = part_of(2, source(d, of), 1 - parity)
        return remote(ref, ref, zsend.at[F // 2 + d], zrecv.at[F // 2 + d], sibling)

    def send_all(g):
        for d in range(F // 2):
            direct(g, d).start()

    def pass_on(g):
        for d in chips:
            came(g, d)
            if g == 2 and shared:
                across(d, parity).start()
            forward(g, d).start()

    def pass_across():
        if shared:
            for d in chips:
                across(d, 1 - parity).wait_recv()
                forward_across(d).start()

    def receive_rest(g):
        came(g, 0)
        for d in chips:
            forward(g, d, sibling).wait_recv()
            if g == 2 and shared:
                forward_across(d, sibling).wait_recv()

    x_out = remote(tok_ref.at[1 - half], xt_ref.at[part], tsend.at[0], trecv.at[0], partner)
    x_sib = remote(tok_ref.at[half], xt_ref.at[part], tsend.at[1], trecv.at[1], sibling)
    x_fwd = remote(xt_ref.at[part2], xt_ref.at[part2], tsend.at[2], trecv.at[2], sibling)
    dy_out = remote(cot_ref.at[1 - half], dy_ref.at[half], tsend.at[3], trecv.at[3], partner)
    x_own = pltpu.make_async_copy(tok_ref.at[half], xt_ref.at[part], osem.at[20])
    dy_own = pltpu.make_async_copy(cot_ref.at[half], dy_ref.at[half], tsend.at[4])

    send_all(0)
    send_all(1)
    x_out.start()
    x_sib.start()
    x_own.start()
    dy_own.start()
    woi_ref[own, 0:width] = wo_ref[...].astype(bf16)
    woi_ref[own, width:] = wi_ref[...].astype(bf16)
    wuf_ref[ownu, :] = wu_ref[...].astype(bf16)
    pass_on(0)
    pass_on(1)
    receive_rest(0)

    table = jnp.max(vecs[...], axis=1).astype(bf16)
    words = table.shape[1]

    def vector_row(first, m, length):
        col = iota((words, length), 1)
        pick = iota((words, length), 0) == first + (col & (m - 1))
        spread = mm(table, pick.astype(bf16))
        shift = m.bit_length() - 1
        mine = iota((F, length), 0) == (iota((F, length), 1) >> shift)
        return jnp.sum(jnp.where(mine, spread, 0.0), axis=0, keepdims=True)

    def all_rows(first, last):
        for i in range(first, last):
            rows_ref[:, i * width:(i + 1) * width] = jnp.broadcast_to(vector_row(i * n, n, width), (8, width))

    all_rows(0, 2)
    hidden = rows_ref.shape[1] - 6 * width
    receive_rest(1)

    lane = iota((seg, 128), 1)
    offs = iota((seg, 128), 0)
    arow = iota((64, rows), 0)

    def project(p):
        x = xt_ref[p].astype(f32)
        gain = rows_ref[0:1, 0:width]
        shift = rows_ref[0:1, width:2 * width]
        mean = jnp.mean(x, axis=-1, keepdims=True)
        x = x - mean
        inv = lax.rsqrt(jnp.mean(x * x, axis=-1, keepdims=True) + 1e-06)
        a1 = (x * inv * gain + shift).astype(bf16)

        def proj(i):
            return mm(a1, wqkv_ref[:, pl.ds(pl.multiple_of(i * width + core * hw, hw), hw)])

        cols = pl.ds(pl.multiple_of(p * rows, rows), rows)
        a1T_ref[:, cols] = a1.T
        q = (proj(0) * 0.125).astype(bf16)
        qn_ref[cols, :] = q
        qT = q.T
        k = proj(1).astype(bf16)
        kT_ref[:, cols] = k.T
        v = proj(2).astype(bf16)
        v_ref[pl.ds(p * 5, 5)] = v.reshape(5, seg, hw)
        vT = v.T
        for h in range(heads):
            a, b = slope_parts(h, H, tree), slope_parts(heads + h, H, tree)
            aug = jnp.zeros((64, rows), f32)
            for j in range(3):
                s = jnp.where(core == 0, a[j], b[j])
                aug = jnp.where((arow == j) | (arow == j + 3), s, aug)
            aug = aug.astype(bf16)
            lo, hi = 128 * h + 64 * (h % 2), 128 * h + 64 - 64 * (h % 2)
            qT_ref[lo:lo + 64, cols] = qT[64 * h:64 * h + 64]
            qT_ref[hi:hi + 64, cols] = aug
            vT_scr[80 * h:80 * h + 64, cols] = vT[64 * h:64 * h + 64]
            vT_scr[80 * h + 64:80 * h + 80, cols] = jnp.ones((16, rows), bf16)
        for b in range(5):
            blk = p * 5 + b
            start = jnp.where(blk < 8, blk * seg, jnp.where(blk < 12, 8 * seg, 9 * seg))
            spot = offs + start
            hi = (spot & -8).astype(f32)
            lo = (spot & 7).astype(f32)
            for h in range(heads):
                at = 64 - 64 * (h % 2)
                l = lane - at
                aug = jnp.where((l >= 0) & (l < 3), hi, jnp.where((l >= 3) & (l < 6), lo, 0.0)).astype(bf16)
                keep = (lane < 64) if h % 2 == 0 else (lane >= 64)
                kk = k[b * seg:(b + 1) * seg, 128 * (h // 2):128 * (h // 2) + 128]
                kaug_ref[blk, :, 128 * h:128 * h + 128] = jnp.where(keep, kk, aug)

    x_own.wait()
    x_sib.wait_recv()

    def visit(i, c):
        @pl.when(i == 1)
        def _():
            all_rows(2, 6)
            rows_ref[:, 6 * width:] = jnp.broadcast_to(vector_row(6 * n, hidden // F, hidden), (8, hidden))
            x_out.wait_recv()
            x_fwd.start()
            send_all(2)
            send_all(3)

        @pl.when(i == 3)
        def _():
            x_fwd.wait_recv()

        project(jnp.where(i == 0, part, jnp.where(i == 1, part1, jnp.where(i == 2, part2, part3))))
        return c

    lax.fori_loop(0, 4, visit, 0)
    for i in range(heads // 2):
        for k in range(3):
            src = pl.ds(pl.multiple_of(k * width + core * hw + 128 * i, 128), 128)
            wc[:, 384 * i + 128 * k:384 * i + 128 * k + 128] = wqkv_ref[:, src]

    outs = [(a1T_ref, a1T_out), (kaug_ref, kaug_out), (v_ref, v_out), (kT_ref, kT_out), (qn_ref, qn_out),
            (qT_ref, qT_out), (wc, wc_out), (xt_ref.at[core], xs_out.at[0]), (xt_ref.at[core + 2], xs_out.at[1]),
            (oT_ref, oT_out), (lse_ref, lse_out),
            (woi_ref.at[pl.ds(pl.multiple_of(core * hw, hw), hw), 0:width], wo_out),
            (dxl_ref.at[0:rows], dxl_out.at[0]), (dxl_ref.at[rows:2 * rows], dxl_out.at[1]),
            (dx2_ref.at[0:rows], dx2_out.at[0]), (dx2_ref.at[rows:2 * rows], dx2_out.at[1]), (ga_ref, ga_out), (gb_ref, gb_out)]
    copies = [pltpu.make_async_copy(a, b, osem.at[i]) for i, (a, b) in enumerate(outs)]
    for c in copies[:9]:
        c.start()

    s_refs = [dx2_ref.at[0:8 * seg, 0:T], dx2_ref.at[0:8 * seg, T:2 * T], s_scr.at[0], s_scr.at[1]]

    def hook(stage, i=None):
        if stage == 1:
            pass_on(2)
        if stage == 2:
            dy_out.start()

    attend(heads, seg, parents_ref, kaug_ref, qT_ref, vT_scr, oT_ref, lse_ref, s_refs, hook)

    other = 1 - core
    sent = []
    for i in range(2):
        cols = pl.ds(pl.multiple_of((other + 2 * i) * rows, rows), rows)
        at = (pl.ds(pl.multiple_of(core * hw, hw), hw), slice(i * rows, (i + 1) * rows))
        c = remote(oT_ref.at[:, cols], oF_ref.at[at], tsend.at[5 + i], trecv.at[5 + i], sibling)
        c.start()
        sent.append(c)
    for i in range(2):
        mine = pl.ds(pl.multiple_of((core + 2 * i) * rows, rows), rows)
        at = (pl.ds(pl.multiple_of(core * hw, hw), hw), slice(i * rows, (i + 1) * rows))
        oF_ref[at] = oT_ref[:, mine]
    copies[9].start()
    copies[10].start()
    pass_across()
    pass_on(3)
    receive_rest(2)
    copies[11].start()
    for c in sent:
        c.wait_recv()
    receive_rest(3)
    dy_own.wait()

    vin_ref[...] = jnp.zeros_like(vin_ref)
    dense = Dense(rows, width, oF_ref, dy_ref, woi_ref, wuf_ref, rows_ref, dxl_ref, dx2_ref, ga_ref, gb_ref, vin_ref,
                  a2s, gs, dus)
    y_out = remote(xt_ref.at[other + 2 * (1 - half)], lo_ref.at[half], tsend.at[7], trecv.at[7], partner)
    keep_y = pltpu.make_async_copy(xt_ref.at[other + 2 * half], lo_ref.at[half], osem.at[18])
    dense.chunk((1 - half) * rows, xt_ref[core + 2 * (1 - half)], xt_ref.at[other + 2 * (1 - half)], False)
    y_out.start()
    dense.chunk(half * rows, xt_ref[core + 2 * half], xt_ref.at[other + 2 * half])
    keep_y.start()
    dy_out.wait_recv()
    dense.chunk((1 - half) * rows, xt_ref[core + 2 * (1 - half)])
    for c in copies[12:16]:
        c.start()
    dense.gradients(F)
    copies[16].start()
    copies[17].start()
    for c in copies + [keep_y]:
        c.wait()
    y_out.wait()
    dy_out.wait_send()
    x_out.wait_send()
    x_sib.wait_send()
    x_fwd.wait_send()
    for c in sent:
        c.wait_send()
    for g in range(4):
        for d in range(F // 2):
            direct(g, d).wait_send()
        for d in chips:
            forward(g, d).wait_send()
    if shared:
        for d in chips:
            across(d, parity).wait_send()
            forward_across(d).wait_send()


def first(F, parents, tokens, cotangent, weights, vec, n):
    _, rows, width = tokens.shape
    tree = 4 * rows
    heads = H // 2
    hw = heads * 64
    seg = rows // 5
    hidden = weights[4].shape[1]
    r, ru = width // F, hidden // F
    R1 = (hidden // width + 1) * r
    two = 2 * rows
    keep = [((width, tree), bf16), ((20, seg, heads * 128), bf16), ((20, seg, hw), bf16), ((hw, tree), bf16),
            ((tree, hw), bf16), ((heads * 128, tree), bf16), ((hw, tree), bf16), ((heads * 8, tree), f32)]
    out = keep + [((width, 3 * hw), bf16), ((hw, width), bf16), ((2, rows, width), bf16), ((2, rows, width), bf16),
                  ((2, rows, width), f32), ((F, ru, width), bf16), ((F, R1, width), bf16), ((2, rows, width), bf16),
                  ((16, width), f32), ((8, 6 * width + hidden), f32)]
    scratch = [((4, rows, width), bf16)] + keep + [
        ((2 * hw, two), bf16), ((2, rows, width), bf16), ((width, 3 * width), bf16), ((width, width + hidden), bf16),
        ((hidden, width), bf16), ((width, 3 * hw), bf16), ((two, width), bf16),
        ((two, width), f32), ((F, ru, width), bf16), ((F, R1, width), bf16), ((two, width), bf16), ((two, hidden), bf16),
        ((two, hidden), bf16), ((F,) + vec.shape, f32), ((heads * 80, tree), bf16), ((2, 8 * seg, T), f32)]
    ANY = pl.BlockSpec(memory_space=pl.ANY)
    dma = pltpu.SemaphoreType.DMA
    return pl.pallas_call(
        functools.partial(first_kernel, F, n),
        out_shape=[jax.ShapeDtypeStruct(s, d) for s, d in out],
        in_specs=[SM, ANY, ANY] + [VM] * 7,
        out_specs=[ANY] * 16 + [VM] * 2,
        scratch_shapes=[pltpu.VMEM(s, d) for s, d in scratch] + [
            dma((8,)), dma((8,)), dma((4, F)), dma((4, F)), dma((F,)), dma((F,)), dma((21,))],
        name="front",
        compiler_params=pltpu.CompilerParams(vmem_limit_bytes=64 << 20, collective_id=0, has_side_effects=True),
    )(parents, tokens, cotangent, *weights, vec)


def fold(x):
    return x.astype(f32)


class Chain:
    def __init__(self, F, f, sums, got, block, zgot, final, send, recv, stages=2):
        self.square = F == 8 and stages == 2
        self.F, self.f, self.sums, self.got, self.block = F, f, sums, got, block
        self.zgot, self.final, self.send, self.recv = zgot, final, send, recv
        self.chip = f // 2
        self.chips = F // 2
        self.planes = lax.axis_size("dp")
        self.plane = lax.axis_index("dp")
        self.rows = sums.shape[1]
        self.zrows = block.shape[0] // self.planes

    def _b(self, d):
        return remote(self.sums.at[lax.rem(self.chip + d, self.chips)], self.got.at[d - 1],
                      self.send.at[d], self.recv.at[d], lax.rem(self.f + 2 * d, self.F))

    def _square(self):
        core = lax.rem(self.f, 2)
        x, y = lax.rem(self.chip, 2), self.chip // 2
        along_x, along_y = 2 * y + 1 - x, 2 * (1 - y) + x
        first = jnp.where(core == 0, along_x, along_y)
        second = jnp.where(core == 0, along_y, along_x)
        last = 2 * (1 - y) + 1 - x
        one = [remote(self.sums.at[first], self.got.at[0], self.send.at[1], self.recv.at[1], 2 * first + core),
               remote(self.sums.at[last], self.got.at[1], self.send.at[2], self.recv.at[2], 2 * first + core)]
        two = remote(self.sums.at[second], self.got.at[2], self.send.at[3], self.recv.at[3], 2 * second + core)
        return one, two, second

    def _chunk(self, z):
        return pl.ds(pl.multiple_of(z * self.zrows, 16), self.zrows)

    def _c(self, e):
        z = lax.rem(self.plane + e, self.planes)
        i = self.chips + e
        return pltpu.make_async_remote_copy(
            src_ref=self.block.at[self._chunk(z)], dst_ref=self.zgot.at[e - 1],
            send_sem=self.send.at[i], recv_sem=self.recv.at[i],
            device_id={"dp": z}, device_id_type=pl.DeviceIdType.MESH)

    def _d(self, e, src=None):
        z = lax.rem(self.plane + e, self.planes)
        i = self.chips + self.planes + e
        here = self._chunk(self.plane if src is None else src)
        return pltpu.make_async_remote_copy(
            src_ref=self.final.at[here], dst_ref=self.final.at[here],
            send_sem=self.send.at[i], recv_sem=self.recv.at[i],
            device_id={"dp": z}, device_id_type=pl.DeviceIdType.MESH)

    def start_plane(self):
        if self.square:
            for c in self._square()[0]:
                c.start()
            return
        for d in range(1, self.chips):
            self._b(d).start()

    def mid_plane(self):
        if self.square:
            one, two, second = self._square()
            for c in one:
                c.wait_recv()
            self.sums[second] = (fold(self.sums[second]) + fold(self.got[1])).astype(bf16)
            two.start()

    def start_z(self):
        if self.square:
            self._square()[1].wait_recv()
            total = fold(self.sums[self.chip]) + fold(self.got[0]) + fold(self.got[2])
        else:
            for d in range(1, self.chips):
                self._b(d).wait_recv()
            total = fold(self.sums[self.chip])
            for d in range(1, self.chips):
                total = total + fold(self.got[d - 1])
        self.block[0:self.rows] = total.astype(bf16)
        for e in range(1, self.planes):
            self._c(e).start()

    def start_back(self):
        for e in range(1, self.planes):
            self._c(e).wait_recv()
        here = self._chunk(self.plane)
        total = fold(self.block[here])
        for e in range(1, self.planes):
            total = total + fold(self.zgot[e - 1])
        self.final[here] = total.astype(bf16)
        for e in range(1, self.planes):
            self._d(e).start()

    def receive(self):
        for e in range(1, self.planes):
            self._d(e, lax.rem(self.plane + self.planes - e, self.planes)).wait_recv()

    def close(self):
        if self.square:
            one, two, _ = self._square()
            for c in one + [two]:
                c.wait_send()
        else:
            for d in range(1, self.chips):
                self._b(d).wait_send()
        for e in range(1, self.planes):
            self._c(e).wait_send()
            self._d(e).wait_send()


def last_kernel(F, parents_ref, kaug_h, v_h, qT_h, kT_h, qn_h, oT_h, lse_h, a1T_h, wc_h, wo_h, xs_h, dxl_ref, dx2_h,
                ga_ref, gb_ref, vin_ref, n1_ref,
                gt_ref, gq_ref, fina, finb, vout_ref,
                kaug_ref, v_ref, qT_ref, kT_ref, qn_ref, oT_ref, lse_ref, a1T_ref, wc, wo_scr, xs, dx2s,
                dxs, doT, do, dqT, dqkv, accK, accV, das, dar,
                suma, sumb, gota, gotb, planea, planeb, blka, blkb, za, zb, sum2, got2, blk2, z2, fin2,
                vs, vgot, dxo, tsend, trecv, senda, recva, sendb, recvb, send2, recv2, vsend, vrecv, lsem):
    f, part, half, core, partner, sibling = where_am_i(F)
    planes = lax.axis_size("dp")
    plane = lax.axis_index("dp")
    heads = H // 2
    hw = heads * 64
    _, rows, width = dxl_ref.shape
    chips = F // 2
    other = 1 - core
    tree = 4 * rows
    seg = rows // 5

    pairs = [(wo_h, wo_scr), (qT_h, qT_ref), (kaug_h, kaug_ref), (v_h, v_ref), (kT_h, kT_ref), (qn_h, qn_ref),
             (oT_h, oT_ref), (lse_h, lse_ref), (ga_ref.at[:, core], suma), (gb_ref.at[:, core], sumb), (a1T_h, a1T_ref), (wc_h, wc), (xs_h, xs),
             (dx2_h, dx2s)]
    loads = [pltpu.make_async_copy(a, b, lsem.at[i]) for i, (a, b) in enumerate(pairs)]
    for c in loads:
        c.start()

    barrier = pltpu.get_barrier_semaphore()
    for d in range(1, chips):
        pl.semaphore_signal(barrier, inc=1, device_id={"fsdp": lax.rem(f + 2 * d, F)},
                            device_id_type=pl.DeviceIdType.MESH)
    for e in range(1, planes):
        pl.semaphore_signal(barrier, inc=1, device_id={"dp": lax.rem(plane + e, planes)},
                            device_id_type=pl.DeviceIdType.MESH)
    pl.semaphore_signal(barrier, inc=1, device_id={"fsdp": sibling}, device_id_type=pl.DeviceIdType.MESH)
    pl.semaphore_wait(barrier, chips + planes - 1)

    dx_sw = remote(dxl_ref, dxs, tsend.at[0], trecv.at[0], sibling)
    out_a = remote(ga_ref.at[:, other], gota, tsend.at[1], trecv.at[1], sibling)
    out_b = remote(gb_ref.at[:, other], gotb, tsend.at[7], trecv.at[7], sibling)
    dx_sw.start()
    out_a.start()
    out_b.start()

    def make_do(p, x):
        cols = pl.ds(pl.multiple_of(p * rows, rows), rows)
        d = mm_nt(x, wo_scr[...]).astype(bf16)
        do[cols, :] = d
        doT[:, cols] = d.T

    loads[0].wait()
    lax.fori_loop(0, 2, lambda i, c: (make_do(core + 2 * i, dxl_ref[i]), c)[1], 0)

    one_a = Chain(F, f, suma, planea, blka, za, fina, senda, recva)
    one_b = Chain(F, f, sumb, planeb, blkb, zb, finb, sendb, recvb)

    def add_sibling(load, arrived, mine, got):
        load.wait()
        arrived.wait_recv()

        def add_block(j, c):
            mine[j] = (fold(mine[j]) + fold(got[j])).astype(bf16)
            return c

        lax.fori_loop(0, chips, add_block, 0)

    dx_sw.wait_recv()
    lax.fori_loop(0, 2, lambda i, c: (make_do(other + 2 * i, dxs[i]), c)[1], 0)
    add_sibling(loads[8], out_a, suma, gota)
    one_a.start_plane()
    for c in loads[1:8]:
        c.wait()

    def chain(pr):
        return Chain(F, f, sum2.at[pr], got2.at[pr], blk2.at[pr], z2.at[pr], fin2.at[pr], send2.at[pr], recv2.at[pr], 1)

    two = [chain(0), chain(1)]
    r = width // F
    r2 = 2 * r

    def hook(name, pr, i=None):
        if name == "mid":
            @pl.when(pr == 0)
            def _():
                add_sibling(loads[9], out_b, sumb, gotb)
                one_b.start_plane()

            @pl.when(pr == 1)
            def _():
                one_a.start_z()
        if name == "late":
            @pl.when(pr == 1)
            def _():
                one_b.start_z()
        if name == "leaf":
            @pl.when((pr == 0) & (i == 3))
            def _():
                one_a.mid_plane()

            @pl.when((pr == 1) & (i == 5))
            def _():
                one_a.start_back()
                two[0].start_z()
        if name == "end":
            @pl.when(pr == 0)
            def _():
                one_b.mid_plane()
                for c in loads[10:14]:
                    c.wait()

            g = mm(a1T_ref[...], dqkv[:, :, pl.ds(pl.multiple_of(pr * 384, 384), 384)].reshape(tree, 384)).astype(bf16)
            for j in range(chips):
                sum2[pr, j] = g[j * r2:(j + 1) * r2]
            chain(pr).start_plane()

    attend_back(heads, seg, parents_ref, kaug_ref, v_ref, qT_ref, doT, kT_ref, do, qn_ref, oT_ref, lse_ref,
                dqT, dqkv, accK, accV, hook)

    def da1_of(p):
        return mm_nt(dqkv[pl.ds(p * 5, 5)].reshape(rows, 3 * hw), wc[...])

    def da_out(s):
        i = (1 - half) if s == 0 else half
        return remote(das.at[i], dar.at[i], tsend.at[2 + s], trecv.at[2 + s], sibling)

    dx_out = remote(dxo.at[1 - half], gt_ref.at[half], tsend.at[4], trecv.at[4], partner)
    keep_dx = pltpu.make_async_copy(dxo.at[half], gt_ref.at[half], lsem.at[15])
    vs[0] = vin_ref[...]
    row = iota((16, width), 0)

    def finish_rows(s, c):
        i = jnp.where(s == 0, 1 - half, half)
        das[i] = da1_of(other + 2 * i).astype(bf16)
        for k in range(2):
            @pl.when(s == k)
            def _():
                da_out(k).start()
        x = fold(xs[i])
        x = x - jnp.mean(x, axis=-1, keepdims=True)
        inv = lax.rsqrt(jnp.mean(x * x, axis=-1, keepdims=True) + 1e-06)
        unit = x * inv
        da = da1_of(core + 2 * i)
        for k in range(2):
            @pl.when(s == k)
            def _():
                da_out(k).wait_recv()
        da = da + fold(dar[i])
        dn = da * n1_ref[0:1, 0:width]
        m1 = jnp.mean(dn, axis=-1, keepdims=True)
        m2 = jnp.mean(dn * unit, axis=-1, keepdims=True)
        dxo[i] = (dx2s[i] + (dn - m1 - unit * m2) * inv).astype(bf16)
        gs = jnp.sum(da * unit, axis=0, keepdims=True)
        bs = jnp.sum(da, axis=0, keepdims=True)
        vs[0] += jnp.where(row == 0, gs, 0.0) + jnp.where(row == 1, bs, 0.0)

        @pl.when(s == 0)
        def _():
            dx_out.start()
            one_b.start_back()
            two[0].start_back()

        @pl.when(s == 1)
        def _():
            keep_dx.start()

        return c

    lax.fori_loop(0, 2, finish_rows, 0)
    v_sib = remote(vs.at[0], vgot.at[0], vsend.at[0], vrecv.at[0], sibling)
    v_sib.start()
    two[1].start_z()
    v_sib.wait_recv()
    vgot[chips + plane] = vs[0] + vgot[0]

    def v_z(e, sender):
        return pltpu.make_async_remote_copy(
            src_ref=vgot.at[chips + sender], dst_ref=vgot.at[chips + sender],
            send_sem=vsend.at[chips + e], recv_sem=vrecv.at[chips + e],
            device_id={"dp": lax.rem(plane + e, planes)}, device_id_type=pl.DeviceIdType.MESH)

    for e in range(1, planes):
        v_z(e, plane).start()
    for e in range(1, planes):
        v_z(e, lax.rem(plane + planes - e, planes)).wait_recv()
    total = vgot[chips]
    for z in range(1, planes):
        total = total + vgot[chips + z]
    vs[1] = total
    v_chip = [remote(vs.at[1], vgot.at[d], vsend.at[d], vrecv.at[d], lax.rem(f + 2 * d, F)) for d in range(1, chips)]
    for c in v_chip:
        c.start()
    two[1].start_back()
    one_a.receive()
    one_b.receive()
    s_out = []
    for pr in range(2):
        two[pr].receive()
        c = remote(fin2.at[pr, pl.ds(pl.multiple_of(other * r, r), r)], gq_ref.at[core, pr],
                   tsend.at[5 + pr], trecv.at[5 + pr], sibling)
        c.start()
        gq_ref[core, pr] = fin2[pr, pl.ds(pl.multiple_of(core * r, r), r), :]
        s_out.append(c)
    for c in v_chip:
        c.wait_recv()
    total = vs[1]
    for d in range(1, chips):
        total = total + vgot[d]
    vout_ref[...] = total
    for c in s_out:
        c.wait()
    dx_out.wait()
    keep_dx.wait()
    one_a.close()
    one_b.close()
    for c in two:
        c.close()
    for c in [dx_sw, out_a, out_b, v_sib, da_out(0), da_out(1)] + v_chip:
        c.wait_send()
    for e in range(1, planes):
        v_z(e, plane).wait_send()


def last(F, DP, parents, kept, wc, wo, xs, dxl, dx2, ga, gb, vin, rows_vec):
    a1T, kaug, v, kT, qn, qT, oT, lse = kept
    _, rows, width = dxl.shape
    heads = H // 2
    hw = heads * 64
    tree = 4 * rows
    seg = rows // 5
    chips = F // 2
    r = width // F
    RA, RB = ga.shape[2], gb.shape[2]
    r2 = 2 * r

    def zrows(n):
        return -(-n // (16 * DP)) * 16

    ZA, ZB, Z2 = zrows(RA), zrows(RB), zrows(r2)
    ANY = pl.BlockSpec(memory_space=pl.ANY)
    dma = pltpu.SemaphoreType.DMA
    out = [((2, rows, width), bf16), ((2, 2, r, 384), bf16), ((ZA * DP, width), bf16),
           ((ZB * DP, width), bf16), ((16, width), f32)]
    big = [kaug, v, qT, kT, qn, oT, lse, a1T, wc, wo, xs]
    scratch = [(a.shape, a.dtype) for a in big] + [
        ((2, rows, width), f32),
        ((2, rows, width), bf16), ((hw, tree), bf16), ((tree, hw), bf16), ((128, tree), bf16),
        ((20, seg, 3 * hw), bf16), ((20, seg, 128), f32), ((20, seg, 128), f32),
        ((2, rows, width), bf16), ((2, rows, width), bf16),
        ((chips, RA, width), bf16), ((chips, RB, width), bf16), ((chips, RA, width), bf16), ((chips, RB, width), bf16),
        ((chips - 1, RA, width), bf16), ((chips - 1, RB, width), bf16), ((ZA * DP, width), bf16),
        ((ZB * DP, width), bf16), ((DP - 1, ZA, width), bf16), ((DP - 1, ZB, width), bf16),
        ((2, chips, r2, 384), bf16), ((2, chips - 1, r2, 384), bf16), ((2, Z2 * DP, 384), bf16),
        ((2, DP - 1, Z2, 384), bf16), ((2, Z2 * DP, 384), bf16),
        ((2, 16, width), f32), ((chips + DP, 16, width), f32), ((2, rows, width), bf16),
    ]
    nsem = chips + 2 * DP
    return pl.pallas_call(
        functools.partial(last_kernel, F),
        out_shape=[jax.ShapeDtypeStruct(s, d) for s, d in out],
        in_specs=[SM] + [ANY] * 11 + [VM, ANY, ANY, ANY, VM, VM],
        out_specs=[ANY] + [VM] * 4,
        scratch_shapes=[pltpu.VMEM(s, d) for s, d in scratch] + [
            dma((9,)), dma((9,)), dma((nsem,)), dma((nsem,)), dma((nsem,)), dma((nsem,)), dma((2, nsem)), dma((2, nsem)),
            dma((chips + DP,)), dma((chips + DP,)), dma((17,))],
        name="back",
        compiler_params=pltpu.CompilerParams(vmem_limit_bytes=64 << 20, collective_id=1, has_side_effects=True),
    )(parents, *big, dxl, dx2, ga, gb, vin, rows_vec)


def finish_kernel(lo_in, gt_in, fina, finb, gq, lo_ref, gt_ref, gwq_ref, gwk_ref, gwv_ref, gwo_ref, gwi_ref, gwu_ref):
    lo_ref[...] = lo_in[...]
    gt_ref[...] = gt_in[...]
    r, width = gwo_ref.shape
    ru = gwu_ref.shape[0]
    gwu_ref[...] = fold(fina[0:ru])
    pieces = gwi_ref.shape[1] // width
    for c in range(pieces):
        gwi_ref[:, c * width:(c + 1) * width] = fold(finb[c * r:(c + 1) * r])
    gwo_ref[...] = fold(finb[pieces * r:(pieces + 1) * r])
    for k, ref in enumerate((gwq_ref, gwk_ref, gwv_ref)):
        for c in range(2):
            for pr in range(2):
                at = (2 * c + pr) * 128
                ref[:, at:at + 128] = fold(gq[c, pr, :, 128 * k:128 * k + 128])


def finish(F, lo, gt, fina, finb, gq, hidden):
    width = lo.shape[2]
    r, ru = width // F, hidden // F
    shapes = [(r, width)] * 4 + [(r, hidden), (ru, width)]
    return pl.pallas_call(
        finish_kernel,
        out_shape=[jax.ShapeDtypeStruct(lo.shape, bf16), jax.ShapeDtypeStruct(gt.shape, bf16)]
        + [jax.ShapeDtypeStruct(s, f32) for s in shapes],
        in_specs=[VM] * 5,
        out_specs=[VM] * 8,
        name="finish",
    )(lo, gt, fina, finb, gq)


def on_device(tokens, parents, n1g, n1b, wq, wk, wv, wo, ob, n2g, n2b, wi, ib, wu, ub, cotangent):
    F = lax.axis_size("fsdp")
    fi = lax.axis_index("fsdp")
    place = (fi + 2) % F
    half = (place % 4) // 2
    quad = lax.axis_index("dp") * (F // 4) + place // 4
    parent_row = parents[quad, half]
    _, _, rows, width = tokens.shape

    n = n1g.shape[0]
    vec = jnp.concatenate([n1g, n1b, ob, n2g, n2b, ub, ib])
    vec = lax.reduce_precision(vec, 8, 7)
    vec = jnp.broadcast_to(jnp.pad(vec, (0, -vec.shape[0] % 128)), (8, vec.shape[0] + -vec.shape[0] % 128))
    hidden = wi.shape[1]
    ru = hidden // F
    (a1T, kaug, v, kT, qn, qT, oT, lse, wc, wo_own, xs, dxl, dx2, ga, gb, lo, vin, vrows) = first(
        F, parent_row, tokens[0], cotangent[0], (wq, wk, wv, wo, wi, wu), vec, n)
    gt, gq, fina, finb, vout = last(
        F, lax.axis_size("dp"), parent_row, (a1T, kaug, v, kT, qn, qT, oT, lse), wc, wo_own, xs, dxl, dx2,
        ga.reshape(F // 2, 2, -1, width), gb.reshape(F // 2, 2, -1, width), vin, vrows)
    lo, gt, gwq, gwk, gwv, gwo, gwi, gwu = finish(F, lo, gt, fina, finb, gq, hidden)
    sv = lax.dynamic_slice_in_dim(vout[:6], fi * n, n, 1)
    sib = lax.dynamic_slice_in_dim(vout[6:6 + hidden // width].reshape(-1), fi * ru, ru, 0)
    return (lo[None], gt[None], sv[0], sv[1], gwq, gwk, gwv, gwo, sv[2], sv[3], sv[4], gwi, sib, gwu, sv[5])


def solution(mesh):
    tok = P(("dp", "fsdp"), None, None, None)
    v, m = P("fsdp"), P("fsdp", None)
    return jax.shard_map(
        on_device,
        mesh=mesh,
        in_specs=(tok, P(), v, v, m, m, m, m, v, v, v, m, v, m, v, tok),
        out_specs=(tok, tok, v, v, m, m, m, m, v, v, v, m, v, m, v),
        check_vma=False,
    )
```

```python
import functools
import math

import jax
import jax.numpy as jnp
import ml_dtypes
import numpy as np
from jax import lax
from jax.experimental import pallas as pl
from jax.experimental.pallas import tpu as pltpu
from jax.sharding import PartitionSpec as P

H = 8
T = 256
f32, bf16 = jnp.float32, jnp.bfloat16
VM = pl.BlockSpec(memory_space=pltpu.VMEM)
SM = pl.BlockSpec(memory_space=pltpu.SMEM)


def mm(a, b):
    return jnp.dot(a, b, preferred_element_type=f32)


def mm_tn(a, b):
    return lax.dot_general(a, b, (((0,), (0,)), ((), ())), preferred_element_type=f32)


def mm_nt(a, b):
    return lax.dot_general(a, b, (((1,), (1,)), ((), ())), preferred_element_type=f32)


def iota(shape, dim):
    return lax.broadcasted_iota(jnp.int32, shape, dim)


def chosen(par, read):
    out = read(0)
    for b in range(1, 4):
        out = jnp.where(par == b + 1, read(b), out)
    return out


def attend(heads, seg, parents_ref, kaug_ref, qT_ref, vT_ref, oT_ref, lse_ref, s_refs, hook):
    ntr = 8 * seg // T
    vr = vT_ref.shape[0] // heads
    causal_t = iota((T, T), 0) <= iota((T, T), 1)
    causal_b = iota((seg, seg), 0) <= iota((seg, seg), 1)
    G = heads

    def group(g, _):
        hook(0)
        hs = [g * G + e for e in range(G)]
        hk = [pl.ds(pl.multiple_of(h * 128, 128), 128) for h in hs]
        hv = [pl.ds(pl.multiple_of(h * vr, vr), vr) for h in hs]

        def keys(e, blk, n):
            return kaug_ref[pl.ds(blk, n), :, hk[e]].reshape(n * seg, 128)

        def finish(e, cols, m, acc):
            h = hs[e]
            l = acc[64:65, :]
            oT_ref[pl.ds(pl.multiple_of(h * 64, 64), 64), cols] = (acc[:64] / l).astype(bf16)
            lse_ref[pl.ds(pl.multiple_of(h * 8, 8), 8), cols] = jnp.broadcast_to(m + jnp.log(l), (8, T))

        def full_scores(e, q, n):
            m = None
            for c in range(n):
                s = mm(keys(e, 2 * c, 2), q)
                s_refs[e][c * T:(c + 1) * T, :] = s
                cm = jnp.max(s, axis=0, keepdims=True)
                m = cm if m is None else jnp.maximum(m, cm)
            return m

        def full_mix(e, m, n, acc):
            for c in range(n):
                p = jnp.exp(s_refs[e][c * T:(c + 1) * T, :] - m).astype(bf16)
                t = mm(vT_ref[hv[e], c * T:(c + 1) * T], p)
                acc = t if acc is None else acc + t
            return acc

        for t in range(ntr):
            cols = slice(t * T, (t + 1) * T)
            sds, ms = [], []
            for e in range(G):
                q = qT_ref[hk[e], cols]
                sd = jnp.where(causal_t, mm(keys(e, 2 * t, 2), q), -1e30)
                m = jnp.max(sd, axis=0, keepdims=True)
                if t:
                    m = jnp.maximum(m, full_scores(e, q, t))
                sds.append(sd)
                ms.append(m)
            for e in range(G):
                acc = mm(vT_ref[hv[e], cols], jnp.exp(sds[e] - ms[e]).astype(bf16))
                acc = full_mix(e, ms[e], t, acc)
                finish(e, cols, ms[e], acc)

        def tail_tile(i, leaf):
            b0 = 8 + 2 * i
            cols = pl.ds(pl.multiple_of(b0 * seg, T), T)
            pars = [parents_ref[b0 + half - 7] for half in range(2)] if leaf else None
            exts, ms = [], []
            for e in range(G):
                q = qT_ref[hk[e], cols]
                m = full_scores(e, q, ntr)
                ext = []
                for x in range(2 if leaf else 1):
                    pieces = []
                    for half in range(2):
                        kk = keys(e, b0 + half, 1) if x == 0 else chosen(pars[half], lambda b: keys(e, 8 + b, 1))
                        s = mm(kk, q[:, half * seg:(half + 1) * seg])
                        if x == 0:
                            s = jnp.where(causal_b, s, -1e30)
                        pieces.append(s)
                    s = jnp.concatenate(pieces, axis=1)
                    m = jnp.maximum(m, jnp.max(s, axis=0, keepdims=True))
                    ext.append(s)
                exts.append(ext)
                ms.append(m)
            for e in range(G):
                acc = None
                for x, s in enumerate(exts[e]):
                    p = jnp.exp(s - ms[e]).astype(bf16)
                    t = []
                    for half in range(2):
                        if x == 0:
                            vv = vT_ref[hv[e], pl.ds(pl.multiple_of((b0 + half) * seg, seg), seg)]
                        else:
                            vv = chosen(pars[half], lambda b: vT_ref[hv[e], (8 + b) * seg:(9 + b) * seg])
                        t.append(mm(vv, p[:, half * seg:(half + 1) * seg]))
                    t = jnp.concatenate(t, axis=1)
                    acc = t if acc is None else acc + t
                acc = full_mix(e, ms[e], ntr, acc)
                finish(e, cols, ms[e], acc)

        hook(1)
        lax.fori_loop(0, 2, lambda i, c: (tail_tile(i, False), c)[1], 0)
        hook(2)
        lax.fori_loop(2, 6, lambda i, c: (hook(3, i), tail_tile(i, True), c)[2], 0)
        return 0

    lax.fori_loop(0, heads // G, group, 0)


def attend_back(heads, seg, parents_ref, kaug_ref, v_ref, qT_ref, doT_ref, kT_ref, do_ref, qn_ref,
                oT_ref, lse_ref, dqT_ref, dqkv_ref, accK, accV, hook):
    ntr = 8 * seg // T
    causal_t = iota((T, T), 0) <= iota((T, T), 1)
    causal_b = iota((seg, seg), 0) <= iota((seg, seg), 1)
    low_rows = iota((128, T), 0) < 64
    low_lanes = iota((T, 128), 1) < 64

    def pair(pr, _):
        hook("start", pr)
        lanes = pl.ds(pl.multiple_of(pr * 128, 128), 128)
        hk = [pl.ds(pl.multiple_of(pr * 256 + 128 * e, 128), 128) for e in range(2)]
        h64 = [pl.ds(pl.multiple_of(pr * 128 + 64 * e, 64), 64) for e in range(2)]
        accK[...] = jnp.zeros_like(accK)
        accV[...] = jnp.zeros_like(accV)

        def stack(x):
            z = jnp.zeros_like(x)
            return jnp.concatenate([jnp.where(low_lanes, x, z), jnp.where(low_lanes, z, x)], axis=0)

        def prep(cols):
            doT = doT_ref[lanes, cols]
            z = jnp.zeros_like(doT)
            prod = doT.astype(f32) * oT_ref[lanes, cols].astype(f32)
            q, do, lse, delta = [], [], [], []
            for e in range(2):
                q.append(qT_ref[hk[e], cols])
                do.append(jnp.where(low_rows, doT, z) if e == 0 else jnp.where(low_rows, z, doT))
                at = pl.multiple_of((pr * 2 + e) * 8, 8)
                lse.append(jnp.max(lse_ref[pl.ds(at, 8), cols], axis=0, keepdims=True))
                delta.append(jnp.sum(prod[64 * e:64 * e + 64], axis=0, keepdims=True))
            return q, do, lse, delta, stack(do_ref[cols, lanes]), stack(qn_ref[cols, lanes])

        def front(blk, n, sl, args, mask, par=None):
            q, do, lse, delta, rv, rk = args

            def rows_of(ref, at):
                if par is None:
                    return ref[pl.ds(blk, n), :, at].reshape(n * seg, 128)
                return chosen(par, lambda b: ref[8 + b, :, at])

            vv = rows_of(v_ref, lanes)
            s = [mm(rows_of(kaug_ref, hk[e]), q[e][:, sl]) for e in range(2)]
            dp = [mm(vv, do[e][:, sl]) for e in range(2)]
            return s, dp

        def rear(blk, n, sl, args, mask, par, s, dp):
            q, do, lse, delta, rv, rk = args
            ps, dss, dq = [], [], []
            for e in range(2):
                p = jnp.exp(s[e] - lse[e][:, sl])
                if mask is not None:
                    p = jnp.where(mask, p, 0.0)
                dss.append((p * (dp[e] - delta[e][:, sl])).astype(bf16))
                ps.append(p.astype(bf16))
            for e in range(2):
                if par is None:
                    kT = kT_ref[h64[e], pl.ds(pl.multiple_of(blk * seg, seg), n * seg)]
                else:
                    kT = chosen(par, lambda b: kT_ref[h64[e], (8 + b) * seg:(9 + b) * seg])
                dq.append(mm(kT, dss[e]))
            if sl.stop - sl.start != T:
                rv = jnp.concatenate([rv[sl], rv[T + sl.start:T + sl.stop]], axis=0)
                rk = jnp.concatenate([rk[sl], rk[T + sl.start:T + sl.stop]], axis=0)
            av = mm(jnp.concatenate(ps, axis=1), rv)
            ak = mm(jnp.concatenate(dss, axis=1), rk)
            if par is None:
                accV[pl.ds(blk, n)] += av.reshape(n, seg, 128)
                accK[pl.ds(blk, n)] += ak.reshape(n, seg, 128)
            else:
                for b in range(4):
                    here = jnp.where(par == b + 1, 1.0, 0.0)
                    accK[8 + b] += ak * here
                    accV[8 + b] += av * here
            return dq

        def run(items):
            out = []
            ready = []
            for item in items:
                ready.append((item, front(*item)))
                if len(ready) > 2:
                    it, (s, dp) = ready.pop(0)
                    out.append(rear(*it, s, dp))
            for it, (s, dp) in ready:
                out.append(rear(*it, s, dp))
            return out

        def emit(cols, dq):
            for e in range(2):
                dqT_ref[64 * e:64 * e + 64, cols] = (dq[e] * 0.125).astype(bf16)

        full = slice(0, T)
        for t in range(ntr):
            cols = slice(t * T, (t + 1) * T)
            args = prep(cols)
            items = [(2 * t, 2, full, args, causal_t, None)] + [(2 * c, 2, full, args, None, None) for c in range(t)]
            res = run(items)
            emit(cols, [sum(x[e] for x in res) for e in range(2)])

        def tail_tile(i, leaf):
            b0 = 8 + 2 * i
            cols = pl.ds(pl.multiple_of(b0 * seg, T), T)
            args = prep(cols)
            items = []
            for half in range(2):
                sl = slice(half * seg, (half + 1) * seg)
                items.append((b0 + half, 1, sl, args, causal_b, None))
                if leaf:
                    items.append((8, 1, sl, args, None, parents_ref[b0 + half - 7]))
            k = len(items) // 2
            items += [(2 * c, 2, full, args, None, None) for c in range(ntr)]
            res = run(items)
            dq = []
            for e in range(2):
                halves = [sum(x[e] for x in res[h * k:(h + 1) * k]) for h in range(2)]
                dq.append(jnp.concatenate(halves, axis=1) + sum(x[e] for x in res[2 * k:]))
            emit(cols, dq)

        hook("mid", pr)
        lax.fori_loop(0, 2, lambda i, c: (tail_tile(i, False), c)[1], 0)
        hook("late", pr)
        lax.fori_loop(2, 6, lambda i, c: (hook("leaf", pr, i), tail_tile(i, True), c)[2], 0)
        first = pr * 384

        def put(i, x):
            dqkv_ref[:, :, pl.ds(pl.multiple_of(first + 128 * i, 128), 128)] = x

        put(0, dqT_ref[...].T.reshape(20, seg, 128))
        put(1, accK[...].astype(bf16))
        put(2, accV[...].astype(bf16))
        hook("end", pr)
        return 0

    lax.fori_loop(0, heads // 2, pair, 0)


class Dense:
    def __init__(self, rows, width, oF_ref, dy_ref, woi_ref, wu_ref, rows_ref, dxl_ref, dx2_ref, ga_ref, gb_ref, vin_ref,
                 gs, dus):
        self.__dict__.update({k: v for k, v in locals().items() if k != "self"})
        self.hidden = wu_ref.shape[0]
        self.tiles = self.hidden // width

    def chunk(self, start, x, y_ref, a2_ref=None):
        back = a2_ref is not None
        width, rows_ref, vin_ref = self.width, self.rows_ref, self.vin_ref
        woi_ref, wu_ref = self.woi_ref, self.wu_ref
        c1 = math.sqrt(2.0 / math.pi)
        c2 = c1 * 0.044715

        def vector(i):
            return rows_ref[0:1, i * width:(i + 1) * width]

        def add_sum(i, x):
            vin_ref[i:i + 1, :] += jnp.sum(x, axis=0, keepdims=True)

        at = pl.ds(pl.multiple_of(start, 128), x.shape[0])
        x2 = fold(x) + mm_tn(self.oF_ref[:, at], woi_ref[:, 0:width]) + vector(2)
        centred = x2 - jnp.mean(x2, axis=-1, keepdims=True)
        inv = lax.rsqrt(jnp.mean(centred * centred, axis=-1, keepdims=True) + 1e-06)
        unit = centred * inv
        a2 = (unit * vector(3) + vector(4)).astype(bf16)
        if back:
            dy = self.dy_ref[start // x.shape[0]]
        y = x2 + vector(5)
        da2 = None
        for t in range(self.tiles):
            ft = slice(t * width, (t + 1) * width)
            wt = slice(width + t * width, width + (t + 1) * width)
            u = mm(a2, woi_ref[:, wt]) + rows_ref[0:1, 6 * width + t * width:6 * width + (t + 1) * width]
            uu = u * u
            th = jnp.tanh(u * (c1 + c2 * uu))
            p = 0.5 + 0.5 * th
            g = (u * p).astype(bf16)
            y = y + mm(g, wu_ref[ft, :])
            if not back:
                continue
            slope = p + u * (0.5 - 0.5 * th * th) * (c1 + 3.0 * c2 * uu)
            self.gs[at, ft] = g
            du = (mm_nt(dy, wu_ref[ft, :]) * slope).astype(bf16)
            self.dus[at, ft] = du
            add_sum(6 + t, fold(du))
            d = mm_nt(du, woi_ref[:, wt])
            da2 = d if da2 is None else da2 + d
        y_ref[...] = y.astype(bf16)
        if not back:
            return
        a2_ref[...] = a2
        dyf = fold(dy)
        dn = da2 * vector(3)
        m1 = jnp.mean(dn, axis=-1, keepdims=True)
        m2 = jnp.mean(dn * unit, axis=-1, keepdims=True)
        dx2 = dyf + (dn - m1 - unit * m2) * inv
        dxl = dx2.astype(bf16)
        self.dx2_ref[at, :] = dx2
        self.dxl_ref[at, :] = dxl
        add_sum(2, fold(dxl))
        add_sum(3, da2 * unit)
        add_sum(4, da2)
        add_sum(5, dyf)

    def gradients(self, F, a2):
        width, hidden, tiles, gb_ref = self.width, self.hidden, self.tiles, self.gb_ref
        r, ru = width // F, hidden // F
        nb = T // ru
        dy = self.dy_ref[...].reshape(2 * self.rows, width)

        def outer(t, c):
            val = mm_tn(self.gs[:, pl.ds(pl.multiple_of(t * T, T), T)], dy).astype(bf16)
            self.ga_ref[pl.ds(t * nb, nb)] = val.reshape(nb, ru, width)
            return c

        lax.fori_loop(0, hidden // T, outer, 0)
        a2T = a2.T
        for t in range(tiles):
            val = mm(a2T, self.dus[:, t * width:(t + 1) * width]).astype(bf16)
            gb_ref[:, t * r:(t + 1) * r, :] = val.reshape(F, r, width)
        val = mm(self.oF_ref[...], self.dxl_ref[...]).astype(bf16)
        gb_ref[:, tiles * r:(tiles + 1) * r, :] = val.reshape(F, r, width)


def slope_parts(head, head_count, length):
    x = np.float32(2.0 ** (2.0 - 4.0 * head / head_count) / length)
    out = []
    for _ in range(3):
        low = np.float32(ml_dtypes.bfloat16(x))
        out.append(float(low))
        x = np.float32(x - low)
    return out


def remote(src, dst, send_sem, recv_sem, target):
    return pltpu.make_async_remote_copy(
        src_ref=src, dst_ref=dst, send_sem=send_sem, recv_sem=recv_sem,
        device_id={"fsdp": target}, device_id_type=pl.DeviceIdType.MESH)


def where_am_i(F):
    f = lax.axis_index("fsdp")
    place = lax.rem(f + 2, F)
    part = lax.rem(place, 4)
    half = part // 2
    core = lax.rem(f, 2)
    base = place - part
    partner = lax.rem(base + lax.rem(part + 2, 4) + F - 2, F)
    sibling = f + 1 - 2 * core
    return f, part, half, core, partner, sibling


def greet(F, f, core, sibling, across):
    barrier = pltpu.get_barrier_semaphore()
    peers = [{"fsdp": lax.rem(f + 2 * d, F)} for d in range(1, F // 2)] + [{"fsdp": sibling}]
    if across:
        plane = lax.axis_index("dp")
        peers.append({"dp": plane + 1 - 2 * lax.rem(plane, 2)})
    for peer in peers:
        pl.semaphore_signal(barrier, inc=1, device_id=peer, device_id_type=pl.DeviceIdType.MESH)
    pl.semaphore_wait(barrier, len(peers))


def first_kernel(F, n, parents_ref, tok_ref, cot_ref, wq_ref, wk_ref, wv_ref, wo_ref, wi_ref, wu_ref, vec_ref,
                 a1T_out, kaug_out, v_out, kT_out, qn_out, qT_out, oT_out, lse_out, wc_out, wo_out, xs_out, dxl_out,
                 dx2_out, ga_out, gb_out, lo_ref, vin_ref, rows_ref,
                 xt_ref, a1T_ref, kaug_ref, v_ref, kT_ref, qn_ref, qT_ref, oT_ref, lse_ref, oF_ref, dy_ref,
                 wqkv_ref, woi_ref, wuf_ref, dxl_ref, dx2_ref, ga_ref, gb_ref, gs, dus,
                 vecs, vT_scr, s_scr, tsend, trecv, gsend, grecv, zsend, zrecv, osem):
    f, part, half, core, partner, sibling = where_am_i(F)
    rows, width = tok_ref.shape[1:]
    seg = rows // 5
    heads = H // 2
    hw = heads * 64
    tree = 4 * rows
    r = wq_ref.shape[0]
    ru = wu_ref.shape[0]
    part1 = part + 1 - 2 * core
    part2 = lax.rem(part + 2, 4)
    part3 = lax.rem(part1 + 2, 4)

    own = pl.ds(pl.multiple_of(f * r, r), r)
    ownu = pl.ds(pl.multiple_of(f * ru, ru), ru)
    vecs[f] = vec_ref[...]
    blocks = [wq_ref, wk_ref, wv_ref, wo_ref] + [
        wi_ref.at[:, c * width:(c + 1) * width] for c in range(wi_ref.shape[1] // width)]
    staged = [pltpu.make_async_copy(b, dx2_ref.at[i * r:(i + 1) * r], osem.at[27 + i]) for i, b in enumerate(blocks)]
    last_rows = slice(len(blocks) * r, len(blocks) * r + ru)
    staged.append(pltpu.make_async_copy(wu_ref, dx2_ref.at[last_rows], osem.at[27 + len(blocks)]))
    for c in staged:
        c.start()
    for i in range(3):
        staged[i].wait()
        wqkv_ref[own, i * width:(i + 1) * width] = dx2_ref[i * r:(i + 1) * r].astype(bf16)

    greet(F, f, core, sibling, lax.axis_size("dp") % 2 == 0)

    def slot(g, src):
        if g == 0:
            return vecs.at[src]
        if g == 3:
            return wuf_ref.at[pl.ds(pl.multiple_of(src * ru, ru), ru)]
        ref = wqkv_ref if g == 1 else woi_ref
        return ref.at[pl.ds(pl.multiple_of(src * r, r), r)]

    planes = lax.axis_size("dp")
    plane = lax.axis_index("dp")
    shared = r % 32 == 0 and planes % 2 == 0
    parity = lax.rem(plane, 2)
    opposite = plane + 1 - 2 * parity
    chips = range(1, F // 2)

    def part_of(g, src, which=None):
        if g != 2 or not shared or which is None:
            return slot(g, src)
        return woi_ref.at[pl.ds(pl.multiple_of(src * r + which * (r // 2), 16), r // 2)]

    def source(d, of=None):
        return lax.rem((f if of is None else of) + F - 2 * d, F)

    def direct(g, d):
        if d == 0:
            return remote(slot(g, f), slot(g, f), gsend.at[g, 0], grecv.at[g, 0], sibling)
        return remote(part_of(g, f, parity), part_of(g, f, parity), gsend.at[g, d], grecv.at[g, d], lax.rem(f + 2 * d, F))

    def came(g, d):
        ref = slot(g, sibling) if d == 0 else part_of(g, source(d), parity)
        remote(ref, ref, gsend.at[g, d], grecv.at[g, d], sibling).wait_recv()

    def forward(g, d, of=None):
        ref = part_of(g, source(d, of), parity)
        return remote(ref, ref, gsend.at[g, F // 2 + d], grecv.at[g, F // 2 + d], sibling)

    def across(d, which):
        ref = part_of(2, source(d), which)
        return pltpu.make_async_remote_copy(
            src_ref=ref, dst_ref=ref, send_sem=zsend.at[d], recv_sem=zrecv.at[d],
            device_id={"dp": opposite}, device_id_type=pl.DeviceIdType.MESH)

    def forward_across(d, of=None):
        ref = part_of(2, source(d, of), 1 - parity)
        return remote(ref, ref, zsend.at[F // 2 + d], zrecv.at[F // 2 + d], sibling)

    def send_all(g):
        for d in range(F // 2):
            direct(g, d).start()

    def pass_on(g):
        for d in chips:
            came(g, d)
            if g == 2 and shared:
                across(d, parity).start()
            forward(g, d).start()

    def pass_across():
        if shared:
            for d in chips:
                across(d, 1 - parity).wait_recv()
                forward_across(d).start()

    def receive_rest(g):
        came(g, 0)
        for d in chips:
            forward(g, d, sibling).wait_recv()
            if g == 2 and shared:
                forward_across(d, sibling).wait_recv()

    x_out = remote(tok_ref.at[1 - half], xt_ref.at[part], tsend.at[0], trecv.at[0], partner)
    x_sib = remote(tok_ref.at[half], xt_ref.at[part], tsend.at[1], trecv.at[1], sibling)
    x_fwd = remote(xt_ref.at[part2], xt_ref.at[part2], tsend.at[2], trecv.at[2], sibling)
    dy_out = remote(cot_ref.at[1 - half], dy_ref.at[half], tsend.at[3], trecv.at[3], partner)
    x_own = pltpu.make_async_copy(tok_ref.at[half], xt_ref.at[part], osem.at[20])
    dy_own = pltpu.make_async_copy(cot_ref.at[half], dy_ref.at[half], tsend.at[4])

    send_all(0)
    send_all(1)
    x_out.start()
    x_sib.start()
    x_own.start()
    dy_own.start()
    for c in staged[3:]:
        c.wait()
    for i in range(3, len(blocks)):
        woi_ref[own, (i - 3) * width:(i - 2) * width] = dx2_ref[i * r:(i + 1) * r].astype(bf16)
    wuf_ref[ownu, :] = dx2_ref[last_rows].astype(bf16)
    pass_on(0)
    pass_on(1)
    receive_rest(0)

    table = jnp.max(vecs[...], axis=1).astype(bf16)
    words = table.shape[1]

    def vector_row(first, m, length):
        col = iota((words, length), 1)
        pick = iota((words, length), 0) == first + (col & (m - 1))
        spread = mm(table, pick.astype(bf16))
        shift = m.bit_length() - 1
        mine = iota((F, length), 0) == (iota((F, length), 1) >> shift)
        return jnp.sum(jnp.where(mine, spread, 0.0), axis=0, keepdims=True)

    def all_rows(first, last):
        for i in range(first, last):
            rows_ref[:, i * width:(i + 1) * width] = jnp.broadcast_to(vector_row(i * n, n, width), (8, width))

    all_rows(0, 2)
    hidden = rows_ref.shape[1] - 6 * width
    receive_rest(1)

    lane = iota((seg, 128), 1)
    offs = iota((seg, 128), 0)
    arow = iota((64, rows), 0)

    def project(p):
        x = xt_ref[p].astype(f32)
        gain = rows_ref[0:1, 0:width]
        shift = rows_ref[0:1, width:2 * width]
        mean = jnp.mean(x, axis=-1, keepdims=True)
        x = x - mean
        inv = lax.rsqrt(jnp.mean(x * x, axis=-1, keepdims=True) + 1e-06)
        a1 = (x * inv * gain + shift).astype(bf16)

        def proj(i):
            return mm(a1, wqkv_ref[:, pl.ds(pl.multiple_of(i * width + core * hw, hw), hw)])

        cols = pl.ds(pl.multiple_of(p * rows, rows), rows)
        a1T_ref[:, cols] = a1.T
        q = (proj(0) * 0.125).astype(bf16)
        qn_ref[cols, :] = q
        qT = q.T
        k = proj(1).astype(bf16)
        kT_ref[:, cols] = k.T
        v = proj(2).astype(bf16)
        v_ref[pl.ds(p * 5, 5)] = v.reshape(5, seg, hw)
        vT = v.T
        for h in range(heads):
            a, b = slope_parts(h, H, tree), slope_parts(heads + h, H, tree)
            aug = jnp.zeros((64, rows), f32)
            for j in range(3):
                s = jnp.where(core == 0, a[j], b[j])
                aug = jnp.where((arow == j) | (arow == j + 3), s, aug)
            aug = aug.astype(bf16)
            lo, hi = 128 * h + 64 * (h % 2), 128 * h + 64 - 64 * (h % 2)
            qT_ref[lo:lo + 64, cols] = qT[64 * h:64 * h + 64]
            qT_ref[hi:hi + 64, cols] = aug
            vT_scr[80 * h:80 * h + 64, cols] = vT[64 * h:64 * h + 64]
            vT_scr[80 * h + 64:80 * h + 80, cols] = jnp.ones((16, rows), bf16)
        for b in range(5):
            blk = p * 5 + b
            start = jnp.where(blk < 8, blk * seg, jnp.where(blk < 12, 8 * seg, 9 * seg))
            spot = offs + start
            hi = (spot & -8).astype(f32)
            lo = (spot & 7).astype(f32)
            for h in range(heads):
                at = 64 - 64 * (h % 2)
                l = lane - at
                aug = jnp.where((l >= 0) & (l < 3), hi, jnp.where((l >= 3) & (l < 6), lo, 0.0)).astype(bf16)
                keep = (lane < 64) if h % 2 == 0 else (lane >= 64)
                kk = k[b * seg:(b + 1) * seg, 128 * (h // 2):128 * (h // 2) + 128]
                kaug_ref[blk, :, 128 * h:128 * h + 128] = jnp.where(keep, kk, aug)

    x_own.wait()
    x_sib.wait_recv()

    def visit(i, c):
        @pl.when(i == 1)
        def _():
            all_rows(2, 6)
            rows_ref[:, 6 * width:] = jnp.broadcast_to(vector_row(6 * n, hidden // F, hidden), (8, hidden))
            x_out.wait_recv()
            x_fwd.start()
            send_all(2)
            send_all(3)

        @pl.when(i == 3)
        def _():
            x_fwd.wait_recv()

        project(jnp.where(i == 0, part, jnp.where(i == 1, part1, jnp.where(i == 2, part2, part3))))
        return c

    lax.fori_loop(0, 4, visit, 0)
    wc_copies = []
    for i in range(heads // 2):
        for k in range(3):
            src = wqkv_ref.at[:, pl.ds(pl.multiple_of(k * width + core * hw + 128 * i, 128), 128)]
            at = 384 * i + 128 * k
            wc_copies.append(pltpu.make_async_copy(src, wc_out.at[:, at:at + 128], osem.at[21 + 3 * i + k]))

    outs = [(a1T_ref, a1T_out), (kaug_ref, kaug_out), (v_ref, v_out), (kT_ref, kT_out), (qn_ref, qn_out),
            (qT_ref, qT_out), (xt_ref.at[core], xs_out.at[0]), (xt_ref.at[core + 2], xs_out.at[1]),
            (oT_ref, oT_out), (lse_ref, lse_out),
            (woi_ref.at[pl.ds(pl.multiple_of(core * hw, hw), hw), 0:width], wo_out),
            (dxl_ref.at[0:rows], dxl_out.at[0]), (dxl_ref.at[rows:2 * rows], dxl_out.at[1]),
            (dx2_ref.at[0:rows], dx2_out.at[0]), (dx2_ref.at[rows:2 * rows], dx2_out.at[1]), (ga_ref, ga_out), (gb_ref, gb_out)]
    copies = [pltpu.make_async_copy(a, b, osem.at[i]) for i, (a, b) in enumerate(outs)]
    for c in copies[:8] + wc_copies:
        c.start()

    s_refs = [dx2_ref.at[0:8 * seg, 0:T], dx2_ref.at[0:8 * seg, T:2 * T], s_scr.at[0], s_scr.at[1]]

    def hook(stage, i=None):
        if stage == 1:
            pass_on(2)
        if stage == 2:
            dy_out.start()

    attend(heads, seg, parents_ref, kaug_ref, qT_ref, vT_scr, oT_ref, lse_ref, s_refs, hook)

    other = 1 - core
    sent = []
    for i in range(2):
        cols = pl.ds(pl.multiple_of((other + 2 * i) * rows, rows), rows)
        at = (pl.ds(pl.multiple_of(core * hw, hw), hw), slice(i * rows, (i + 1) * rows))
        c = remote(oT_ref.at[:, cols], oF_ref.at[at], tsend.at[5 + i], trecv.at[5 + i], sibling)
        c.start()
        sent.append(c)
    for i in range(2):
        mine = pl.ds(pl.multiple_of((core + 2 * i) * rows, rows), rows)
        at = (pl.ds(pl.multiple_of(core * hw, hw), hw), slice(i * rows, (i + 1) * rows))
        oF_ref[at] = oT_ref[:, mine]
    copies[8].start()
    copies[9].start()
    pass_across()
    pass_on(3)
    receive_rest(2)
    copies[10].start()
    for c in sent:
        c.wait_recv()
    receive_rest(3)
    dy_own.wait()

    vin_ref[...] = jnp.zeros_like(vin_ref)
    dense = Dense(rows, width, oF_ref, dy_ref, woi_ref, wuf_ref, rows_ref, dxl_ref, dx2_ref, ga_ref, gb_ref, vin_ref,
                  gs, dus)
    y_out = remote(xt_ref.at[other + 2 * (1 - half)], lo_ref.at[half], tsend.at[7], trecv.at[7], partner)
    keep_y = pltpu.make_async_copy(xt_ref.at[other + 2 * half], lo_ref.at[half], osem.at[18])
    dense.chunk((1 - half) * rows, xt_ref[core + 2 * (1 - half)], xt_ref.at[other + 2 * (1 - half)])
    y_out.start()
    copies[6].wait()
    copies[7].wait()
    x_fwd.wait_send()

    def dense_step(s, c):
        i = jnp.where(s == 0, half, 1 - half)

        @pl.when(s == 1)
        def _():
            keep_y.start()
            dy_out.wait_recv()

        dense.chunk(i * rows, xt_ref[core + 2 * i], xt_ref.at[jnp.where(s == 0, other, core) + 2 * i], xt_ref.at[core + 2 * i])
        return c

    lax.fori_loop(0, 2, dense_step, 0)
    for c in copies[11:15]:
        c.start()
    dense.gradients(F, jnp.concatenate([xt_ref[core], xt_ref[core + 2]], axis=0))
    copies[15].start()
    copies[16].start()
    for c in copies[:6] + copies[8:] + wc_copies + [keep_y]:
        c.wait()
    y_out.wait()
    dy_out.wait_send()
    x_out.wait_send()
    x_sib.wait_send()
    for c in sent:
        c.wait_send()
    for g in range(4):
        for d in range(F // 2):
            direct(g, d).wait_send()
        for d in chips:
            forward(g, d).wait_send()
    if shared:
        for d in chips:
            across(d, parity).wait_send()
            forward_across(d).wait_send()


def first(F, parents, tokens, cotangent, weights, vec, n):
    _, rows, width = tokens.shape
    tree = 4 * rows
    heads = H // 2
    hw = heads * 64
    seg = rows // 5
    hidden = weights[4].shape[1]
    r, ru = width // F, hidden // F
    R1 = (hidden // width + 1) * r
    two = 2 * rows
    keep = [((width, tree), bf16), ((20, seg, heads * 128), bf16), ((20, seg, hw), bf16), ((hw, tree), bf16),
            ((tree, hw), bf16), ((heads * 128, tree), bf16), ((hw, tree), bf16), ((heads * 8, tree), f32)]
    out = keep + [((width, 3 * hw), bf16), ((hw, width), bf16), ((2, rows, width), bf16), ((2, rows, width), bf16),
                  ((2, rows, width), f32), ((F, ru, width), bf16), ((F, R1, width), bf16), ((2, rows, width), bf16),
                  ((16, width), f32), ((8, 6 * width + hidden), f32)]
    scratch = [((4, rows, width), bf16)] + keep + [
        ((2 * hw, two), bf16), ((2, rows, width), bf16), ((width, 3 * width), bf16), ((width, width + hidden), bf16),
        ((hidden, width), bf16), ((two, width), bf16),
        ((two, width), f32), ((F, ru, width), bf16), ((F, R1, width), bf16), ((two, hidden), bf16),
        ((two, hidden), bf16), ((F,) + vec.shape, f32), ((heads * 80, tree), bf16), ((2, 8 * seg, T), f32)]
    ANY = pl.BlockSpec(memory_space=pl.ANY)
    dma = pltpu.SemaphoreType.DMA
    return pl.pallas_call(
        functools.partial(first_kernel, F, n),
        out_shape=[jax.ShapeDtypeStruct(s, d) for s, d in out],
        in_specs=[SM] + [ANY] * 8 + [VM],
        out_specs=[ANY] * 16 + [VM] * 2,
        scratch_shapes=[pltpu.VMEM(s, d) for s, d in scratch] + [
            dma((8,)), dma((8,)), dma((4, F)), dma((4, F)), dma((F,)), dma((F,)), dma((28 + 4 + hidden // width,))],
        name="front",
        compiler_params=pltpu.CompilerParams(vmem_limit_bytes=64 << 20, collective_id=0, has_side_effects=True),
    )(parents, tokens, cotangent, *weights, vec)


def fold(x):
    return x.astype(f32)


class Chain:
    def __init__(self, F, f, sums, got, block, zgot, final, send, recv, stages=2):
        self.square = F == 8 and stages == 2
        self.F, self.f, self.sums, self.got, self.block = F, f, sums, got, block
        self.zgot, self.final, self.send, self.recv = zgot, final, send, recv
        self.chip = f // 2
        self.chips = F // 2
        self.planes = lax.axis_size("dp")
        self.plane = lax.axis_index("dp")
        self.rows = sums.shape[1]
        self.zrows = block.shape[0] // self.planes

    def _b(self, d):
        return remote(self.sums.at[lax.rem(self.chip + d, self.chips)], self.got.at[d - 1],
                      self.send.at[d], self.recv.at[d], lax.rem(self.f + 2 * d, self.F))

    def _square(self):
        core = lax.rem(self.f, 2)
        x, y = lax.rem(self.chip, 2), self.chip // 2
        along_x, along_y = 2 * y + 1 - x, 2 * (1 - y) + x
        first = jnp.where(core == 0, along_x, along_y)
        second = jnp.where(core == 0, along_y, along_x)
        last = 2 * (1 - y) + 1 - x
        one = [remote(self.sums.at[first], self.got.at[0], self.send.at[1], self.recv.at[1], 2 * first + core),
               remote(self.sums.at[last], self.got.at[1], self.send.at[2], self.recv.at[2], 2 * first + core)]
        two = remote(self.sums.at[second], self.got.at[2], self.send.at[3], self.recv.at[3], 2 * second + core)
        return one, two, second

    def _chunk(self, z):
        return pl.ds(pl.multiple_of(z * self.zrows, 16), self.zrows)

    def _c(self, e):
        z = lax.rem(self.plane + e, self.planes)
        i = self.chips + e
        return pltpu.make_async_remote_copy(
            src_ref=self.block.at[self._chunk(z)], dst_ref=self.zgot.at[e - 1],
            send_sem=self.send.at[i], recv_sem=self.recv.at[i],
            device_id={"dp": z}, device_id_type=pl.DeviceIdType.MESH)

    def _d(self, e, src=None):
        z = lax.rem(self.plane + e, self.planes)
        i = self.chips + self.planes + e
        here = self._chunk(self.plane if src is None else src)
        return pltpu.make_async_remote_copy(
            src_ref=self.final.at[here], dst_ref=self.final.at[here],
            send_sem=self.send.at[i], recv_sem=self.recv.at[i],
            device_id={"dp": z}, device_id_type=pl.DeviceIdType.MESH)

    def start_plane(self):
        if self.square:
            for c in self._square()[0]:
                c.start()
            return
        for d in range(1, self.chips):
            self._b(d).start()

    def mid_plane(self):
        if self.square:
            one, two, second = self._square()
            for c in one:
                c.wait_recv()
            self.sums[second] = (fold(self.sums[second]) + fold(self.got[1])).astype(bf16)
            two.start()

    def start_z(self):
        if self.square:
            self._square()[1].wait_recv()
            total = fold(self.sums[self.chip]) + fold(self.got[0]) + fold(self.got[2])
        else:
            for d in range(1, self.chips):
                self._b(d).wait_recv()
            total = fold(self.sums[self.chip])
            for d in range(1, self.chips):
                total = total + fold(self.got[d - 1])
        self.block[0:self.rows] = total.astype(bf16)
        for e in range(1, self.planes):
            self._c(e).start()

    def start_back(self):
        for e in range(1, self.planes):
            self._c(e).wait_recv()
        here = self._chunk(self.plane)
        total = fold(self.block[here])
        for e in range(1, self.planes):
            total = total + fold(self.zgot[e - 1])
        self.final[here] = total.astype(bf16)
        for e in range(1, self.planes):
            self._d(e).start()

    def receive(self):
        for e in range(1, self.planes):
            self._d(e, lax.rem(self.plane + self.planes - e, self.planes)).wait_recv()

    def close(self):
        if self.square:
            one, two, _ = self._square()
            for c in one + [two]:
                c.wait_send()
        else:
            for d in range(1, self.chips):
                self._b(d).wait_send()
        for e in range(1, self.planes):
            self._c(e).wait_send()
            self._d(e).wait_send()


def last_kernel(F, parents_ref, kaug_h, v_h, qT_h, kT_h, qn_h, oT_h, lse_h, a1T_h, wc_h, wo_h, xs_h, dxl_ref, dx2_h,
                ga_ref, gb_ref, vin_ref, n1_ref,
                gt_ref, gq_ref, fina, finb, vout_ref,
                kaug_ref, v_ref, qT_ref, kT_ref, qn_ref, oT_ref, lse_ref, a1T_ref, wc, wo_scr, xs, dx2s,
                dxs, doT, do, dqT, dqkv, accK, accV, das, dar,
                suma, sumb, gota, gotb, planea, planeb, blka, blkb, za, zb, sum2, got2, blk2, z2, fin2,
                vs, vgot, dxo, tsend, trecv, senda, recva, sendb, recvb, send2, recv2, vsend, vrecv, lsem):
    f, part, half, core, partner, sibling = where_am_i(F)
    planes = lax.axis_size("dp")
    plane = lax.axis_index("dp")
    heads = H // 2
    hw = heads * 64
    _, rows, width = dxl_ref.shape
    chips = F // 2
    other = 1 - core
    tree = 4 * rows
    seg = rows // 5

    pairs = [(wo_h, wo_scr), (qT_h, qT_ref), (kaug_h, kaug_ref), (v_h, v_ref), (kT_h, kT_ref), (qn_h, qn_ref),
             (oT_h, oT_ref), (lse_h, lse_ref), (ga_ref.at[:, core], suma), (gb_ref.at[:, core], sumb), (a1T_h, a1T_ref), (wc_h, wc), (xs_h, xs),
             (dx2_h, dx2s)]
    loads = [pltpu.make_async_copy(a, b, lsem.at[i]) for i, (a, b) in enumerate(pairs)]
    for c in loads:
        c.start()

    barrier = pltpu.get_barrier_semaphore()
    for d in range(1, chips):
        pl.semaphore_signal(barrier, inc=1, device_id={"fsdp": lax.rem(f + 2 * d, F)},
                            device_id_type=pl.DeviceIdType.MESH)
    for e in range(1, planes):
        pl.semaphore_signal(barrier, inc=1, device_id={"dp": lax.rem(plane + e, planes)},
                            device_id_type=pl.DeviceIdType.MESH)
    pl.semaphore_signal(barrier, inc=1, device_id={"fsdp": sibling}, device_id_type=pl.DeviceIdType.MESH)
    pl.semaphore_wait(barrier, chips + planes - 1)

    dx_sw = remote(dxl_ref, dxs, tsend.at[0], trecv.at[0], sibling)
    out_a = remote(ga_ref.at[:, other], gota, tsend.at[1], trecv.at[1], sibling)
    out_b = remote(gb_ref.at[:, other], gotb, tsend.at[7], trecv.at[7], sibling)
    dx_sw.start()
    out_a.start()
    out_b.start()

    def make_do(p, x):
        cols = pl.ds(pl.multiple_of(p * rows, rows), rows)
        d = mm_nt(x, wo_scr[...]).astype(bf16)
        do[cols, :] = d
        doT[:, cols] = d.T

    loads[0].wait()
    lax.fori_loop(0, 2, lambda i, c: (make_do(core + 2 * i, dxl_ref[i]), c)[1], 0)

    one_a = Chain(F, f, suma, planea, blka, za, fina, senda, recva)
    one_b = Chain(F, f, sumb, planeb, blkb, zb, finb, sendb, recvb)

    def add_sibling(load, arrived, mine, got):
        load.wait()
        arrived.wait_recv()

        def add_block(j, c):
            mine[j] = (fold(mine[j]) + fold(got[j])).astype(bf16)
            return c

        lax.fori_loop(0, chips, add_block, 0)

    dx_sw.wait_recv()
    lax.fori_loop(0, 2, lambda i, c: (make_do(other + 2 * i, dxs[i]), c)[1], 0)
    add_sibling(loads[8], out_a, suma, gota)
    one_a.start_plane()
    for c in loads[1:8]:
        c.wait()

    def chain(pr):
        return Chain(F, f, sum2.at[pr], got2.at[pr], blk2.at[pr], z2.at[pr], fin2.at[pr], send2.at[pr], recv2.at[pr], 1)

    two = [chain(0), chain(1)]
    r = width // F
    r2 = 2 * r

    def hook(name, pr, i=None):
        if name == "mid":
            @pl.when(pr == 0)
            def _():
                add_sibling(loads[9], out_b, sumb, gotb)
                one_b.start_plane()

            @pl.when(pr == 1)
            def _():
                one_a.start_z()
        if name == "late":
            @pl.when(pr == 1)
            def _():
                one_b.start_z()
        if name == "leaf":
            @pl.when((pr == 0) & (i == 3))
            def _():
                one_a.mid_plane()

            @pl.when((pr == 1) & (i == 5))
            def _():
                one_a.start_back()
                two[0].start_z()
        if name == "end":
            @pl.when(pr == 0)
            def _():
                one_b.mid_plane()
                for c in loads[10:14]:
                    c.wait()

            g = mm(a1T_ref[...], dqkv[:, :, pl.ds(pl.multiple_of(pr * 384, 384), 384)].reshape(tree, 384)).astype(bf16)
            for j in range(chips):
                sum2[pr, j] = g[j * r2:(j + 1) * r2]
            chain(pr).start_plane()

    attend_back(heads, seg, parents_ref, kaug_ref, v_ref, qT_ref, doT, kT_ref, do, qn_ref, oT_ref, lse_ref,
                dqT, dqkv, accK, accV, hook)

    def da1_of(p):
        return mm_nt(dqkv[pl.ds(p * 5, 5)].reshape(rows, 3 * hw), wc[...])

    def da_out(s):
        i = (1 - half) if s == 0 else half
        return remote(das.at[i], dar.at[i], tsend.at[2 + s], trecv.at[2 + s], sibling)

    dx_out = remote(dxo.at[1 - half], gt_ref.at[half], tsend.at[4], trecv.at[4], partner)
    keep_dx = pltpu.make_async_copy(dxo.at[half], gt_ref.at[half], lsem.at[15])
    vs[0] = vin_ref[...]
    row = iota((16, width), 0)

    def finish_rows(s, c):
        i = jnp.where(s == 0, 1 - half, half)
        das[i] = da1_of(other + 2 * i).astype(bf16)
        for k in range(2):
            @pl.when(s == k)
            def _():
                da_out(k).start()
        x = fold(xs[i])
        x = x - jnp.mean(x, axis=-1, keepdims=True)
        inv = lax.rsqrt(jnp.mean(x * x, axis=-1, keepdims=True) + 1e-06)
        unit = x * inv
        da = da1_of(core + 2 * i)
        for k in range(2):
            @pl.when(s == k)
            def _():
                da_out(k).wait_recv()
        da = da + fold(dar[i])
        dn = da * n1_ref[0:1, 0:width]
        m1 = jnp.mean(dn, axis=-1, keepdims=True)
        m2 = jnp.mean(dn * unit, axis=-1, keepdims=True)
        dxo[i] = (dx2s[i] + (dn - m1 - unit * m2) * inv).astype(bf16)
        gs = jnp.sum(da * unit, axis=0, keepdims=True)
        bs = jnp.sum(da, axis=0, keepdims=True)
        vs[0] += jnp.where(row == 0, gs, 0.0) + jnp.where(row == 1, bs, 0.0)

        @pl.when(s == 0)
        def _():
            dx_out.start()
            one_b.start_back()
            two[0].start_back()

        @pl.when(s == 1)
        def _():
            keep_dx.start()

        return c

    lax.fori_loop(0, 2, finish_rows, 0)
    v_sib = remote(vs.at[0], vgot.at[0], vsend.at[0], vrecv.at[0], sibling)
    v_sib.start()
    two[1].start_z()
    v_sib.wait_recv()
    vgot[chips + plane] = vs[0] + vgot[0]

    def v_z(e, sender):
        return pltpu.make_async_remote_copy(
            src_ref=vgot.at[chips + sender], dst_ref=vgot.at[chips + sender],
            send_sem=vsend.at[chips + e], recv_sem=vrecv.at[chips + e],
            device_id={"dp": lax.rem(plane + e, planes)}, device_id_type=pl.DeviceIdType.MESH)

    for e in range(1, planes):
        v_z(e, plane).start()
    for e in range(1, planes):
        v_z(e, lax.rem(plane + planes - e, planes)).wait_recv()
    total = vgot[chips]
    for z in range(1, planes):
        total = total + vgot[chips + z]
    vs[1] = total
    v_chip = [remote(vs.at[1], vgot.at[d], vsend.at[d], vrecv.at[d], lax.rem(f + 2 * d, F)) for d in range(1, chips)]
    for c in v_chip:
        c.start()
    two[1].start_back()
    one_a.receive()
    one_b.receive()
    s_out = []
    for pr in range(2):
        two[pr].receive()
        c = remote(fin2.at[pr, pl.ds(pl.multiple_of(other * r, r), r)], gq_ref.at[core, pr],
                   tsend.at[5 + pr], trecv.at[5 + pr], sibling)
        c.start()
        gq_ref[core, pr] = fin2[pr, pl.ds(pl.multiple_of(core * r, r), r), :]
        s_out.append(c)
    for c in v_chip:
        c.wait_recv()
    total = vs[1]
    for d in range(1, chips):
        total = total + vgot[d]
    vout_ref[...] = total
    for c in s_out:
        c.wait()
    dx_out.wait()
    keep_dx.wait()
    one_a.close()
    one_b.close()
    for c in two:
        c.close()
    for c in [dx_sw, out_a, out_b, v_sib, da_out(0), da_out(1)] + v_chip:
        c.wait_send()
    for e in range(1, planes):
        v_z(e, plane).wait_send()


def last(F, DP, parents, kept, wc, wo, xs, dxl, dx2, ga, gb, vin, rows_vec):
    a1T, kaug, v, kT, qn, qT, oT, lse = kept
    _, rows, width = dxl.shape
    heads = H // 2
    hw = heads * 64
    tree = 4 * rows
    seg = rows // 5
    chips = F // 2
    r = width // F
    RA, RB = ga.shape[2], gb.shape[2]
    r2 = 2 * r

    def zrows(n):
        return -(-n // (16 * DP)) * 16

    ZA, ZB, Z2 = zrows(RA), zrows(RB), zrows(r2)
    ANY = pl.BlockSpec(memory_space=pl.ANY)
    dma = pltpu.SemaphoreType.DMA
    out = [((2, rows, width), bf16), ((2, 2, r, 384), bf16), ((ZA * DP, width), bf16),
           ((ZB * DP, width), bf16), ((16, width), f32)]
    big = [kaug, v, qT, kT, qn, oT, lse, a1T, wc, wo, xs]
    scratch = [(a.shape, a.dtype) for a in big] + [
        ((2, rows, width), f32),
        ((2, rows, width), bf16), ((hw, tree), bf16), ((tree, hw), bf16), ((128, tree), bf16),
        ((20, seg, 3 * hw), bf16), ((20, seg, 128), f32), ((20, seg, 128), f32),
        ((2, rows, width), bf16), ((2, rows, width), bf16),
        ((chips, RA, width), bf16), ((chips, RB, width), bf16), ((chips, RA, width), bf16), ((chips, RB, width), bf16),
        ((chips - 1, RA, width), bf16), ((chips - 1, RB, width), bf16), ((ZA * DP, width), bf16),
        ((ZB * DP, width), bf16), ((DP - 1, ZA, width), bf16), ((DP - 1, ZB, width), bf16),
        ((2, chips, r2, 384), bf16), ((2, chips - 1, r2, 384), bf16), ((2, Z2 * DP, 384), bf16),
        ((2, DP - 1, Z2, 384), bf16), ((2, Z2 * DP, 384), bf16),
        ((2, 16, width), f32), ((chips + DP, 16, width), f32), ((2, rows, width), bf16),
    ]
    nsem = chips + 2 * DP
    return pl.pallas_call(
        functools.partial(last_kernel, F),
        out_shape=[jax.ShapeDtypeStruct(s, d) for s, d in out],
        in_specs=[SM] + [ANY] * 11 + [VM, ANY, ANY, ANY, VM, VM],
        out_specs=[ANY] + [VM] * 4,
        scratch_shapes=[pltpu.VMEM(s, d) for s, d in scratch] + [
            dma((9,)), dma((9,)), dma((nsem,)), dma((nsem,)), dma((nsem,)), dma((nsem,)), dma((2, nsem)), dma((2, nsem)),
            dma((chips + DP,)), dma((chips + DP,)), dma((17,))],
        name="back",
        compiler_params=pltpu.CompilerParams(vmem_limit_bytes=64 << 20, collective_id=1, has_side_effects=True),
    )(parents, *big, dxl, dx2, ga, gb, vin, rows_vec)


def finish_kernel(lo_in, gt_in, fina, finb, gq, lo_ref, gt_ref, gwq_ref, gwk_ref, gwv_ref, gwo_ref, gwi_ref, gwu_ref):
    lo_ref[...] = lo_in[...]
    gt_ref[...] = gt_in[...]
    r, width = gwo_ref.shape
    ru = gwu_ref.shape[0]
    gwu_ref[...] = fold(fina[0:ru])
    pieces = gwi_ref.shape[1] // width
    for c in range(pieces):
        gwi_ref[:, c * width:(c + 1) * width] = fold(finb[c * r:(c + 1) * r])
    gwo_ref[...] = fold(finb[pieces * r:(pieces + 1) * r])
    for k, ref in enumerate((gwq_ref, gwk_ref, gwv_ref)):
        for c in range(2):
            for pr in range(2):
                at = (2 * c + pr) * 128
                ref[:, at:at + 128] = fold(gq[c, pr, :, 128 * k:128 * k + 128])


def finish(F, lo, gt, fina, finb, gq, hidden):
    width = lo.shape[2]
    r, ru = width // F, hidden // F
    shapes = [(r, width)] * 4 + [(r, hidden), (ru, width)]
    return pl.pallas_call(
        finish_kernel,
        out_shape=[jax.ShapeDtypeStruct(lo.shape, bf16), jax.ShapeDtypeStruct(gt.shape, bf16)]
        + [jax.ShapeDtypeStruct(s, f32) for s in shapes],
        in_specs=[VM] * 5,
        out_specs=[VM] * 8,
        name="finish",
    )(lo, gt, fina, finb, gq)


def on_device(tokens, parents, n1g, n1b, wq, wk, wv, wo, ob, n2g, n2b, wi, ib, wu, ub, cotangent):
    F = lax.axis_size("fsdp")
    fi = lax.axis_index("fsdp")
    place = (fi + 2) % F
    half = (place % 4) // 2
    quad = lax.axis_index("dp") * (F // 4) + place // 4
    parent_row = parents[quad, half]
    _, _, rows, width = tokens.shape

    n = n1g.shape[0]
    vec = jnp.concatenate([n1g, n1b, ob, n2g, n2b, ub, ib])
    vec = lax.reduce_precision(vec, 8, 7)
    vec = jnp.broadcast_to(jnp.pad(vec, (0, -vec.shape[0] % 128)), (8, vec.shape[0] + -vec.shape[0] % 128))
    hidden = wi.shape[1]
    ru = hidden // F
    (a1T, kaug, v, kT, qn, qT, oT, lse, wc, wo_own, xs, dxl, dx2, ga, gb, lo, vin, vrows) = first(
        F, parent_row, tokens[0], cotangent[0], (wq, wk, wv, wo, wi, wu), vec, n)
    gt, gq, fina, finb, vout = last(
        F, lax.axis_size("dp"), parent_row, (a1T, kaug, v, kT, qn, qT, oT, lse), wc, wo_own, xs, dxl, dx2,
        ga.reshape(F // 2, 2, -1, width), gb.reshape(F // 2, 2, -1, width), vin, vrows)
    lo, gt, gwq, gwk, gwv, gwo, gwi, gwu = finish(F, lo, gt, fina, finb, gq, hidden)
    sv = lax.dynamic_slice_in_dim(vout[:6], fi * n, n, 1)
    sib = lax.dynamic_slice_in_dim(vout[6:6 + hidden // width].reshape(-1), fi * ru, ru, 0)
    return (lo[None], gt[None], sv[0], sv[1], gwq, gwk, gwv, gwo, sv[2], sv[3], sv[4], gwi, sib, gwu, sv[5])


def solution(mesh):
    tok = P(("dp", "fsdp"), None, None, None)
    v, m = P("fsdp"), P("fsdp", None)
    return jax.shard_map(
        on_device,
        mesh=mesh,
        in_specs=(tok, P(), v, v, m, m, m, m, v, v, v, m, v, m, v, tok),
        out_specs=(tok, tok, v, v, m, m, m, m, v, v, v, m, v, m, v),
        check_vma=False,
    )
```

```python
import functools
import math

import jax
import jax.numpy as jnp
import ml_dtypes
import numpy as np
from jax import lax
from jax.experimental import pallas as pl
from jax.experimental.pallas import tpu as pltpu
from jax.sharding import PartitionSpec as P

H = 8
T = 256
f32, bf16 = jnp.float32, jnp.bfloat16
VM = pl.BlockSpec(memory_space=pltpu.VMEM)
SM = pl.BlockSpec(memory_space=pltpu.SMEM)


def mm(a, b):
    return jnp.dot(a, b, preferred_element_type=f32)


def mm_tn(a, b):
    return lax.dot_general(a, b, (((0,), (0,)), ((), ())), preferred_element_type=f32)


def mm_nt(a, b):
    return lax.dot_general(a, b, (((1,), (1,)), ((), ())), preferred_element_type=f32)


def iota(shape, dim):
    return lax.broadcasted_iota(jnp.int32, shape, dim)


def chosen(par, read):
    out = read(0)
    for b in range(1, 4):
        out = jnp.where(par == b + 1, read(b), out)
    return out


def attend(heads, seg, parents_ref, kaug_ref, qT_ref, vT_ref, oT_ref, lse_ref, s_refs, hook):
    ntr = 8 * seg // T
    vr = vT_ref.shape[0] // heads
    causal_t = iota((T, T), 0) <= iota((T, T), 1)
    causal_b = iota((seg, seg), 0) <= iota((seg, seg), 1)
    G = heads

    def group(g, _):
        hook(0)
        hs = [g * G + e for e in range(G)]
        hk = [pl.ds(pl.multiple_of(h * 128, 128), 128) for h in hs]
        hv = [pl.ds(pl.multiple_of(h * vr, vr), vr) for h in hs]

        def keys(e, blk, n):
            return kaug_ref[pl.ds(blk, n), :, hk[e]].reshape(n * seg, 128)

        def finish(e, cols, m, acc):
            h = hs[e]
            l = acc[64:65, :]
            oT_ref[pl.ds(pl.multiple_of(h * 64, 64), 64), cols] = (acc[:64] / l).astype(bf16)
            lse_ref[pl.ds(pl.multiple_of(h * 8, 8), 8), cols] = jnp.broadcast_to(m + jnp.log(l), (8, T))

        def full_scores(e, q, n):
            m = None
            for c in range(n):
                s = mm(keys(e, 2 * c, 2), q)
                s_refs[e][c * T:(c + 1) * T, :] = s
                cm = jnp.max(s, axis=0, keepdims=True)
                m = cm if m is None else jnp.maximum(m, cm)
            return m

        def full_mix(e, m, n, acc):
            for c in range(n):
                p = jnp.exp(s_refs[e][c * T:(c + 1) * T, :] - m).astype(bf16)
                t = mm(vT_ref[hv[e], c * T:(c + 1) * T], p)
                acc = t if acc is None else acc + t
            return acc

        for t in range(ntr):
            cols = slice(t * T, (t + 1) * T)
            sds, ms = [], []
            for e in range(G):
                q = qT_ref[hk[e], cols]
                sd = jnp.where(causal_t, mm(keys(e, 2 * t, 2), q), -1e30)
                m = jnp.max(sd, axis=0, keepdims=True)
                if t:
                    m = jnp.maximum(m, full_scores(e, q, t))
                sds.append(sd)
                ms.append(m)
            for e in range(G):
                acc = mm(vT_ref[hv[e], cols], jnp.exp(sds[e] - ms[e]).astype(bf16))
                acc = full_mix(e, ms[e], t, acc)
                finish(e, cols, ms[e], acc)

        def tail_tile(i, leaf):
            b0 = 8 + 2 * i
            cols = pl.ds(pl.multiple_of(b0 * seg, T), T)
            pars = [parents_ref[b0 + half - 7] for half in range(2)] if leaf else None
            exts, ms = [], []
            for e in range(G):
                q = qT_ref[hk[e], cols]
                m = full_scores(e, q, ntr)
                ext = []
                for x in range(2 if leaf else 1):
                    pieces = []
                    for half in range(2):
                        kk = keys(e, b0 + half, 1) if x == 0 else chosen(pars[half], lambda b: keys(e, 8 + b, 1))
                        s = mm(kk, q[:, half * seg:(half + 1) * seg])
                        if x == 0:
                            s = jnp.where(causal_b, s, -1e30)
                        pieces.append(s)
                    s = jnp.concatenate(pieces, axis=1)
                    m = jnp.maximum(m, jnp.max(s, axis=0, keepdims=True))
                    ext.append(s)
                exts.append(ext)
                ms.append(m)
            for e in range(G):
                acc = None
                for x, s in enumerate(exts[e]):
                    p = jnp.exp(s - ms[e]).astype(bf16)
                    t = []
                    for half in range(2):
                        if x == 0:
                            vv = vT_ref[hv[e], pl.ds(pl.multiple_of((b0 + half) * seg, seg), seg)]
                        else:
                            vv = chosen(pars[half], lambda b: vT_ref[hv[e], (8 + b) * seg:(9 + b) * seg])
                        t.append(mm(vv, p[:, half * seg:(half + 1) * seg]))
                    t = jnp.concatenate(t, axis=1)
                    acc = t if acc is None else acc + t
                acc = full_mix(e, ms[e], ntr, acc)
                finish(e, cols, ms[e], acc)

        hook(1)
        lax.fori_loop(0, 2, lambda i, c: (tail_tile(i, False), c)[1], 0)
        hook(2)
        lax.fori_loop(2, 6, lambda i, c: (hook(3, i), tail_tile(i, True), c)[2], 0)
        return 0

    lax.fori_loop(0, heads // G, group, 0)


def attend_back(heads, seg, parents_ref, kaug_ref, v_ref, qT_ref, doT_ref, kT_ref, do_ref, qn_ref,
                oT_ref, lse_ref, dqT_ref, dqkv_ref, accK, accV, hook):
    ntr = 8 * seg // T
    causal_t = iota((T, T), 0) <= iota((T, T), 1)
    causal_b = iota((seg, seg), 0) <= iota((seg, seg), 1)
    low_rows = iota((128, T), 0) < 64
    low_lanes = iota((T, 128), 1) < 64

    def pair(pr, _):
        hook("start", pr)
        lanes = pl.ds(pl.multiple_of(pr * 128, 128), 128)
        hk = [pl.ds(pl.multiple_of(pr * 256 + 128 * e, 128), 128) for e in range(2)]
        h64 = [pl.ds(pl.multiple_of(pr * 128 + 64 * e, 64), 64) for e in range(2)]
        accK[...] = jnp.zeros_like(accK)
        accV[...] = jnp.zeros_like(accV)

        def stack(x):
            z = jnp.zeros_like(x)
            return jnp.concatenate([jnp.where(low_lanes, x, z), jnp.where(low_lanes, z, x)], axis=0)

        def prep(cols):
            doT = doT_ref[lanes, cols]
            z = jnp.zeros_like(doT)
            prod = doT.astype(f32) * oT_ref[lanes, cols].astype(f32)
            q, do, lse, delta = [], [], [], []
            for e in range(2):
                q.append(qT_ref[hk[e], cols])
                do.append(jnp.where(low_rows, doT, z) if e == 0 else jnp.where(low_rows, z, doT))
                at = pl.multiple_of((pr * 2 + e) * 8, 8)
                lse.append(jnp.max(lse_ref[pl.ds(at, 8), cols], axis=0, keepdims=True))
                delta.append(jnp.sum(prod[64 * e:64 * e + 64], axis=0, keepdims=True))
            return q, do, lse, delta, stack(do_ref[cols, lanes]), stack(qn_ref[cols, lanes])

        def front(blk, n, sl, args, mask, par=None):
            q, do, lse, delta, rv, rk = args

            def rows_of(ref, at):
                if par is None:
                    return ref[pl.ds(blk, n), :, at].reshape(n * seg, 128)
                return chosen(par, lambda b: ref[8 + b, :, at])

            vv = rows_of(v_ref, lanes)
            s = [mm(rows_of(kaug_ref, hk[e]), q[e][:, sl]) for e in range(2)]
            dp = [mm(vv, do[e][:, sl]) for e in range(2)]
            return s, dp

        def rear(blk, n, sl, args, mask, par, s, dp):
            q, do, lse, delta, rv, rk = args
            ps, dss, dq = [], [], []
            for e in range(2):
                p = jnp.exp(s[e] - lse[e][:, sl])
                if mask is not None:
                    p = jnp.where(mask, p, 0.0)
                dss.append((p * (dp[e] - delta[e][:, sl])).astype(bf16))
                ps.append(p.astype(bf16))
            for e in range(2):
                if par is None:
                    kT = kT_ref[h64[e], pl.ds(pl.multiple_of(blk * seg, seg), n * seg)]
                else:
                    kT = chosen(par, lambda b: kT_ref[h64[e], (8 + b) * seg:(9 + b) * seg])
                dq.append(mm(kT, dss[e]))
            if sl.stop - sl.start != T:
                rv = jnp.concatenate([rv[sl], rv[T + sl.start:T + sl.stop]], axis=0)
                rk = jnp.concatenate([rk[sl], rk[T + sl.start:T + sl.stop]], axis=0)
            av = mm(jnp.concatenate(ps, axis=1), rv)
            ak = mm(jnp.concatenate(dss, axis=1), rk)
            if par is None:
                accV[pl.ds(blk, n)] += av.reshape(n, seg, 128)
                accK[pl.ds(blk, n)] += ak.reshape(n, seg, 128)
            else:
                for b in range(4):
                    here = jnp.where(par == b + 1, 1.0, 0.0)
                    accK[8 + b] += ak * here
                    accV[8 + b] += av * here
            return dq

        def run(items):
            out = []
            ready = []
            for item in items:
                ready.append((item, front(*item)))
                if len(ready) > 2:
                    it, (s, dp) = ready.pop(0)
                    out.append(rear(*it, s, dp))
            for it, (s, dp) in ready:
                out.append(rear(*it, s, dp))
            return out

        def emit(cols, dq):
            for e in range(2):
                dqT_ref[64 * e:64 * e + 64, cols] = (dq[e] * 0.125).astype(bf16)

        full = slice(0, T)
        for t in range(ntr):
            cols = slice(t * T, (t + 1) * T)
            args = prep(cols)
            items = [(2 * t, 2, full, args, causal_t, None)] + [(2 * c, 2, full, args, None, None) for c in range(t)]
            res = run(items)
            emit(cols, [sum(x[e] for x in res) for e in range(2)])

        def tail_tile(i, leaf):
            b0 = 8 + 2 * i
            cols = pl.ds(pl.multiple_of(b0 * seg, T), T)
            args = prep(cols)
            items = []
            for half in range(2):
                sl = slice(half * seg, (half + 1) * seg)
                items.append((b0 + half, 1, sl, args, causal_b, None))
                if leaf:
                    items.append((8, 1, sl, args, None, parents_ref[b0 + half - 7]))
            k = len(items) // 2
            items += [(2 * c, 2, full, args, None, None) for c in range(ntr)]
            res = run(items)
            dq = []
            for e in range(2):
                halves = [sum(x[e] for x in res[h * k:(h + 1) * k]) for h in range(2)]
                dq.append(jnp.concatenate(halves, axis=1) + sum(x[e] for x in res[2 * k:]))
            emit(cols, dq)

        hook("mid", pr)
        lax.fori_loop(0, 2, lambda i, c: (tail_tile(i, False), c)[1], 0)
        hook("late", pr)
        lax.fori_loop(2, 6, lambda i, c: (hook("leaf", pr, i), tail_tile(i, True), c)[2], 0)
        first = pr * 384

        def put(i, x):
            dqkv_ref[:, :, pl.ds(pl.multiple_of(first + 128 * i, 128), 128)] = x

        put(0, dqT_ref[...].T.reshape(20, seg, 128))
        put(1, accK[...].astype(bf16))
        put(2, accV[...].astype(bf16))
        hook("end", pr)
        return 0

    lax.fori_loop(0, heads // 2, pair, 0)


class Dense:
    def __init__(self, rows, width, oF_ref, dy_ref, woi_ref, wu_ref, rows_ref, dxl_ref, dx2_ref, ga_ref, gb_ref, vin_ref,
                 gs, dus):
        self.__dict__.update({k: v for k, v in locals().items() if k != "self"})
        self.hidden = wu_ref.shape[0]
        self.tiles = self.hidden // width

    def chunk(self, start, x, y_ref, a2_ref=None):
        back = a2_ref is not None
        width, rows_ref, vin_ref = self.width, self.rows_ref, self.vin_ref
        woi_ref, wu_ref = self.woi_ref, self.wu_ref
        c1 = math.sqrt(2.0 / math.pi)
        c2 = c1 * 0.044715

        def vector(i):
            return rows_ref[0:1, i * width:(i + 1) * width]

        def add_sum(i, x):
            vin_ref[i:i + 1, :] += jnp.sum(x, axis=0, keepdims=True)

        at = pl.ds(pl.multiple_of(start, 128), x.shape[0])
        x2 = fold(x) + mm_tn(self.oF_ref[:, at], woi_ref[:, 0:width]) + vector(2)
        centred = x2 - jnp.mean(x2, axis=-1, keepdims=True)
        inv = lax.rsqrt(jnp.mean(centred * centred, axis=-1, keepdims=True) + 1e-06)
        unit = centred * inv
        a2 = (unit * vector(3) + vector(4)).astype(bf16)
        if back:
            dy = self.dy_ref[start // x.shape[0]]
        y = x2 + vector(5)
        da2 = None
        for t in range(self.tiles):
            ft = slice(t * width, (t + 1) * width)
            wt = slice(width + t * width, width + (t + 1) * width)
            u = mm(a2, woi_ref[:, wt]) + rows_ref[0:1, 6 * width + t * width:6 * width + (t + 1) * width]
            uu = u * u
            th = jnp.tanh(u * (c1 + c2 * uu))
            p = 0.5 + 0.5 * th
            g = (u * p).astype(bf16)
            y = y + mm(g, wu_ref[ft, :])
            if not back:
                continue
            slope = p + u * (0.5 - 0.5 * th * th) * (c1 + 3.0 * c2 * uu)
            self.gs[at, ft] = g
            du = (mm_nt(dy, wu_ref[ft, :]) * slope).astype(bf16)
            self.dus[at, ft] = du
            add_sum(6 + t, fold(du))
            d = mm_nt(du, woi_ref[:, wt])
            da2 = d if da2 is None else da2 + d
        y_ref[...] = y.astype(bf16)
        if not back:
            return
        a2_ref[...] = a2
        dyf = fold(dy)
        dn = da2 * vector(3)
        m1 = jnp.mean(dn, axis=-1, keepdims=True)
        m2 = jnp.mean(dn * unit, axis=-1, keepdims=True)
        dx2 = dyf + (dn - m1 - unit * m2) * inv
        dxl = dx2.astype(bf16)
        self.dx2_ref[at, :] = dx2
        self.dxl_ref[at, :] = dxl
        add_sum(2, fold(dxl))
        add_sum(3, da2 * unit)
        add_sum(4, da2)
        add_sum(5, dyf)

    def gradients(self, F, a2):
        width, hidden, tiles, gb_ref = self.width, self.hidden, self.tiles, self.gb_ref
        r, ru = width // F, hidden // F
        nb = T // ru
        dy = self.dy_ref[...].reshape(2 * self.rows, width)

        def outer(t, c):
            val = mm_tn(self.gs[:, pl.ds(pl.multiple_of(t * T, T), T)], dy).astype(bf16)
            self.ga_ref[pl.ds(t * nb, nb)] = val.reshape(nb, ru, width)
            return c

        lax.fori_loop(0, hidden // T, outer, 0)
        a2T = a2.T
        for t in range(tiles):
            val = mm(a2T, self.dus[:, t * width:(t + 1) * width]).astype(bf16)
            gb_ref[:, t * r:(t + 1) * r, :] = val.reshape(F, r, width)
        val = mm(self.oF_ref[...], self.dxl_ref[...]).astype(bf16)
        gb_ref[:, tiles * r:(tiles + 1) * r, :] = val.reshape(F, r, width)


def slope_parts(head, head_count, length):
    x = np.float32(2.0 ** (2.0 - 4.0 * head / head_count) / length)
    out = []
    for _ in range(3):
        low = np.float32(ml_dtypes.bfloat16(x))
        out.append(float(low))
        x = np.float32(x - low)
    return out


def remote(src, dst, send_sem, recv_sem, target):
    return pltpu.make_async_remote_copy(
        src_ref=src, dst_ref=dst, send_sem=send_sem, recv_sem=recv_sem,
        device_id={"fsdp": target}, device_id_type=pl.DeviceIdType.MESH)


def where_am_i(F):
    f = lax.axis_index("fsdp")
    place = lax.rem(f + 2, F)
    part = lax.rem(place, 4)
    half = part // 2
    core = lax.rem(f, 2)
    base = place - part
    partner = lax.rem(base + lax.rem(part + 2, 4) + F - 2, F)
    sibling = f + 1 - 2 * core
    return f, part, half, core, partner, sibling


def greet(F, f, core, sibling, across):
    barrier = pltpu.get_barrier_semaphore()
    peers = [{"fsdp": lax.rem(f + 2 * d, F)} for d in range(1, F // 2)] + [{"fsdp": sibling}]
    if across:
        plane = lax.axis_index("dp")
        peers.append({"dp": plane + 1 - 2 * lax.rem(plane, 2)})
    for peer in peers:
        pl.semaphore_signal(barrier, inc=1, device_id=peer, device_id_type=pl.DeviceIdType.MESH)
    pl.semaphore_wait(barrier, len(peers))


def first_kernel(F, n, parents_ref, tok_ref, cot_ref, wq_ref, wk_ref, wv_ref, wo_ref, wi_ref, wu_ref, vec_ref,
                 a1T_out, kaug_out, v_out, kT_out, qn_out, qT_out, oT_out, lse_out, wc_out, wo_out, xs_out, dxl_out,
                 dx2_out, ga_out, gb_out, lo_ref, vin_ref, rows_ref,
                 xt_ref, a1T_ref, kaug_ref, v_ref, kT_ref, qn_ref, qT_ref, oT_ref, lse_ref, oF_ref, dy_ref,
                 wqkv_ref, woi_ref, wuf_ref, dxl_ref, dx2_ref, ga_ref, gb_ref, gs, dus,
                 vecs, vT_scr, s_scr, tsend, trecv, gsend, grecv, zsend, zrecv, osem):
    f, part, half, core, partner, sibling = where_am_i(F)
    rows, width = tok_ref.shape[1:]
    seg = rows // 5
    heads = H // 2
    hw = heads * 64
    tree = 4 * rows
    r = wq_ref.shape[0]
    ru = wu_ref.shape[0]
    part1 = part + 1 - 2 * core
    part2 = lax.rem(part + 2, 4)
    part3 = lax.rem(part1 + 2, 4)

    own = pl.ds(pl.multiple_of(f * r, r), r)
    ownu = pl.ds(pl.multiple_of(f * ru, ru), ru)
    vecs[f] = vec_ref[...]
    blocks = [wq_ref, wk_ref, wv_ref, wo_ref] + [
        wi_ref.at[:, c * width:(c + 1) * width] for c in range(wi_ref.shape[1] // width)]
    staged = [pltpu.make_async_copy(b, dx2_ref.at[i * r:(i + 1) * r], osem.at[27 + i]) for i, b in enumerate(blocks)]
    last_rows = slice(len(blocks) * r, len(blocks) * r + ru)
    staged.append(pltpu.make_async_copy(wu_ref, dx2_ref.at[last_rows], osem.at[27 + len(blocks)]))
    for c in staged:
        c.start()
    for i in range(3):
        staged[i].wait()
        wqkv_ref[own, i * width:(i + 1) * width] = dx2_ref[i * r:(i + 1) * r].astype(bf16)

    greet(F, f, core, sibling, lax.axis_size("dp") % 2 == 0)

    def slot(g, src):
        if g == 0:
            return vecs.at[src]
        if g == 3:
            return wuf_ref.at[pl.ds(pl.multiple_of(src * ru, ru), ru)]
        ref = wqkv_ref if g == 1 else woi_ref
        return ref.at[pl.ds(pl.multiple_of(src * r, r), r)]

    planes = lax.axis_size("dp")
    plane = lax.axis_index("dp")
    shared = r % 32 == 0 and planes % 2 == 0
    parity = lax.rem(plane, 2)
    opposite = plane + 1 - 2 * parity
    chips = range(1, F // 2)

    def part_of(g, src, which=None):
        if g not in (1, 2) or not shared or which is None:
            return slot(g, src)
        ref = wqkv_ref if g == 1 else woi_ref
        return ref.at[pl.ds(pl.multiple_of(src * r + which * (r // 2), 16), r // 2)]

    def source(d, of=None):
        return lax.rem((f if of is None else of) + F - 2 * d, F)

    def direct(g, d):
        if d == 0:
            return remote(slot(g, f), slot(g, f), gsend.at[g, 0], grecv.at[g, 0], sibling)
        return remote(part_of(g, f, parity), part_of(g, f, parity), gsend.at[g, d], grecv.at[g, d], lax.rem(f + 2 * d, F))

    def came(g, d):
        ref = slot(g, sibling) if d == 0 else part_of(g, source(d), parity)
        remote(ref, ref, gsend.at[g, d], grecv.at[g, d], sibling).wait_recv()

    def forward(g, d, of=None):
        ref = part_of(g, source(d, of), parity)
        return remote(ref, ref, gsend.at[g, F // 2 + d], grecv.at[g, F // 2 + d], sibling)

    def across(g, d, which):
        ref = part_of(g, source(d), which)
        return pltpu.make_async_remote_copy(
            src_ref=ref, dst_ref=ref, send_sem=zsend.at[g - 1, d], recv_sem=zrecv.at[g - 1, d],
            device_id={"dp": opposite}, device_id_type=pl.DeviceIdType.MESH)

    def forward_across(g, d, of=None):
        ref = part_of(g, source(d, of), 1 - parity)
        return remote(ref, ref, zsend.at[g - 1, F // 2 + d], zrecv.at[g - 1, F // 2 + d], sibling)

    def send_all(g):
        for d in range(F // 2):
            direct(g, d).start()

    def pass_on(g):
        for d in chips:
            came(g, d)
            if g in (1, 2) and shared:
                across(g, d, parity).start()
            forward(g, d).start()

    def pass_across(g):
        if shared:
            for d in chips:
                across(g, d, 1 - parity).wait_recv()
                forward_across(g, d).start()

    def receive_rest(g):
        came(g, 0)
        for d in chips:
            forward(g, d, sibling).wait_recv()
            if g in (1, 2) and shared:
                forward_across(g, d, sibling).wait_recv()

    x_out = remote(tok_ref.at[1 - half], xt_ref.at[part], tsend.at[0], trecv.at[0], partner)
    x_sib = remote(tok_ref.at[half], xt_ref.at[part], tsend.at[1], trecv.at[1], sibling)
    x_fwd = remote(xt_ref.at[part2], xt_ref.at[part2], tsend.at[2], trecv.at[2], sibling)
    dy_out = remote(cot_ref.at[1 - half], dy_ref.at[half], tsend.at[3], trecv.at[3], partner)
    x_own = pltpu.make_async_copy(tok_ref.at[half], xt_ref.at[part], osem.at[20])
    dy_own = pltpu.make_async_copy(cot_ref.at[half], dy_ref.at[half], tsend.at[4])

    send_all(0)
    send_all(1)
    x_out.start()
    x_sib.start()
    x_own.start()
    dy_own.start()
    for c in staged[3:]:
        c.wait()
    for i in range(3, len(blocks)):
        woi_ref[own, (i - 3) * width:(i - 2) * width] = dx2_ref[i * r:(i + 1) * r].astype(bf16)
    wuf_ref[ownu, :] = dx2_ref[last_rows].astype(bf16)
    pass_on(0)
    pass_on(1)
    receive_rest(0)

    table = jnp.max(vecs[...], axis=1).astype(bf16)
    words = table.shape[1]

    def vector_row(first, m, length):
        col = iota((words, length), 1)
        pick = iota((words, length), 0) == first + (col & (m - 1))
        spread = mm(table, pick.astype(bf16))
        shift = m.bit_length() - 1
        mine = iota((F, length), 0) == (iota((F, length), 1) >> shift)
        return jnp.sum(jnp.where(mine, spread, 0.0), axis=0, keepdims=True)

    def all_rows(first, last):
        for i in range(first, last):
            rows_ref[:, i * width:(i + 1) * width] = jnp.broadcast_to(vector_row(i * n, n, width), (8, width))

    hidden = rows_ref.shape[1] - 6 * width
    all_rows(0, 6)
    rows_ref[:, 6 * width:] = jnp.broadcast_to(vector_row(6 * n, hidden // F, hidden), (8, hidden))
    pass_across(1)
    receive_rest(1)

    lane = iota((seg, 128), 1)
    offs = iota((seg, 128), 0)
    arow = iota((64, rows), 0)

    def project(p):
        x = xt_ref[p].astype(f32)
        gain = rows_ref[0:1, 0:width]
        shift = rows_ref[0:1, width:2 * width]
        mean = jnp.mean(x, axis=-1, keepdims=True)
        x = x - mean
        inv = lax.rsqrt(jnp.mean(x * x, axis=-1, keepdims=True) + 1e-06)
        a1 = (x * inv * gain + shift).astype(bf16)

        def proj(i):
            return mm(a1, wqkv_ref[:, pl.ds(pl.multiple_of(i * width + core * hw, hw), hw)])

        cols = pl.ds(pl.multiple_of(p * rows, rows), rows)
        a1T_ref[:, cols] = a1.T
        q = (proj(0) * 0.125).astype(bf16)
        qn_ref[cols, :] = q
        qT = q.T
        k = proj(1).astype(bf16)
        kT_ref[:, cols] = k.T
        v = proj(2).astype(bf16)
        v_ref[pl.ds(p * 5, 5)] = v.reshape(5, seg, hw)
        vT = v.T
        for h in range(heads):
            a, b = slope_parts(h, H, tree), slope_parts(heads + h, H, tree)
            aug = jnp.zeros((64, rows), f32)
            for j in range(3):
                s = jnp.where(core == 0, a[j], b[j])
                aug = jnp.where((arow == j) | (arow == j + 3), s, aug)
            aug = aug.astype(bf16)
            lo, hi = 128 * h + 64 * (h % 2), 128 * h + 64 - 64 * (h % 2)
            qT_ref[lo:lo + 64, cols] = qT[64 * h:64 * h + 64]
            qT_ref[hi:hi + 64, cols] = aug
            vT_scr[80 * h:80 * h + 64, cols] = vT[64 * h:64 * h + 64]
            vT_scr[80 * h + 64:80 * h + 80, cols] = jnp.ones((16, rows), bf16)
        for b in range(5):
            blk = p * 5 + b
            start = jnp.where(blk < 8, blk * seg, jnp.where(blk < 12, 8 * seg, 9 * seg))
            spot = offs + start
            hi = (spot & -8).astype(f32)
            lo = (spot & 7).astype(f32)
            for h in range(heads):
                at = 64 - 64 * (h % 2)
                l = lane - at
                aug = jnp.where((l >= 0) & (l < 3), hi, jnp.where((l >= 3) & (l < 6), lo, 0.0)).astype(bf16)
                keep = (lane < 64) if h % 2 == 0 else (lane >= 64)
                kk = k[b * seg:(b + 1) * seg, 128 * (h // 2):128 * (h // 2) + 128]
                kaug_ref[blk, :, 128 * h:128 * h + 128] = jnp.where(keep, kk, aug)

    x_own.wait()
    x_sib.wait_recv()

    def visit(i, c):
        @pl.when(i == 1)
        def _():
            x_out.wait_recv()
            x_fwd.start()
            send_all(2)
            send_all(3)

        @pl.when(i == 3)
        def _():
            x_fwd.wait_recv()

        project(jnp.where(i == 0, part, jnp.where(i == 1, part1, jnp.where(i == 2, part2, part3))))
        return c

    lax.fori_loop(0, 4, visit, 0)
    wc_copies = []
    for i in range(heads // 2):
        for k in range(3):
            src = wqkv_ref.at[:, pl.ds(pl.multiple_of(k * width + core * hw + 128 * i, 128), 128)]
            at = 384 * i + 128 * k
            wc_copies.append(pltpu.make_async_copy(src, wc_out.at[:, at:at + 128], osem.at[21 + 3 * i + k]))

    outs = [(a1T_ref, a1T_out), (kaug_ref, kaug_out), (v_ref, v_out), (kT_ref, kT_out), (qn_ref, qn_out),
            (qT_ref, qT_out), (xt_ref.at[core], xs_out.at[0]), (xt_ref.at[core + 2], xs_out.at[1]),
            (oT_ref, oT_out), (lse_ref, lse_out),
            (woi_ref.at[pl.ds(pl.multiple_of(core * hw, hw), hw), 0:width], wo_out),
            (dxl_ref.at[0:rows], dxl_out.at[0]), (dxl_ref.at[rows:2 * rows], dxl_out.at[1]),
            (dx2_ref.at[0:rows], dx2_out.at[0]), (dx2_ref.at[rows:2 * rows], dx2_out.at[1]), (ga_ref, ga_out), (gb_ref, gb_out)]
    copies = [pltpu.make_async_copy(a, b, osem.at[i]) for i, (a, b) in enumerate(outs)]
    for c in copies[:8] + wc_copies:
        c.start()

    s_refs = [dx2_ref.at[0:8 * seg, 0:T], dx2_ref.at[0:8 * seg, T:2 * T], s_scr.at[0], s_scr.at[1]]

    def hook(stage, i=None):
        if stage == 1:
            pass_on(2)
        if stage == 2:
            dy_out.start()

    attend(heads, seg, parents_ref, kaug_ref, qT_ref, vT_scr, oT_ref, lse_ref, s_refs, hook)

    other = 1 - core
    sent = []
    for i in range(2):
        cols = pl.ds(pl.multiple_of((other + 2 * i) * rows, rows), rows)
        at = (pl.ds(pl.multiple_of(core * hw, hw), hw), slice(i * rows, (i + 1) * rows))
        c = remote(oT_ref.at[:, cols], oF_ref.at[at], tsend.at[5 + i], trecv.at[5 + i], sibling)
        c.start()
        sent.append(c)
    for i in range(2):
        mine = pl.ds(pl.multiple_of((core + 2 * i) * rows, rows), rows)
        at = (pl.ds(pl.multiple_of(core * hw, hw), hw), slice(i * rows, (i + 1) * rows))
        oF_ref[at] = oT_ref[:, mine]
    copies[8].start()
    copies[9].start()
    pass_across(2)
    pass_on(3)
    receive_rest(2)
    copies[10].start()
    for c in sent:
        c.wait_recv()
    receive_rest(3)
    dy_own.wait()

    vin_ref[...] = jnp.zeros_like(vin_ref)
    dense = Dense(rows, width, oF_ref, dy_ref, woi_ref, wuf_ref, rows_ref, dxl_ref, dx2_ref, ga_ref, gb_ref, vin_ref,
                  gs, dus)
    y_out = remote(xt_ref.at[other + 2 * (1 - half)], lo_ref.at[half], tsend.at[7], trecv.at[7], partner)
    keep_y = pltpu.make_async_copy(xt_ref.at[other + 2 * half], lo_ref.at[half], osem.at[18])
    dense.chunk((1 - half) * rows, xt_ref[core + 2 * (1 - half)], xt_ref.at[other + 2 * (1 - half)])
    y_out.start()
    copies[6].wait()
    copies[7].wait()
    x_fwd.wait_send()

    def dense_step(s, c):
        i = jnp.where(s == 0, half, 1 - half)

        @pl.when(s == 1)
        def _():
            keep_y.start()
            dy_out.wait_recv()

        dense.chunk(i * rows, xt_ref[core + 2 * i], xt_ref.at[jnp.where(s == 0, other, core) + 2 * i], xt_ref.at[core + 2 * i])
        return c

    lax.fori_loop(0, 2, dense_step, 0)
    for c in copies[11:15]:
        c.start()
    dense.gradients(F, jnp.concatenate([xt_ref[core], xt_ref[core + 2]], axis=0))
    copies[15].start()
    copies[16].start()
    for c in copies[:6] + copies[8:] + wc_copies + [keep_y]:
        c.wait()
    y_out.wait()
    dy_out.wait_send()
    x_out.wait_send()
    x_sib.wait_send()
    for c in sent:
        c.wait_send()
    for g in range(4):
        for d in range(F // 2):
            direct(g, d).wait_send()
        for d in chips:
            forward(g, d).wait_send()
    if shared:
        for g in (1, 2):
            for d in chips:
                across(g, d, parity).wait_send()
                forward_across(g, d).wait_send()


def first(F, parents, tokens, cotangent, weights, vec, n):
    _, rows, width = tokens.shape
    tree = 4 * rows
    heads = H // 2
    hw = heads * 64
    seg = rows // 5
    hidden = weights[4].shape[1]
    r, ru = width // F, hidden // F
    R1 = (hidden // width + 1) * r
    two = 2 * rows
    keep = [((width, tree), bf16), ((20, seg, heads * 128), bf16), ((20, seg, hw), bf16), ((hw, tree), bf16),
            ((tree, hw), bf16), ((heads * 128, tree), bf16), ((hw, tree), bf16), ((heads * 8, tree), f32)]
    out = keep + [((width, 3 * hw), bf16), ((hw, width), bf16), ((2, rows, width), bf16), ((2, rows, width), bf16),
                  ((2, rows, width), f32), ((F, ru, width), bf16), ((F, R1, width), bf16), ((2, rows, width), bf16),
                  ((16, width), f32), ((8, 6 * width + hidden), f32)]
    scratch = [((4, rows, width), bf16)] + keep + [
        ((2 * hw, two), bf16), ((2, rows, width), bf16), ((width, 3 * width), bf16), ((width, width + hidden), bf16),
        ((hidden, width), bf16), ((two, width), bf16),
        ((two, width), f32), ((F, ru, width), bf16), ((F, R1, width), bf16), ((two, hidden), bf16),
        ((two, hidden), bf16), ((F,) + vec.shape, f32), ((heads * 80, tree), bf16), ((2, 8 * seg, T), f32)]
    ANY = pl.BlockSpec(memory_space=pl.ANY)
    dma = pltpu.SemaphoreType.DMA
    return pl.pallas_call(
        functools.partial(first_kernel, F, n),
        out_shape=[jax.ShapeDtypeStruct(s, d) for s, d in out],
        in_specs=[SM] + [ANY] * 8 + [VM],
        out_specs=[ANY] * 16 + [VM] * 2,
        scratch_shapes=[pltpu.VMEM(s, d) for s, d in scratch] + [
            dma((8,)), dma((8,)), dma((4, F)), dma((4, F)), dma((2, F)), dma((2, F)), dma((28 + 4 + hidden // width,))],
        name="front",
        compiler_params=pltpu.CompilerParams(vmem_limit_bytes=64 << 20, collective_id=0, has_side_effects=True),
    )(parents, tokens, cotangent, *weights, vec)


def fold(x):
    return x.astype(f32)


class Chain:
    def __init__(self, F, f, sums, got, block, zgot, final, send, recv, stages=2):
        self.square = F == 8 and stages == 2
        self.F, self.f, self.sums, self.got, self.block = F, f, sums, got, block
        self.zgot, self.final, self.send, self.recv = zgot, final, send, recv
        self.chip = f // 2
        self.chips = F // 2
        self.planes = lax.axis_size("dp")
        self.plane = lax.axis_index("dp")
        self.rows = sums.shape[1]
        self.zrows = block.shape[0] // self.planes

    def _b(self, d):
        return remote(self.sums.at[lax.rem(self.chip + d, self.chips)], self.got.at[d - 1],
                      self.send.at[d], self.recv.at[d], lax.rem(self.f + 2 * d, self.F))

    def _square(self):
        core = lax.rem(self.f, 2)
        x, y = lax.rem(self.chip, 2), self.chip // 2
        along_x, along_y = 2 * y + 1 - x, 2 * (1 - y) + x
        first = jnp.where(core == 0, along_x, along_y)
        second = jnp.where(core == 0, along_y, along_x)
        last = 2 * (1 - y) + 1 - x
        one = [remote(self.sums.at[first], self.got.at[0], self.send.at[1], self.recv.at[1], 2 * first + core),
               remote(self.sums.at[last], self.got.at[1], self.send.at[2], self.recv.at[2], 2 * first + core)]
        two = remote(self.sums.at[second], self.got.at[2], self.send.at[3], self.recv.at[3], 2 * second + core)
        return one, two, second

    def _chunk(self, z):
        return pl.ds(pl.multiple_of(z * self.zrows, 16), self.zrows)

    def _c(self, e):
        z = lax.rem(self.plane + e, self.planes)
        i = self.chips + e
        return pltpu.make_async_remote_copy(
            src_ref=self.block.at[self._chunk(z)], dst_ref=self.zgot.at[e - 1],
            send_sem=self.send.at[i], recv_sem=self.recv.at[i],
            device_id={"dp": z}, device_id_type=pl.DeviceIdType.MESH)

    def _d(self, e, src=None):
        z = lax.rem(self.plane + e, self.planes)
        i = self.chips + self.planes + e
        here = self._chunk(self.plane if src is None else src)
        return pltpu.make_async_remote_copy(
            src_ref=self.final.at[here], dst_ref=self.final.at[here],
            send_sem=self.send.at[i], recv_sem=self.recv.at[i],
            device_id={"dp": z}, device_id_type=pl.DeviceIdType.MESH)

    def start_plane(self):
        if self.square:
            for c in self._square()[0]:
                c.start()
            return
        for d in range(1, self.chips):
            self._b(d).start()

    def mid_plane(self):
        if self.square:
            one, two, second = self._square()
            for c in one:
                c.wait_recv()
            self.sums[second] = (fold(self.sums[second]) + fold(self.got[1])).astype(bf16)
            two.start()

    def start_z(self):
        if self.square:
            self._square()[1].wait_recv()
            total = fold(self.sums[self.chip]) + fold(self.got[0]) + fold(self.got[2])
        else:
            for d in range(1, self.chips):
                self._b(d).wait_recv()
            total = fold(self.sums[self.chip])
            for d in range(1, self.chips):
                total = total + fold(self.got[d - 1])
        self.block[0:self.rows] = total.astype(bf16)
        for e in range(1, self.planes):
            self._c(e).start()

    def start_back(self):
        for e in range(1, self.planes):
            self._c(e).wait_recv()
        here = self._chunk(self.plane)
        total = fold(self.block[here])
        for e in range(1, self.planes):
            total = total + fold(self.zgot[e - 1])
        self.final[here] = total.astype(bf16)
        for e in range(1, self.planes):
            self._d(e).start()

    def receive(self):
        for e in range(1, self.planes):
            self._d(e, lax.rem(self.plane + self.planes - e, self.planes)).wait_recv()

    def close(self):
        if self.square:
            one, two, _ = self._square()
            for c in one + [two]:
                c.wait_send()
        else:
            for d in range(1, self.chips):
                self._b(d).wait_send()
        for e in range(1, self.planes):
            self._c(e).wait_send()
            self._d(e).wait_send()


def last_kernel(F, parents_ref, kaug_h, v_h, qT_h, kT_h, qn_h, oT_h, lse_h, a1T_h, wc_h, wo_h, xs_h, dxl_ref, dx2_h,
                ga_ref, gb_ref, vin_ref, n1_ref,
                gt_ref, gq_ref, fina, finb, vout_ref,
                kaug_ref, v_ref, qT_ref, kT_ref, qn_ref, oT_ref, lse_ref, a1T_ref, wc, wo_scr, xs, dx2s,
                dxs, doT, do, dqT, dqkv, accK, accV, das, dar,
                suma, sumb, gota, gotb, planea, planeb, blka, blkb, za, zb, sum2, got2, blk2, z2, fin2,
                vs, vgot, dxo, tsend, trecv, senda, recva, sendb, recvb, send2, recv2, vsend, vrecv, lsem):
    f, part, half, core, partner, sibling = where_am_i(F)
    planes = lax.axis_size("dp")
    plane = lax.axis_index("dp")
    heads = H // 2
    hw = heads * 64
    _, rows, width = dxl_ref.shape
    chips = F // 2
    other = 1 - core
    tree = 4 * rows
    seg = rows // 5

    pairs = [(wo_h, wo_scr), (qT_h, qT_ref), (kaug_h, kaug_ref), (v_h, v_ref), (kT_h, kT_ref), (qn_h, qn_ref),
             (oT_h, oT_ref), (lse_h, lse_ref), (ga_ref.at[:, core], suma), (gb_ref.at[:, core], sumb), (a1T_h, a1T_ref), (wc_h, wc), (xs_h, xs),
             (dx2_h, dx2s)]
    loads = [pltpu.make_async_copy(a, b, lsem.at[i]) for i, (a, b) in enumerate(pairs)]
    for c in loads:
        c.start()

    barrier = pltpu.get_barrier_semaphore()
    for d in range(1, chips):
        pl.semaphore_signal(barrier, inc=1, device_id={"fsdp": lax.rem(f + 2 * d, F)},
                            device_id_type=pl.DeviceIdType.MESH)
    for e in range(1, planes):
        pl.semaphore_signal(barrier, inc=1, device_id={"dp": lax.rem(plane + e, planes)},
                            device_id_type=pl.DeviceIdType.MESH)
    pl.semaphore_signal(barrier, inc=1, device_id={"fsdp": sibling}, device_id_type=pl.DeviceIdType.MESH)
    pl.semaphore_wait(barrier, chips + planes - 1)

    dx_sw = remote(dxl_ref, dxs, tsend.at[0], trecv.at[0], sibling)
    out_a = remote(ga_ref.at[:, other], gota, tsend.at[1], trecv.at[1], sibling)
    out_b = remote(gb_ref.at[:, other], gotb, tsend.at[7], trecv.at[7], sibling)
    dx_sw.start()
    out_a.start()
    out_b.start()

    def make_do(p, x):
        cols = pl.ds(pl.multiple_of(p * rows, rows), rows)
        d = mm_nt(x, wo_scr[...]).astype(bf16)
        do[cols, :] = d
        doT[:, cols] = d.T

    loads[0].wait()
    lax.fori_loop(0, 2, lambda i, c: (make_do(core + 2 * i, dxl_ref[i]), c)[1], 0)

    one_a = Chain(F, f, suma, planea, blka, za, fina, senda, recva)
    one_b = Chain(F, f, sumb, planeb, blkb, zb, finb, sendb, recvb)

    def add_sibling(load, arrived, mine, got):
        load.wait()
        arrived.wait_recv()

        def add_block(j, c):
            mine[j] = (fold(mine[j]) + fold(got[j])).astype(bf16)
            return c

        lax.fori_loop(0, chips, add_block, 0)

    dx_sw.wait_recv()
    lax.fori_loop(0, 2, lambda i, c: (make_do(other + 2 * i, dxs[i]), c)[1], 0)
    add_sibling(loads[8], out_a, suma, gota)
    one_a.start_plane()
    for c in loads[1:8]:
        c.wait()

    def chain(pr):
        return Chain(F, f, sum2.at[pr], got2.at[pr], blk2.at[pr], z2.at[pr], fin2.at[pr], send2.at[pr], recv2.at[pr], 1)

    two = [chain(0), chain(1)]
    r = width // F
    r2 = 2 * r

    def hook(name, pr, i=None):
        if name == "mid":
            @pl.when(pr == 0)
            def _():
                add_sibling(loads[9], out_b, sumb, gotb)
                one_b.start_plane()

            @pl.when(pr == 1)
            def _():
                one_a.start_z()
        if name == "late":
            @pl.when(pr == 1)
            def _():
                one_b.start_z()
        if name == "leaf":
            @pl.when((pr == 0) & (i == 3))
            def _():
                one_a.mid_plane()

            @pl.when((pr == 1) & (i == 5))
            def _():
                one_a.start_back()
                two[0].start_z()
        if name == "end":
            @pl.when(pr == 0)
            def _():
                one_b.mid_plane()
                for c in loads[10:14]:
                    c.wait()

            g = mm(a1T_ref[...], dqkv[:, :, pl.ds(pl.multiple_of(pr * 384, 384), 384)].reshape(tree, 384)).astype(bf16)
            for j in range(chips):
                sum2[pr, j] = g[j * r2:(j + 1) * r2]
            chain(pr).start_plane()

    attend_back(heads, seg, parents_ref, kaug_ref, v_ref, qT_ref, doT, kT_ref, do, qn_ref, oT_ref, lse_ref,
                dqT, dqkv, accK, accV, hook)

    def da1_of(p):
        return mm_nt(dqkv[pl.ds(p * 5, 5)].reshape(rows, 3 * hw), wc[...])

    def da_out(s):
        i = (1 - half) if s == 0 else half
        return remote(das.at[i], dar.at[i], tsend.at[2 + s], trecv.at[2 + s], sibling)

    dx_out = remote(dxo.at[1 - half], gt_ref.at[half], tsend.at[4], trecv.at[4], partner)
    keep_dx = pltpu.make_async_copy(dxo.at[half], gt_ref.at[half], lsem.at[15])
    vs[0] = vin_ref[...]
    row = iota((16, width), 0)

    def finish_rows(s, c):
        i = jnp.where(s == 0, 1 - half, half)
        das[i] = da1_of(other + 2 * i).astype(bf16)
        for k in range(2):
            @pl.when(s == k)
            def _():
                da_out(k).start()
        x = fold(xs[i])
        x = x - jnp.mean(x, axis=-1, keepdims=True)
        inv = lax.rsqrt(jnp.mean(x * x, axis=-1, keepdims=True) + 1e-06)
        unit = x * inv
        da = da1_of(core + 2 * i)
        for k in range(2):
            @pl.when(s == k)
            def _():
                da_out(k).wait_recv()
        da = da + fold(dar[i])
        dn = da * n1_ref[0:1, 0:width]
        m1 = jnp.mean(dn, axis=-1, keepdims=True)
        m2 = jnp.mean(dn * unit, axis=-1, keepdims=True)
        dxo[i] = (dx2s[i] + (dn - m1 - unit * m2) * inv).astype(bf16)
        gs = jnp.sum(da * unit, axis=0, keepdims=True)
        bs = jnp.sum(da, axis=0, keepdims=True)
        vs[0] += jnp.where(row == 0, gs, 0.0) + jnp.where(row == 1, bs, 0.0)

        @pl.when(s == 0)
        def _():
            dx_out.start()
            one_b.start_back()
            two[0].start_back()

        @pl.when(s == 1)
        def _():
            keep_dx.start()

        return c

    lax.fori_loop(0, 2, finish_rows, 0)
    v_sib = remote(vs.at[0], vgot.at[0], vsend.at[0], vrecv.at[0], sibling)
    v_sib.start()
    two[1].start_z()
    v_sib.wait_recv()
    vgot[chips + plane] = vs[0] + vgot[0]

    def v_z(e, sender):
        return pltpu.make_async_remote_copy(
            src_ref=vgot.at[chips + sender], dst_ref=vgot.at[chips + sender],
            send_sem=vsend.at[chips + e], recv_sem=vrecv.at[chips + e],
            device_id={"dp": lax.rem(plane + e, planes)}, device_id_type=pl.DeviceIdType.MESH)

    for e in range(1, planes):
        v_z(e, plane).start()
    for e in range(1, planes):
        v_z(e, lax.rem(plane + planes - e, planes)).wait_recv()
    total = vgot[chips]
    for z in range(1, planes):
        total = total + vgot[chips + z]
    vs[1] = total
    v_chip = [remote(vs.at[1], vgot.at[d], vsend.at[d], vrecv.at[d], lax.rem(f + 2 * d, F)) for d in range(1, chips)]
    for c in v_chip:
        c.start()
    two[1].start_back()
    one_a.receive()
    one_b.receive()
    s_out = []
    for pr in range(2):
        two[pr].receive()
        c = remote(fin2.at[pr, pl.ds(pl.multiple_of(other * r, r), r)], gq_ref.at[core, pr],
                   tsend.at[5 + pr], trecv.at[5 + pr], sibling)
        c.start()
        gq_ref[core, pr] = fin2[pr, pl.ds(pl.multiple_of(core * r, r), r), :]
        s_out.append(c)
    for c in v_chip:
        c.wait_recv()
    total = vs[1]
    for d in range(1, chips):
        total = total + vgot[d]
    vout_ref[...] = total
    for c in s_out:
        c.wait()
    dx_out.wait()
    keep_dx.wait()
    one_a.close()
    one_b.close()
    for c in two:
        c.close()
    for c in [dx_sw, out_a, out_b, v_sib, da_out(0), da_out(1)] + v_chip:
        c.wait_send()
    for e in range(1, planes):
        v_z(e, plane).wait_send()


def last(F, DP, parents, kept, wc, wo, xs, dxl, dx2, ga, gb, vin, rows_vec):
    a1T, kaug, v, kT, qn, qT, oT, lse = kept
    _, rows, width = dxl.shape
    heads = H // 2
    hw = heads * 64
    tree = 4 * rows
    seg = rows // 5
    chips = F // 2
    r = width // F
    RA, RB = ga.shape[2], gb.shape[2]
    r2 = 2 * r

    def zrows(n):
        return -(-n // (16 * DP)) * 16

    ZA, ZB, Z2 = zrows(RA), zrows(RB), zrows(r2)
    ANY = pl.BlockSpec(memory_space=pl.ANY)
    dma = pltpu.SemaphoreType.DMA
    out = [((2, rows, width), bf16), ((2, 2, r, 384), bf16), ((ZA * DP, width), bf16),
           ((ZB * DP, width), bf16), ((16, width), f32)]
    big = [kaug, v, qT, kT, qn, oT, lse, a1T, wc, wo, xs]
    scratch = [(a.shape, a.dtype) for a in big] + [
        ((2, rows, width), f32),
        ((2, rows, width), bf16), ((hw, tree), bf16), ((tree, hw), bf16), ((128, tree), bf16),
        ((20, seg, 3 * hw), bf16), ((20, seg, 128), f32), ((20, seg, 128), f32),
        ((2, rows, width), bf16), ((2, rows, width), bf16),
        ((chips, RA, width), bf16), ((chips, RB, width), bf16), ((chips, RA, width), bf16), ((chips, RB, width), bf16),
        ((chips - 1, RA, width), bf16), ((chips - 1, RB, width), bf16), ((ZA * DP, width), bf16),
        ((ZB * DP, width), bf16), ((DP - 1, ZA, width), bf16), ((DP - 1, ZB, width), bf16),
        ((2, chips, r2, 384), bf16), ((2, chips - 1, r2, 384), bf16), ((2, Z2 * DP, 384), bf16),
        ((2, DP - 1, Z2, 384), bf16), ((2, Z2 * DP, 384), bf16),
        ((2, 16, width), f32), ((chips + DP, 16, width), f32), ((2, rows, width), bf16),
    ]
    nsem = chips + 2 * DP
    return pl.pallas_call(
        functools.partial(last_kernel, F),
        out_shape=[jax.ShapeDtypeStruct(s, d) for s, d in out],
        in_specs=[SM] + [ANY] * 11 + [VM, ANY, ANY, ANY, VM, VM],
        out_specs=[ANY] + [VM] * 4,
        scratch_shapes=[pltpu.VMEM(s, d) for s, d in scratch] + [
            dma((9,)), dma((9,)), dma((nsem,)), dma((nsem,)), dma((nsem,)), dma((nsem,)), dma((2, nsem)), dma((2, nsem)),
            dma((chips + DP,)), dma((chips + DP,)), dma((17,))],
        name="back",
        compiler_params=pltpu.CompilerParams(vmem_limit_bytes=64 << 20, collective_id=1, has_side_effects=True),
    )(parents, *big, dxl, dx2, ga, gb, vin, rows_vec)


def finish_kernel(lo_in, gt_in, fina, finb, gq, lo_ref, gt_ref, gwq_ref, gwk_ref, gwv_ref, gwo_ref, gwi_ref, gwu_ref):
    lo_ref[...] = lo_in[...]
    gt_ref[...] = gt_in[...]
    r, width = gwo_ref.shape
    ru = gwu_ref.shape[0]
    gwu_ref[...] = fold(fina[0:ru])
    pieces = gwi_ref.shape[1] // width
    for c in range(pieces):
        gwi_ref[:, c * width:(c + 1) * width] = fold(finb[c * r:(c + 1) * r])
    gwo_ref[...] = fold(finb[pieces * r:(pieces + 1) * r])
    for k, ref in enumerate((gwq_ref, gwk_ref, gwv_ref)):
        for c in range(2):
            for pr in range(2):
                at = (2 * c + pr) * 128
                ref[:, at:at + 128] = fold(gq[c, pr, :, 128 * k:128 * k + 128])


def finish(F, lo, gt, fina, finb, gq, hidden):
    width = lo.shape[2]
    r, ru = width // F, hidden // F
    shapes = [(r, width)] * 4 + [(r, hidden), (ru, width)]
    return pl.pallas_call(
        finish_kernel,
        out_shape=[jax.ShapeDtypeStruct(lo.shape, bf16), jax.ShapeDtypeStruct(gt.shape, bf16)]
        + [jax.ShapeDtypeStruct(s, f32) for s in shapes],
        in_specs=[VM] * 5,
        out_specs=[VM] * 8,
        name="finish",
    )(lo, gt, fina, finb, gq)


def on_device(tokens, parents, n1g, n1b, wq, wk, wv, wo, ob, n2g, n2b, wi, ib, wu, ub, cotangent):
    F = lax.axis_size("fsdp")
    fi = lax.axis_index("fsdp")
    place = (fi + 2) % F
    half = (place % 4) // 2
    quad = lax.axis_index("dp") * (F // 4) + place // 4
    parent_row = parents[quad, half]
    _, _, rows, width = tokens.shape

    n = n1g.shape[0]
    vec = jnp.concatenate([n1g, n1b, ob, n2g, n2b, ub, ib])
    vec = lax.reduce_precision(vec, 8, 7)
    vec = jnp.broadcast_to(jnp.pad(vec, (0, -vec.shape[0] % 128)), (8, vec.shape[0] + -vec.shape[0] % 128))
    hidden = wi.shape[1]
    ru = hidden // F
    (a1T, kaug, v, kT, qn, qT, oT, lse, wc, wo_own, xs, dxl, dx2, ga, gb, lo, vin, vrows) = first(
        F, parent_row, tokens[0], cotangent[0], (wq, wk, wv, wo, wi, wu), vec, n)
    gt, gq, fina, finb, vout = last(
        F, lax.axis_size("dp"), parent_row, (a1T, kaug, v, kT, qn, qT, oT, lse), wc, wo_own, xs, dxl, dx2,
        ga.reshape(F // 2, 2, -1, width), gb.reshape(F // 2, 2, -1, width), vin, vrows)
    lo, gt, gwq, gwk, gwv, gwo, gwi, gwu = finish(F, lo, gt, fina, finb, gq, hidden)
    sv = lax.dynamic_slice_in_dim(vout[:6], fi * n, n, 1)
    sib = lax.dynamic_slice_in_dim(vout[6:6 + hidden // width].reshape(-1), fi * ru, ru, 0)
    return (lo[None], gt[None], sv[0], sv[1], gwq, gwk, gwv, gwo, sv[2], sv[3], sv[4], gwi, sib, gwu, sv[5])


def solution(mesh):
    tok = P(("dp", "fsdp"), None, None, None)
    v, m = P("fsdp"), P("fsdp", None)
    return jax.shard_map(
        on_device,
        mesh=mesh,
        in_specs=(tok, P(), v, v, m, m, m, m, v, v, v, m, v, m, v, tok),
        out_specs=(tok, tok, v, v, m, m, m, m, v, v, v, m, v, m, v),
        check_vma=False,
    )
```
